32 devices in a mesh: batch: 8 (over z, core), rows: 4 (over y, x).
Axes of the slice: x: 2, y: 2, z: 4, core: 2. Of those that a mesh axis runs over, the one named last changes fastest.
Arguments:
- x_clean: float32 [1024, 3, 16, 16], P('batch', None, 'rows'), may hold values from -1 to 1
- noise: float32 [1024, 3, 16, 16], P('batch', None, 'rows'), may hold values from -5 to 5
- timesteps: int32 [1024], P('batch'), may hold values from 0 to 999
- keep_mask: int32 [1024, 16, 16, 256], P('batch', 'rows'), may hold values 0 or 1
- adam_step: int32 [1], replicated, may hold values from 2 to 20
- inlet_weight: float32 [27, 256], replicated, may hold values from -1.25 to 1.25
- kernel_weight: float32 [2, 2304, 256], replicated, may hold values from -0.125 to 0.125
- attention_weight: float32 [4, 256, 256], replicated, may hold values from -0.375 to 0.375
- time_weight: float32 [640, 512], replicated, may hold values from -0.25 to 0.25
- shift_weight: float32 [512, 256], replicated, may hold values from -0.25 to 0.25
- outlet_weight: float32 [3, 2304], replicated, may hold values from -0.125 to 0.125
- small_params: float32 [19, 256], replicated, may hold values from 0.5 to 1.5
- state_inlet: float32 [2, 27, 256], replicated, as said below
- state_kernel: float32 [2, 2, 2304, 256], P(None, None, 'batch'), as said below
- state_attention: float32 [2, 4, 256, 256], P(None, None, 'batch'), as said below
- state_time: float32 [2, 640, 512], replicated, as said below
- state_shift: float32 [2, 512, 256], replicated, as said below
- state_outlet: float32 [2, 3, 2304], replicated, as said below
- state_small: float32 [2, 19, 256], replicated, as said below
- average_inlet: float32 [27, 256], replicated, may hold values from -1.25 to 1.25
- average_kernel: float32 [2, 2304, 256], P(None, 'batch'), may hold values from -0.125 to 0.125
- average_attention: float32 [4, 256, 256], P(None, 'batch'), may hold values from -0.375 to 0.375
- average_time: float32 [640, 512], replicated, may hold values from -0.25 to 0.25
- average_shift: float32 [512, 256], replicated, may hold values from -0.25 to 0.25
- average_outlet: float32 [3, 2304], replicated, may hold values from -0.125 to 0.125
- average_small: float32 [19, 256], replicated, may hold values from 0.5 to 1.5
Outputs:
- updated_inlet: float32 [2, 27, 256], replicated
- updated_kernel: float32 [2, 2, 2304, 256], replicated
- updated_attention: float32 [2, 4, 256, 256], replicated
- updated_time: float32 [2, 640, 512], replicated
- updated_shift: float32 [2, 512, 256], replicated
- updated_outlet: float32 [2, 3, 2304], replicated
- updated_small: float32 [2, 19, 256], replicated
- first_inlet: float32 [27, 256], replicated
- first_kernel: float32 [2, 2304, 256], P(None, 'batch')
- first_attention: float32 [4, 256, 256], P(None, 'batch')
- first_time: float32 [640, 512], replicated
- first_shift: float32 [512, 256], replicated
- first_outlet: float32 [3, 2304], replicated
- first_small: float32 [19, 256], replicated
- second_inlet: float32 [27, 256], replicated
- second_kernel: float32 [2, 2304, 256], P(None, 'batch')
- second_attention: float32 [4, 256, 256], P(None, 'batch')
- second_time: float32 [640, 512], replicated
- second_shift: float32 [512, 256], replicated
- second_outlet: float32 [3, 2304], replicated
- second_small: float32 [19, 256], replicated
- loss: float32 [], replicated
- gradient_norm: float32 [], replicated
The draws below stay inside these ranges and needn't reach their ends.
Inputs may be any that keep to these rules, and one draw needn't show every extreme that they name: `state_inlet`: index 0 of each state holds first moments of both signs, index 1 positive second moments. `state_kernel`: as for state_inlet. `state_attention`: as for state_inlet. `state_time`: as for state_inlet. `state_shift`: as for state_inlet. `state_outlet`: as for state_inlet. `state_small`: as for state_inlet.
All inputs are finite; a program needn't handle non-finite values. No bound on the sum of `keep_mask` on one device may be relied on, other than what follows from the above.
Results may differ from the reference program's by a relative error of at most 0.0014.
The reference program's roundings to bfloat16 on the way count: a program that leaves them out, or rounds other values in their place, can miss the bound.
Values may be sent and summed in bfloat16 or wider, within the bound.
A program may use at most 640 MiB of HBM per device.

```python
import math
import jax
import jax.numpy as jnp
import numpy as np
from jax import lax

CHANNEL_COUNT = 256
G = 32
TD = 512
TS = 128
HH = 16
WW = 16
IMG_DEV = 128
IMAGES = 1024
N_BATCH = 8


def moment_pair(key, shape):
    first = 4e-06 * jnp.clip(jax.random.normal(jax.random.fold_in(key, 11), shape, jnp.float32), -5.0, 5.0)
    second = jnp.exp(jax.random.uniform(jax.random.fold_in(key, 12), shape, jnp.float32, math.log(1.3e-12), math.log(5.2e-12)))
    return jnp.stack([first, second])


def draw_state_inlet(key, part):
    return moment_pair(key, (27, CHANNEL_COUNT))


def draw_state_kernel(key, part):
    return moment_pair(key, (2, 9 * CHANNEL_COUNT, CHANNEL_COUNT))


def draw_state_attention(key, part):
    return moment_pair(key, (4, CHANNEL_COUNT, CHANNEL_COUNT))


def draw_state_time(key, part):
    return moment_pair(key, (TS + TD, TD))


def draw_state_shift(key, part):
    return moment_pair(key, (TD, CHANNEL_COUNT))


def draw_state_outlet(key, part):
    return moment_pair(key, (3, 9 * CHANNEL_COUNT))


def draw_state_small(key, part):
    return moment_pair(key, (19, CHANNEL_COUNT))


def set_ends(entries, rng, least, high):
    index_at = [jax.random.randint(jax.random.fold_in(rng, axis), (), 0, length) for axis, length in enumerate(entries.shape)]
    longest = entries.shape.index(max(entries.shape))
    next_to = index_at[:longest] + [(index_at[longest] + 1) % entries.shape[longest]] + index_at[longest + 1:]
    return entries.at[tuple(index_at)].set(least).at[tuple(next_to)].set(high)


def block_scale(own_key, dims, cuts, least, top_value):
    def one(position, parts):
        heights = jax.random.uniform(jax.random.fold_in(jax.random.fold_in(own_key, 6), position), (parts,), jnp.float32, least / len(cuts), top_value / len(cuts))
        return jnp.repeat(jnp.exp(heights), dims[position] // parts).reshape((-1,) + (1,) * (len(dims) - position - 1))

    level = one(*cuts[0])
    for cut in cuts[1:]:
        level = level * one(*cut)
    return level


def rank_bounds(number_of, skew):
    loads = [(1 << 20) // math.isqrt(rank ** skew) + 1 for rank in range(1, number_of + 1)]
    scale = 1 + sum(loads) // (1 << 30)
    return np.cumsum(np.array([max(1, weight // scale) for weight in loads]))


def ranked(own_key, dims, count, slope):
    listing = rank_bounds(count, slope)
    ticket = jax.random.randint(jax.random.fold_in(own_key, 1), dims, 0, int(listing[count - 1]))
    standing = jnp.searchsorted(jnp.asarray(listing, jnp.int32), ticket, side="right")
    return jax.random.permutation(jax.random.fold_in(own_key, 2), count)[standing].astype(jnp.int32)


def scatter_about(rng, dims, scale, most, split=(), held_as=jnp.bfloat16):
    result = jax.random.normal(rng, dims, jnp.float32) * scale
    if len(split) > 0:
        result = block_scale(rng, dims, split, -0.22, 0.18) * result
    return jnp.clip(result, min=-most, max=most).astype(held_as)


def setup_inputs(seed: int = 0) -> dict:
    seeds = jax.random.split(jax.random.key(seed), 27)
    x_clean = jnp.clip(jax.random.uniform(seeds[0], (IMAGES, 3, HH, WW), jnp.float32, -1.0, 1.0) * block_scale(seeds[0], (IMAGES, 3, HH, WW), ((0, 8), (2, 4)), -0.4, 0.0), -1.0, 1.0)
    noise = scatter_about(seeds[1], (IMAGES, 3, HH, WW), 1.0, 5.0, ((0, 8), (2, 4)), jnp.float32)
    timesteps = set_ends(ranked(seeds[2], (IMAGES,), 1000, 2), jax.random.fold_in(seeds[2], 3), 0, 999).astype(jnp.int32)
    keep_mask = set_ends((jax.random.randint(seeds[3], (IMAGES, HH, WW, CHANNEL_COUNT), 0, 10) < 9).astype(jnp.int32), jax.random.fold_in(seeds[3], 1), 0, 1)
    adam_step = jax.random.randint(seeds[4], (1,), 2, 21).astype(jnp.int32)
    inlet_weight = scatter_about(seeds[5], (27, CHANNEL_COUNT), 27 ** -0.5, 1.25, (), jnp.float32)
    kernel_weight = scatter_about(seeds[6], (2, 9 * CHANNEL_COUNT, CHANNEL_COUNT), (9 * CHANNEL_COUNT) ** -0.5, 0.125, (), jnp.float32)
    attention_weight = scatter_about(seeds[7], (4, CHANNEL_COUNT, CHANNEL_COUNT), CHANNEL_COUNT ** -0.5, 0.375, (), jnp.float32)
    time_weight = scatter_about(seeds[8], (TS + TD, TD), TD ** -0.5, 0.25, (), jnp.float32)
    shift_weight = scatter_about(seeds[9], (TD, CHANNEL_COUNT), TD ** -0.5, 0.25, (), jnp.float32)
    outlet_weight = scatter_about(seeds[10], (3, 9 * CHANNEL_COUNT), (9 * CHANNEL_COUNT) ** -0.5, 0.125, (), jnp.float32)
    small_params = jnp.clip(1.0 + 0.1 * jax.random.normal(seeds[11], (19, CHANNEL_COUNT), jnp.float32), 0.5, 1.5)
    state_inlet = draw_state_inlet(jax.random.fold_in(seeds[26], 71), 0)
    state_kernel = draw_state_kernel(jax.random.fold_in(seeds[26], 71), 0)
    state_attention = draw_state_attention(jax.random.fold_in(seeds[26], 71), 0)
    state_time = draw_state_time(jax.random.fold_in(seeds[26], 71), 0)
    state_shift = draw_state_shift(jax.random.fold_in(seeds[26], 71), 0)
    state_outlet = draw_state_outlet(jax.random.fold_in(seeds[26], 71), 0)
    state_small = draw_state_small(jax.random.fold_in(seeds[26], 71), 0)
    average_inlet = scatter_about(seeds[19], (27, CHANNEL_COUNT), 27 ** -0.5, 1.25, (), jnp.float32)
    average_kernel = scatter_about(seeds[20], (2, 9 * CHANNEL_COUNT, CHANNEL_COUNT), (9 * CHANNEL_COUNT) ** -0.5, 0.125, ((1, 8),), jnp.float32)
    average_attention = scatter_about(seeds[21], (4, CHANNEL_COUNT, CHANNEL_COUNT), CHANNEL_COUNT ** -0.5, 0.375, ((1, 8),), jnp.float32)
    average_time = scatter_about(seeds[22], (TS + TD, TD), TD ** -0.5, 0.25, (), jnp.float32)
    average_shift = scatter_about(seeds[23], (TD, CHANNEL_COUNT), TD ** -0.5, 0.25, (), jnp.float32)
    average_outlet = scatter_about(seeds[24], (3, 9 * CHANNEL_COUNT), (9 * CHANNEL_COUNT) ** -0.5, 0.125, (), jnp.float32)
    average_small = jnp.clip(1.0 + 0.1 * jax.random.normal(seeds[25], (19, CHANNEL_COUNT), jnp.float32), 0.5, 1.5)
    return dict(x_clean=x_clean, noise=noise, timesteps=timesteps, keep_mask=keep_mask, adam_step=adam_step, inlet_weight=inlet_weight, kernel_weight=kernel_weight, attention_weight=attention_weight, time_weight=time_weight, shift_weight=shift_weight, outlet_weight=outlet_weight, small_params=small_params, state_inlet=state_inlet, state_kernel=state_kernel, state_attention=state_attention, state_time=state_time, state_shift=state_shift, state_outlet=state_outlet, state_small=state_small, average_inlet=average_inlet, average_kernel=average_kernel, average_attention=average_attention, average_time=average_time, average_shift=average_shift, average_outlet=average_outlet, average_small=average_small)


@jax.custom_vjp
def lower_precision(v):
    return lax.optimization_barrier(v.astype(jnp.bfloat16)).astype(jnp.float32)

@jax.custom_vjp
def lower_precision_backward(v):
    return v

def low_keep(v):
    return (lower_precision(v), None)

def low_pass(kept, grad):
    return (grad,)

def back_keep(v):
    return (v, None)

def back_low(kept, grad):
    return (lower_precision(grad),)
lower_precision.defvjp(low_keep, low_pass)
lower_precision_backward.defvjp(back_keep, back_low)
HIGH_PRECISION = lax.Precision.HIGHEST
CLIP = 0.05
GAMMA = 5.0
KEEP = 0.9
EPS_NORM = 1e-05
BETA_ONE = 0.9
BETA_TWO = 0.999
EPS_ADAM = 1e-08
DECAY = 0.01
EMA_TOP = 0.9999
RATES = (0.1, 0.01, 0.03, 0.05, 0.02, 0.01, 0.2)

def alpha_bars(timesteps):
    steps_all = jnp.arange(1000).astype(jnp.float32)
    beta_rates = 0.0001 + (0.02 - 0.0001) * steps_all / 999.0
    bar_table = jnp.exp(jnp.cumsum(jnp.log(1.0 - beta_rates)))
    one_hot = (timesteps[:, None] == jnp.arange(1000).astype(jnp.int32)[None, :]).astype(jnp.float32)
    return lax.optimization_barrier(jnp.sum(one_hot * bar_table[None, :], axis=1))

def sinusoid(timesteps, width):
    half = width // 2
    rates = jnp.exp(-math.log(10000.0) * jnp.arange(half).astype(jnp.float32) / (half - 1))
    angles = timesteps.astype(jnp.float32)[:, None] * rates[None, :]
    return jnp.concatenate([jnp.sin(angles), jnp.cos(angles)], axis=1)

def patches(field):
    height, breadth = (field.shape[1], field.shape[2])
    padded = jnp.pad(field, ((0, 0), (1, 1), (1, 1), (0, 0)))
    return jnp.concatenate([padded[:, row_off:row_off + height, col_off:col_off + breadth, :] for row_off in range(3) for col_off in range(3)], axis=3)

def conv(field, weight):
    return jnp.einsum('bhwk,kc->bhwc', patches(field), weight, precision=HIGH_PRECISION)

def group_norm(field, gain, shift):
    images, height, breadth, chans = field.shape
    grouped = field.reshape(images, height * breadth, G, chans // G)
    mean = lax.optimization_barrier(jnp.mean(grouped, axis=(1, 3), keepdims=True))
    spread = lax.optimization_barrier(jnp.mean(grouped * grouped, axis=(1, 3), keepdims=True)) - mean * mean
    normed = (grouped - mean) * lax.rsqrt(spread + EPS_NORM)
    return normed.reshape(field.shape) * gain + shift

def image_loss(params, x_clean, noise, timesteps, keep_mask):
    inlet_weight, kernel_weight, attention_weight, time_weight, shift_weight, outlet_weight, small = params
    images = x_clean.shape[0]
    bars = alpha_bars(timesteps)
    level = bars[:, None, None, None]
    clean = jnp.transpose(x_clean, (0, 2, 3, 1))
    target = jnp.transpose(noise, (0, 2, 3, 1))
    noisy = lower_precision(jnp.sqrt(level) * clean + jnp.sqrt(1.0 - level) * target)
    embed = lower_precision(sinusoid(timesteps, TS))
    hidden_pre = jnp.dot(embed, lower_precision(time_weight[:TS]), precision=HIGH_PRECISION) + small[15:17].reshape(-1)
    hidden = lower_precision(jax.nn.silu(hidden_pre))
    time_emb = jnp.dot(hidden, lower_precision(time_weight[TS:]), precision=HIGH_PRECISION) + small[17:19].reshape(-1)
    time_act = lower_precision(jax.nn.silu(time_emb))
    time_shift = jnp.dot(time_act, lower_precision(shift_weight), precision=HIGH_PRECISION) + small[14]
    start = lower_precision_backward(conv(noisy, lower_precision(inlet_weight))) + small[8]
    first_act = lower_precision(jax.nn.silu(group_norm(start, small[0], small[4])))
    inner = lower_precision_backward(conv(first_act, lower_precision(kernel_weight[0]))) + small[9] + time_shift[:, None, None, :]
    second_act = lower_precision(jax.nn.silu(group_norm(inner, small[1], small[5])) * keep_mask.astype(jnp.float32) / KEEP)
    middle = start + lower_precision_backward(conv(second_act, lower_precision(kernel_weight[1]))) + small[10]
    tokens = lower_precision(group_norm(middle, small[2], small[6])).reshape(images, HH * WW, CHANNEL_COUNT)
    query_rows = lower_precision(lower_precision_backward(jnp.einsum('bpc,cd->bpd', tokens, lower_precision(attention_weight[0]), precision=HIGH_PRECISION) + small[11]))
    key_rows = lower_precision(lower_precision_backward(jnp.einsum('bpc,cd->bpd', tokens, lower_precision(attention_weight[1]), precision=HIGH_PRECISION)))
    value_rows = lower_precision(lower_precision_backward(jnp.einsum('bpc,cd->bpd', tokens, lower_precision(attention_weight[2]), precision=HIGH_PRECISION) + small[12]))
    attention_scores = lower_precision_backward(jnp.einsum('zji,zxi->zjx', query_rows, key_rows, precision=HIGH_PRECISION) * CHANNEL_COUNT ** (-0.5))
    attention_block = lower_precision(jax.nn.softmax(attention_scores, axis=-1))
    attended_tokens = lower_precision(lower_precision_backward(jnp.einsum('pvg,pgj->pvj', attention_block, value_rows, precision=HIGH_PRECISION)))
    branch = lower_precision_backward(jnp.einsum('bpc,cd->bpd', attended_tokens, lower_precision(attention_weight[3]), precision=HIGH_PRECISION)) + small[13]
    final = middle + branch.reshape(middle.shape)
    last_act = lower_precision(jax.nn.silu(group_norm(final, small[3], small[7])))
    predicted = lower_precision_backward(jnp.einsum('bhwk,ck->bhwc', patches(last_act), lower_precision(outlet_weight), precision=HIGH_PRECISION))
    ratio = bars / (1.0 - bars)
    snr_weight = jnp.minimum(ratio, GAMMA) / ratio
    errors = lax.optimization_barrier(jnp.mean((predicted - target) ** 2, axis=(1, 2, 3)))
    return jnp.sum(snr_weight * errors) / IMAGES

def adam(weight, state, average, grad, rate, count):
    first_new = BETA_ONE * state[0] + (1.0 - BETA_ONE) * grad
    second_new = BETA_TWO * state[1] + (1.0 - BETA_TWO) * grad * grad
    first_hat = first_new / (1.0 - BETA_ONE ** count)
    second_hat = second_new / (1.0 - BETA_TWO ** count)
    weight_new = weight - rate * (first_hat / (jnp.sqrt(second_hat) + EPS_ADAM) + DECAY * weight)
    keep = jnp.minimum(EMA_TOP, (1.0 + count) / (10.0 + count))
    average_new = keep * average + (1.0 - keep) * weight_new
    return (jnp.stack([weight_new, average_new]), first_new, second_new)

def reference(x_clean, noise, timesteps, keep_mask, adam_step, inlet_weight, kernel_weight, attention_weight, time_weight, shift_weight, outlet_weight, small_params, state_inlet, state_kernel, state_attention, state_time, state_shift, state_outlet, state_small, average_inlet, average_kernel, average_attention, average_time, average_shift, average_outlet, average_small):
    params = (inlet_weight, kernel_weight, attention_weight, time_weight, shift_weight, outlet_weight, small_params)
    states = (state_inlet, state_kernel, state_attention, state_time, state_shift, state_outlet, state_small)
    averages = (average_inlet, average_kernel, average_attention, average_time, average_shift, average_outlet, average_small)
    batches = tuple((array.reshape((N_BATCH, IMG_DEV) + array.shape[1:]) for array in (x_clean, noise, timesteps, keep_mask)))

    def total(weight_tensors):

        def one_group(carry, batch):
            return (carry + jax.checkpoint(image_loss)(weight_tensors, *batch), None)
        summed, unused = lax.scan(one_group, jnp.zeros((), jnp.float32), batches)
        return summed
    loss, pull = jax.vjp(total, params)
    grads = pull(jnp.ones((), jnp.float32))[0]
    norm = jnp.sqrt(sum((jnp.sum(item * item) for item in grads)))
    scale_factor = CLIP / jnp.maximum(norm, CLIP)
    count = adam_step[0].astype(jnp.float32)
    results = [adam(params[index], states[index], averages[index], grads[index] * scale_factor, RATES[index], count) for index in range(7)]
    return (results[0][0], results[1][0], results[2][0], results[3][0], results[4][0], results[5][0], results[6][0], results[0][1], results[1][1], results[2][1], results[3][1], results[4][1], results[5][1], results[6][1], results[0][2], results[1][2], results[2][2], results[3][2], results[4][2], results[5][2], results[6][2], loss, norm)
```

```python
import math

import jax
import jax.numpy as jnp
import numpy as np
from jax import lax
from jax.sharding import PartitionSpec as P

G = 32


HIGH_PRECISION = lax.Precision.HIGHEST
CLIP = 0.05
GAMMA = 5.0
KEEP = 0.9
EPS_NORM = 1e-05
BETA_ONE = 0.9
BETA_TWO = 0.999
EPS_ADAM = 1e-08
DECAY = 0.01
EMA_TOP = 0.9999
RATES = (0.1, 0.01, 0.03, 0.05, 0.02, 0.01, 0.2)


def bar_table():
    beta_rates = 0.0001 + (0.02 - 0.0001) * np.arange(1000, dtype=np.float64) / 999.0
    return np.exp(np.cumsum(np.log(1.0 - beta_rates))).astype(np.float32)


def alpha_bars(timesteps):
    one_hot = (timesteps[:, None] == jnp.arange(1000)[None, :]).astype(jnp.float32)
    return jnp.sum(one_hot * bar_table()[None, :], axis=1)


def sinusoid(timesteps, width):
    half = width // 2
    rates = jnp.exp(-math.log(10000.0) * jnp.arange(half).astype(jnp.float32) / (half - 1))
    angles = timesteps.astype(jnp.float32)[:, None] * rates[None, :]
    return jnp.concatenate([jnp.sin(angles), jnp.cos(angles)], axis=1)


DIMS = ("NHWC", "HWIO", "NHWC")


def conv_apply(field, weight):
    kernel = weight.reshape(3, 3, -1, weight.shape[1])
    return lax.conv_general_dilated(
        field, kernel, (1, 1), "SAME", dimension_numbers=DIMS, preferred_element_type=jnp.float32
    )


def conv_weight_grad(field, grad_out):
    out = lax.conv_general_dilated(
        field,
        grad_out,
        (1, 1),
        ((1, 1), (1, 1)),
        dimension_numbers=("CHWN", "IHWO", "HWNC"),
        preferred_element_type=jnp.float32,
    )
    return out.reshape(-1, grad_out.shape[3])


def conv_input_grad(grad_out, weight):
    inputs = weight.shape[0] // 9
    outputs = weight.shape[1]
    flipped = jnp.transpose(weight.reshape(9, inputs, outputs)[::-1], (0, 2, 1)).reshape(
        9 * outputs, inputs
    )
    return conv_apply(grad_out, flipped)


def grouped_view(field):
    return field.reshape(field.shape[0], -1, G, field.shape[3] // G)


def norm_stats(field):
    grouped = grouped_view(field)
    total = jnp.sum(grouped, axis=(1, 3))
    square = jnp.sum(grouped * grouped, axis=(1, 3))
    count = grouped.shape[1] * grouped.shape[3]
    mean = total / count
    return (mean, lax.rsqrt(square / count - mean * mean + EPS_NORM))


def standard(field, stats):
    grouped = grouped_view(field)
    return ((grouped - stats[0][:, None, :, None]) * stats[1][:, None, :, None]).reshape(
        field.shape
    )


def norm_back(grad_out, field, stats, gain):
    normed = standard(field, stats)
    gain_grad = jnp.sum(grad_out * normed, axis=(0, 1, 2))
    shift_grad = jnp.sum(grad_out, axis=(0, 1, 2))
    scaled = grouped_view(grad_out * gain)
    grouped = grouped_view(normed)
    first_sum = jnp.sum(scaled, axis=(1, 3))
    second_sum = jnp.sum(scaled * grouped, axis=(1, 3))
    count = grouped.shape[1] * grouped.shape[3]
    input_grad = (
        scaled
        - first_sum[:, None, :, None] / count
        - grouped * second_sum[:, None, :, None] / count
    ) * stats[1][:, None, :, None]
    return (input_grad.reshape(field.shape), gain_grad, shift_grad)


def swish_grad(pre):
    logistic = jax.nn.sigmoid(pre)
    return logistic * (1.0 + pre * (1.0 - logistic))


def attend(query_rows, key_rows, value_rows):
    attention_scores = jnp.einsum(
        "zji,zxi->zjx", query_rows, key_rows, preferred_element_type=jnp.float32
    ) * query_rows.shape[2] ** (-0.5)
    top = jnp.max(attention_scores, axis=-1, keepdims=True)
    expo = jnp.exp(attention_scores - top)
    total = jnp.sum(expo, axis=-1, keepdims=True)
    weight_tensors = (expo / total).astype(jnp.bfloat16)
    attended_tokens = jnp.einsum(
        "pvg,pgj->pvj", weight_tensors, value_rows, preferred_element_type=jnp.float32
    )
    return (attended_tokens.astype(jnp.bfloat16), top + jnp.log(total))


def attend_back(query_rows, key_rows, value_rows, logsum, gradient_mixed_tokens):
    scale_factor = query_rows.shape[2] ** (-0.5)
    attention_scores = (
        jnp.einsum("zji,zxi->zjx", query_rows, key_rows, preferred_element_type=jnp.float32)
        * scale_factor
    )
    softmax_probs = jnp.exp(attention_scores - logsum)
    gradient_softmax_probs = jnp.einsum(
        "zji,zxi->zjx", gradient_mixed_tokens, value_rows, preferred_element_type=jnp.float32
    )
    value_grad = jnp.einsum(
        "jio,jiz->joz",
        softmax_probs.astype(jnp.bfloat16),
        gradient_mixed_tokens,
        preferred_element_type=jnp.float32,
    )
    scores_gradient = (
        softmax_probs
        * (
            gradient_softmax_probs
            - jnp.sum(softmax_probs * gradient_softmax_probs, axis=-1, keepdims=True)
        )
    ).astype(jnp.bfloat16)
    query_grad = (
        jnp.einsum("pvg,pgj->pvj", scores_gradient, key_rows, preferred_element_type=jnp.float32)
        * scale_factor
    )
    key_grad = (
        jnp.einsum("jio,jiz->joz", scores_gradient, query_rows, preferred_element_type=jnp.float32)
        * scale_factor
    )
    return (query_grad, key_grad, value_grad)


def adam(weight, state, average, grad, rate, count):
    first_new = BETA_ONE * state[0] + (1.0 - BETA_ONE) * grad
    second_new = BETA_TWO * state[1] + (1.0 - BETA_TWO) * grad * grad
    first_hat = first_new / (1.0 - BETA_ONE**count)
    second_hat = second_new / (1.0 - BETA_TWO**count)
    weight_new = weight - rate * (first_hat / (jnp.sqrt(second_hat) + EPS_ADAM) + DECAY * weight)
    keep = jnp.minimum(EMA_TOP, (1.0 + count) / (10.0 + count))
    average_new = keep * average + (1.0 - keep) * weight_new
    return (jnp.stack([weight_new, average_new]), first_new, second_new)


def local(
    x_clean,
    noise,
    timesteps,
    keep_mask,
    adam_step,
    inlet_weight,
    kernel_weight,
    attention_weight,
    time_weight,
    shift_weight,
    outlet_weight,
    small_params,
    state_inlet,
    state_kernel,
    state_attention,
    state_time,
    state_shift,
    state_outlet,
    state_small,
    average_inlet,
    average_kernel,
    average_attention,
    average_time,
    average_shift,
    average_outlet,
    average_small,
):
    chans = kernel_weight.shape[2]
    width_sin = time_weight.shape[0] - time_weight.shape[1]
    rows = lax.axis_size("rows")
    own = timesteps.shape[0] // rows
    timesteps = lax.dynamic_slice_in_dim(timesteps, lax.axis_index("rows") * own, own, 0)
    x_clean = lax.all_to_all(x_clean, "rows", 0, 2, tiled=True)
    noise = lax.all_to_all(noise, "rows", 0, 2, tiled=True)
    keep_mask = lax.all_to_all(keep_mask.astype(jnp.bfloat16), "rows", 0, 1, tiled=True)
    bars = alpha_bars(timesteps)
    level = bars[:, None, None, None]
    clean = jnp.transpose(x_clean, (0, 2, 3, 1))
    target = jnp.transpose(noise, (0, 2, 3, 1))
    noisy = (jnp.sqrt(level) * clean + jnp.sqrt(1.0 - level) * target).astype(jnp.bfloat16)
    dropped = keep_mask.astype(jnp.float32) / KEEP
    images, height, breadth = (noisy.shape[0], noisy.shape[1], noisy.shape[2])
    inlet = inlet_weight.astype(jnp.bfloat16)
    kernels = kernel_weight.astype(jnp.bfloat16)
    projections = attention_weight.astype(jnp.bfloat16)
    time_low = time_weight.astype(jnp.bfloat16)
    shift_low = shift_weight.astype(jnp.bfloat16)
    outlet = outlet_weight.astype(jnp.bfloat16)
    embed = sinusoid(timesteps, width_sin).astype(jnp.bfloat16)
    hidden_pre = jnp.dot(
        embed, time_low[:width_sin], preferred_element_type=jnp.float32
    ) + small_params[15:17].reshape(-1)
    hidden = jax.nn.silu(hidden_pre).astype(jnp.bfloat16)
    time_emb = jnp.dot(
        hidden, time_low[width_sin:], preferred_element_type=jnp.float32
    ) + small_params[17:19].reshape(-1)
    time_act = jax.nn.silu(time_emb).astype(jnp.bfloat16)
    time_shift = jnp.dot(time_act, shift_low, preferred_element_type=jnp.float32) + small_params[14]
    padded_noisy = noisy
    start = conv_apply(padded_noisy, inlet) + small_params[8]
    stats_one = norm_stats(start)
    normed_one = standard(start, stats_one) * small_params[0] + small_params[4]
    padded_one = jax.nn.silu(normed_one).astype(jnp.bfloat16)
    inner = conv_apply(padded_one, kernels[0]) + small_params[9] + time_shift[:, None, None, :]
    stats_two = norm_stats(inner)
    normed_two = standard(inner, stats_two) * small_params[1] + small_params[5]
    padded_two = (jax.nn.silu(normed_two) * dropped).astype(jnp.bfloat16)
    middle = start + conv_apply(padded_two, kernels[1]) + small_params[10]
    stats_three = norm_stats(middle)
    tokens = (standard(middle, stats_three) * small_params[2] + small_params[6]).astype(
        jnp.bfloat16
    )
    tokens = tokens.reshape(images, height * breadth, chans)
    query_rows = (
        jnp.einsum("bpc,cd->bpd", tokens, projections[0], preferred_element_type=jnp.float32)
        + small_params[11]
    ).astype(jnp.bfloat16)
    key_rows = jnp.einsum(
        "bpc,cd->bpd", tokens, projections[1], preferred_element_type=jnp.float32
    ).astype(jnp.bfloat16)
    value_rows = (
        jnp.einsum("bpc,cd->bpd", tokens, projections[2], preferred_element_type=jnp.float32)
        + small_params[12]
    ).astype(jnp.bfloat16)
    all_keys, all_values = key_rows, value_rows
    attended_tokens, logsum = attend(query_rows, all_keys, all_values)
    branch = (
        jnp.einsum(
            "bpc,cd->bpd", attended_tokens, projections[3], preferred_element_type=jnp.float32
        )
        + small_params[13]
    )
    final = middle + branch.reshape(middle.shape)
    stats_four = norm_stats(final)
    normed_four = standard(final, stats_four) * small_params[3] + small_params[7]
    padded_four = jax.nn.silu(normed_four).astype(jnp.bfloat16)
    predicted = conv_apply(padded_four, outlet.T)
    ratio = bars / (1.0 - bars)
    snr_weight = jnp.minimum(ratio, GAMMA) / ratio
    denom = 3 * height * breadth * lax.axis_size("rows") * images * lax.axis_size("batch")
    errors = predicted - target
    loss_part = jnp.sum(snr_weight * jnp.sum(errors * errors, axis=(1, 2, 3))) / denom
    grad_pred = (2.0 * snr_weight[:, None, None, None] * errors / denom).astype(jnp.bfloat16)
    outlet_grad = conv_weight_grad(padded_four, grad_pred).T
    grad_four = conv_input_grad(grad_pred, outlet.T) * swish_grad(normed_four)
    grad_final, gain_four, shift_four = norm_back(grad_four, final, stats_four, small_params[3])
    grad_branch = grad_final.reshape(images, height * breadth, chans)
    branch_low = grad_branch.astype(jnp.bfloat16)
    out_proj_grad = jnp.einsum(
        "bpc,bpd->cd", attended_tokens, branch_low, preferred_element_type=jnp.float32
    )
    gradient_mixed_tokens = jnp.einsum(
        "bpd,cd->bpc", branch_low, projections[3], preferred_element_type=jnp.float32
    ).astype(jnp.bfloat16)
    local_dq, part_dk, part_dv = attend_back(
        query_rows, all_keys, all_values, logsum, gradient_mixed_tokens
    )
    sum_dk, sum_dv = part_dk, part_dv
    query_grad = local_dq.astype(jnp.bfloat16)
    key_grad = sum_dk.astype(jnp.bfloat16)
    value_grad = sum_dv.astype(jnp.bfloat16)
    projection_grads = jnp.stack(
        [
            jnp.einsum("bpc,bpd->cd", tokens, query_grad, preferred_element_type=jnp.float32),
            jnp.einsum("bpc,bpd->cd", tokens, key_grad, preferred_element_type=jnp.float32),
            jnp.einsum("bpc,bpd->cd", tokens, value_grad, preferred_element_type=jnp.float32),
            out_proj_grad,
        ]
    )
    grad_tokens = (
        jnp.einsum("bpd,cd->bpc", query_grad, projections[0], preferred_element_type=jnp.float32)
        + jnp.einsum("bpd,cd->bpc", key_grad, projections[1], preferred_element_type=jnp.float32)
        + jnp.einsum("bpd,cd->bpc", value_grad, projections[2], preferred_element_type=jnp.float32)
    )
    grad_norm_three, gain_three, shift_three = norm_back(
        grad_tokens.reshape(middle.shape), middle, stats_three, small_params[2]
    )
    grad_middle = grad_final + grad_norm_three
    middle_low = grad_middle.astype(jnp.bfloat16)
    kernel_two_grad = conv_weight_grad(padded_two, middle_low)
    grad_two = conv_input_grad(middle_low, kernels[1]) * dropped * swish_grad(normed_two)
    grad_inner, gain_two, shift_two = norm_back(grad_two, inner, stats_two, small_params[1])
    shift_time_grad = jnp.sum(grad_inner, axis=(1, 2))
    inner_low = grad_inner.astype(jnp.bfloat16)
    kernel_one_grad = conv_weight_grad(padded_one, inner_low)
    grad_one = conv_input_grad(inner_low, kernels[0]) * swish_grad(normed_one)
    grad_norm_one, gain_one, shift_one = norm_back(grad_one, start, stats_one, small_params[0])
    grad_start = grad_middle + grad_norm_one
    inlet_grad = conv_weight_grad(padded_noisy, grad_start.astype(jnp.bfloat16))
    shift_weight_grad = jnp.dot(
        time_act.astype(jnp.float32).T, shift_time_grad, precision=HIGH_PRECISION
    )
    grad_act = jnp.dot(
        shift_time_grad, shift_low.astype(jnp.float32).T, precision=HIGH_PRECISION
    ) * swish_grad(time_emb)
    time_two_grad = jnp.dot(hidden.astype(jnp.float32).T, grad_act, precision=HIGH_PRECISION)
    grad_hidden = jnp.dot(
        grad_act, time_low[width_sin:].astype(jnp.float32).T, precision=HIGH_PRECISION
    ) * swish_grad(hidden_pre)
    time_one_grad = jnp.dot(embed.astype(jnp.float32).T, grad_hidden, precision=HIGH_PRECISION)
    small_grad = jnp.concatenate(
        [
            jnp.stack(
                [
                    gain_one,
                    gain_two,
                    gain_three,
                    gain_four,
                    shift_one,
                    shift_two,
                    shift_three,
                    shift_four,
                    jnp.sum(grad_start, axis=(0, 1, 2)),
                    jnp.sum(grad_inner, axis=(0, 1, 2)),
                    jnp.sum(grad_middle, axis=(0, 1, 2)),
                    jnp.sum(query_grad.astype(jnp.float32), axis=(0, 1)),
                    jnp.sum(value_grad.astype(jnp.float32), axis=(0, 1)),
                    jnp.sum(grad_branch, axis=(0, 1)),
                    jnp.sum(shift_time_grad, axis=0),
                ]
            ),
            jnp.sum(grad_hidden, axis=0).reshape(2, chans),
            jnp.sum(grad_act, axis=0).reshape(2, chans),
        ],
        axis=0,
    )
    summed = lax.psum(
        (
            inlet_grad,
            jnp.stack([kernel_one_grad, kernel_two_grad]),
            projection_grads,
            jnp.concatenate([time_one_grad, time_two_grad], axis=0),
            shift_weight_grad,
            outlet_grad,
            small_grad,
            loss_part,
        ),
        ("batch", "rows"),
    )
    loss = summed[7]
    grads = summed[:7]
    norm = jnp.sqrt(sum((jnp.sum(item * item) for item in grads)))
    scale_factor = CLIP / jnp.maximum(norm, CLIP)
    count = adam_step[0].astype(jnp.float32)
    weight_tensors = (
        inlet_weight,
        kernel_weight,
        attention_weight,
        time_weight,
        shift_weight,
        outlet_weight,
        small_params,
    )
    states = (
        state_inlet,
        state_kernel,
        state_attention,
        state_time,
        state_shift,
        state_outlet,
        state_small,
    )
    averages = (
        average_inlet,
        average_kernel,
        average_attention,
        average_time,
        average_shift,
        average_outlet,
        average_small,
    )
    members = lax.axis_size("batch")
    mine = lax.axis_index("batch")
    results = [None] * 7
    for position in (1, 2):
        length = weight_tensors[position].shape[1] // members
        own_weight = lax.dynamic_slice_in_dim(weight_tensors[position], mine * length, length, 1)
        own_grad = lax.dynamic_slice_in_dim(grads[position], mine * length, length, 1)
        results[position] = adam(
            own_weight,
            states[position],
            averages[position],
            own_grad * scale_factor,
            RATES[position],
            count,
        )
    kernel_pair, attention_pair = (
        lax.all_gather(results[1][0], "batch", axis=2, tiled=True),
        lax.all_gather(results[2][0], "batch", axis=2, tiled=True),
    )
    results[1] = (kernel_pair, results[1][1], results[1][2])
    results[2] = (attention_pair, results[2][1], results[2][2])
    for position in (0, 3, 4, 5, 6):
        results[position] = adam(
            weight_tensors[position],
            states[position],
            averages[position],
            grads[position] * scale_factor,
            RATES[position],
            count,
        )
    return (
        results[0][0],
        results[1][0],
        results[2][0],
        results[3][0],
        results[4][0],
        results[5][0],
        results[6][0],
        results[0][1],
        results[1][1],
        results[2][1],
        results[3][1],
        results[4][1],
        results[5][1],
        results[6][1],
        results[0][2],
        results[1][2],
        results[2][2],
        results[3][2],
        results[4][2],
        results[5][2],
        results[6][2],
        loss,
        norm,
    )


def solution(mesh):
    return jax.shard_map(
        local,
        mesh=mesh,
        in_specs=(
            P("batch", None, "rows", None),
            P("batch", None, "rows", None),
            P("batch"),
            P("batch", "rows", None, None),
            P(),
            P(),
            P(),
            P(),
            P(),
            P(),
            P(),
            P(),
            P(),
            P(None, None, "batch", None),
            P(None, None, "batch", None),
            P(),
            P(),
            P(),
            P(),
            P(),
            P(None, "batch", None),
            P(None, "batch", None),
            P(),
            P(),
            P(),
            P(),
        ),
        out_specs=(
            P(),
            P(),
            P(),
            P(),
            P(),
            P(),
            P(),
            P(),
            P(None, "batch", None),
            P(None, "batch", None),
            P(),
            P(),
            P(),
            P(),
            P(),
            P(None, "batch", None),
            P(None, "batch", None),
            P(),
            P(),
            P(),
            P(),
            P(),
            P(),
        ),
        check_vma=False,
    )
```

```python
import math

import jax
import jax.numpy as jnp
import numpy as np
from jax import lax
from jax.experimental import pallas as pl
from jax.experimental.pallas import tpu as pltpu
from jax.sharding import PartitionSpec as P

G = 32


HIGH_PRECISION = lax.Precision.HIGHEST
CLIP = 0.05
GAMMA = 5.0
KEEP = 0.9
EPS_NORM = 1e-05
BETA_ONE = 0.9
BETA_TWO = 0.999
EPS_ADAM = 1e-08
DECAY = 0.01
EMA_TOP = 0.9999
VMEM_LIMIT = 60 << 20
CHUNK = 4
COUNT = 2048.0
RATES = (0.1, 0.01, 0.03, 0.05, 0.02, 0.01, 0.2)


def bar_table():
    beta_rates = 0.0001 + (0.02 - 0.0001) * np.arange(1000, dtype=np.float64) / 999.0
    return np.exp(np.cumsum(np.log(1.0 - beta_rates))).astype(np.float32)


def alpha_bars(timesteps):
    one_hot = (timesteps[:, None] == jnp.arange(1000)[None, :]).astype(jnp.float32)
    return jnp.sum(one_hot * bar_table()[None, :], axis=1)


def sinusoid(timesteps, width):
    half = width // 2
    rates = jnp.exp(-math.log(10000.0) * jnp.arange(half).astype(jnp.float32) / (half - 1))
    angles = timesteps.astype(jnp.float32)[:, None] * rates[None, :]
    return jnp.concatenate([jnp.sin(angles), jnp.cos(angles)], axis=1)


def swish_grad(pre):
    logistic = jax.nn.sigmoid(pre)
    return logistic * (1.0 + pre * (1.0 - logistic))


def wrap(shift, size):
    return shift % size


def tap_masks():
    lane = lax.broadcasted_iota(jnp.int32, (8, 256), 1)
    row, col = lane // 16, lane % 16
    masks = []
    for i in range(3):
        for j in range(3):
            ok = (row + (i - 1) >= 0) & (row + (i - 1) < 16) & (col + (j - 1) >= 0) & (col + (j - 1) < 16)
            masks.append(ok)
    return masks


def tap_stack(tile, masks, sign):
    parts = []
    for tap in range(9):
        step = sign * (16 * (tap // 3 - 1) + tap % 3 - 1)
        moved = tile if step == 0 else pltpu.roll(tile, wrap(-step, 256), 1)
        parts.append(jnp.where(masks[tap if sign > 0 else 8 - tap], moved, 0.0))
    parts.append(jnp.zeros_like(tile))
    return jnp.concatenate(parts, axis=0).astype(jnp.bfloat16)


def group_sum(rows):
    halves = []
    for half in range(2):
        part = rows[:, 128 * half : 128 * half + 128]
        lane = lax.broadcasted_iota(jnp.int32, part.shape, 1)
        for step in (1, 2, 4):
            upper = (lane // step) % 2 == 1
            part = part + jnp.where(upper, pltpu.roll(part, step, 1), pltpu.roll(part, 128 - step, 1))
        halves.append(part)
    return jnp.concatenate(halves, axis=1)


def col_sum(x):
    return jnp.sum(x, axis=0, keepdims=True)


def stats_of(fields):
    sums = jnp.concatenate([col_sum(x) for x in fields] + [col_sum(x * x) for x in fields], axis=0)
    both = group_sum(sums) / COUNT
    n = len(fields)
    mean = both[:n]
    spread = both[n:] - mean * mean
    return mean, lax.rsqrt(spread + EPS_NORM)


def logistic(z):
    return 0.5 * jnp.tanh(0.5 * z) + 0.5


def put_shifted(buf, c, y, not_first, not_last):
    buf[c, 16:272, 256:512] = y.astype(jnp.bfloat16)
    buf[c, 16:272, 0:256] = jnp.where(not_first, pltpu.roll(y, 1, 0), 0.0).astype(jnp.bfloat16)
    buf[c, 16:272, 512:768] = jnp.where(not_last, pltpu.roll(y, 255, 0), 0.0).astype(jnp.bfloat16)


def edge_masks():
    col = lax.broadcasted_iota(jnp.int32, (256, 256), 0) % 16
    return col != 0, col != 15


def stacked(buf, i):
    chunk = buf.shape[0]
    return buf[:, 16 * i : 16 * i + 256, :].reshape(chunk * 256, 768)


def dot(a, b, dims=((1,), (0,))):
    return lax.dot_general(a, b, (dims, ((), ())), preferred_element_type=jnp.float32)


NT = ((1,), (1,))
TN = ((0,), (0,))


def conv_shifted(buf, weight):
    field = jnp.concatenate([stacked(buf, i) for i in range(3)], axis=1)
    return dot(field, weight[...])


def zero_edges(buf):
    edge = jnp.zeros((buf.shape[0], 16, 768), jnp.bfloat16)
    buf[:, 0:16, :] = edge
    buf[:, 272:288, :] = edge


def first_kernel(noisy, tshift, inlet, kernel_one, small, start_out, inner_out, stats_out, buf):
    chunk = noisy.shape[0]

    @pl.when(pl.program_id(0) == 0)
    def _():
        zero_edges(buf)

    masks = tap_masks()
    not_first, not_last = edge_masks()
    starts = []
    for c in range(chunk):
        patch = tap_stack(noisy[c], masks, 1)
        start = dot(patch, inlet[...], TN) + small[8:9]
        start_out[c] = start
        starts.append(start)
    mean, rstd = stats_of(starts)
    for c in range(chunk):
        scale = rstd[c : c + 1] * small[0:1]
        z = starts[c] * scale + (small[4:5] - mean[c : c + 1] * scale)
        put_shifted(buf, c, z * logistic(z), not_first, not_last)
    inner_all = conv_shifted(buf, kernel_one)
    inners = []
    for c in range(chunk):
        inner = inner_all[256 * c : 256 * c + 256] + tshift[c]
        inner_out[c] = inner
        inners.append(inner)
    mean_two, rstd_two = stats_of(inners)
    for c in range(chunk):
        stats_out[c] = jnp.concatenate(
            [mean[c : c + 1], rstd[c : c + 1], mean_two[c : c + 1], rstd_two[c : c + 1]]
            + [jnp.zeros((4, 256), jnp.float32)],
            axis=0,
        )


def norm_grad(dys, fields, means, rstds, gain):
    n = len(dys)
    shift_sums, gain_sums = [], []
    for dy, x, mean, rstd in zip(dys, fields, means, rstds):
        shift_sums.append(col_sum(dy))
        gain_sums.append(col_sum(dy * (x * rstd - mean * rstd)))
    both = group_sum(jnp.concatenate(shift_sums + gain_sums, axis=0) * gain) / COUNT
    grads = []
    for c in range(n):
        rstd, mean = rstds[c], means[c]
        slope = -rstd * rstd * both[n + c : n + c + 1]
        base = -rstd * both[c : c + 1] - mean * slope
        grads.append(dys[c] * (rstd * gain) + (fields[c] * slope + base))
    return grads, sum(gain_sums), sum(shift_sums)


def second_kernel(
    coef,
    start_in,
    inner_in,
    stats_in,
    noisy,
    target,
    keep,
    kernel_one_flip,
    kernel_two,
    kernel_two_flip,
    qkv,
    qkv_t,
    proj,
    proj_t,
    outlet,
    small,
    bias_qkv,
    grad_one_out,
    grad_two_out,
    grad_qkv_out,
    grad_proj_out,
    grad_outlet_out,
    grad_inlet_out,
    grad_small_out,
    loss_out,
    tshift_grad_out,
    buf,
    grad_buf,
):
    chunk = noisy.shape[0]
    images = range(chunk)
    step = pl.program_id(0)
    sums = (
        grad_one_out,
        grad_two_out,
        grad_qkv_out,
        grad_proj_out,
        grad_outlet_out,
        grad_inlet_out,
        grad_small_out,
        loss_out,
    )

    @pl.when(step == 0)
    def _():
        zero_edges(buf)
        zero_edges(grad_buf)
        for ref in sums:
            ref[...] = jnp.zeros(ref.shape, jnp.float32)

    masks = tap_masks()
    not_first, not_last = edge_masks()

    def gain(k):
        return small[k : k + 1]

    def shift(k):
        return small[4 + k : 5 + k]

    def normed(x, mean, rstd, k):
        scale = rstd * gain(k)
        return x * scale + (shift(k) - mean * scale)

    def row(values, c):
        return values[c : c + 1]

    mean_one = [stats_in[c, 0:1] for c in images]
    rstd_one = [stats_in[c, 1:2] for c in images]
    mean_two = [stats_in[c, 2:3] for c in images]
    rstd_two = [stats_in[c, 3:4] for c in images]

    slope_two, act_two = [], []
    for c in images:
        z = normed(inner_in[c], mean_two[c], rstd_two[c], 1)
        s = logistic(z)
        kept = keep[c].astype(jnp.float32) * (1.0 / KEEP)
        act = z * s * kept
        slope_two.append(s * (1.0 + z * (1.0 - s)) * kept)
        act_two.append(act.astype(jnp.bfloat16))
        put_shifted(buf, c, act, not_first, not_last)
    conv_two = conv_shifted(buf, kernel_two)
    middle = [start_in[c] + conv_two[256 * c : 256 * c + 256] + small[10:11] for c in images]
    mean, rstd = stats_of(middle)
    mean_three = [row(mean, c) for c in images]
    rstd_three = [row(rstd, c) for c in images]

    tokens = [normed(middle[c], mean_three[c], rstd_three[c], 2).astype(jnp.bfloat16) for c in images]
    qkv_all = (dot(jnp.concatenate(tokens, axis=0), qkv[...]) + bias_qkv[0:1]).astype(jnp.bfloat16)
    probs, probs_low, mixed = [], [], []
    scale = 256 ** (-0.5)
    for c in images:
        three = qkv_all[256 * c : 256 * c + 256]
        q, k, v = three[:, 0:256], three[:, 256:512], three[:, 512:768]
        scores = dot(q, k, NT) * scale
        expo = jnp.exp(scores - jnp.max(scores, axis=1, keepdims=True))
        p = expo * (1.0 / jnp.sum(expo, axis=1, keepdims=True))
        probs.append(p)
        probs_low.append(p.astype(jnp.bfloat16))
        mixed.append(dot(probs_low[c], v).astype(jnp.bfloat16))
    branch = dot(jnp.concatenate(mixed, axis=0), proj[...])
    final = [middle[c] + branch[256 * c : 256 * c + 256] + small[13:14] for c in images]
    mean, rstd = stats_of(final)
    mean_four = [row(mean, c) for c in images]
    rstd_four = [row(rstd, c) for c in images]

    grad_four = []
    outlet_sum, loss_sum = 0.0, 0.0
    for c in images:
        z = normed(final[c], mean_four[c], rstd_four[c], 3)
        s = logistic(z)
        act = (z * s).astype(jnp.bfloat16)
        taps = dot(outlet[...], act, NT)
        predicted = 0.0
        for tap in range(9):
            move = 16 * (tap // 3 - 1) + tap % 3 - 1
            part = taps[8 * tap : 8 * tap + 8]
            part = part if move == 0 else pltpu.roll(part, wrap(-move, 256), 1)
            predicted = predicted + jnp.where(masks[tap], part, 0.0)
        error = predicted - target[c]
        weight = coef[step * chunk + c]
        loss_sum = loss_sum + (0.5 * weight) * (error * error)
        grad_pred = (weight * error).astype(jnp.bfloat16).astype(jnp.float32)
        spread = tap_stack(grad_pred, masks, -1)
        outlet_sum = outlet_sum + dot(spread, act)
        grad_four.append(dot(spread, outlet[...], TN) * (s * (1.0 + z * (1.0 - s))))
    loss_out[...] += loss_sum
    grad_outlet_out[...] += outlet_sum
    grad_final, gain_four, shift_four = norm_grad(grad_four, final, mean_four, rstd_four, gain(3))

    branch_low = [g.astype(jnp.bfloat16) for g in grad_final]
    branch_all = jnp.concatenate(branch_low, axis=0)
    grad_proj_out[...] += dot(jnp.concatenate(mixed, axis=0), branch_all, TN)
    grad_mixed = dot(branch_all, proj_t[...]).astype(jnp.bfloat16)
    grad_qkv = []
    for c in images:
        three = qkv_all[256 * c : 256 * c + 256]
        q, k, v = three[:, 0:256], three[:, 256:512], three[:, 512:768]
        dm = grad_mixed[256 * c : 256 * c + 256]
        dp = dot(dm, v, NT)
        dv = dot(probs_low[c], dm, TN)
        p = probs[c]
        ds = (p * (dp - jnp.sum(p * dp, axis=1, keepdims=True))).astype(jnp.bfloat16)
        dq = dot(ds, k) * scale
        dk = dot(ds, q, TN) * scale
        grad_qkv.append(jnp.concatenate([dq, dk, dv], axis=1).astype(jnp.bfloat16))
    grad_qkv_all = jnp.concatenate(grad_qkv, axis=0)
    grad_qkv_out[...] += dot(jnp.concatenate(tokens, axis=0), grad_qkv_all, TN)
    bias_sums = col_sum(grad_qkv_all.astype(jnp.float32))
    grad_tokens = dot(grad_qkv_all, qkv_t[...])
    grad_tokens = [grad_tokens[256 * c : 256 * c + 256] for c in images]
    grad_norm, gain_three, shift_three = norm_grad(
        grad_tokens, middle, mean_three, rstd_three, gain(2)
    )
    grad_middle = [grad_final[c] + grad_norm[c] for c in images]

    for c in images:
        put_shifted(grad_buf, c, grad_middle[c], not_first, not_last)
    field = jnp.concatenate(act_two, axis=0)
    for i in range(3):
        grad_two_out[i] += dot(field, stacked(grad_buf, i), TN)
    grad_act = conv_shifted(grad_buf, kernel_two_flip)
    grad_two = [grad_act[256 * c : 256 * c + 256] * slope_two[c] for c in images]
    grad_inner, gain_two, shift_two = norm_grad(
        grad_two, [inner_in[c] for c in images], mean_two, rstd_two, gain(1)
    )

    for c in images:
        put_shifted(grad_buf, c, grad_inner[c], not_first, not_last)
    act_one, slope_one = [], []
    for c in images:
        z = normed(start_in[c], mean_one[c], rstd_one[c], 0)
        s = logistic(z)
        act_one.append((z * s).astype(jnp.bfloat16))
        slope_one.append(s * (1.0 + z * (1.0 - s)))
    field = jnp.concatenate(act_one, axis=0)
    for i in range(3):
        grad_one_out[i] += dot(field, stacked(grad_buf, i), TN)
    grad_act = conv_shifted(grad_buf, kernel_one_flip)
    grad_one = [grad_act[256 * c : 256 * c + 256] * slope_one[c] for c in images]
    grad_norm, gain_one, shift_one = norm_grad(
        grad_one, [start_in[c] for c in images], mean_one, rstd_one, gain(0)
    )
    grad_start = [grad_middle[c] + grad_norm[c] for c in images]
    inlet_sum = 0.0
    for c in images:
        patch = tap_stack(noisy[c], masks, 1)
        inlet_sum = inlet_sum + dot(patch, grad_start[c].astype(jnp.bfloat16))
    grad_inlet_out[...] += inlet_sum
    inner_sums = [col_sum(grad_inner[c]) for c in images]
    for c in images:
        tshift_grad_out[c] = inner_sums[c]
    grad_small_out[...] += jnp.concatenate(
        [
            gain_one,
            gain_two,
            gain_three,
            gain_four,
            shift_one,
            shift_two,
            shift_three,
            shift_four,
            sum(col_sum(g) for g in grad_start),
            sum(inner_sums),
            sum(col_sum(g) for g in grad_middle),
            bias_sums[:, 0:256],
            bias_sums[:, 512:768],
            sum(col_sum(g) for g in grad_final),
            jnp.zeros((2, 256), jnp.float32),
        ],
        axis=0,
    )


def resident(shape):
    return pl.BlockSpec(shape, lambda i: (0,) * len(shape), pipeline_mode=pl.Buffered(1))


def per_chunk(chunk, *tail):
    return pl.BlockSpec((chunk,) + tail, lambda i: (i,) + (0,) * len(tail))


def forward_part(chunk, noisy, tshift, inlet, kernel_one, small):
    n = noisy.shape[0]
    return pl.pallas_call(
        first_kernel,
        grid=(n // chunk,),
        in_specs=[
            per_chunk(chunk, 8, 256),
            per_chunk(chunk, 1, 256),
            resident(inlet.shape),
            resident(kernel_one.shape),
            resident(small.shape),
        ],
        out_specs=[
            per_chunk(chunk, 256, 256),
            per_chunk(chunk, 256, 256),
            per_chunk(chunk, 8, 256),
        ],
        out_shape=[
            jax.ShapeDtypeStruct((n, 256, 256), jnp.float32),
            jax.ShapeDtypeStruct((n, 256, 256), jnp.float32),
            jax.ShapeDtypeStruct((n, 8, 256), jnp.float32),
        ],
        scratch_shapes=[pltpu.VMEM((chunk, 288, 768), jnp.bfloat16)],
        compiler_params=pltpu.CompilerParams(vmem_limit_bytes=VMEM_LIMIT),
        cost_estimate=pl.CostEstimate(
            flops=2 * n * 256 * 256 * 2400, bytes_accessed=n * 1 << 19, transcendentals=n * 1 << 16
        ),
        name="forward_part",
    )(noisy, tshift, inlet, kernel_one, small)


def main_part(chunk, coef, start, inner, stats, noisy, target, keep, weights, small, bias_qkv):
    n = noisy.shape[0]
    grads = [(3, 256, 768), (3, 256, 768), (256, 768), (256, 256), (80, 256), (80, 256), (16, 256), (8, 256)]
    return pl.pallas_call(
        second_kernel,
        grid=(n // chunk,),
        in_specs=[
            pl.BlockSpec(memory_space=pltpu.SMEM),
            per_chunk(chunk, 256, 256),
            per_chunk(chunk, 256, 256),
            per_chunk(chunk, 8, 256),
            per_chunk(chunk, 8, 256),
            per_chunk(chunk, 8, 256),
            per_chunk(chunk, 256, 256),
        ]
        + [resident(w.shape) for w in weights]
        + [resident(small.shape), resident(bias_qkv.shape)],
        out_specs=[resident(g) for g in grads] + [per_chunk(chunk, 1, 256)],
        out_shape=[jax.ShapeDtypeStruct(g, jnp.float32) for g in grads]
        + [jax.ShapeDtypeStruct((n, 1, 256), jnp.float32)],
        scratch_shapes=[pltpu.VMEM((chunk, 288, 768), jnp.bfloat16)] * 2,
        compiler_params=pltpu.CompilerParams(vmem_limit_bytes=VMEM_LIMIT),
        cost_estimate=pl.CostEstimate(
            flops=70 * n * 2 * 256**3, bytes_accessed=n * 5 << 17, transcendentals=n * 5 << 16
        ),
        name="main_part",
    )(coef, start, inner, stats, noisy, target, keep, *weights, small, bias_qkv)


def rows_first(weight):
    inputs, outputs = weight.shape[0] // 9, weight.shape[1]
    flipped = jnp.transpose(weight.reshape(9, inputs, outputs)[::-1], (0, 2, 1))
    return flipped.reshape(9 * outputs, inputs)


def taps_of(grad):
    parts = grad.reshape(3, 256, 3, 256)[::-1, :, ::-1]
    return jnp.transpose(parts, (0, 2, 1, 3)).reshape(2304, 256)


def padded_taps(rows):
    padded = jnp.pad(rows.reshape(9, 3, 256), ((0, 1), (0, 5), (0, 0)))
    return padded.reshape(80, 256)


def unpadded_taps(rows):
    return rows.reshape(10, 8, 256)[:9, :3]


def adam(weight, state, average, grad, rate, count):
    first_new = BETA_ONE * state[0] + (1.0 - BETA_ONE) * grad
    second_new = BETA_TWO * state[1] + (1.0 - BETA_TWO) * grad * grad
    first_hat = first_new / (1.0 - BETA_ONE**count)
    second_hat = second_new / (1.0 - BETA_TWO**count)
    weight_new = weight - rate * (first_hat / (jnp.sqrt(second_hat) + EPS_ADAM) + DECAY * weight)
    keep = jnp.minimum(EMA_TOP, (1.0 + count) / (10.0 + count))
    average_new = keep * average + (1.0 - keep) * weight_new
    return (jnp.stack([weight_new, average_new]), first_new, second_new)


def local(
    x_clean,
    noise,
    timesteps,
    keep_mask,
    adam_step,
    inlet_weight,
    kernel_weight,
    attention_weight,
    time_weight,
    shift_weight,
    outlet_weight,
    small_params,
    state_inlet,
    state_kernel,
    state_attention,
    state_time,
    state_shift,
    state_outlet,
    state_small,
    average_inlet,
    average_kernel,
    average_attention,
    average_time,
    average_shift,
    average_outlet,
    average_small,
):
    chans = kernel_weight.shape[2]
    width_sin = time_weight.shape[0] - time_weight.shape[1]
    rows = lax.axis_size("rows")
    own = timesteps.shape[0] // rows
    timesteps = lax.dynamic_slice_in_dim(timesteps, lax.axis_index("rows") * own, own, 0)
    pair = lax.all_to_all(jnp.concatenate([x_clean, noise], axis=1), "rows", 0, 2, tiled=True)
    keep = lax.all_to_all(keep_mask.astype(jnp.bfloat16), "rows", 0, 1, tiled=True)
    keep = keep.reshape(own, -1, chans)
    bars = alpha_bars(timesteps)
    level = bars[:, None, None]
    pair = jnp.pad(pair.reshape(own, 2, 3, -1), ((0, 0), (0, 0), (0, 5), (0, 0)))
    clean, target = pair[:, 0], pair[:, 1]
    noisy = (jnp.sqrt(level) * clean + jnp.sqrt(1.0 - level) * target).astype(jnp.bfloat16)
    noisy = noisy.astype(jnp.float32)
    kernels = kernel_weight.astype(jnp.bfloat16)
    projections = attention_weight.astype(jnp.bfloat16)
    time_low = time_weight.astype(jnp.bfloat16)
    shift_low = shift_weight.astype(jnp.bfloat16)
    inlet = padded_taps(inlet_weight).astype(jnp.bfloat16)
    outlet = padded_taps(
        jnp.transpose(outlet_weight.reshape(3, 9, chans), (1, 0, 2)).reshape(27, chans)
    ).astype(jnp.bfloat16)
    qkv = jnp.concatenate([projections[0], projections[1], projections[2]], axis=1)
    embed = sinusoid(timesteps, width_sin).astype(jnp.bfloat16)
    hidden_pre = jnp.dot(
        embed, time_low[:width_sin], preferred_element_type=jnp.float32
    ) + small_params[15:17].reshape(-1)
    hidden = jax.nn.silu(hidden_pre).astype(jnp.bfloat16)
    time_emb = jnp.dot(
        hidden, time_low[width_sin:], preferred_element_type=jnp.float32
    ) + small_params[17:19].reshape(-1)
    time_act = jax.nn.silu(time_emb).astype(jnp.bfloat16)
    time_shift = jnp.dot(time_act, shift_low, preferred_element_type=jnp.float32) + small_params[14]
    ratio = bars / (1.0 - bars)
    snr_weight = jnp.minimum(ratio, GAMMA) / ratio
    denom = 3 * noisy.shape[2] * own * rows * lax.axis_size("batch")
    coef = 2.0 * snr_weight / denom
    start, inner, stats = forward_part(
        CHUNK, noisy, (time_shift + small_params[9])[:, None, :], inlet, kernels[0], small_params
    )
    bias_qkv = jnp.concatenate([small_params[11], jnp.zeros_like(small_params[0]), small_params[12]])
    (
        kernel_one_grad,
        kernel_two_grad,
        grad_qkv,
        grad_proj,
        grad_outlet,
        grad_inlet,
        grad_small,
        loss_rows,
        shift_time_grad,
    ) = main_part(
        CHUNK,
        coef,
        start,
        inner,
        stats,
        noisy,
        target,
        keep,
        (
            rows_first(kernels[0]),
            kernels[1],
            rows_first(kernels[1]),
            qkv,
            qkv.T,
            projections[3],
            projections[3].T,
            outlet,
        ),
        small_params,
        bias_qkv[None],
    )
    shift_time_grad = shift_time_grad[:, 0]
    loss_part = jnp.sum(loss_rows)
    inlet_grad = unpadded_taps(grad_inlet).reshape(27, chans)
    outlet_grad = jnp.transpose(unpadded_taps(grad_outlet), (1, 0, 2)).reshape(3, 9 * chans)
    projection_grads = jnp.stack(
        [grad_qkv[:, :chans], grad_qkv[:, chans : 2 * chans], grad_qkv[:, 2 * chans :], grad_proj]
    )
    shift_weight_grad = jnp.dot(
        time_act.astype(jnp.float32).T, shift_time_grad, precision=HIGH_PRECISION
    )
    grad_act = jnp.dot(
        shift_time_grad, shift_low.astype(jnp.float32).T, precision=HIGH_PRECISION
    ) * swish_grad(time_emb)
    time_two_grad = jnp.dot(hidden.astype(jnp.float32).T, grad_act, precision=HIGH_PRECISION)
    grad_hidden = jnp.dot(
        grad_act, time_low[width_sin:].astype(jnp.float32).T, precision=HIGH_PRECISION
    ) * swish_grad(hidden_pre)
    time_one_grad = jnp.dot(embed.astype(jnp.float32).T, grad_hidden, precision=HIGH_PRECISION)
    small_grad = jnp.concatenate(
        [
            grad_small[:14],
            jnp.sum(shift_time_grad, axis=0)[None],
            jnp.sum(grad_hidden, axis=0).reshape(2, chans),
            jnp.sum(grad_act, axis=0).reshape(2, chans),
        ],
        axis=0,
    )
    summed = lax.psum(
        (
            inlet_grad,
            jnp.stack([taps_of(kernel_one_grad), taps_of(kernel_two_grad)]),
            projection_grads,
            jnp.concatenate([time_one_grad, time_two_grad], axis=0),
            shift_weight_grad,
            outlet_grad,
            small_grad,
            loss_part,
        ),
        ("batch", "rows"),
    )
    loss = summed[7]
    grads = summed[:7]
    norm = jnp.sqrt(sum((jnp.sum(item * item) for item in grads)))
    scale_factor = CLIP / jnp.maximum(norm, CLIP)
    count = adam_step[0].astype(jnp.float32)
    weight_tensors = (
        inlet_weight,
        kernel_weight,
        attention_weight,
        time_weight,
        shift_weight,
        outlet_weight,
        small_params,
    )
    states = (
        state_inlet,
        state_kernel,
        state_attention,
        state_time,
        state_shift,
        state_outlet,
        state_small,
    )
    averages = (
        average_inlet,
        average_kernel,
        average_attention,
        average_time,
        average_shift,
        average_outlet,
        average_small,
    )
    members = lax.axis_size("batch")
    mine = lax.axis_index("batch")
    results = [None] * 7
    for position in (1, 2):
        length = weight_tensors[position].shape[1] // members
        own_weight = lax.dynamic_slice_in_dim(weight_tensors[position], mine * length, length, 1)
        own_grad = lax.dynamic_slice_in_dim(grads[position], mine * length, length, 1)
        results[position] = adam(
            own_weight,
            states[position],
            averages[position],
            own_grad * scale_factor,
            RATES[position],
            count,
        )
    kernel_pair, attention_pair = (
        lax.all_gather(results[1][0], "batch", axis=2, tiled=True),
        lax.all_gather(results[2][0], "batch", axis=2, tiled=True),
    )
    results[1] = (kernel_pair, results[1][1], results[1][2])
    results[2] = (attention_pair, results[2][1], results[2][2])
    for position in (0, 3, 4, 5, 6):
        results[position] = adam(
            weight_tensors[position],
            states[position],
            averages[position],
            grads[position] * scale_factor,
            RATES[position],
            count,
        )
    return (
        results[0][0],
        results[1][0],
        results[2][0],
        results[3][0],
        results[4][0],
        results[5][0],
        results[6][0],
        results[0][1],
        results[1][1],
        results[2][1],
        results[3][1],
        results[4][1],
        results[5][1],
        results[6][1],
        results[0][2],
        results[1][2],
        results[2][2],
        results[3][2],
        results[4][2],
        results[5][2],
        results[6][2],
        loss,
        norm,
    )


def solution(mesh):
    return jax.shard_map(
        local,
        mesh=mesh,
        in_specs=(
            P("batch", None, "rows", None),
            P("batch", None, "rows", None),
            P("batch"),
            P("batch", "rows", None, None),
            P(),
            P(),
            P(),
            P(),
            P(),
            P(),
            P(),
            P(),
            P(),
            P(None, None, "batch", None),
            P(None, None, "batch", None),
            P(),
            P(),
            P(),
            P(),
            P(),
            P(None, "batch", None),
            P(None, "batch", None),
            P(),
            P(),
            P(),
            P(),
        ),
        out_specs=(
            P(),
            P(),
            P(),
            P(),
            P(),
            P(),
            P(),
            P(),
            P(None, "batch", None),
            P(None, "batch", None),
            P(),
            P(),
            P(),
            P(),
            P(),
            P(None, "batch", None),
            P(None, "batch", None),
            P(),
            P(),
            P(),
            P(),
            P(),
            P(),
        ),
        check_vma=False,
    )
```

```python
import functools
import math

import jax
import jax.numpy as jnp
import numpy as np
from jax import lax
from jax.experimental import pallas as pl
from jax.experimental.pallas import tpu as pltpu
from jax.sharding import PartitionSpec as P

G = 32


HIGH_PRECISION = lax.Precision.HIGHEST
CLIP = 0.05
GAMMA = 5.0
KEEP = 0.9
EPS_NORM = 1e-05
BETA_ONE = 0.9
BETA_TWO = 0.999
EPS_ADAM = 1e-08
DECAY = 0.01
EMA_TOP = 0.9999
VMEM_LIMIT = 60 << 20
CHUNK = 4
COUNT = 2048.0
RATES = (0.1, 0.01, 0.03, 0.05, 0.02, 0.01, 0.2)


def bar_table():
    beta_rates = 0.0001 + (0.02 - 0.0001) * np.arange(1000, dtype=np.float64) / 999.0
    return np.exp(np.cumsum(np.log(1.0 - beta_rates))).astype(np.float32)


def alpha_bars(timesteps):
    one_hot = (timesteps[:, None] == jnp.arange(1000)[None, :]).astype(jnp.float32)
    return jnp.sum(one_hot * bar_table()[None, :], axis=1)


def sinusoid(timesteps, width):
    half = width // 2
    rates = jnp.exp(-math.log(10000.0) * jnp.arange(half).astype(jnp.float32) / (half - 1))
    angles = timesteps.astype(jnp.float32)[:, None] * rates[None, :]
    return jnp.concatenate([jnp.sin(angles), jnp.cos(angles)], axis=1)


def swish_grad(pre):
    logistic = jax.nn.sigmoid(pre)
    return logistic * (1.0 + pre * (1.0 - logistic))


def wrap(shift, size):
    return shift % size


def tap_masks():
    lane = lax.broadcasted_iota(jnp.int32, (8, 256), 1)
    row, col = lane // 16, lane % 16
    masks = []
    for i in range(3):
        for j in range(3):
            ok = (row + (i - 1) >= 0) & (row + (i - 1) < 16) & (col + (j - 1) >= 0) & (col + (j - 1) < 16)
            masks.append(ok)
    return masks


def tap_stack(tile, masks, sign):
    parts = []
    for tap in range(9):
        step = sign * (16 * (tap // 3 - 1) + tap % 3 - 1)
        moved = tile if step == 0 else pltpu.roll(tile, wrap(-step, 256), 1)
        parts.append(jnp.where(masks[tap if sign > 0 else 8 - tap], moved, 0.0))
    parts.append(jnp.zeros_like(tile))
    return jnp.concatenate(parts, axis=0).astype(jnp.bfloat16)


def group_sum(rows):
    halves = []
    for half in range(2):
        part = rows[:, 128 * half : 128 * half + 128]
        lane = lax.broadcasted_iota(jnp.int32, part.shape, 1)
        for step in (1, 2, 4):
            upper = (lane // step) % 2 == 1
            part = part + jnp.where(upper, pltpu.roll(part, step, 1), pltpu.roll(part, 128 - step, 1))
        halves.append(part)
    return jnp.concatenate(halves, axis=1)


def col_sum(x):
    return jnp.sum(x, axis=0, keepdims=True)


def stats_of(fields):
    sums = jnp.concatenate([col_sum(x) for x in fields] + [col_sum(x * x) for x in fields], axis=0)
    both = group_sum(sums) / COUNT
    n = len(fields)
    mean = both[:n]
    spread = both[n:] - mean * mean
    return mean, lax.rsqrt(spread + EPS_NORM)


def logistic(z):
    return 0.5 * jnp.tanh(0.5 * z) + 0.5


def put_shifted(buf, c, y, not_first, not_last):
    buf[c, 16:272, 256:512] = y.astype(jnp.bfloat16)
    buf[c, 16:272, 0:256] = jnp.where(not_first, pltpu.roll(y, 1, 0), 0.0).astype(jnp.bfloat16)
    buf[c, 16:272, 512:768] = jnp.where(not_last, pltpu.roll(y, 255, 0), 0.0).astype(jnp.bfloat16)


def edge_masks():
    col = lax.broadcasted_iota(jnp.int32, (256, 256), 0) % 16
    return col != 0, col != 15


def stacked(buf, i):
    chunk = buf.shape[0]
    return buf[:, 16 * i : 16 * i + 256, :].reshape(chunk * 256, 768)


def dot(a, b, dims=((1,), (0,))):
    return lax.dot_general(a, b, (dims, ((), ())), preferred_element_type=jnp.float32)


NT = ((1,), (1,))
TN = ((0,), (0,))


def conv_shifted(buf, weight):
    field = jnp.concatenate([stacked(buf, i) for i in range(3)], axis=1)
    return dot(field, weight[...])


def zero_edges(buf):
    edge = jnp.zeros((buf.shape[0], 16, 768), jnp.bfloat16)
    buf[:, 0:16, :] = edge
    buf[:, 272:288, :] = edge


def first_kernel(noisy, tshift, inlet, kernel_one, small, start_out, inner_out, stats_out, buf):
    chunk = noisy.shape[0]

    @pl.when(pl.program_id(0) == 0)
    def _():
        zero_edges(buf)

    masks = tap_masks()
    not_first, not_last = edge_masks()
    starts = []
    for c in range(chunk):
        patch = tap_stack(noisy[c], masks, 1)
        start = dot(patch, inlet[...], TN) + small[8:9]
        start_out[c] = start
        starts.append(start)
    mean, rstd = stats_of(starts)
    for c in range(chunk):
        scale = rstd[c : c + 1] * small[0:1]
        z = starts[c] * scale + (small[4:5] - mean[c : c + 1] * scale)
        put_shifted(buf, c, z * logistic(z), not_first, not_last)
    inner_all = conv_shifted(buf, kernel_one)
    inners = []
    for c in range(chunk):
        inner = inner_all[256 * c : 256 * c + 256] + tshift[c]
        inner_out[c] = inner
        inners.append(inner)
    mean_two, rstd_two = stats_of(inners)
    for c in range(chunk):
        stats_out[c] = jnp.concatenate(
            [mean[c : c + 1], rstd[c : c + 1], mean_two[c : c + 1], rstd_two[c : c + 1]]
            + [jnp.zeros((4, 256), jnp.float32)],
            axis=0,
        )


def norm_grad(dys, fields, means, rstds, gain):
    n = len(dys)
    shift_sums, gain_sums = [], []
    for dy, x, mean, rstd in zip(dys, fields, means, rstds):
        shift_sums.append(col_sum(dy))
        gain_sums.append(col_sum(dy * (x * rstd - mean * rstd)))
    both = group_sum(jnp.concatenate(shift_sums + gain_sums, axis=0) * gain) / COUNT
    grads = []
    for c in range(n):
        rstd, mean = rstds[c], means[c]
        slope = -rstd * rstd * both[n + c : n + c + 1]
        base = -rstd * both[c : c + 1] - mean * slope
        grads.append(dys[c] * (rstd * gain) + (fields[c] * slope + base))
    return grads, sum(gain_sums), sum(shift_sums)


def second_kernel(
    tall,
    short,
    coef,
    start_in,
    inner_in,
    stats_in,
    noisy,
    target,
    keep,
    kernel_one_flip,
    kernel_two,
    kernel_two_flip,
    qkv,
    qkv_t,
    proj,
    proj_t,
    outlet,
    small,
    bias_qkv,
    embed,
    hidden,
    hidden_slope,
    time_act,
    time_slope,
    time_two,
    shift_low,
    shard_out,
    rest_out,
    grad_one_out,
    grad_two_out,
    grad_qkv_out,
    grad_proj_out,
    grad_outlet_out,
    grad_inlet_out,
    grad_small_out,
    loss_out,
    tshift_grad,
    buf,
    grad_buf,
):
    chunk = noisy.shape[0]
    images = range(chunk)
    step = pl.program_id(0)
    sums = (
        grad_one_out,
        grad_two_out,
        grad_qkv_out,
        grad_proj_out,
        grad_outlet_out,
        grad_inlet_out,
        grad_small_out,
        loss_out,
    )

    @pl.when(step == 0)
    def _():
        zero_edges(buf)
        zero_edges(grad_buf)
        for ref in sums:
            ref[...] = jnp.zeros(ref.shape, jnp.float32)

    masks = tap_masks()
    not_first, not_last = edge_masks()

    def gain(k):
        return small[k : k + 1]

    def shift(k):
        return small[4 + k : 5 + k]

    def normed(x, mean, rstd, k):
        scale = rstd * gain(k)
        return x * scale + (shift(k) - mean * scale)

    def row(values, c):
        return values[c : c + 1]

    mean_one = [stats_in[c, 0:1] for c in images]
    rstd_one = [stats_in[c, 1:2] for c in images]
    mean_two = [stats_in[c, 2:3] for c in images]
    rstd_two = [stats_in[c, 3:4] for c in images]

    slope_two, act_two = [], []
    for c in images:
        z = normed(inner_in[c], mean_two[c], rstd_two[c], 1)
        s = logistic(z)
        kept = keep[c].astype(jnp.float32) * (1.0 / KEEP)
        act = z * s * kept
        slope_two.append(s * (1.0 + z * (1.0 - s)) * kept)
        act_two.append(act.astype(jnp.bfloat16))
        put_shifted(buf, c, act, not_first, not_last)
    conv_two = conv_shifted(buf, kernel_two)
    middle = [start_in[c] + conv_two[256 * c : 256 * c + 256] + small[10:11] for c in images]
    mean, rstd = stats_of(middle)
    mean_three = [row(mean, c) for c in images]
    rstd_three = [row(rstd, c) for c in images]

    tokens = [normed(middle[c], mean_three[c], rstd_three[c], 2).astype(jnp.bfloat16) for c in images]
    qkv_all = (dot(jnp.concatenate(tokens, axis=0), qkv[...]) + bias_qkv[0:1]).astype(jnp.bfloat16)
    probs, probs_low, mixed = [], [], []
    scale = 256 ** (-0.5)
    for c in images:
        three = qkv_all[256 * c : 256 * c + 256]
        q, k, v = three[:, 0:256], three[:, 256:512], three[:, 512:768]
        scores = dot(q, k, NT) * scale
        expo = jnp.exp(scores - jnp.max(scores, axis=1, keepdims=True))
        p = expo * (1.0 / jnp.sum(expo, axis=1, keepdims=True))
        probs.append(p)
        probs_low.append(p.astype(jnp.bfloat16))
        mixed.append(dot(probs_low[c], v).astype(jnp.bfloat16))
    branch = dot(jnp.concatenate(mixed, axis=0), proj[...])
    final = [middle[c] + branch[256 * c : 256 * c + 256] + small[13:14] for c in images]
    mean, rstd = stats_of(final)
    mean_four = [row(mean, c) for c in images]
    rstd_four = [row(rstd, c) for c in images]

    grad_four = []
    outlet_sum, loss_sum = 0.0, 0.0
    for c in images:
        z = normed(final[c], mean_four[c], rstd_four[c], 3)
        s = logistic(z)
        act = (z * s).astype(jnp.bfloat16)
        taps = dot(outlet[...], act, NT)
        predicted = 0.0
        for tap in range(9):
            move = 16 * (tap // 3 - 1) + tap % 3 - 1
            part = taps[8 * tap : 8 * tap + 8]
            part = part if move == 0 else pltpu.roll(part, wrap(-move, 256), 1)
            predicted = predicted + jnp.where(masks[tap], part, 0.0)
        error = predicted - target[c]
        weight = coef[step * chunk + c]
        loss_sum = loss_sum + (0.5 * weight) * (error * error)
        grad_pred = (weight * error).astype(jnp.bfloat16).astype(jnp.float32)
        spread = tap_stack(grad_pred, masks, -1)
        outlet_sum = outlet_sum + dot(spread, act)
        grad_four.append(dot(spread, outlet[...], TN) * (s * (1.0 + z * (1.0 - s))))
    loss_out[...] += loss_sum
    grad_outlet_out[...] += outlet_sum
    grad_final, gain_four, shift_four = norm_grad(grad_four, final, mean_four, rstd_four, gain(3))

    branch_low = [g.astype(jnp.bfloat16) for g in grad_final]
    branch_all = jnp.concatenate(branch_low, axis=0)
    grad_proj_out[...] += dot(jnp.concatenate(mixed, axis=0), branch_all, TN)
    grad_mixed = dot(branch_all, proj_t[...]).astype(jnp.bfloat16)
    grad_qkv = []
    for c in images:
        three = qkv_all[256 * c : 256 * c + 256]
        q, k, v = three[:, 0:256], three[:, 256:512], three[:, 512:768]
        dm = grad_mixed[256 * c : 256 * c + 256]
        dp = dot(dm, v, NT)
        dv = dot(probs_low[c], dm, TN)
        p = probs[c]
        ds = (p * (dp - jnp.sum(p * dp, axis=1, keepdims=True))).astype(jnp.bfloat16)
        dq = dot(ds, k) * scale
        dk = dot(ds, q, TN) * scale
        grad_qkv.append(jnp.concatenate([dq, dk, dv], axis=1).astype(jnp.bfloat16))
    grad_qkv_all = jnp.concatenate(grad_qkv, axis=0)
    grad_qkv_out[...] += dot(jnp.concatenate(tokens, axis=0), grad_qkv_all, TN)
    bias_sums = col_sum(grad_qkv_all.astype(jnp.float32))
    grad_tokens = dot(grad_qkv_all, qkv_t[...])
    grad_tokens = [grad_tokens[256 * c : 256 * c + 256] for c in images]
    grad_norm, gain_three, shift_three = norm_grad(
        grad_tokens, middle, mean_three, rstd_three, gain(2)
    )
    grad_middle = [grad_final[c] + grad_norm[c] for c in images]

    for c in images:
        put_shifted(grad_buf, c, grad_middle[c], not_first, not_last)
    field = jnp.concatenate(act_two, axis=0)
    for i in range(3):
        grad_two_out[i] += dot(field, stacked(grad_buf, i), TN)
    grad_act = conv_shifted(grad_buf, kernel_two_flip)
    grad_two = [grad_act[256 * c : 256 * c + 256] * slope_two[c] for c in images]
    grad_inner, gain_two, shift_two = norm_grad(
        grad_two, [inner_in[c] for c in images], mean_two, rstd_two, gain(1)
    )

    for c in images:
        put_shifted(grad_buf, c, grad_inner[c], not_first, not_last)
    act_one, slope_one = [], []
    for c in images:
        z = normed(start_in[c], mean_one[c], rstd_one[c], 0)
        s = logistic(z)
        act_one.append((z * s).astype(jnp.bfloat16))
        slope_one.append(s * (1.0 + z * (1.0 - s)))
    field = jnp.concatenate(act_one, axis=0)
    for i in range(3):
        grad_one_out[i] += dot(field, stacked(grad_buf, i), TN)
    grad_act = conv_shifted(grad_buf, kernel_one_flip)
    grad_one = [grad_act[256 * c : 256 * c + 256] * slope_one[c] for c in images]
    grad_norm, gain_one, shift_one = norm_grad(
        grad_one, [start_in[c] for c in images], mean_one, rstd_one, gain(0)
    )
    grad_start = [grad_middle[c] + grad_norm[c] for c in images]
    inlet_sum = 0.0
    for c in images:
        patch = tap_stack(noisy[c], masks, 1)
        inlet_sum = inlet_sum + dot(patch, grad_start[c].astype(jnp.bfloat16))
    grad_inlet_out[...] += inlet_sum
    inner_sums = [col_sum(grad_inner[c]) for c in images]
    for c in images:
        tshift_grad[pl.ds(step * chunk + c, 1), :] = inner_sums[c]
    grad_small_out[...] += jnp.concatenate(
        [
            gain_one,
            gain_two,
            gain_three,
            gain_four,
            shift_one,
            shift_two,
            shift_three,
            shift_four,
            sum(col_sum(g) for g in grad_start),
            sum(inner_sums),
            sum(col_sum(g) for g in grad_middle),
            bias_sums[:, 0:256],
            bias_sums[:, 512:768],
            sum(col_sum(g) for g in grad_final),
            jnp.zeros((2, 256), jnp.float32),
        ],
        axis=0,
    )

    @pl.when(step == pl.num_programs(0) - 1)
    def _():
        for k, grad in enumerate((grad_one_out, grad_two_out)):
            for tap in range(9):
                at = 256 * (2 - tap % 3)
                for shard, off, row, size in cuts(tap * 256, 256, tall):
                    shard_out[shard, k * tall + off : k * tall + off + size, :] = grad[
                        2 - tap // 3, row : row + size, at : at + 256
                    ]
        for k in range(4):
            grad, at = (grad_qkv_out, 256 * k) if k < 3 else (grad_proj_out, 0)
            for shard, off, row, size in cuts(0, 256, short):
                low = 2 * tall + k * short + off
                shard_out[shard, low : low + size, :] = grad[row : row + size, at : at + 256]
        used = 2 * tall + 4 * short
        if used < shard_out.shape[1]:
            shard_out[:, used:, :] = jnp.zeros(
                (shard_out.shape[0], shard_out.shape[1] - used, 256), jnp.float32
            )
        total = tshift_grad[...]
        shift_grad = full_dot(time_act[...], total, TN)
        grad_act = full_dot(total, shift_low[...], NT) * time_slope[...]
        two_grad = full_dot(hidden[...], grad_act, TN)
        grad_hidden = full_dot(grad_act, time_two[...], NT) * hidden_slope[...]
        one_grad = full_dot(embed[...], grad_hidden, TN)
        width = one_grad.shape[0]
        height = width + two_grad.shape[0]
        for half in range(2):
            span = slice(256 * half, 256 * half + 256)
            rest_out[half * height : half * height + width, :] = one_grad[:, span]
            rest_out[half * height + width : half * height + height, :] = two_grad[:, span]
        act_sum, hidden_sum = col_sum(grad_act), col_sum(grad_hidden)
        parts = [
            shift_grad,
            grad_inlet_out[...],
            grad_outlet_out[...],
            jnp.concatenate(
                [
                    grad_small_out[0:14],
                    col_sum(total),
                    hidden_sum[:, 0:256],
                    hidden_sum[:, 256:512],
                    act_sum[:, 0:256],
                    act_sum[:, 256:512],
                    jnp.zeros((5, 256), jnp.float32),
                ],
                axis=0,
            ),
            loss_out[...],
        ]
        at = 2 * height
        for part in parts:
            rest_out[at : at + part.shape[0], :] = part
            at += part.shape[0]
        if at < rest_out.shape[0]:
            rest_out[at:, :] = jnp.zeros((rest_out.shape[0] - at, 256), jnp.float32)


def cuts(first, size, height):
    parts, row = [], 0
    while row < size:
        shard, off = divmod(first + row, height)
        take = min(height - off, size - row)
        parts.append((shard, off, row, take))
        row += take
    return parts


def full_dot(a, b, dims):
    return lax.dot_general(
        a.astype(jnp.float32),
        b.astype(jnp.float32),
        (dims, ((), ())),
        precision=HIGH_PRECISION,
        preferred_element_type=jnp.float32,
    )


def resident(shape):
    return pl.BlockSpec(shape, lambda i: (0,) * len(shape), pipeline_mode=pl.Buffered(1))


def per_chunk(chunk, *tail):
    return pl.BlockSpec((chunk,) + tail, lambda i: (i,) + (0,) * len(tail))


def forward_part(chunk, noisy, tshift, inlet, kernel_one, small):
    n = noisy.shape[0]
    return pl.pallas_call(
        first_kernel,
        grid=(n // chunk,),
        in_specs=[
            per_chunk(chunk, 8, 256),
            per_chunk(chunk, 1, 256),
            resident(inlet.shape),
            resident(kernel_one.shape),
            resident(small.shape),
        ],
        out_specs=[
            per_chunk(chunk, 256, 256),
            per_chunk(chunk, 256, 256),
            per_chunk(chunk, 8, 256),
        ],
        out_shape=[
            jax.ShapeDtypeStruct((n, 256, 256), jnp.float32),
            jax.ShapeDtypeStruct((n, 256, 256), jnp.float32),
            jax.ShapeDtypeStruct((n, 8, 256), jnp.float32),
        ],
        scratch_shapes=[pltpu.VMEM((chunk, 288, 768), jnp.bfloat16)],
        compiler_params=pltpu.CompilerParams(vmem_limit_bytes=VMEM_LIMIT),
        cost_estimate=pl.CostEstimate(
            flops=2 * n * 256 * 256 * 2400, bytes_accessed=n * 1 << 19, transcendentals=n * 1 << 16
        ),
        name="forward_part",
    )(noisy, tshift, inlet, kernel_one, small)


def main_part(chunk, sizes, coef, start, inner, stats, noisy, target, keep, weights, small, bias_qkv, times):
    n = noisy.shape[0]
    batch, shard_rows, tall, short, rest_rows = sizes
    outs = [(batch, shard_rows, 256), (rest_rows, 256)]
    sums = [(3, 256, 768), (3, 256, 768), (256, 768), (256, 256), (80, 256), (80, 256), (16, 256), (8, 256)]
    return pl.pallas_call(
        functools.partial(second_kernel, tall, short),
        grid=(n // chunk,),
        in_specs=[
            pl.BlockSpec(memory_space=pltpu.SMEM),
            per_chunk(chunk, 256, 256),
            per_chunk(chunk, 256, 256),
            per_chunk(chunk, 8, 256),
            per_chunk(chunk, 8, 256),
            per_chunk(chunk, 8, 256),
            per_chunk(chunk, 256, 256),
        ]
        + [resident(w.shape) for w in weights]
        + [resident(small.shape), resident(bias_qkv.shape)]
        + [resident(t.shape) for t in times],
        out_specs=[resident(g) for g in outs],
        out_shape=[jax.ShapeDtypeStruct(g, jnp.float32) for g in outs],
        scratch_shapes=[pltpu.VMEM(g, jnp.float32) for g in sums + [(n, 256)]]
        + [pltpu.VMEM((chunk, 288, 768), jnp.bfloat16)] * 2,
        compiler_params=pltpu.CompilerParams(vmem_limit_bytes=VMEM_LIMIT),
        cost_estimate=pl.CostEstimate(
            flops=70 * n * 2 * 256**3, bytes_accessed=n * 5 << 17, transcendentals=n * 5 << 16
        ),
        name="main_part",
    )(coef, start, inner, stats, noisy, target, keep, *weights, small, bias_qkv, *times)


def rows_first(weight):
    inputs, outputs = weight.shape[0] // 9, weight.shape[1]
    flipped = jnp.transpose(weight.reshape(9, inputs, outputs)[::-1], (0, 2, 1))
    return flipped.reshape(9 * outputs, inputs)


def padded_taps(rows):
    padded = jnp.pad(rows.reshape(9, 3, 256), ((0, 1), (0, 5), (0, 0)))
    return padded.reshape(80, 256)


def unpadded_taps(rows):
    return rows.reshape(10, 8, 256)[:9, :3]


MESH = pl.DeviceIdType.MESH
MISC_ROWS = (640, 640, 512, 80, 80, 24, 8)


def padded_rows(total, parts):
    return -(-total // (8 * parts)) * 8


def exchange_kernel(
    shard_shape,
    rates,
    grads_a,
    grads_b,
    state_kernel,
    state_attention,
    weight_kernel,
    weight_attention,
    scalars,
    out_a,
    out_b,
    first_kernel_out,
    first_attention_out,
    second_kernel_out,
    second_attention_out,
    norm_out,
    half_a,
    half_b,
    row_a,
    row_b,
    deep_a,
    deep_b,
    shard_grad,
    shard_weight,
    shard_first,
    shard_second,
    square_core,
    square_rows,
    square_deep,
    local_sem,
    core_send,
    core_recv,
    row_send,
    row_recv,
    deep_send,
    deep_recv,
    shard_send,
    shard_recv,
    square_send,
    square_recv,
    deep_send_two,
    deep_recv_two,
    row_send_two,
    row_recv_two,
    core_send_two,
    core_recv_two,
):
    depth, _, rows, piece, _ = grads_a.shape
    lanes = grads_b.shape[3]
    pairs, tall, quads, short = shard_shape
    batch, r = lax.axis_index("batch"), lax.axis_index("rows")
    z, c = batch // 2, batch % 2
    partner = z * 2 + (1 - c)
    row_peers = [(r + d) % rows for d in range(1, rows)]
    deep_peers = [(z + d) % depth for d in range(1, depth)]

    def remote(src, dst, send, recv, where):
        return pltpu.make_async_remote_copy(
            src_ref=src, dst_ref=dst, send_sem=send, recv_sem=recv, device_id=where, device_id_type=MESH
        )

    def blocks(kernel_ref, attention_ref, flat, base, offset, outward):
        copies = []
        for k in range(pairs + quads):
            ref, own, size = (kernel_ref, k, tall) if k < pairs else (attention_ref, k - pairs, short)
            at = k * tall if k < pairs else pairs * tall + own * short
            far = ref.at[own] if offset is None else ref.at[own, pl.ds(offset * size, size)]
            near = flat.at[pl.ds(at, size)]
            src, dst = (near, far) if outward else (far, near)
            copies.append(pltpu.make_async_copy(src, dst, local_sem.at[base * (pairs + quads) + k]))
        for copy in copies:
            copy.start()
        return copies

    fetches = (
        blocks(weight_kernel, weight_attention, shard_weight, 0, batch, False)
        + blocks(state_kernel.at[0], state_attention.at[0], shard_first, 1, None, False)
        + blocks(state_kernel.at[1], state_attention.at[1], shard_second, 2, None, False)
    )

    barrier = pltpu.get_barrier_semaphore()
    pl.semaphore_signal(barrier, inc=1, device_id=(partner, r), device_id_type=MESH)
    for peer in row_peers:
        pl.semaphore_signal(barrier, inc=1, device_id=(batch, peer), device_id_type=MESH)
    for peer in deep_peers:
        pl.semaphore_signal(barrier, inc=1, device_id=(peer * 2 + c, r), device_id_type=MESH)
    pl.semaphore_wait(barrier, rows + depth - 1)

    cut = (piece // 8 + 1) // 2 * 8
    chunks = [
        (grads_b, half_b, row_b, deep_b, 0, lanes),
        (grads_a, half_a, row_a, deep_a, 0, cut),
        (grads_a, half_a, row_a, deep_a, cut, piece - cut),
    ]
    pending = []

    core_copies = []
    for k, (grads, half, _, _, at, size) in enumerate(chunks):
        copy = remote(
            grads.at[:, 1 - c, :, pl.ds(at, size)],
            half.at[:, :, pl.ds(at, size)],
            core_send.at[k],
            core_recv.at[k],
            (partner, r),
        )
        copy.start()
        core_copies.append(copy)
    row_copies = []
    for k, (grads, half, row, _, at, size) in enumerate(chunks):
        core_copies[k].wait_recv()

        def add_own(t, carry, grads=grads, half=half, at=at, size=size):
            i, j = t // rows, t % rows
            span = pl.ds(at, size)
            half[i, j, span] = half[i, j, span] + grads[i, c, j, span]
            return carry

        lax.fori_loop(0, depth * rows, add_own, 0)
        copies = []
        for d, peer in enumerate(row_peers):
            copy = remote(
                half.at[:, peer, pl.ds(at, size)],
                row.at[d, :, pl.ds(at, size)],
                row_send.at[k, d],
                row_recv.at[k, d],
                (batch, peer),
            )
            copy.start()
            copies.append(copy)
        row_copies.append(copies)
    deep_copies = []
    for k, (grads, half, row, deep, at, size) in enumerate(chunks):
        for copy in row_copies[k]:
            copy.wait_recv()

        def add_rows(i, carry, half=half, row=row, at=at, size=size):
            span = pl.ds(at, size)
            total = half[i, r, span]
            for d in range(rows - 1):
                total = total + row[d, i, span]
            half[i, r, span] = total
            return carry

        lax.fori_loop(0, depth, add_rows, 0)
        copies = []
        for d, peer in enumerate(deep_peers):
            copy = remote(
                half.at[peer, r, pl.ds(at, size)],
                deep.at[d, pl.ds(at, size)],
                deep_send.at[k, d],
                deep_recv.at[k, d],
                (peer * 2 + c, r),
            )
            copy.start()
            copies.append(copy)
        deep_copies.append(copies)

    def finish(k):
        _, half, _, deep, at, size = chunks[k]
        for copy in deep_copies[k]:
            copy.wait_recv()
        span = pl.ds(at, size)
        total = half[z, r, span]
        for d in range(depth - 1):
            total = total + deep[d, span]
        return total

    def squares(x):
        return jnp.sum((x * x).reshape(-1, 8, 256), axis=0)

    def gather(bufs, k, at, size, stage):
        span = pl.ds(at, size)
        copies = []
        if stage == 0:
            for d, peer in enumerate(deep_peers):
                copies.append(
                    remote(
                        bufs.at[z, c, r, span],
                        bufs.at[z, c, r, span],
                        deep_send_two.at[k, d],
                        deep_recv_two.at[k, d],
                        (peer * 2 + c, r),
                    )
                )
        elif stage == 1:
            for d, peer in enumerate(row_peers):
                copies.append(
                    remote(
                        bufs.at[:, c, r, span],
                        bufs.at[:, c, r, span],
                        row_send_two.at[k, d],
                        row_recv_two.at[k, d],
                        (batch, peer),
                    )
                )
        else:
            copies.append(
                remote(
                    bufs.at[:, c, :, span],
                    bufs.at[:, c, :, span],
                    core_send_two.at[k],
                    core_recv_two.at[k],
                    (partner, r),
                )
            )
        for copy in copies:
            copy.start()
        return copies

    total = finish(0)
    out_b[z, c, r] = total
    stage_zero = [gather(out_b, 0, 0, lanes, 0)]
    line = (batch * rows + r) * lanes + lax.broadcasted_iota(jnp.int32, total.shape, 0)
    square = squares(jnp.where(line < sum(MISC_ROWS[:-1]), total, 0.0))
    for k in (1, 2):
        total = finish(k)
        shard_grad[r, pl.ds(chunks[k][4], chunks[k][5])] = total
        square = square + squares(total)
    square_core[0] = square
    copy = remote(square_core.at[0], square_core.at[1], square_send.at[0], square_recv.at[0], (partner, r))
    copy.start()
    pending.append(copy)
    shard_copies = []
    for d, peer in enumerate(row_peers):
        share = remote(
            shard_grad.at[r], shard_grad.at[r], shard_send.at[d], shard_recv.at[d], (batch, peer)
        )
        share.start()
        shard_copies.append(share)
    copy.wait_recv()
    square_rows[r] = square_core[0] + square_core[1]
    copies = []
    for d, peer in enumerate(row_peers):
        copy = remote(
            square_rows.at[r], square_rows.at[r], square_send.at[1 + d], square_recv.at[1 + d], (batch, peer)
        )
        copy.start()
        copies.append(copy)
    pending += copies
    for copy in copies:
        copy.wait_recv()
    square_deep[z] = sum(square_rows[j] for j in range(rows))
    copies = []
    for d, peer in enumerate(deep_peers):
        copy = remote(
            square_deep.at[z],
            square_deep.at[z],
            square_send.at[rows + d],
            square_recv.at[rows + d],
            (peer * 2 + c, r),
        )
        copy.start()
        copies.append(copy)
    pending += copies
    for copy in copies:
        copy.wait_recv()
    square = sum(square_deep[j] for j in range(depth))
    norm = jnp.sqrt(jnp.sum(jnp.sum(square, axis=0, keepdims=True), axis=1, keepdims=True))
    clip = CLIP / jnp.maximum(norm, CLIP)
    norm_out[...] = jnp.broadcast_to(norm, norm_out.shape)

    def moments(at, g):
        span = pl.ds(at, piece)
        first = BETA_ONE * shard_first[span] + (1.0 - BETA_ONE) * g
        second = BETA_TWO * shard_second[span] + (1.0 - BETA_TWO) * g * g
        return first, second

    for fetch in fetches:
        fetch.wait()
    mine = pl.multiple_of(r * piece, 8)
    first, second = moments(mine, shard_grad[r] * clip)
    line = mine + lax.broadcasted_iota(jnp.int32, first.shape, 0)
    rate = jnp.where(line < pairs * tall, rates[0], rates[1])
    weight = shard_weight[pl.ds(mine, piece)]
    step = first * scalars[0] / (jnp.sqrt(second * scalars[1]) + EPS_ADAM)
    out_a[z, c, r] = weight - rate * (step + DECAY * weight)
    for k in (1, 2):
        stage_zero.append(gather(out_a, k, chunks[k][4], chunks[k][5], 0))
    for copy in shard_copies:
        copy.wait_recv()
    for j in range(rows):
        first, second = moments(j * piece, shard_grad[j] * clip)
        shard_first[j * piece : j * piece + piece] = first
        shard_second[j * piece : j * piece + piece] = second
    stores = blocks(first_kernel_out, first_attention_out, shard_first, 3, None, True) + blocks(
        second_kernel_out, second_attention_out, shard_second, 4, None, True
    )
    stage_one, stage_two = [], []
    for k in range(3):
        for copy in stage_zero[k]:
            copy.wait_recv()
        stage_one.append(gather(out_b if k == 0 else out_a, k, chunks[k][4], chunks[k][5], 1))
    for k in range(3):
        for copy in stage_one[k]:
            copy.wait_recv()
        stage_two.append(gather(out_b if k == 0 else out_a, k, chunks[k][4], chunks[k][5], 2))
    for copies in stage_two:
        for copy in copies:
            copy.wait_recv()
    pending += core_copies + shard_copies
    for copies in row_copies + deep_copies + stage_zero + stage_one + stage_two:
        pending += copies
    for copy in pending:
        copy.wait_send()
    for copy in stores:
        copy.wait()


def exchange(grads_a, grads_b, state_kernel, state_attention, weight_kernel, weight_attention, scalars):
    depth, _, rows, piece, width = grads_a.shape
    lanes = grads_b.shape[3]
    pairs, tall = state_kernel.shape[1:3]
    quads, short = state_attention.shape[1:3]
    shape = functools.partial(jax.ShapeDtypeStruct, dtype=jnp.float32)
    whole = pl.BlockSpec(memory_space=pltpu.VMEM)
    dma = pltpu.SemaphoreType.DMA
    vmem = functools.partial(pltpu.VMEM, dtype=jnp.float32)
    return pl.pallas_call(
        functools.partial(exchange_kernel, (pairs, tall, quads, short), (RATES[1], RATES[2])),
        in_specs=[whole] * 2
        + [pl.BlockSpec(memory_space=pl.ANY)] * 4
        + [pl.BlockSpec(memory_space=pltpu.SMEM)],
        out_specs=[whole] * 2 + [pl.BlockSpec(memory_space=pl.ANY)] * 4 + [whole],
        out_shape=[
            shape(grads_a.shape),
            shape(grads_b.shape),
            shape(state_kernel.shape[1:]),
            shape(state_attention.shape[1:]),
            shape(state_kernel.shape[1:]),
            shape(state_attention.shape[1:]),
            shape((8, 128)),
        ],
        scratch_shapes=[
            vmem((depth, rows, piece, width)),
            vmem((depth, rows, lanes, width)),
            vmem((rows - 1, depth, piece, width)),
            vmem((rows - 1, depth, lanes, width)),
            vmem((depth - 1, piece, width)),
            vmem((depth - 1, lanes, width)),
            vmem((rows, piece, width)),
            vmem((rows * piece, width)),
            vmem((rows * piece, width)),
            vmem((rows * piece, width)),
            vmem((2, 8, width)),
            vmem((rows, 8, width)),
            vmem((depth, 8, width)),
            dma((5 * (pairs + quads),)),
            dma((3,)),
            dma((3,)),
            dma((3, rows - 1)),
            dma((3, rows - 1)),
            dma((3, depth - 1)),
            dma((3, depth - 1)),
            dma((rows - 1,)),
            dma((rows - 1,)),
            dma((rows + depth - 1,)),
            dma((rows + depth - 1,)),
            dma((3, depth - 1)),
            dma((3, depth - 1)),
            dma((3, rows - 1)),
            dma((3, rows - 1)),
            dma((3,)),
            dma((3,)),
        ],
        compiler_params=pltpu.CompilerParams(
            collective_id=0, has_side_effects=True, vmem_limit_bytes=VMEM_LIMIT
        ),
        name="exchange",
    )(grads_a, grads_b, state_kernel, state_attention, weight_kernel, weight_attention, scalars)


def adam(weight, state, average, grad, rate, count):
    first_new = BETA_ONE * state[0] + (1.0 - BETA_ONE) * grad
    second_new = BETA_TWO * state[1] + (1.0 - BETA_TWO) * grad * grad
    first_hat = first_new / (1.0 - BETA_ONE**count)
    second_hat = second_new / (1.0 - BETA_TWO**count)
    weight_new = weight - rate * (first_hat / (jnp.sqrt(second_hat) + EPS_ADAM) + DECAY * weight)
    keep = jnp.minimum(EMA_TOP, (1.0 + count) / (10.0 + count))
    average_new = keep * average + (1.0 - keep) * weight_new
    return (jnp.stack([weight_new, average_new]), first_new, second_new)


def local(
    x_clean,
    noise,
    timesteps,
    keep_mask,
    adam_step,
    inlet_weight,
    kernel_weight,
    attention_weight,
    time_weight,
    shift_weight,
    outlet_weight,
    small_params,
    state_inlet,
    state_kernel,
    state_attention,
    state_time,
    state_shift,
    state_outlet,
    state_small,
    average_inlet,
    average_kernel,
    average_attention,
    average_time,
    average_shift,
    average_outlet,
    average_small,
):
    chans = kernel_weight.shape[2]
    width_sin = time_weight.shape[0] - time_weight.shape[1]
    rows = lax.axis_size("rows")
    own = timesteps.shape[0] // rows
    timesteps = lax.dynamic_slice_in_dim(timesteps, lax.axis_index("rows") * own, own, 0)
    pair = lax.all_to_all(jnp.concatenate([x_clean, noise], axis=1), "rows", 0, 2, tiled=True)
    keep = lax.all_to_all(keep_mask.astype(jnp.bfloat16), "rows", 0, 1, tiled=True)
    keep = keep.reshape(own, -1, chans)
    bars = alpha_bars(timesteps)
    level = bars[:, None, None]
    pair = jnp.pad(pair.reshape(own, 2, 3, -1), ((0, 0), (0, 0), (0, 5), (0, 0)))
    clean, target = pair[:, 0], pair[:, 1]
    noisy = (jnp.sqrt(level) * clean + jnp.sqrt(1.0 - level) * target).astype(jnp.bfloat16)
    noisy = noisy.astype(jnp.float32)
    kernels = kernel_weight.astype(jnp.bfloat16)
    projections = attention_weight.astype(jnp.bfloat16)
    time_low = time_weight.astype(jnp.bfloat16)
    shift_low = shift_weight.astype(jnp.bfloat16)
    inlet = padded_taps(inlet_weight).astype(jnp.bfloat16)
    outlet = padded_taps(
        jnp.transpose(outlet_weight.reshape(3, 9, chans), (1, 0, 2)).reshape(27, chans)
    ).astype(jnp.bfloat16)
    qkv = jnp.concatenate([projections[0], projections[1], projections[2]], axis=1)
    embed = sinusoid(timesteps, width_sin).astype(jnp.bfloat16)
    hidden_pre = jnp.dot(
        embed, time_low[:width_sin], preferred_element_type=jnp.float32
    ) + small_params[15:17].reshape(-1)
    hidden = jax.nn.silu(hidden_pre).astype(jnp.bfloat16)
    time_emb = jnp.dot(
        hidden, time_low[width_sin:], preferred_element_type=jnp.float32
    ) + small_params[17:19].reshape(-1)
    time_act = jax.nn.silu(time_emb).astype(jnp.bfloat16)
    time_shift = jnp.dot(time_act, shift_low, preferred_element_type=jnp.float32) + small_params[14]
    ratio = bars / (1.0 - bars)
    snr_weight = jnp.minimum(ratio, GAMMA) / ratio
    denom = 3 * noisy.shape[2] * own * rows * lax.axis_size("batch")
    coef = 2.0 * snr_weight / denom
    start, inner, stats = forward_part(
        CHUNK, noisy, (time_shift + small_params[9])[:, None, :], inlet, kernels[0], small_params
    )
    bias_qkv = jnp.concatenate([small_params[11], jnp.zeros_like(small_params[0]), small_params[12]])
    batch = lax.axis_size("batch")
    tall, short = state_kernel.shape[2], state_attention.shape[2]
    shard_rows = rows * padded_rows(2 * tall + 4 * short, rows)
    lanes = padded_rows(sum(MISC_ROWS), batch * rows)
    shards, rest = main_part(
        CHUNK,
        (batch, shard_rows, tall, short, batch * rows * lanes),
        coef,
        start,
        inner,
        stats,
        noisy,
        target,
        keep,
        (
            rows_first(kernels[0]),
            kernels[1],
            rows_first(kernels[1]),
            qkv,
            qkv.T,
            projections[3],
            projections[3].T,
            outlet,
        ),
        small_params,
        bias_qkv[None],
        (
            embed,
            hidden,
            swish_grad(hidden_pre),
            time_act,
            swish_grad(time_emb),
            time_low[width_sin:],
            shift_low,
        ),
    )
    count = adam_step[0].astype(jnp.float32)
    scalars = jnp.stack([1.0 / (1.0 - BETA_ONE**count), 1.0 / (1.0 - BETA_TWO**count)])
    fresh, rest, first_kernel, first_attention, second_kernel, second_attention, norm_tile = exchange(
        shards.reshape(batch // 2, 2, rows, shard_rows // rows, chans),
        rest.reshape(batch // 2, 2, rows, lanes, chans),
        state_kernel,
        state_attention,
        kernel_weight,
        attention_weight,
        scalars,
    )
    fresh = fresh.reshape(batch, shard_rows, chans)
    fresh_kernel = jnp.transpose(fresh[:, : 2 * tall].reshape(batch, 2, tall, chans), (1, 0, 2, 3))
    fresh_attention = jnp.transpose(
        fresh[:, 2 * tall : 2 * tall + 4 * short].reshape(batch, 4, short, chans), (1, 0, 2, 3)
    )
    all_kernel = lax.all_gather(average_kernel, "batch", axis=1, tiled=True)
    all_attention = lax.all_gather(average_attention, "batch", axis=1, tiled=True)

    def averaged(new, average):
        kept = jnp.minimum(EMA_TOP, (1.0 + count) / (10.0 + count))
        return jnp.stack([new, kept * average + (1.0 - kept) * new])

    updated_kernel = averaged(fresh_kernel.reshape(kernel_weight.shape), all_kernel)
    updated_attention = averaged(fresh_attention.reshape(attention_weight.shape), all_attention)
    rest = rest.reshape(-1, chans)
    height = time_weight.shape[0]
    marks = [0]
    for size in MISC_ROWS:
        marks.append(marks[-1] + size)
    part = [rest[low:high] for low, high in zip(marks[:-1], marks[1:])]
    norm = norm_tile[0, 0]
    scale_factor = CLIP / jnp.maximum(norm, CLIP)
    results = {}
    for position, weight, state, average, grad in (
        (0, inlet_weight, state_inlet, average_inlet, unpadded_taps(part[3]).reshape(27, chans)),
        (3, time_weight, state_time, average_time, jnp.concatenate([part[0], part[1]], axis=1)),
        (4, shift_weight, state_shift, average_shift, part[2]),
        (
            5,
            outlet_weight,
            state_outlet,
            average_outlet,
            jnp.transpose(unpadded_taps(part[4]), (1, 0, 2)).reshape(3, 9 * chans),
        ),
        (6, small_params, state_small, average_small, part[5][:19]),
    ):
        results[position] = adam(weight, state, average, grad * scale_factor, RATES[position], count)
    loss = jnp.sum(part[6])
    return (
        results[0][0],
        updated_kernel,
        updated_attention,
        results[3][0],
        results[4][0],
        results[5][0],
        results[6][0],
        results[0][1],
        first_kernel,
        first_attention,
        results[3][1],
        results[4][1],
        results[5][1],
        results[6][1],
        results[0][2],
        second_kernel,
        second_attention,
        results[3][2],
        results[4][2],
        results[5][2],
        results[6][2],
        loss,
        norm,
    )


def solution(mesh):
    return jax.shard_map(
        local,
        mesh=mesh,
        in_specs=(
            P("batch", None, "rows", None),
            P("batch", None, "rows", None),
            P("batch"),
            P("batch", "rows", None, None),
            P(),
            P(),
            P(),
            P(),
            P(),
            P(),
            P(),
            P(),
            P(),
            P(None, None, "batch", None),
            P(None, None, "batch", None),
            P(),
            P(),
            P(),
            P(),
            P(),
            P(None, "batch", None),
            P(None, "batch", None),
            P(),
            P(),
            P(),
            P(),
        ),
        out_specs=(
            P(),
            P(),
            P(),
            P(),
            P(),
            P(),
            P(),
            P(),
            P(None, "batch", None),
            P(None, "batch", None),
            P(),
            P(),
            P(),
            P(),
            P(),
            P(None, "batch", None),
            P(None, "batch", None),
            P(),
            P(),
            P(),
            P(),
            P(),
            P(),
        ),
        check_vma=False,
    )
```

```python
import functools
import math

import jax
import jax.numpy as jnp
import numpy as np
from jax import lax
from jax.experimental import pallas as pl
from jax.experimental.pallas import tpu as pltpu
from jax.sharding import PartitionSpec as P

G = 32


HIGH_PRECISION = lax.Precision.HIGHEST
CLIP = 0.05
GAMMA = 5.0
KEEP = 0.9
EPS_NORM = 1e-05
BETA_ONE = 0.9
BETA_TWO = 0.999
EPS_ADAM = 1e-08
DECAY = 0.01
EMA_TOP = 0.9999
VMEM_LIMIT = 60 << 20
CHUNK = 8
FORWARD_CHUNK = 4
GROUP = 2
COUNT = 2048.0
RATES = (0.1, 0.01, 0.03, 0.05, 0.02, 0.01, 0.2)


def bar_table():
    beta_rates = 0.0001 + (0.02 - 0.0001) * np.arange(1000, dtype=np.float64) / 999.0
    return np.exp(np.cumsum(np.log(1.0 - beta_rates))).astype(np.float32)


def alpha_bars(timesteps):
    one_hot = (timesteps[:, None] == jnp.arange(1000)[None, :]).astype(jnp.float32)
    return jnp.sum(one_hot * bar_table()[None, :], axis=1)


def sinusoid(timesteps, width):
    half = width // 2
    rates = jnp.exp(-math.log(10000.0) * jnp.arange(half).astype(jnp.float32) / (half - 1))
    angles = timesteps.astype(jnp.float32)[:, None] * rates[None, :]
    return jnp.concatenate([jnp.sin(angles), jnp.cos(angles)], axis=1)


def swish_grad(pre):
    logistic = jax.nn.sigmoid(pre)
    return logistic * (1.0 + pre * (1.0 - logistic))


def wrap(shift, size):
    return shift % size


def tap_masks():
    lane = lax.broadcasted_iota(jnp.int32, (8, 256), 1)
    row, col = lane // 16, lane % 16
    masks = []
    for i in range(3):
        for j in range(3):
            ok = (row + (i - 1) >= 0) & (row + (i - 1) < 16) & (col + (j - 1) >= 0) & (col + (j - 1) < 16)
            masks.append(ok)
    return masks


def tap_stack(tile, masks, sign):
    parts = []
    for tap in range(9):
        step = sign * (16 * (tap // 3 - 1) + tap % 3 - 1)
        moved = tile if step == 0 else pltpu.roll(tile, wrap(-step, 256), 1)
        parts.append(jnp.where(masks[tap if sign > 0 else 8 - tap], moved, 0.0))
    parts.append(jnp.zeros_like(tile))
    return jnp.concatenate(parts, axis=0).astype(jnp.bfloat16)


def group_sum(rows):
    halves = []
    for half in range(2):
        part = rows[:, 128 * half : 128 * half + 128]
        lane = lax.broadcasted_iota(jnp.int32, part.shape, 1)
        for step in (1, 2, 4):
            upper = (lane // step) % 2 == 1
            part = part + jnp.where(upper, pltpu.roll(part, step, 1), pltpu.roll(part, 128 - step, 1))
        halves.append(part)
    return jnp.concatenate(halves, axis=1)


def col_sum(x):
    return jnp.sum(x, axis=0, keepdims=True)


def stats_of(fields):
    sums = jnp.concatenate([col_sum(x) for x in fields] + [col_sum(x * x) for x in fields], axis=0)
    both = group_sum(sums) / COUNT
    n = len(fields)
    mean = both[:n]
    spread = both[n:] - mean * mean
    return mean, lax.rsqrt(spread + EPS_NORM)


def logistic(z):
    return 0.5 * jnp.tanh(0.5 * z) + 0.5


def put_shifted(buf, c, y, not_first, not_last):
    buf[c, 16:272, 256:512] = y.astype(jnp.bfloat16)
    buf[c, 16:272, 0:256] = jnp.where(not_first, pltpu.roll(y, 1, 0), 0.0).astype(jnp.bfloat16)
    buf[c, 16:272, 512:768] = jnp.where(not_last, pltpu.roll(y, 255, 0), 0.0).astype(jnp.bfloat16)


def edge_masks():
    col = lax.broadcasted_iota(jnp.int32, (256, 256), 0) % 16
    return col != 0, col != 15


def stacked(buf, i):
    chunk = buf.shape[0]
    return buf[:, 16 * i : 16 * i + 256, :].reshape(chunk * 256, 768)


def dot(a, b, dims=((1,), (0,))):
    return lax.dot_general(a, b, (dims, ((), ())), preferred_element_type=jnp.float32)


NT = ((1,), (1,))
TN = ((0,), (0,))


def conv_shifted(buf, weight):
    field = jnp.concatenate([stacked(buf, i) for i in range(3)], axis=1)
    return dot(field, weight[...])


def zero_edges(buf):
    edge = jnp.zeros((buf.shape[0], 16, 768), jnp.bfloat16)
    buf[:, 0:16, :] = edge
    buf[:, 272:288, :] = edge


def take_turns(workers):
    live, started = [], 0
    while live or started < len(workers):
        if started < len(workers):
            live.append(workers[started])
            started += 1
        live = [w for w in live if next(w, live) is not live]


def lanes_joined(blocks):
    return blocks[0] if len(blocks) == 1 else jnp.concatenate(blocks, axis=1)


def first_kernel(
    mix, pair, tshift, inlet, kernel_one, small, start_out, inner_out, stats_out, noisy_out, target_out, buf
):
    chunk = start_out.shape[0]
    step = pl.program_id(0)

    @pl.when(step == 0)
    def _():
        zero_edges(buf)

    masks = tap_masks()
    not_first, not_last = edge_masks()
    real = lax.broadcasted_iota(jnp.int32, (8, 256), 0) < 3

    def work(images):
        n = len(images)
        every = range(n)
        low, high = images[0], images[-1] + 1
        starts = []
        for c in images:
            both = lanes_joined([pair[s, c] for s in range(pair.shape[0])])
            clean = jnp.where(real, both, 0.0)
            noise = jnp.where(real, pltpu.roll(both, 5, 0), 0.0)
            noisy = mix[0, step * chunk + c] * clean + mix[1, step * chunk + c] * noise
            noisy = noisy.astype(jnp.bfloat16).astype(jnp.float32)
            noisy_out[c] = noisy
            target_out[c] = noise
            start = dot(tap_stack(noisy, masks, 1), inlet[...], TN) + small[8:9]
            start_out[c] = start
            starts.append(start)
        yield
        mean, rstd = stats_of(starts)
        for i, c in enumerate(images):
            scale = rstd[i : i + 1] * small[0:1]
            z = starts[i] * scale + (small[4:5] - mean[i : i + 1] * scale)
            put_shifted(buf, c, z * logistic(z), not_first, not_last)
        yield
        inner_all = conv_shifted(buf.at[low:high], kernel_one)
        yield
        inners = []
        for i, c in enumerate(images):
            inner = inner_all[256 * i : 256 * i + 256] + tshift[c]
            inner_out[c] = inner
            inners.append(inner)
        mean_two, rstd_two = stats_of(inners)
        for i, c in enumerate(images):
            stats_out[c] = jnp.concatenate(
                [mean[i : i + 1], rstd[i : i + 1], mean_two[i : i + 1], rstd_two[i : i + 1]]
                + [jnp.zeros((4, 256), jnp.float32)],
                axis=0,
            )

    take_turns([work(list(range(g, g + GROUP))) for g in range(0, chunk, GROUP)])


def norm_grad(dys, fields, means, rstds, gain):
    n = len(dys)
    shift_sums, gain_sums = [], []
    for dy, x, mean, rstd in zip(dys, fields, means, rstds):
        shift_sums.append(col_sum(dy))
        gain_sums.append(col_sum(dy * (x * rstd - mean * rstd)))
    both = group_sum(jnp.concatenate(shift_sums + gain_sums, axis=0) * gain) / COUNT
    grads = []
    for c in range(n):
        rstd, mean = rstds[c], means[c]
        slope = -rstd * rstd * both[n + c : n + c + 1]
        base = -rstd * both[c : c + 1] - mean * slope
        grads.append(dys[c] * (rstd * gain) + (fields[c] * slope + base))
    return grads, sum(gain_sums), sum(shift_sums)


def second_kernel(
    tall,
    short,
    coef,
    start_in,
    inner_in,
    stats_in,
    noisy,
    target,
    keep,
    kernel_one_flip,
    kernel_two,
    kernel_two_flip,
    qkv,
    qkv_t,
    proj,
    proj_t,
    outlet,
    small,
    bias_qkv,
    embed,
    hidden,
    hidden_slope,
    time_act,
    time_slope,
    time_two,
    shift_low,
    shard_out,
    rest_out,
    grad_one_out,
    grad_two_out,
    grad_qkv_out,
    grad_proj_out,
    grad_outlet_out,
    grad_inlet_out,
    grad_small_out,
    loss_out,
    tshift_grad,
    buf,
    grad_buf,
):
    chunk = noisy.shape[0]
    step = pl.program_id(0)
    sums = (
        grad_one_out,
        grad_two_out,
        grad_qkv_out,
        grad_proj_out,
        grad_outlet_out,
        grad_inlet_out,
        grad_small_out,
        loss_out,
    )

    @pl.when(step == 0)
    def _():
        zero_edges(buf)
        zero_edges(grad_buf)
        for ref in sums:
            ref[...] = jnp.zeros(ref.shape, jnp.float32)

    masks = tap_masks()
    not_first, not_last = edge_masks()
    scale = 256 ** (-0.5)

    def gain(k):
        return small[k : k + 1]

    def shift(k):
        return small[4 + k : 5 + k]

    def normed(x, mean, rstd, k):
        slope = rstd * gain(k)
        return x * slope + (shift(k) - mean * slope)

    def row(values, c):
        return values[c : c + 1]

    def work(images):
        n = len(images)
        every = range(n)
        low, high = images[0], images[-1] + 1

        def part(x, c):
            return x[256 * c : 256 * c + 256]

        slope_two, act_two = [], []
        for c in images:
            z = normed(inner_in[c], stats_in[c, 2:3], stats_in[c, 3:4], 1)
            s = logistic(z)
            kept = jnp.concatenate([keep[s, c] for s in range(keep.shape[0])], axis=0)
            kept = kept.astype(jnp.float32) * (1.0 / KEEP)
            act = z * s * kept
            slope_two.append(s * (1.0 + z * (1.0 - s)) * kept)
            act_two.append(act.astype(jnp.bfloat16))
            put_shifted(buf, c, act, not_first, not_last)
        yield
        conv_two = conv_shifted(buf.at[low:high], kernel_two)
        yield
        middle = [start_in[c] + part(conv_two, i) + small[10:11] for i, c in enumerate(images)]
        mean, rstd = stats_of(middle)
        mean_three, rstd_three = [row(mean, i) for i in every], [row(rstd, i) for i in every]
        tokens = [
            normed(middle[i], mean_three[i], rstd_three[i], 2).astype(jnp.bfloat16) for i in every
        ]
        tokens = jnp.concatenate(tokens, axis=0)
        yield
        qkv_all = (dot(tokens, qkv[...]) + bias_qkv[0:1]).astype(jnp.bfloat16)
        triples = []
        for i in every:
            three = part(qkv_all, i)
            triples.append((three[:, 0:256], three[:, 256:512], three[:, 512:768]))
        scores = [dot(q, k, NT) for q, k, _ in triples]
        yield
        probs, probs_low = [], []
        for i in every:
            expo = jnp.exp((scores[i] - jnp.max(scores[i], axis=1, keepdims=True)) * scale)
            p = expo * (1.0 / jnp.sum(expo, axis=1, keepdims=True))
            probs.append(p)
            probs_low.append(p.astype(jnp.bfloat16))
        yield
        mixed = [dot(probs_low[i], triples[i][2]).astype(jnp.bfloat16) for i in every]
        mixed = jnp.concatenate(mixed, axis=0)
        branch = dot(mixed, proj[...])
        yield
        final = [middle[i] + part(branch, i) + small[13:14] for i in every]
        mean, rstd = stats_of(final)
        mean_four, rstd_four = [row(mean, i) for i in every], [row(rstd, i) for i in every]
        act_four, slope_four = [], []
        for i in every:
            z = normed(final[i], mean_four[i], rstd_four[i], 3)
            s = logistic(z)
            act_four.append((z * s).astype(jnp.bfloat16))
            slope_four.append(s * (1.0 + z * (1.0 - s)))
        yield
        taps_all = [dot(outlet[...], act, NT) for act in act_four]
        yield
        spreads = []
        loss_sum = 0.0
        for i, c in enumerate(images):
            predicted = 0.0
            for tap in range(9):
                move = 16 * (tap // 3 - 1) + tap % 3 - 1
                moved = taps_all[i][8 * tap : 8 * tap + 8]
                moved = moved if move == 0 else pltpu.roll(moved, wrap(-move, 256), 1)
                predicted = predicted + jnp.where(masks[tap], moved, 0.0)
            error = predicted - target[c]
            weight = coef[step * chunk + c]
            loss_sum = loss_sum + (0.5 * weight) * (error * error)
            grad_pred = (weight * error).astype(jnp.bfloat16).astype(jnp.float32)
            spreads.append(tap_stack(grad_pred, masks, -1))
        loss_out[...] += loss_sum
        yield
        grad_outlet_out[...] += sum(dot(s, act) for s, act in zip(spreads, act_four))
        grad_act = [dot(s, outlet[...], TN) for s in spreads]
        yield
        grad_four = [grad_act[i] * slope_four[i] for i in every]
        grad_final, gain_four, shift_four = norm_grad(grad_four, final, mean_four, rstd_four, gain(3))
        branch_all = jnp.concatenate([g.astype(jnp.bfloat16) for g in grad_final], axis=0)
        yield
        grad_proj_out[...] += dot(mixed, branch_all, TN)
        grad_mixed = dot(branch_all, proj_t[...]).astype(jnp.bfloat16)
        dps = [dot(part(grad_mixed, i), triples[i][2], NT) for i in every]
        dvs = [dot(probs_low[i], part(grad_mixed, i), TN) for i in every]
        yield
        dss = []
        for i in every:
            p, dp = probs[i], dps[i]
            dss.append((p * (dp - jnp.sum(p * dp, axis=1, keepdims=True))).astype(jnp.bfloat16))
        yield
        grad_qkv = []
        for i in every:
            q, k, _ = triples[i]
            dq = dot(dss[i], k) * scale
            dk = dot(dss[i], q, TN) * scale
            grad_qkv.append(jnp.concatenate([dq, dk, dvs[i]], axis=1).astype(jnp.bfloat16))
        grad_qkv_all = jnp.concatenate(grad_qkv, axis=0)
        grad_qkv_out[...] += dot(tokens, grad_qkv_all, TN)
        grad_tokens = dot(grad_qkv_all, qkv_t[...])
        yield
        bias_sums = col_sum(grad_qkv_all.astype(jnp.float32))
        grad_norm, gain_three, shift_three = norm_grad(
            [part(grad_tokens, i) for i in every], middle, mean_three, rstd_three, gain(2)
        )
        grad_middle = [grad_final[i] + grad_norm[i] for i in every]
        for i, c in enumerate(images):
            put_shifted(grad_buf, c, grad_middle[i], not_first, not_last)
        yield
        field = jnp.concatenate(act_two, axis=0)
        for i in range(3):
            grad_two_out[i] += dot(field, stacked(grad_buf.at[low:high], i), TN)
        grad_act = conv_shifted(grad_buf.at[low:high], kernel_two_flip)
        yield
        grad_two = [part(grad_act, i) * slope_two[i] for i in every]
        grad_inner, gain_two, shift_two = norm_grad(
            grad_two,
            [inner_in[c] for c in images],
            [stats_in[c, 2:3] for c in images],
            [stats_in[c, 3:4] for c in images],
            gain(1),
        )
        for i, c in enumerate(images):
            put_shifted(grad_buf, c, grad_inner[i], not_first, not_last)
        act_one, slope_one = [], []
        for c in images:
            z = normed(start_in[c], stats_in[c, 0:1], stats_in[c, 1:2], 0)
            s = logistic(z)
            act_one.append((z * s).astype(jnp.bfloat16))
            slope_one.append(s * (1.0 + z * (1.0 - s)))
        yield
        field = jnp.concatenate(act_one, axis=0)
        for i in range(3):
            grad_one_out[i] += dot(field, stacked(grad_buf.at[low:high], i), TN)
        grad_act = conv_shifted(grad_buf.at[low:high], kernel_one_flip)
        yield
        grad_one = [part(grad_act, i) * slope_one[i] for i in every]
        grad_norm, gain_one, shift_one = norm_grad(
            grad_one,
            [start_in[c] for c in images],
            [stats_in[c, 0:1] for c in images],
            [stats_in[c, 1:2] for c in images],
            gain(0),
        )
        grad_start = [grad_middle[i] + grad_norm[i] for i in every]
        patches = [tap_stack(noisy[c], masks, 1) for c in images]
        inner_sums = [col_sum(g) for g in grad_inner]
        for i, c in enumerate(images):
            tshift_grad[pl.ds(step * chunk + c, 1), :] = inner_sums[i]
        grad_small_out[...] += jnp.concatenate(
            [
                gain_one,
                gain_two,
                gain_three,
                gain_four,
                shift_one,
                shift_two,
                shift_three,
                shift_four,
                sum(col_sum(g) for g in grad_start),
                sum(inner_sums),
                sum(col_sum(g) for g in grad_middle),
                bias_sums[:, 0:256],
                bias_sums[:, 512:768],
                sum(col_sum(g) for g in grad_final),
                jnp.zeros((2, 256), jnp.float32),
            ],
            axis=0,
        )
        yield
        grad_inlet_out[...] += sum(
            dot(patch, g.astype(jnp.bfloat16)) for patch, g in zip(patches, grad_start)
        )

    take_turns([work(list(range(g, g + GROUP))) for g in range(0, chunk, GROUP)])

    @pl.when(step == pl.num_programs(0) - 1)
    def _():
        for k, grad in enumerate((grad_one_out, grad_two_out)):
            for tap in range(9):
                at = 256 * (2 - tap % 3)
                for shard, off, row, size in cuts(tap * 256, 256, tall):
                    shard_out[shard, k * tall + off : k * tall + off + size, :] = grad[
                        2 - tap // 3, row : row + size, at : at + 256
                    ]
        for k in range(4):
            grad, at = (grad_qkv_out, 256 * k) if k < 3 else (grad_proj_out, 0)
            for shard, off, row, size in cuts(0, 256, short):
                low = 2 * tall + k * short + off
                shard_out[shard, low : low + size, :] = grad[row : row + size, at : at + 256]
        used = 2 * tall + 4 * short
        if used < shard_out.shape[1]:
            shard_out[:, used:, :] = jnp.zeros(
                (shard_out.shape[0], shard_out.shape[1] - used, 256), jnp.float32
            )
        total = tshift_grad[...]
        shift_grad = full_dot(time_act[...], total, TN)
        grad_act = full_dot(total, shift_low[...], NT) * time_slope[...]
        two_grad = full_dot(hidden[...], grad_act, TN)
        grad_hidden = full_dot(grad_act, time_two[...], NT) * hidden_slope[...]
        one_grad = full_dot(embed[...], grad_hidden, TN)
        width = one_grad.shape[0]
        height = width + two_grad.shape[0]
        for half in range(2):
            span = slice(256 * half, 256 * half + 256)
            rest_out[half * height : half * height + width, :] = one_grad[:, span]
            rest_out[half * height + width : half * height + height, :] = two_grad[:, span]
        act_sum, hidden_sum = col_sum(grad_act), col_sum(grad_hidden)
        parts = [
            shift_grad,
            grad_inlet_out[...],
            grad_outlet_out[...],
            jnp.concatenate(
                [
                    grad_small_out[0:14],
                    col_sum(total),
                    hidden_sum[:, 0:256],
                    hidden_sum[:, 256:512],
                    act_sum[:, 0:256],
                    act_sum[:, 256:512],
                    jnp.zeros((5, 256), jnp.float32),
                ],
                axis=0,
            ),
            loss_out[...],
        ]
        at = 2 * height
        for part in parts:
            rest_out[at : at + part.shape[0], :] = part
            at += part.shape[0]
        if at < rest_out.shape[0]:
            rest_out[at:, :] = jnp.zeros((rest_out.shape[0] - at, 256), jnp.float32)


def cuts(first, size, height):
    parts, row = [], 0
    while row < size:
        shard, off = divmod(first + row, height)
        take = min(height - off, size - row)
        parts.append((shard, off, row, take))
        row += take
    return parts


def full_dot(a, b, dims):
    return lax.dot_general(
        a.astype(jnp.float32),
        b.astype(jnp.float32),
        (dims, ((), ())),
        precision=HIGH_PRECISION,
        preferred_element_type=jnp.float32,
    )


def resident(shape):
    return pl.BlockSpec(shape, lambda i: (0,) * len(shape), pipeline_mode=pl.Buffered(1))


def per_chunk(chunk, *tail):
    return pl.BlockSpec((chunk,) + tail, lambda i: (i,) + (0,) * len(tail))


def by_source(chunk, block):
    return pl.BlockSpec((block[0], chunk) + block[2:], lambda i: (0, i, 0, 0))


def forward_part(chunk, mix, pair, tshift, inlet, kernel_one, small):
    n = pair.shape[1]
    shapes = [(n, 256, 256), (n, 256, 256), (n, 8, 256), (n, 8, 256), (n, 8, 256)]
    return pl.pallas_call(
        first_kernel,
        grid=(n // chunk,),
        in_specs=[
            pl.BlockSpec(memory_space=pltpu.SMEM),
            by_source(chunk, pair.shape),
            per_chunk(chunk, 1, 256),
            resident(inlet.shape),
            resident(kernel_one.shape),
            resident(small.shape),
        ],
        out_specs=[per_chunk(chunk, *s[1:]) for s in shapes],
        out_shape=[jax.ShapeDtypeStruct(s, jnp.float32) for s in shapes],
        scratch_shapes=[pltpu.VMEM((chunk, 288, 768), jnp.bfloat16)],
        compiler_params=pltpu.CompilerParams(vmem_limit_bytes=VMEM_LIMIT),
        cost_estimate=pl.CostEstimate(
            flops=2 * n * 256 * 256 * 2400, bytes_accessed=n * 1 << 19, transcendentals=n * 1 << 16
        ),
        name="forward_part",
    )(mix, pair, tshift, inlet, kernel_one, small)


def main_part(chunk, sizes, coef, start, inner, stats, noisy, target, keep, weights, small, bias_qkv, times):
    n = noisy.shape[0]
    batch, shard_rows, tall, short, rest_rows = sizes
    outs = [(batch, shard_rows, 256), (rest_rows, 256)]
    sums = [(3, 256, 768), (3, 256, 768), (256, 768), (256, 256), (80, 256), (80, 256), (16, 256), (8, 256)]
    return pl.pallas_call(
        functools.partial(second_kernel, tall, short),
        grid=(n // chunk,),
        in_specs=[
            pl.BlockSpec(memory_space=pltpu.SMEM),
            per_chunk(chunk, 256, 256),
            per_chunk(chunk, 256, 256),
            per_chunk(chunk, 8, 256),
            per_chunk(chunk, 8, 256),
            per_chunk(chunk, 8, 256),
            by_source(chunk, keep.shape),
        ]
        + [resident(w.shape) for w in weights]
        + [resident(small.shape), resident(bias_qkv.shape)]
        + [resident(t.shape) for t in times],
        out_specs=[resident(g) for g in outs],
        out_shape=[jax.ShapeDtypeStruct(g, jnp.float32) for g in outs],
        scratch_shapes=[pltpu.VMEM(g, jnp.float32) for g in sums + [(n, 256)]]
        + [pltpu.VMEM((chunk, 288, 768), jnp.bfloat16)] * 2,
        compiler_params=pltpu.CompilerParams(vmem_limit_bytes=VMEM_LIMIT),
        cost_estimate=pl.CostEstimate(
            flops=70 * n * 2 * 256**3, bytes_accessed=n * 5 << 17, transcendentals=n * 5 << 16
        ),
        name="main_part",
    )(coef, start, inner, stats, noisy, target, keep, *weights, small, bias_qkv, *times)


def rows_first(weight):
    inputs, outputs = weight.shape[0] // 9, weight.shape[1]
    flipped = jnp.transpose(weight.reshape(9, inputs, outputs)[::-1], (0, 2, 1))
    return flipped.reshape(9 * outputs, inputs)


def padded_taps(rows):
    padded = jnp.pad(rows.reshape(9, 3, 256), ((0, 1), (0, 5), (0, 0)))
    return padded.reshape(80, 256)


MESH = pl.DeviceIdType.MESH
MISC_ROWS = (640, 640, 512, 80, 80, 24, 8)
MISC_TOTAL = 2048


def padded_rows(total, parts):
    return -(-total // (8 * parts)) * 8


def exchange_kernel(
    shard_shape,
    rates,
    grads_a,
    grads_b,
    state_kernel,
    state_attention,
    weight_kernel,
    weight_attention,
    scalars,
    out_a,
    out_b,
    shard_grad,
    norm_out,
    half_a,
    half_b,
    row_a,
    row_b,
    deep_a,
    deep_b,
    shard_weight,
    shard_first,
    shard_second,
    square_core,
    square_rows,
    square_deep,
    local_sem,
    core_send,
    core_recv,
    row_send,
    row_recv,
    deep_send,
    deep_recv,
    shard_send,
    shard_recv,
    square_send,
    square_recv,
    deep_send_two,
    deep_recv_two,
    row_send_two,
    row_recv_two,
    core_send_two,
    core_recv_two,
):
    depth, _, rows, piece, _ = grads_a.shape
    lanes = grads_b.shape[3]
    pairs, tall, quads, short = shard_shape
    batch, r = lax.axis_index("batch"), lax.axis_index("rows")
    z, c = batch // 2, batch % 2
    partner = z * 2 + (1 - c)
    row_peers = [(r + d) % rows for d in range(1, rows)]
    deep_peers = [(z + d) % depth for d in range(1, depth)]

    def remote(src, dst, send, recv, where):
        return pltpu.make_async_remote_copy(
            src_ref=src, dst_ref=dst, send_sem=send, recv_sem=recv, device_id=where, device_id_type=MESH
        )

    def blocks(kernel_ref, attention_ref, flat, base, offset):
        copies = []
        for k in range(pairs + quads):
            ref, own, size = (kernel_ref, k, tall) if k < pairs else (attention_ref, k - pairs, short)
            at = k * tall if k < pairs else pairs * tall + own * short
            far = ref.at[own] if offset is None else ref.at[own, pl.ds(offset * size, size)]
            near = flat.at[pl.ds(at, size)]
            copies.append(pltpu.make_async_copy(far, near, local_sem.at[base * (pairs + quads) + k]))
        for copy in copies:
            copy.start()
        return copies

    fetches = (
        blocks(weight_kernel, weight_attention, shard_weight, 0, batch)
        + blocks(state_kernel.at[0], state_attention.at[0], shard_first, 1, None)
        + blocks(state_kernel.at[1], state_attention.at[1], shard_second, 2, None)
    )

    barrier = pltpu.get_barrier_semaphore()
    pl.semaphore_signal(barrier, inc=1, device_id=(partner, r), device_id_type=MESH)
    for peer in row_peers:
        pl.semaphore_signal(barrier, inc=1, device_id=(batch, peer), device_id_type=MESH)
    for peer in deep_peers:
        pl.semaphore_signal(barrier, inc=1, device_id=(peer * 2 + c, r), device_id_type=MESH)
    pl.semaphore_wait(barrier, rows + depth - 1)

    cut = (piece // 8 + 1) // 2 * 8
    chunks = [
        (grads_b, half_b, row_b, deep_b, 0, lanes),
        (grads_a, half_a, row_a, deep_a, 0, cut),
        (grads_a, half_a, row_a, deep_a, cut, piece - cut),
    ]
    pending = []

    core_copies = []
    for k, (grads, half, _, _, at, size) in enumerate(chunks):
        copy = remote(
            grads.at[:, 1 - c, :, pl.ds(at, size)],
            half.at[:, :, pl.ds(at, size)],
            core_send.at[k],
            core_recv.at[k],
            (partner, r),
        )
        copy.start()
        core_copies.append(copy)
    row_copies = []
    for k, (grads, half, row, _, at, size) in enumerate(chunks):
        core_copies[k].wait_recv()

        def add_own(t, carry, grads=grads, half=half, at=at, size=size):
            i, j = t // rows, t % rows
            span = pl.ds(at, size)
            half[i, j, span] = half[i, j, span] + grads[i, c, j, span]
            return carry

        lax.fori_loop(0, depth * rows, add_own, 0)
        copies = []
        for d, peer in enumerate(row_peers):
            copy = remote(
                half.at[:, peer, pl.ds(at, size)],
                row.at[d, :, pl.ds(at, size)],
                row_send.at[k, d],
                row_recv.at[k, d],
                (batch, peer),
            )
            copy.start()
            copies.append(copy)
        row_copies.append(copies)
    deep_copies = []
    for k, (grads, half, row, deep, at, size) in enumerate(chunks):
        for copy in row_copies[k]:
            copy.wait_recv()

        def add_rows(i, carry, half=half, row=row, at=at, size=size):
            span = pl.ds(at, size)
            total = half[i, r, span]
            for d in range(rows - 1):
                total = total + row[d, i, span]
            half[i, r, span] = total
            return carry

        lax.fori_loop(0, depth, add_rows, 0)
        copies = []
        for d, peer in enumerate(deep_peers):
            copy = remote(
                half.at[peer, r, pl.ds(at, size)],
                deep.at[d, pl.ds(at, size)],
                deep_send.at[k, d],
                deep_recv.at[k, d],
                (peer * 2 + c, r),
            )
            copy.start()
            copies.append(copy)
        deep_copies.append(copies)

    def finish(k):
        _, half, _, deep, at, size = chunks[k]
        for copy in deep_copies[k]:
            copy.wait_recv()
        span = pl.ds(at, size)
        total = half[z, r, span]
        for d in range(depth - 1):
            total = total + deep[d, span]
        return total

    def squares(x):
        return jnp.sum((x * x).reshape(-1, 8, 256), axis=0)

    def gather(bufs, k, at, size, stage):
        span = pl.ds(at, size)
        copies = []
        if stage == 0:
            for d, peer in enumerate(deep_peers):
                copies.append(
                    remote(
                        bufs.at[z, c, r, span],
                        bufs.at[z, c, r, span],
                        deep_send_two.at[k, d],
                        deep_recv_two.at[k, d],
                        (peer * 2 + c, r),
                    )
                )
        elif stage == 1:
            for d, peer in enumerate(row_peers):
                copies.append(
                    remote(
                        bufs.at[:, c, r, span],
                        bufs.at[:, c, r, span],
                        row_send_two.at[k, d],
                        row_recv_two.at[k, d],
                        (batch, peer),
                    )
                )
        else:
            copies.append(
                remote(
                    bufs.at[:, c, :, span],
                    bufs.at[:, c, :, span],
                    core_send_two.at[k],
                    core_recv_two.at[k],
                    (partner, r),
                )
            )
        for copy in copies:
            copy.start()
        return copies

    total = finish(0)
    out_b[z, c, r] = total
    stage_zero = [gather(out_b, 0, 0, lanes, 0)]
    line = (batch * rows + r) * lanes + lax.broadcasted_iota(jnp.int32, total.shape, 0)
    square = squares(jnp.where(line < sum(MISC_ROWS[:-1]), total, 0.0))
    for k in (1, 2):
        total = finish(k)
        shard_grad[r, pl.ds(chunks[k][4], chunks[k][5])] = total
        square = square + squares(total)
    square_core[0] = square
    copy = remote(square_core.at[0], square_core.at[1], square_send.at[0], square_recv.at[0], (partner, r))
    copy.start()
    pending.append(copy)
    shard_copies = []
    for d, peer in enumerate(row_peers):
        share = remote(
            shard_grad.at[r], shard_grad.at[r], shard_send.at[d], shard_recv.at[d], (batch, peer)
        )
        share.start()
        shard_copies.append(share)
    copy.wait_recv()
    square_rows[r] = square_core[0] + square_core[1]
    copies = []
    for d, peer in enumerate(row_peers):
        copy = remote(
            square_rows.at[r], square_rows.at[r], square_send.at[1 + d], square_recv.at[1 + d], (batch, peer)
        )
        copy.start()
        copies.append(copy)
    pending += copies
    for copy in copies:
        copy.wait_recv()
    square_deep[z] = sum(square_rows[j] for j in range(rows))
    copies = []
    for d, peer in enumerate(deep_peers):
        copy = remote(
            square_deep.at[z],
            square_deep.at[z],
            square_send.at[rows + d],
            square_recv.at[rows + d],
            (peer * 2 + c, r),
        )
        copy.start()
        copies.append(copy)
    pending += copies
    for copy in copies:
        copy.wait_recv()
    square = sum(square_deep[j] for j in range(depth))
    norm = jnp.sqrt(jnp.sum(jnp.sum(square, axis=0, keepdims=True), axis=1, keepdims=True))
    clip = CLIP / jnp.maximum(norm, CLIP)
    norm_out[...] = jnp.broadcast_to(norm, norm_out.shape)

    def moments(at, g):
        span = pl.ds(at, piece)
        first = BETA_ONE * shard_first[span] + (1.0 - BETA_ONE) * g
        second = BETA_TWO * shard_second[span] + (1.0 - BETA_TWO) * g * g
        return first, second

    for fetch in fetches:
        fetch.wait()
    mine = pl.multiple_of(r * piece, 8)
    first, second = moments(mine, shard_grad[r] * clip)
    line = mine + lax.broadcasted_iota(jnp.int32, first.shape, 0)
    rate = jnp.where(line < pairs * tall, rates[0], rates[1])
    weight = shard_weight[pl.ds(mine, piece)]
    step = first * scalars[0] / (jnp.sqrt(second * scalars[1]) + EPS_ADAM)
    out_a[z, c, r] = weight - rate * (step + DECAY * weight)
    for k in (1, 2):
        stage_zero.append(gather(out_a, k, chunks[k][4], chunks[k][5], 0))
    stage_one, stage_two = [], []
    for k in range(3):
        for copy in stage_zero[k]:
            copy.wait_recv()
        stage_one.append(gather(out_b if k == 0 else out_a, k, chunks[k][4], chunks[k][5], 1))
    for k in range(3):
        for copy in stage_one[k]:
            copy.wait_recv()
        stage_two.append(gather(out_b if k == 0 else out_a, k, chunks[k][4], chunks[k][5], 2))
    for copy in shard_copies:
        copy.wait_recv()
    for copies in stage_two:
        for copy in copies:
            copy.wait_recv()
    pending += core_copies + shard_copies
    for copies in row_copies + deep_copies + stage_zero + stage_one + stage_two:
        pending += copies
    for copy in pending:
        copy.wait_send()


def exchange(grads_a, grads_b, state_kernel, state_attention, weight_kernel, weight_attention, scalars):
    depth, _, rows, piece, width = grads_a.shape
    lanes = grads_b.shape[3]
    pairs, tall = state_kernel.shape[1:3]
    quads, short = state_attention.shape[1:3]
    shape = functools.partial(jax.ShapeDtypeStruct, dtype=jnp.float32)
    whole = pl.BlockSpec(memory_space=pltpu.VMEM)
    dma = pltpu.SemaphoreType.DMA
    vmem = functools.partial(pltpu.VMEM, dtype=jnp.float32)
    return pl.pallas_call(
        functools.partial(exchange_kernel, (pairs, tall, quads, short), (RATES[1], RATES[2])),
        in_specs=[whole] * 2
        + [pl.BlockSpec(memory_space=pl.ANY)] * 4
        + [pl.BlockSpec(memory_space=pltpu.SMEM)],
        out_specs=[whole] * 4,
        out_shape=[
            shape(grads_a.shape),
            shape(grads_b.shape),
            shape((rows, piece, width)),
            shape((8, 128)),
        ],
        scratch_shapes=[
            vmem((depth, rows, piece, width)),
            vmem((depth, rows, lanes, width)),
            vmem((rows - 1, depth, piece, width)),
            vmem((rows - 1, depth, lanes, width)),
            vmem((depth - 1, piece, width)),
            vmem((depth - 1, lanes, width)),
            vmem((rows * piece, width)),
            vmem((rows * piece, width)),
            vmem((rows * piece, width)),
            vmem((2, 8, width)),
            vmem((rows, 8, width)),
            vmem((depth, 8, width)),
            dma((3 * (pairs + quads),)),
            dma((3,)),
            dma((3,)),
            dma((3, rows - 1)),
            dma((3, rows - 1)),
            dma((3, depth - 1)),
            dma((3, depth - 1)),
            dma((rows - 1,)),
            dma((rows - 1,)),
            dma((rows + depth - 1,)),
            dma((rows + depth - 1,)),
            dma((3, depth - 1)),
            dma((3, depth - 1)),
            dma((3, rows - 1)),
            dma((3, rows - 1)),
            dma((3,)),
            dma((3,)),
        ],
        compiler_params=pltpu.CompilerParams(
            collective_id=0, has_side_effects=True, vmem_limit_bytes=VMEM_LIMIT
        ),
        name="exchange",
    )(grads_a, grads_b, state_kernel, state_attention, weight_kernel, weight_attention, scalars)


def finish_kernel(
    scalars,
    norm_tile,
    fresh,
    average_kernel,
    average_attention,
    shard_grad,
    state_kernel,
    state_attention,
    time_left,
    time_right,
    shift_rows,
    rest_rows,
    *refs,
):
    weights, states, averages, refs = refs[:5], refs[5:10], refs[10:15], refs[15:]
    (kernel_out, attention_out), refs = refs[:2], refs[2:]
    updated, firsts, seconds, refs = refs[:5], refs[5:10], refs[10:15], refs[15:]
    first_kernel_out, first_attention_out, second_kernel_out, second_attention_out, loss_out, norm_out = refs
    norm = norm_tile[0:1, 0:1]
    clip = CLIP / jnp.maximum(norm, CLIP)
    kept = scalars[2]

    def averaged(out, index, new, average):
        out[(0,) + index] = new
        out[(1,) + index] = kept * average + (1.0 - kept) * new

    tall, short = state_kernel.shape[2], state_attention.shape[2]
    for k in range(2):
        averaged(kernel_out, (k,), fresh[0, k * tall : k * tall + tall], average_kernel[k])
    for k in range(4):
        at = 2 * tall + k * short
        averaged(attention_out, (k,), fresh[0, at : at + short], average_attention[k])

    def moments(first, second, g):
        return BETA_ONE * first + (1.0 - BETA_ONE) * g, BETA_TWO * second + (1.0 - BETA_TWO) * g * g

    def update(k, rate, grad):
        weight = weights[k][...]
        first, second = moments(states[k][0], states[k][1], grad * clip)
        firsts[k][...] = first
        seconds[k][...] = second
        step = first * scalars[0] / (jnp.sqrt(second * scalars[1]) + EPS_ADAM)
        averaged(updated[k], (), weight - rate * (step + DECAY * weight), averages[k][...])

    update(0, RATES[3], jnp.concatenate([time_left[...], time_right[...]], axis=1))
    update(1, RATES[4], shift_rows[...])

    @pl.when(pl.program_id(0) == 0)
    def _():
        for refs, outs, count, height in (
            (state_kernel, (first_kernel_out, second_kernel_out), 2, tall),
            (state_attention, (first_attention_out, second_attention_out), 4, short),
        ):
            for k in range(count):
                at = k * height + (0 if count == 2 else 2 * tall)
                first, second = moments(refs[0, k], refs[1, k], shard_grad[at : at + height] * clip)
                outs[0][k] = first
                outs[1][k] = second
        inlet = jnp.concatenate([rest_rows[8 * tap : 8 * tap + 3] for tap in range(9)], axis=0)
        outlet = jnp.concatenate([rest_rows[80 + 8 * tap : 83 + 8 * tap] for tap in range(9)], axis=1)
        update(2, RATES[0], inlet)
        update(3, RATES[5], outlet)
        update(4, RATES[6], rest_rows[160:179])
        loss_out[...] = jnp.sum(col_sum(rest_rows[184:192]), axis=1, keepdims=True)
        norm_out[...] = norm


def finish(scalars, norm_tile, fresh, average_kernel, average_attention, shard_grad, state_kernel, state_attention, rest, weights, states, averages):
    batch, shard_rows, width = fresh.shape
    tall, short = state_kernel.shape[2], state_attention.shape[2]
    (time_rows, time_width), (shift_rows, _) = weights[0].shape, weights[1].shape
    time_part, shift_part = time_rows // batch, shift_rows // batch
    shape = functools.partial(jax.ShapeDtypeStruct, dtype=jnp.float32)

    def at(block, index):
        return pl.BlockSpec(block, index)

    def rows_of(k, lead):
        part, wide = ((time_part, time_width), (shift_part, width))[k]
        return pl.BlockSpec(lead + (part, wide), lambda b: (0,) * len(lead) + (b, 0))

    def five(lead):
        return [rows_of(0, lead), rows_of(1, lead)] + [resident(lead + w.shape) for w in weights[2:]]

    shift_at = 2 * time_rows // shift_part
    rest_at = (2 * time_rows + shift_rows) // 256
    return pl.pallas_call(
        finish_kernel,
        grid=(batch,),
        in_specs=[
            pl.BlockSpec(memory_space=pltpu.SMEM),
            resident(norm_tile.shape),
            at((1, shard_rows, width), lambda b: (b, 0, 0)),
            at((2, tall, width), lambda b: (0, b, 0)),
            at((4, short, width), lambda b: (0, b, 0)),
            resident(shard_grad.shape),
            resident(state_kernel.shape),
            resident(state_attention.shape),
            at((time_part, width), lambda b: (b, 0)),
            at((time_part, width), lambda b: (batch + b, 0)),
            at((shift_part, width), lambda b: (shift_at + b, 0)),
            pl.BlockSpec((256, width), lambda b: (rest_at, 0), pipeline_mode=pl.Buffered(1)),
        ]
        + five(())
        + five((2,))
        + five(()),
        out_specs=[
            at((2, 2, tall, width), lambda b: (0, 0, b, 0)),
            at((2, 4, short, width), lambda b: (0, 0, b, 0)),
        ]
        + five((2,))
        + five(())
        + five(())
        + [resident(state_kernel.shape[1:]), resident(state_attention.shape[1:])] * 2
        + [resident((1, 1))] * 2,
        out_shape=[
            shape((2, 2, batch * tall, width)),
            shape((2, 4, batch * short, width)),
        ]
        + [shape((2,) + w.shape) for w in weights]
        + [shape(w.shape) for w in weights] * 2
        + [shape(state_kernel.shape[1:]), shape(state_attention.shape[1:])] * 2
        + [shape((1, 1))] * 2,
        compiler_params=pltpu.CompilerParams(vmem_limit_bytes=VMEM_LIMIT),
        cost_estimate=pl.CostEstimate(flops=40 << 20, bytes_accessed=36 << 20, transcendentals=1 << 20),
        name="finish",
    )(
        scalars,
        norm_tile,
        fresh,
        average_kernel,
        average_attention,
        shard_grad,
        state_kernel,
        state_attention,
        rest,
        rest,
        rest,
        rest,
        *weights,
        *states,
        *averages,
    )


def local(
    x_clean,
    noise,
    timesteps,
    keep_mask,
    adam_step,
    inlet_weight,
    kernel_weight,
    attention_weight,
    time_weight,
    shift_weight,
    outlet_weight,
    small_params,
    state_inlet,
    state_kernel,
    state_attention,
    state_time,
    state_shift,
    state_outlet,
    state_small,
    average_inlet,
    average_kernel,
    average_attention,
    average_time,
    average_shift,
    average_outlet,
    average_small,
):
    chans = kernel_weight.shape[2]
    width_sin = time_weight.shape[0] - time_weight.shape[1]
    rows, batch = lax.axis_size("rows"), lax.axis_size("batch")
    own = timesteps.shape[0] // rows
    pair = jnp.concatenate([x_clean, noise], axis=1)
    pair = pair.reshape(rows, own, 6, -1)
    pair = jnp.pad(pair, ((0, 0), (0, 0), (0, 2), (0, 0)))
    pair = lax.all_to_all(pair, "rows", 0, 0, tiled=True)
    keep = keep_mask.reshape(rows, own, -1, chans).astype(jnp.bfloat16)
    (
        keep,
        timesteps,
        adam_step,
        inlet_low,
        kernels,
        projections,
        time_low,
        shift_low,
        outlet_low,
        small_low,
    ) = lax.optimization_barrier(
        (
            keep,
            timesteps,
            adam_step,
            inlet_weight,
            kernel_weight,
            attention_weight,
            time_weight,
            shift_weight,
            outlet_weight,
            small_params,
        )
    )
    keep = lax.all_to_all(keep, "rows", 0, 0, tiled=True)
    timesteps = lax.dynamic_slice_in_dim(timesteps, lax.axis_index("rows") * own, own, 0)
    bars = alpha_bars(timesteps)
    mix = jnp.stack([jnp.sqrt(bars), jnp.sqrt(1.0 - bars)])
    kernels = kernels.astype(jnp.bfloat16)
    projections = projections.astype(jnp.bfloat16)
    time_low = time_low.astype(jnp.bfloat16)
    shift_low = shift_low.astype(jnp.bfloat16)
    inlet = padded_taps(inlet_low).astype(jnp.bfloat16)
    outlet = padded_taps(
        jnp.transpose(outlet_low.reshape(3, 9, chans), (1, 0, 2)).reshape(27, chans)
    ).astype(jnp.bfloat16)
    qkv = jnp.concatenate([projections[0], projections[1], projections[2]], axis=1)
    embed = sinusoid(timesteps, width_sin).astype(jnp.bfloat16)
    hidden_pre = jnp.dot(
        embed, time_low[:width_sin], preferred_element_type=jnp.float32
    ) + small_low[15:17].reshape(-1)
    hidden = jax.nn.silu(hidden_pre).astype(jnp.bfloat16)
    time_emb = jnp.dot(
        hidden, time_low[width_sin:], preferred_element_type=jnp.float32
    ) + small_low[17:19].reshape(-1)
    time_act = jax.nn.silu(time_emb).astype(jnp.bfloat16)
    time_shift = jnp.dot(time_act, shift_low, preferred_element_type=jnp.float32) + small_low[14]
    ratio = bars / (1.0 - bars)
    snr_weight = jnp.minimum(ratio, GAMMA) / ratio
    denom = 3 * 256 * own * rows * batch
    coef = 2.0 * snr_weight / denom
    start, inner, stats, noisy, target = forward_part(
        FORWARD_CHUNK, mix, pair, (time_shift + small_low[9])[:, None, :], inlet, kernels[0], small_low
    )
    bias_qkv = jnp.concatenate([small_low[11], jnp.zeros_like(small_low[0]), small_low[12]])
    tall, short = state_kernel.shape[2], state_attention.shape[2]
    shard_rows = rows * padded_rows(2 * tall + 4 * short, rows)
    lanes = padded_rows(MISC_TOTAL, batch * rows)
    shards, rest = main_part(
        CHUNK,
        (batch, shard_rows, tall, short, batch * rows * lanes),
        coef,
        start,
        inner,
        stats,
        noisy,
        target,
        keep,
        (
            rows_first(kernels[0]),
            kernels[1],
            rows_first(kernels[1]),
            qkv,
            qkv.T,
            projections[3],
            projections[3].T,
            outlet,
        ),
        small_low,
        bias_qkv[None],
        (
            embed,
            hidden,
            swish_grad(hidden_pre),
            time_act,
            swish_grad(time_emb),
            time_low[width_sin:],
            shift_low,
        ),
    )
    count = adam_step[0].astype(jnp.float32)
    scalars = jnp.stack(
        [
            1.0 / (1.0 - BETA_ONE**count),
            1.0 / (1.0 - BETA_TWO**count),
            jnp.minimum(EMA_TOP, (1.0 + count) / (10.0 + count)),
        ]
    )
    fresh, rest, shard_grad, norm_tile = exchange(
        shards.reshape(batch // 2, 2, rows, shard_rows // rows, chans),
        rest.reshape(batch // 2, 2, rows, lanes, chans),
        state_kernel,
        state_attention,
        kernel_weight,
        attention_weight,
        scalars,
    )
    results = finish(
        scalars,
        norm_tile,
        fresh.reshape(batch, shard_rows, chans),
        lax.all_gather(average_kernel, "batch", axis=1, tiled=True),
        lax.all_gather(average_attention, "batch", axis=1, tiled=True),
        shard_grad.reshape(shard_rows, chans),
        state_kernel,
        state_attention,
        rest.reshape(-1, chans),
        (time_weight, shift_weight, inlet_weight, outlet_weight, small_params),
        (state_time, state_shift, state_inlet, state_outlet, state_small),
        (average_time, average_shift, average_inlet, average_outlet, average_small),
    )
    kernel_pair, attention_pair = results[:2]
    triples = [results[2 + 5 * k : 7 + 5 * k] for k in range(3)]
    first_conv, first_attention, second_conv, second_attention, loss, norm = results[17:]
    ordered = []
    for (time, shift, inlet, outlet, small), middle in zip(
        triples,
        ((kernel_pair, attention_pair), (first_conv, first_attention), (second_conv, second_attention)),
    ):
        ordered += [inlet, *middle, time, shift, outlet, small]
    return (*ordered, loss.reshape(()), norm.reshape(()))


def solution(mesh):
    return jax.shard_map(
        local,
        mesh=mesh,
        in_specs=(
            P("batch", None, "rows", None),
            P("batch", None, "rows", None),
            P("batch"),
            P("batch", "rows", None, None),
            P(),
            P(),
            P(),
            P(),
            P(),
            P(),
            P(),
            P(),
            P(),
            P(None, None, "batch", None),
            P(None, None, "batch", None),
            P(),
            P(),
            P(),
            P(),
            P(),
            P(None, "batch", None),
            P(None, "batch", None),
            P(),
            P(),
            P(),
            P(),
        ),
        out_specs=(
            P(),
            P(),
            P(),
            P(),
            P(),
            P(),
            P(),
            P(),
            P(None, "batch", None),
            P(None, "batch", None),
            P(),
            P(),
            P(),
            P(),
            P(),
            P(None, "batch", None),
            P(None, "batch", None),
            P(),
            P(),
            P(),
            P(),
            P(),
            P(),
        ),
        check_vma=False,
    )
```

```python
import functools
import math

import jax
import jax.numpy as jnp
import numpy as np
from jax import lax
from jax.experimental import pallas as pl
from jax.experimental.pallas import tpu as pltpu
from jax.sharding import PartitionSpec as P

G = 32


HIGH_PRECISION = lax.Precision.HIGHEST
CLIP = 0.05
GAMMA = 5.0
KEEP = 0.9
EPS_NORM = 1e-05
BETA_ONE = 0.9
BETA_TWO = 0.999
EPS_ADAM = 1e-08
DECAY = 0.01
EMA_TOP = 0.9999
VMEM_LIMIT = 60 << 20
CHUNK = 4
FORWARD_CHUNK = 4
GROUP = 2
COUNT = 2048.0
RATES = (0.1, 0.01, 0.03, 0.05, 0.02, 0.01, 0.2)


def bar_table():
    beta_rates = 0.0001 + (0.02 - 0.0001) * np.arange(1000, dtype=np.float64) / 999.0
    return np.exp(np.cumsum(np.log(1.0 - beta_rates))).astype(np.float32)


def alpha_bars(timesteps):
    one_hot = (timesteps[:, None] == jnp.arange(1000)[None, :]).astype(jnp.float32)
    return jnp.sum(one_hot * bar_table()[None, :], axis=1)


def sinusoid(timesteps, width):
    half = width // 2
    rates = jnp.exp(-math.log(10000.0) * jnp.arange(half).astype(jnp.float32) / (half - 1))
    angles = timesteps.astype(jnp.float32)[:, None] * rates[None, :]
    return jnp.concatenate([jnp.sin(angles), jnp.cos(angles)], axis=1)


def swish_grad(pre):
    logistic = jax.nn.sigmoid(pre)
    return logistic * (1.0 + pre * (1.0 - logistic))


def wrap(shift, size):
    return shift % size


def tap_masks():
    lane = lax.broadcasted_iota(jnp.int32, (8, 256), 1)
    row, col = lane // 16, lane % 16
    masks = []
    for i in range(3):
        for j in range(3):
            ok = (row + (i - 1) >= 0) & (row + (i - 1) < 16) & (col + (j - 1) >= 0) & (col + (j - 1) < 16)
            masks.append(ok)
    return masks


def tap_stack(tile, masks, sign):
    parts = []
    for tap in range(9):
        step = sign * (16 * (tap // 3 - 1) + tap % 3 - 1)
        moved = tile if step == 0 else pltpu.roll(tile, wrap(-step, 256), 1)
        parts.append(jnp.where(masks[tap if sign > 0 else 8 - tap], moved, 0.0))
    parts.append(jnp.zeros_like(tile))
    return jnp.concatenate(parts, axis=0).astype(jnp.bfloat16)


def group_sum(rows):
    halves = []
    for half in range(2):
        part = rows[:, 128 * half : 128 * half + 128]
        lane = lax.broadcasted_iota(jnp.int32, part.shape, 1)
        for step in (1, 2, 4):
            upper = (lane // step) % 2 == 1
            part = part + jnp.where(upper, pltpu.roll(part, step, 1), pltpu.roll(part, 128 - step, 1))
        halves.append(part)
    return jnp.concatenate(halves, axis=1)


def col_sum(x):
    return jnp.sum(x, axis=0, keepdims=True)


def stats_of(fields):
    sums = jnp.concatenate([col_sum(x) for x in fields] + [col_sum(x * x) for x in fields], axis=0)
    both = group_sum(sums) / COUNT
    n = len(fields)
    mean = both[:n]
    spread = both[n:] - mean * mean
    return mean, lax.rsqrt(spread + EPS_NORM)


def logistic(z):
    return 0.5 * jnp.tanh(0.5 * z) + 0.5


def put_shifted(buf, c, y, not_first, not_last):
    buf[c, 16:272, 256:512] = y.astype(jnp.bfloat16)
    buf[c, 16:272, 0:256] = jnp.where(not_first, pltpu.roll(y, 1, 0), 0.0).astype(jnp.bfloat16)
    buf[c, 16:272, 512:768] = jnp.where(not_last, pltpu.roll(y, 255, 0), 0.0).astype(jnp.bfloat16)


def edge_masks():
    col = lax.broadcasted_iota(jnp.int32, (256, 256), 0) % 16
    return col != 0, col != 15


def stacked(buf, i):
    chunk = buf.shape[0]
    return buf[:, 16 * i : 16 * i + 256, :].reshape(chunk * 256, 768)


def dot(a, b, dims=((1,), (0,))):
    return lax.dot_general(a, b, (dims, ((), ())), preferred_element_type=jnp.float32)


NT = ((1,), (1,))
TN = ((0,), (0,))


def conv_shifted(buf, weight):
    field = jnp.concatenate([stacked(buf, i) for i in range(3)], axis=1)
    return dot(field, weight[...])


def zero_edges(buf):
    edge = jnp.zeros((buf.shape[0], 16, 768), jnp.bfloat16)
    buf[:, 0:16, :] = edge
    buf[:, 272:288, :] = edge


def take_turns(workers):
    live, started = [], 0
    while live or started < len(workers):
        if started < len(workers):
            live.append(workers[started])
            started += 1
        live = [w for w in live if next(w, live) is not live]


def lanes_joined(blocks):
    return blocks[0] if len(blocks) == 1 else jnp.concatenate(blocks, axis=1)


def first_kernel(
    mix, pair, tshift, inlet, kernel_one, small, start_out, inner_out, stats_out, noisy_out, target_out, buf
):
    chunk = start_out.shape[0]
    step = pl.program_id(0)

    @pl.when(step == 0)
    def _():
        zero_edges(buf)

    masks = tap_masks()
    not_first, not_last = edge_masks()
    real = lax.broadcasted_iota(jnp.int32, (8, 256), 0) < 3

    def work(images):
        n = len(images)
        every = range(n)
        low, high = images[0], images[-1] + 1
        starts = []
        for c in images:
            both = lanes_joined([pair[s, c] for s in range(pair.shape[0])])
            clean = jnp.where(real, both, 0.0)
            noise = jnp.where(real, pltpu.roll(both, 5, 0), 0.0)
            noisy = mix[0, step * chunk + c] * clean + mix[1, step * chunk + c] * noise
            noisy = noisy.astype(jnp.bfloat16).astype(jnp.float32)
            noisy_out[c] = noisy
            target_out[c] = noise
            start = dot(tap_stack(noisy, masks, 1), inlet[...], TN) + small[8:9]
            start_out[c] = start
            starts.append(start)
        yield
        mean, rstd = stats_of(starts)
        for i, c in enumerate(images):
            scale = rstd[i : i + 1] * small[0:1]
            z = starts[i] * scale + (small[4:5] - mean[i : i + 1] * scale)
            put_shifted(buf, c, z * logistic(z), not_first, not_last)
        yield
        inner_all = conv_shifted(buf.at[low:high], kernel_one)
        yield
        inners = []
        for i, c in enumerate(images):
            inner = inner_all[256 * i : 256 * i + 256] + tshift[c]
            inner_out[c] = inner
            inners.append(inner)
        mean_two, rstd_two = stats_of(inners)
        for i, c in enumerate(images):
            stats_out[c] = jnp.concatenate(
                [mean[i : i + 1], rstd[i : i + 1], mean_two[i : i + 1], rstd_two[i : i + 1]]
                + [jnp.zeros((4, 256), jnp.float32)],
                axis=0,
            )

    take_turns([work(list(range(g, g + GROUP))) for g in range(0, chunk, GROUP)])


def norm_grad(dys, fields, means, rstds, gain):
    n = len(dys)
    shift_sums, gain_sums = [], []
    for dy, x, mean, rstd in zip(dys, fields, means, rstds):
        shift_sums.append(col_sum(dy))
        gain_sums.append(col_sum(dy * (x * rstd - mean * rstd)))
    both = group_sum(jnp.concatenate(shift_sums + gain_sums, axis=0) * gain) / COUNT
    grads = []
    for c in range(n):
        rstd, mean = rstds[c], means[c]
        slope = -rstd * rstd * both[n + c : n + c + 1]
        base = -rstd * both[c : c + 1] - mean * slope
        grads.append(dys[c] * (rstd * gain) + (fields[c] * slope + base))
    return grads, sum(gain_sums), sum(shift_sums)


def second_kernel(
    tall,
    short,
    coef,
    start_in,
    inner_in,
    stats_in,
    noisy,
    target,
    keep,
    kernel_one_flip,
    kernel_two,
    kernel_two_flip,
    qkv,
    qkv_t,
    proj,
    proj_t,
    outlet,
    small,
    bias_qkv,
    embed,
    hidden,
    hidden_slope,
    time_act,
    time_slope,
    time_two,
    shift_low,
    shard_out,
    rest_out,
    grad_one_out,
    grad_two_out,
    grad_qkv_out,
    grad_proj_out,
    grad_outlet_out,
    grad_inlet_out,
    grad_small_out,
    loss_out,
    tshift_grad,
    buf,
    grad_buf,
):
    chunk = noisy.shape[0]
    step = pl.program_id(0)
    sums = (
        grad_one_out,
        grad_two_out,
        grad_qkv_out,
        grad_proj_out,
        grad_outlet_out,
        grad_inlet_out,
        grad_small_out,
        loss_out,
    )

    @pl.when(step == 0)
    def _():
        zero_edges(buf)
        zero_edges(grad_buf)
        for ref in sums:
            ref[...] = jnp.zeros(ref.shape, jnp.float32)

    masks = tap_masks()
    not_first, not_last = edge_masks()
    scale = 256 ** (-0.5)

    def gain(k):
        return small[k : k + 1]

    def shift(k):
        return small[4 + k : 5 + k]

    def normed(x, mean, rstd, k):
        slope = rstd * gain(k)
        return x * slope + (shift(k) - mean * slope)

    def row(values, c):
        return values[c : c + 1]

    def work(images):
        n = len(images)
        every = range(n)
        low, high = images[0], images[-1] + 1

        def part(x, c):
            return x[256 * c : 256 * c + 256]

        slope_two, act_two = [], []
        for c in images:
            z = normed(inner_in[c], stats_in[c, 2:3], stats_in[c, 3:4], 1)
            s = logistic(z)
            kept = jnp.concatenate([keep[s, c] for s in range(keep.shape[0])], axis=0)
            kept = kept.astype(jnp.float32) * (1.0 / KEEP)
            act = z * s * kept
            slope_two.append(s * (1.0 + z * (1.0 - s)) * kept)
            act_two.append(act.astype(jnp.bfloat16))
            put_shifted(buf, c, act, not_first, not_last)
        yield
        conv_two = conv_shifted(buf.at[low:high], kernel_two)
        yield
        middle = [start_in[c] + part(conv_two, i) + small[10:11] for i, c in enumerate(images)]
        mean, rstd = stats_of(middle)
        mean_three, rstd_three = [row(mean, i) for i in every], [row(rstd, i) for i in every]
        tokens = [
            normed(middle[i], mean_three[i], rstd_three[i], 2).astype(jnp.bfloat16) for i in every
        ]
        tokens = jnp.concatenate(tokens, axis=0)
        yield
        qkv_all = (dot(tokens, qkv[...]) + bias_qkv[0:1]).astype(jnp.bfloat16)
        triples = []
        for i in every:
            three = part(qkv_all, i)
            triples.append((three[:, 0:256], three[:, 256:512], three[:, 512:768]))
        scores = [dot(q, k, NT) for q, k, _ in triples]
        yield
        probs, probs_low = [], []
        for i in every:
            expo = jnp.exp((scores[i] - jnp.max(scores[i], axis=1, keepdims=True)) * scale)
            p = expo * (1.0 / jnp.sum(expo, axis=1, keepdims=True))
            probs.append(p)
            probs_low.append(p.astype(jnp.bfloat16))
        yield
        mixed = [dot(probs_low[i], triples[i][2]).astype(jnp.bfloat16) for i in every]
        mixed = jnp.concatenate(mixed, axis=0)
        branch = dot(mixed, proj[...])
        yield
        final = [middle[i] + part(branch, i) + small[13:14] for i in every]
        mean, rstd = stats_of(final)
        mean_four, rstd_four = [row(mean, i) for i in every], [row(rstd, i) for i in every]
        act_four, slope_four = [], []
        for i in every:
            z = normed(final[i], mean_four[i], rstd_four[i], 3)
            s = logistic(z)
            act_four.append((z * s).astype(jnp.bfloat16))
            slope_four.append(s * (1.0 + z * (1.0 - s)))
        yield
        taps_all = [dot(outlet[...], act, NT) for act in act_four]
        yield
        spreads = []
        loss_sum = 0.0
        for i, c in enumerate(images):
            predicted = 0.0
            for tap in range(9):
                move = 16 * (tap // 3 - 1) + tap % 3 - 1
                moved = taps_all[i][8 * tap : 8 * tap + 8]
                moved = moved if move == 0 else pltpu.roll(moved, wrap(-move, 256), 1)
                predicted = predicted + jnp.where(masks[tap], moved, 0.0)
            error = predicted - target[c]
            weight = coef[step * chunk + c]
            loss_sum = loss_sum + (0.5 * weight) * (error * error)
            grad_pred = (weight * error).astype(jnp.bfloat16).astype(jnp.float32)
            spreads.append(tap_stack(grad_pred, masks, -1))
        loss_out[...] += loss_sum
        yield
        grad_outlet_out[...] += sum(dot(s, act) for s, act in zip(spreads, act_four))
        grad_act = [dot(s, outlet[...], TN) for s in spreads]
        yield
        grad_four = [grad_act[i] * slope_four[i] for i in every]
        grad_final, gain_four, shift_four = norm_grad(grad_four, final, mean_four, rstd_four, gain(3))
        branch_all = jnp.concatenate([g.astype(jnp.bfloat16) for g in grad_final], axis=0)
        yield
        grad_proj_out[...] += dot(mixed, branch_all, TN)
        grad_mixed = dot(branch_all, proj_t[...]).astype(jnp.bfloat16)
        dps = [dot(part(grad_mixed, i), triples[i][2], NT) for i in every]
        dvs = [dot(probs_low[i], part(grad_mixed, i), TN) for i in every]
        yield
        dss = []
        for i in every:
            p, dp = probs[i], dps[i]
            dss.append((p * (dp - jnp.sum(p * dp, axis=1, keepdims=True))).astype(jnp.bfloat16))
        yield
        grad_qkv = []
        for i in every:
            q, k, _ = triples[i]
            dq = dot(dss[i], k) * scale
            dk = dot(dss[i], q, TN) * scale
            grad_qkv.append(jnp.concatenate([dq, dk, dvs[i]], axis=1).astype(jnp.bfloat16))
        grad_qkv_all = jnp.concatenate(grad_qkv, axis=0)
        grad_qkv_out[...] += dot(tokens, grad_qkv_all, TN)
        grad_tokens = dot(grad_qkv_all, qkv_t[...])
        yield
        bias_sums = col_sum(grad_qkv_all.astype(jnp.float32))
        grad_norm, gain_three, shift_three = norm_grad(
            [part(grad_tokens, i) for i in every], middle, mean_three, rstd_three, gain(2)
        )
        grad_middle = [grad_final[i] + grad_norm[i] for i in every]
        for i, c in enumerate(images):
            put_shifted(grad_buf, c, grad_middle[i], not_first, not_last)
        yield
        field = jnp.concatenate(act_two, axis=0)
        for i in range(3):
            grad_two_out[i] += dot(field, stacked(grad_buf.at[low:high], i), TN)
        grad_act = conv_shifted(grad_buf.at[low:high], kernel_two_flip)
        yield
        grad_two = [part(grad_act, i) * slope_two[i] for i in every]
        grad_inner, gain_two, shift_two = norm_grad(
            grad_two,
            [inner_in[c] for c in images],
            [stats_in[c, 2:3] for c in images],
            [stats_in[c, 3:4] for c in images],
            gain(1),
        )
        for i, c in enumerate(images):
            put_shifted(grad_buf, c, grad_inner[i], not_first, not_last)
        act_one, slope_one = [], []
        for c in images:
            z = normed(start_in[c], stats_in[c, 0:1], stats_in[c, 1:2], 0)
            s = logistic(z)
            act_one.append((z * s).astype(jnp.bfloat16))
            slope_one.append(s * (1.0 + z * (1.0 - s)))
        yield
        field = jnp.concatenate(act_one, axis=0)
        for i in range(3):
            grad_one_out[i] += dot(field, stacked(grad_buf.at[low:high], i), TN)
        grad_act = conv_shifted(grad_buf.at[low:high], kernel_one_flip)
        yield
        grad_one = [part(grad_act, i) * slope_one[i] for i in every]
        grad_norm, gain_one, shift_one = norm_grad(
            grad_one,
            [start_in[c] for c in images],
            [stats_in[c, 0:1] for c in images],
            [stats_in[c, 1:2] for c in images],
            gain(0),
        )
        grad_start = [grad_middle[i] + grad_norm[i] for i in every]
        patches = [tap_stack(noisy[c], masks, 1) for c in images]
        inner_sums = [col_sum(g) for g in grad_inner]
        for i, c in enumerate(images):
            tshift_grad[pl.ds(step * chunk + c, 1), :] = inner_sums[i]
        grad_small_out[...] += jnp.concatenate(
            [
                gain_one,
                gain_two,
                gain_three,
                gain_four,
                shift_one,
                shift_two,
                shift_three,
                shift_four,
                sum(col_sum(g) for g in grad_start),
                sum(inner_sums),
                sum(col_sum(g) for g in grad_middle),
                bias_sums[:, 0:256],
                bias_sums[:, 512:768],
                sum(col_sum(g) for g in grad_final),
                jnp.zeros((2, 256), jnp.float32),
            ],
            axis=0,
        )
        yield
        grad_inlet_out[...] += sum(
            dot(patch, g.astype(jnp.bfloat16)) for patch, g in zip(patches, grad_start)
        )

    take_turns([work(list(range(g, g + GROUP))) for g in range(0, chunk, GROUP)])

    @pl.when(step == pl.num_programs(0) - 1)
    def _():
        for k, grad in enumerate((grad_one_out, grad_two_out)):
            for tap in range(9):
                at = 256 * (2 - tap % 3)
                for shard, off, row, size in cuts(tap * 256, 256, tall):
                    shard_out[shard, k * tall + off : k * tall + off + size, :] = grad[
                        2 - tap // 3, row : row + size, at : at + 256
                    ]
        for k in range(4):
            grad, at = (grad_qkv_out, 256 * k) if k < 3 else (grad_proj_out, 0)
            for shard, off, row, size in cuts(0, 256, short):
                low = 2 * tall + k * short + off
                shard_out[shard, low : low + size, :] = grad[row : row + size, at : at + 256]
        used = 2 * tall + 4 * short
        if used < shard_out.shape[1]:
            shard_out[:, used:, :] = jnp.zeros(
                (shard_out.shape[0], shard_out.shape[1] - used, 256), jnp.float32
            )
        total = tshift_grad[...]
        shift_grad = full_dot(time_act[...], total, TN)
        grad_act = full_dot(total, shift_low[...], NT) * time_slope[...]
        two_grad = full_dot(hidden[...], grad_act, TN)
        grad_hidden = full_dot(grad_act, time_two[...], NT) * hidden_slope[...]
        one_grad = full_dot(embed[...], grad_hidden, TN)
        width = one_grad.shape[0]
        height = width + two_grad.shape[0]
        for half in range(2):
            span = slice(256 * half, 256 * half + 256)
            rest_out[half * height : half * height + width, :] = one_grad[:, span]
            rest_out[half * height + width : half * height + height, :] = two_grad[:, span]
        act_sum, hidden_sum = col_sum(grad_act), col_sum(grad_hidden)
        parts = [
            shift_grad,
            grad_inlet_out[...],
            grad_outlet_out[...],
            jnp.concatenate(
                [
                    grad_small_out[0:14],
                    col_sum(total),
                    hidden_sum[:, 0:256],
                    hidden_sum[:, 256:512],
                    act_sum[:, 0:256],
                    act_sum[:, 256:512],
                    jnp.zeros((5, 256), jnp.float32),
                ],
                axis=0,
            ),
            loss_out[...],
        ]
        at = 2 * height
        for part in parts:
            rest_out[at : at + part.shape[0], :] = part
            at += part.shape[0]
        if at < rest_out.shape[0]:
            rest_out[at:, :] = jnp.zeros((rest_out.shape[0] - at, 256), jnp.float32)


def cuts(first, size, height):
    parts, row = [], 0
    while row < size:
        shard, off = divmod(first + row, height)
        take = min(height - off, size - row)
        parts.append((shard, off, row, take))
        row += take
    return parts


def full_dot(a, b, dims):
    return lax.dot_general(
        a.astype(jnp.float32),
        b.astype(jnp.float32),
        (dims, ((), ())),
        precision=HIGH_PRECISION,
        preferred_element_type=jnp.float32,
    )


def resident(shape):
    return pl.BlockSpec(shape, lambda i: (0,) * len(shape), pipeline_mode=pl.Buffered(1))


def per_chunk(chunk, *tail):
    return pl.BlockSpec((chunk,) + tail, lambda i: (i,) + (0,) * len(tail))


def by_source(chunk, block):
    return pl.BlockSpec((block[0], chunk) + block[2:], lambda i: (0, i, 0, 0))


def forward_part(chunk, mix, pair, tshift, inlet, kernel_one, small):
    n = pair.shape[1]
    shapes = [(n, 256, 256), (n, 256, 256), (n, 8, 256), (n, 8, 256), (n, 8, 256)]
    return pl.pallas_call(
        first_kernel,
        grid=(n // chunk,),
        in_specs=[
            pl.BlockSpec(memory_space=pltpu.SMEM),
            by_source(chunk, pair.shape),
            per_chunk(chunk, 1, 256),
            resident(inlet.shape),
            resident(kernel_one.shape),
            resident(small.shape),
        ],
        out_specs=[per_chunk(chunk, *s[1:]) for s in shapes],
        out_shape=[jax.ShapeDtypeStruct(s, jnp.float32) for s in shapes],
        scratch_shapes=[pltpu.VMEM((chunk, 288, 768), jnp.bfloat16)],
        compiler_params=pltpu.CompilerParams(vmem_limit_bytes=VMEM_LIMIT),
        cost_estimate=pl.CostEstimate(
            flops=2 * n * 256 * 256 * 2400, bytes_accessed=n * 1 << 19, transcendentals=n * 1 << 16
        ),
        name="forward_part",
    )(mix, pair, tshift, inlet, kernel_one, small)


def main_part(chunk, sizes, coef, start, inner, stats, noisy, target, keep, weights, small, bias_qkv, times):
    n = noisy.shape[0]
    batch, shard_rows, tall, short, rest_rows = sizes
    outs = [(batch, shard_rows, 256), (rest_rows, 256)]
    sums = [(3, 256, 768), (3, 256, 768), (256, 768), (256, 256), (80, 256), (80, 256), (16, 256), (8, 256)]
    return pl.pallas_call(
        functools.partial(second_kernel, tall, short),
        grid=(n // chunk,),
        in_specs=[
            pl.BlockSpec(memory_space=pltpu.SMEM),
            per_chunk(chunk, 256, 256),
            per_chunk(chunk, 256, 256),
            per_chunk(chunk, 8, 256),
            per_chunk(chunk, 8, 256),
            per_chunk(chunk, 8, 256),
            by_source(chunk, keep.shape),
        ]
        + [resident(w.shape) for w in weights]
        + [resident(small.shape), resident(bias_qkv.shape)]
        + [resident(t.shape) for t in times],
        out_specs=[resident(g) for g in outs],
        out_shape=[jax.ShapeDtypeStruct(g, jnp.float32) for g in outs],
        scratch_shapes=[pltpu.VMEM(g, jnp.float32) for g in sums + [(n, 256)]]
        + [pltpu.VMEM((chunk, 288, 768), jnp.bfloat16)] * 2,
        compiler_params=pltpu.CompilerParams(vmem_limit_bytes=VMEM_LIMIT),
        cost_estimate=pl.CostEstimate(
            flops=70 * n * 2 * 256**3, bytes_accessed=n * 5 << 17, transcendentals=n * 5 << 16
        ),
        name="main_part",
    )(coef, start, inner, stats, noisy, target, keep, *weights, small, bias_qkv, *times)


def rows_first(weight):
    inputs, outputs = weight.shape[0] // 9, weight.shape[1]
    flipped = jnp.transpose(weight.reshape(9, inputs, outputs)[::-1], (0, 2, 1))
    return flipped.reshape(9 * outputs, inputs)


def padded_taps(rows):
    padded = jnp.pad(rows.reshape(9, 3, 256), ((0, 1), (0, 5), (0, 0)))
    return padded.reshape(80, 256)


MESH = pl.DeviceIdType.MESH
MISC_ROWS = (640, 640, 512, 80, 80, 24, 8)
MISC_TOTAL = 2048
SPLIT_A = 11
SPLIT_B = 4
LAG = 3


def padded_rows(total, parts):
    return -(-total // (8 * parts)) * 8


def factors(rows):
    low = max(d for d in range(1, rows + 1) if rows % d == 0 and d * d <= rows)
    return low, rows // low


def exchange_kernel(
    shard_shape,
    rates,
    grads_a,
    grads_b,
    state_kernel,
    state_attention,
    weight_kernel,
    weight_attention,
    scalars,
    out_a,
    out_b,
    shard_grad,
    norm_out,
    own_a,
    own_b,
    half_a,
    half_b,
    near_a,
    near_b,
    far_a,
    far_b,
    deep_a,
    deep_b,
    piece_a,
    piece_b,
    shard_weight,
    shard_first,
    shard_second,
    square_core,
    square_rows,
    square_deep,
    local_sem,
    own_sem,
    core_send,
    core_recv,
    near_send,
    near_recv,
    far_send,
    far_recv,
    deep_send,
    deep_recv,
    shard_send,
    shard_recv,
    square_send,
    square_recv,
    deep_send_two,
    deep_recv_two,
    near_send_two,
    near_recv_two,
    far_send_two,
    far_recv_two,
    core_send_two,
    core_recv_two,
    keep_sem,
):
    depth, _, tops, wide, piece, _ = grads_a.shape
    lanes = grads_b.shape[4]
    rows = tops * wide
    pairs, tall, quads, short = shard_shape
    batch, r = lax.axis_index("batch"), lax.axis_index("rows")
    z, c = batch // 2, batch % 2
    y, x = r // wide, r % wide
    partner = z * 2 + (1 - c)
    row_peers = [(r + d) % rows for d in range(1, rows)]
    deep_peers = [(z + d) % depth for d in range(1, depth)]
    x_peers = [(x + d) % wide for d in range(1, wide)]
    y_peers = [(y + d) % tops for d in range(1, tops)]

    def remote(src, dst, send, recv, where):
        return pltpu.make_async_remote_copy(
            src_ref=src, dst_ref=dst, send_sem=send, recv_sem=recv, device_id=where, device_id_type=MESH
        )

    def begin(copies):
        for copy in copies:
            copy.start()
        return copies

    def arrived(copies):
        for copy in copies:
            copy.wait_recv()

    def blocks(kernel_ref, attention_ref, flat, base, offset):
        copies = []
        for k in range(pairs + quads):
            ref, own, size = (kernel_ref, k, tall) if k < pairs else (attention_ref, k - pairs, short)
            at = k * tall if k < pairs else pairs * tall + own * short
            far = ref.at[own] if offset is None else ref.at[own, pl.ds(offset * size, size)]
            near = flat.at[pl.ds(at, size)]
            copies.append(pltpu.make_async_copy(far, near, local_sem.at[base * (pairs + quads) + k]))
        return begin(copies)

    owns = begin(
        [
            pltpu.make_async_copy(grads_b.at[:, c], own_b, own_sem.at[0]),
            pltpu.make_async_copy(grads_a.at[:, c], own_a, own_sem.at[1]),
        ]
    )

    barrier = pltpu.get_barrier_semaphore()
    pl.semaphore_signal(barrier, inc=1, device_id=(partner, r), device_id_type=MESH)
    for peer in row_peers:
        pl.semaphore_signal(barrier, inc=1, device_id=(batch, peer), device_id_type=MESH)
    for peer in deep_peers:
        pl.semaphore_signal(barrier, inc=1, device_id=(peer * 2 + c, r), device_id_type=MESH)
    pl.semaphore_wait(barrier, rows + depth - 1)

    set_a = (grads_a, own_a, half_a, near_a, far_a, deep_a, piece_a, out_a)
    set_b = (grads_b, own_b, half_b, near_b, far_b, deep_b, piece_b, out_b)
    chunks = []
    for group, height, parts in ((set_b, lanes, SPLIT_B), (set_a, piece, SPLIT_A)):
        marks = [height // 8 * k // parts * 8 for k in range(parts + 1)]
        for low, high in zip(marks[:-1], marks[1:]):
            if high > low:
                chunks.append(group + (low, high - low, len(chunks) % 2 == 0))
    count = len(chunks)
    small = sum(1 for chunk in chunks if chunk[0] is grads_b)

    core_copies = []
    for k, (grads, _, half, _, _, _, _, _, at, size, _) in enumerate(chunks):
        span = pl.ds(at, size)
        core_copies.append(
            begin(
                [
                    remote(
                        grads.at[:, 1 - c, :, :, span],
                        half.at[:, :, :, span],
                        core_send.at[k],
                        core_recv.at[k],
                        (partner, r),
                    )
                ]
            )
        )
    fetches = (
        blocks(weight_kernel, weight_attention, shard_weight, 0, batch)
        + blocks(state_kernel.at[0], state_attention.at[0], shard_first, 1, None)
        + blocks(state_kernel.at[1], state_attention.at[1], shard_second, 2, None)
    )
    near_copies, far_copies, deep_copies = [], [], []

    def sum_near(k):
        _, own, half, near, _, _, _, _, at, size, x_first = chunks[k]
        if k == 0:
            owns[0].wait()
        if k == small:
            owns[1].wait()
        arrived(core_copies[k])
        span = pl.ds(at, size)

        def add_own(t, carry):
            i, j, l = t // rows, t // wide % tops, t % wide
            half[i, j, l, span] = half[i, j, l, span] + own[i, j, l, span]
            return carry

        lax.fori_loop(0, depth * rows, add_own, 0)
        copies = []
        for d, peer in enumerate(x_peers if x_first else y_peers):
            src = half.at[:, :, peer, span] if x_first else half.at[:, peer, :, span]
            dst = near.at[d, :, pl.ds(0, tops if x_first else wide), span]
            where = (batch, y * wide + peer) if x_first else (batch, peer * wide + x)
            copies.append(remote(src, dst, near_send.at[k, d], near_recv.at[k, d], where))
        near_copies.append(begin(copies))

    def sum_far(k):
        _, _, half, near, far, _, _, _, at, size, x_first = chunks[k]
        arrived(near_copies[k])
        span = pl.ds(at, size)
        across = tops if x_first else wide

        def add_near(t, carry):
            i, j = t // across, t % across
            place = (i, j, x) if x_first else (i, y, j)
            total = half[place + (span,)]
            for d in range((wide if x_first else tops) - 1):
                total = total + near[d, i, j, span]
            half[place + (span,)] = total
            return carry

        lax.fori_loop(0, depth * across, add_near, 0)
        copies = []
        for d, peer in enumerate(y_peers if x_first else x_peers):
            src = half.at[:, peer, x, span] if x_first else half.at[:, y, peer, span]
            where = (batch, peer * wide + x) if x_first else (batch, y * wide + peer)
            copies.append(
                remote(src, far.at[d, :, span], far_send.at[k, d], far_recv.at[k, d], where)
            )
        far_copies.append(begin(copies))

    def sum_deep(k):
        _, _, half, _, far, deep, _, _, at, size, x_first = chunks[k]
        arrived(far_copies[k])
        span = pl.ds(at, size)

        def add_far(i, carry):
            total = half[i, y, x, span]
            for d in range((tops if x_first else wide) - 1):
                total = total + far[d, i, span]
            half[i, y, x, span] = total
            return carry

        lax.fori_loop(0, depth, add_far, 0)
        copies = []
        for d, peer in enumerate(deep_peers):
            copies.append(
                remote(
                    half.at[peer, y, x, span],
                    deep.at[d, span],
                    deep_send.at[k, d],
                    deep_recv.at[k, d],
                    (peer * 2 + c, r),
                )
            )
        deep_copies.append(begin(copies))

    def finish_sum(k):
        _, _, half, _, _, deep, _, _, at, size, _ = chunks[k]
        arrived(deep_copies[k])
        span = pl.ds(at, size)
        total = half[z, y, x, span]
        for d in range(depth - 1):
            total = total + deep[d, span]
        return total

    def squares(values):
        return jnp.sum((values * values).reshape(-1, 8, 256), axis=0)

    def gather_deep(k):
        _, _, _, _, _, _, part, out, at, size, _ = chunks[k]
        span = pl.ds(at, size)
        keep = pltpu.make_async_copy(part.at[span], out.at[z, c, y, x, span], keep_sem.at[k])
        keep.start()
        copies = []
        for d, peer in enumerate(deep_peers):
            copies.append(
                remote(
                    part.at[span],
                    out.at[z, c, y, x, span],
                    deep_send_two.at[k, d],
                    deep_recv_two.at[k, d],
                    (peer * 2 + c, r),
                )
            )
        return keep, begin(copies)

    def gather_near(k):
        _, _, _, _, _, _, _, out, at, size, x_first = chunks[k]
        place = out.at[:, c, y, x, pl.ds(at, size)]
        copies = []
        for d, peer in enumerate(y_peers if x_first else x_peers):
            where = (batch, peer * wide + x) if x_first else (batch, y * wide + peer)
            copies.append(remote(place, place, near_send_two.at[k, d], near_recv_two.at[k, d], where))
        return begin(copies)

    def gather_far(k):
        _, _, _, _, _, _, _, out, at, size, x_first = chunks[k]
        span = pl.ds(at, size)
        place = out.at[:, c, :, x, span] if x_first else out.at[:, c, y, :, span]
        copies = []
        for d, peer in enumerate(x_peers if x_first else y_peers):
            where = (batch, y * wide + peer) if x_first else (batch, peer * wide + x)
            copies.append(remote(place, place, far_send_two.at[k, d], far_recv_two.at[k, d], where))
        return begin(copies)

    def gather_core(k):
        _, _, _, _, _, _, _, out, at, size, _ = chunks[k]
        place = out.at[:, c, :, :, pl.ds(at, size)]
        return begin([remote(place, place, core_send_two.at[k], core_recv_two.at[k], (partner, r))])

    keeps, firsts, seconds, thirds, lasts = [], [], [], [], []
    partial = []

    def send_deep(k):
        keep, copies = gather_deep(k)
        keeps.append(keep)
        firsts.append(copies)

    def send_near(k):
        keeps[k].wait()
        arrived(firsts[k])
        seconds.append(gather_near(k))

    def send_far(k):
        arrived(seconds[k])
        thirds.append(gather_far(k))

    def send_core(k):
        arrived(thirds[k])
        lasts.append(gather_core(k))

    def sum_last(k):
        total = finish_sum(k)
        at, size = chunks[k][8], chunks[k][9]
        counted = total
        if k < small:
            piece_b[pl.ds(at, size)] = total
            line = (batch * rows + r) * lanes + at + lax.broadcasted_iota(jnp.int32, total.shape, 0)
            counted = jnp.where(line < sum(MISC_ROWS[:-1]), total, 0.0)
            send_deep(k)
        else:
            shard_grad[r, pl.ds(at, size)] = total
        partial.append(squares(counted))

    for t in range(count + 3 * LAG):
        for stage, lag in ((sum_near, 0), (sum_far, LAG), (sum_deep, 2 * LAG), (sum_last, 3 * LAG)):
            if 0 <= t - lag < count:
                stage(t - lag)
    square = sum(partial)
    square_core[0] = square
    square_copies = begin(
        [remote(square_core.at[0], square_core.at[1], square_send.at[0], square_recv.at[0], (partner, r))]
    )
    shard_copies = begin(
        [
            remote(shard_grad.at[r], shard_grad.at[r], shard_send.at[d], shard_recv.at[d], (batch, peer))
            for d, peer in enumerate(row_peers)
        ]
    )
    arrived(square_copies)
    square_rows[r] = square_core[0] + square_core[1]
    copies = begin(
        [
            remote(
                square_rows.at[r],
                square_rows.at[r],
                square_send.at[1 + d],
                square_recv.at[1 + d],
                (batch, peer),
            )
            for d, peer in enumerate(row_peers)
        ]
    )
    for k in range(small):
        send_near(k)
    arrived(copies)
    square_copies += copies
    square_deep[z] = sum(square_rows[j] for j in range(rows))
    copies = begin(
        [
            remote(
                square_deep.at[z],
                square_deep.at[z],
                square_send.at[rows + d],
                square_recv.at[rows + d],
                (peer * 2 + c, r),
            )
            for d, peer in enumerate(deep_peers)
        ]
    )
    for fetch in fetches:
        fetch.wait()
    for k in range(small):
        send_far(k)
    arrived(copies)
    square_copies += copies
    square = sum(square_deep[j] for j in range(depth))
    norm = jnp.sqrt(jnp.sum(jnp.sum(square, axis=0, keepdims=True), axis=1, keepdims=True))
    clip = CLIP / jnp.maximum(norm, CLIP)
    norm_out[...] = jnp.broadcast_to(norm, norm_out.shape)
    for k in range(small, count):
        at, size = chunks[k][8], chunks[k][9]
        span = pl.ds(pl.multiple_of(r * piece + at, 8), size)
        g = shard_grad[r, pl.ds(at, size)] * clip
        first = BETA_ONE * shard_first[span] + (1.0 - BETA_ONE) * g
        second = BETA_TWO * shard_second[span] + (1.0 - BETA_TWO) * g * g
        line = r * piece + at + lax.broadcasted_iota(jnp.int32, g.shape, 0)
        rate = jnp.where(line < pairs * tall, rates[0], rates[1])
        weight = shard_weight[span]
        step = first * scalars[0] / (jnp.sqrt(second * scalars[1]) + EPS_ADAM)
        piece_a[pl.ds(at, size)] = weight - rate * (step + DECAY * weight)
        send_deep(k)
    for k in range(small):
        send_core(k)
    for t in range(small, count + 2 * LAG):
        for stage, lag in ((send_near, 0), (send_far, LAG), (send_core, 2 * LAG)):
            if small <= t - lag < count:
                stage(t - lag)
    arrived(shard_copies)
    for copies in lasts:
        arrived(copies)
    for copies in (
        core_copies + near_copies + far_copies + deep_copies + firsts + seconds + thirds + lasts
    ):
        for copy in copies:
            copy.wait_send()
    for copy in square_copies + shard_copies:
        copy.wait_send()


def exchange(grads_a, grads_b, state_kernel, state_attention, weight_kernel, weight_attention, scalars):
    depth, _, rows, piece, width = grads_a.shape
    tops, wide = factors(rows)
    lanes = grads_b.shape[3]
    grads_a = grads_a.reshape(depth, 2, tops, wide, piece, width)
    grads_b = grads_b.reshape(depth, 2, tops, wide, lanes, width)
    pairs, tall = state_kernel.shape[1:3]
    quads, short = state_attention.shape[1:3]
    shape = functools.partial(jax.ShapeDtypeStruct, dtype=jnp.float32)
    whole = pl.BlockSpec(memory_space=pltpu.VMEM)
    anywhere = pl.BlockSpec(memory_space=pl.ANY)
    dma = pltpu.SemaphoreType.DMA
    vmem = functools.partial(pltpu.VMEM, dtype=jnp.float32)
    most = max(tops, wide)
    return pl.pallas_call(
        functools.partial(exchange_kernel, (pairs, tall, quads, short), (RATES[1], RATES[2])),
        in_specs=[anywhere] * 6 + [pl.BlockSpec(memory_space=pltpu.SMEM)],
        out_specs=[anywhere] * 2 + [whole] * 2,
        out_shape=[
            shape(grads_a.shape),
            shape(grads_b.shape),
            shape((rows, piece, width)),
            shape((8, 128)),
        ],
        scratch_shapes=[
            vmem((depth, tops, wide, piece, width)),
            vmem((depth, tops, wide, lanes, width)),
            vmem((depth, tops, wide, piece, width)),
            vmem((depth, tops, wide, lanes, width)),
            vmem((most - 1, depth, most, piece, width)),
            vmem((most - 1, depth, most, lanes, width)),
            vmem((most - 1, depth, piece, width)),
            vmem((most - 1, depth, lanes, width)),
            vmem((depth - 1, piece, width)),
            vmem((depth - 1, lanes, width)),
            vmem((piece, width)),
            vmem((lanes, width)),
            vmem((rows * piece, width)),
            vmem((rows * piece, width)),
            vmem((rows * piece, width)),
            vmem((2, 8, width)),
            vmem((rows, 8, width)),
            vmem((depth, 8, width)),
            dma((3 * (pairs + quads),)),
            dma((2,)),
            dma((SPLIT_A + SPLIT_B,)),
            dma((SPLIT_A + SPLIT_B,)),
            dma((SPLIT_A + SPLIT_B, most - 1)),
            dma((SPLIT_A + SPLIT_B, most - 1)),
            dma((SPLIT_A + SPLIT_B, most - 1)),
            dma((SPLIT_A + SPLIT_B, most - 1)),
            dma((SPLIT_A + SPLIT_B, depth - 1)),
            dma((SPLIT_A + SPLIT_B, depth - 1)),
            dma((rows - 1,)),
            dma((rows - 1,)),
            dma((rows + depth - 1,)),
            dma((rows + depth - 1,)),
            dma((SPLIT_A + SPLIT_B, depth - 1)),
            dma((SPLIT_A + SPLIT_B, depth - 1)),
            dma((SPLIT_A + SPLIT_B, most - 1)),
            dma((SPLIT_A + SPLIT_B, most - 1)),
            dma((SPLIT_A + SPLIT_B, most - 1)),
            dma((SPLIT_A + SPLIT_B, most - 1)),
            dma((SPLIT_A + SPLIT_B,)),
            dma((SPLIT_A + SPLIT_B,)),
            dma((SPLIT_A + SPLIT_B,)),
        ],
        compiler_params=pltpu.CompilerParams(
            collective_id=0, has_side_effects=True, vmem_limit_bytes=VMEM_LIMIT
        ),
        name="exchange",
    )(grads_a, grads_b, state_kernel, state_attention, weight_kernel, weight_attention, scalars)


def finish_kernel(
    scalars,
    norm_tile,
    fresh,
    average_kernel,
    average_attention,
    shard_grad,
    state_kernel,
    state_attention,
    time_left,
    time_right,
    shift_rows,
    rest_rows,
    *refs,
):
    weights, states, averages, refs = refs[:5], refs[5:10], refs[10:15], refs[15:]
    (kernel_out, attention_out), refs = refs[:2], refs[2:]
    updated, firsts, seconds, refs = refs[:5], refs[5:10], refs[10:15], refs[15:]
    first_kernel_out, first_attention_out, second_kernel_out, second_attention_out, loss_out, norm_out = refs
    norm = norm_tile[0:1, 0:1]
    clip = CLIP / jnp.maximum(norm, CLIP)
    kept = scalars[2]

    def averaged(out, index, new, average):
        out[(0,) + index] = new
        out[(1,) + index] = kept * average + (1.0 - kept) * new

    tall, short = state_kernel.shape[2], state_attention.shape[2]
    for k in range(2):
        averaged(kernel_out, (k,), fresh[0, k * tall : k * tall + tall], average_kernel[k])
    for k in range(4):
        at = 2 * tall + k * short
        averaged(attention_out, (k,), fresh[0, at : at + short], average_attention[k])

    def moments(first, second, g):
        return BETA_ONE * first + (1.0 - BETA_ONE) * g, BETA_TWO * second + (1.0 - BETA_TWO) * g * g

    def update(k, rate, grad):
        weight = weights[k][...]
        first, second = moments(states[k][0], states[k][1], grad * clip)
        firsts[k][...] = first
        seconds[k][...] = second
        step = first * scalars[0] / (jnp.sqrt(second * scalars[1]) + EPS_ADAM)
        averaged(updated[k], (), weight - rate * (step + DECAY * weight), averages[k][...])

    update(0, RATES[3], jnp.concatenate([time_left[...], time_right[...]], axis=1))
    update(1, RATES[4], shift_rows[...])

    @pl.when(pl.program_id(0) == 0)
    def _():
        for refs, outs, count, height in (
            (state_kernel, (first_kernel_out, second_kernel_out), 2, tall),
            (state_attention, (first_attention_out, second_attention_out), 4, short),
        ):
            for k in range(count):
                at = k * height + (0 if count == 2 else 2 * tall)
                first, second = moments(refs[0, k], refs[1, k], shard_grad[at : at + height] * clip)
                outs[0][k] = first
                outs[1][k] = second
        inlet = jnp.concatenate([rest_rows[8 * tap : 8 * tap + 3] for tap in range(9)], axis=0)
        outlet = jnp.concatenate([rest_rows[80 + 8 * tap : 83 + 8 * tap] for tap in range(9)], axis=1)
        update(2, RATES[0], inlet)
        update(3, RATES[5], outlet)
        update(4, RATES[6], rest_rows[160:179])
        loss_out[...] = jnp.sum(col_sum(rest_rows[184:192]), axis=1, keepdims=True)
        norm_out[...] = norm


def finish(scalars, norm_tile, fresh, average_kernel, average_attention, shard_grad, state_kernel, state_attention, rest, weights, states, averages):
    batch, shard_rows, width = fresh.shape
    tall, short = state_kernel.shape[2], state_attention.shape[2]
    (time_rows, time_width), (shift_rows, _) = weights[0].shape, weights[1].shape
    time_part, shift_part = time_rows // batch, shift_rows // batch
    shape = functools.partial(jax.ShapeDtypeStruct, dtype=jnp.float32)

    def at(block, index):
        return pl.BlockSpec(block, index)

    def rows_of(k, lead):
        part, wide = ((time_part, time_width), (shift_part, width))[k]
        return pl.BlockSpec(lead + (part, wide), lambda b: (0,) * len(lead) + (b, 0))

    def five(lead):
        return [rows_of(0, lead), rows_of(1, lead)] + [resident(lead + w.shape) for w in weights[2:]]

    shift_at = 2 * time_rows // shift_part
    rest_at = (2 * time_rows + shift_rows) // 256
    return pl.pallas_call(
        finish_kernel,
        grid=(batch,),
        in_specs=[
            pl.BlockSpec(memory_space=pltpu.SMEM),
            resident(norm_tile.shape),
            at((1, shard_rows, width), lambda b: (b, 0, 0)),
            at((2, tall, width), lambda b: (0, b, 0)),
            at((4, short, width), lambda b: (0, b, 0)),
            resident(shard_grad.shape),
            resident(state_kernel.shape),
            resident(state_attention.shape),
            at((time_part, width), lambda b: (b, 0)),
            at((time_part, width), lambda b: (batch + b, 0)),
            at((shift_part, width), lambda b: (shift_at + b, 0)),
            pl.BlockSpec((256, width), lambda b: (rest_at, 0), pipeline_mode=pl.Buffered(1)),
        ]
        + five(())
        + five((2,))
        + five(()),
        out_specs=[
            at((2, 2, tall, width), lambda b: (0, 0, b, 0)),
            at((2, 4, short, width), lambda b: (0, 0, b, 0)),
        ]
        + five((2,))
        + five(())
        + five(())
        + [resident(state_kernel.shape[1:]), resident(state_attention.shape[1:])] * 2
        + [resident((1, 1))] * 2,
        out_shape=[
            shape((2, 2, batch * tall, width)),
            shape((2, 4, batch * short, width)),
        ]
        + [shape((2,) + w.shape) for w in weights]
        + [shape(w.shape) for w in weights] * 2
        + [shape(state_kernel.shape[1:]), shape(state_attention.shape[1:])] * 2
        + [shape((1, 1))] * 2,
        compiler_params=pltpu.CompilerParams(vmem_limit_bytes=VMEM_LIMIT),
        cost_estimate=pl.CostEstimate(flops=40 << 20, bytes_accessed=36 << 20, transcendentals=1 << 20),
        name="finish",
    )(
        scalars,
        norm_tile,
        fresh,
        average_kernel,
        average_attention,
        shard_grad,
        state_kernel,
        state_attention,
        rest,
        rest,
        rest,
        rest,
        *weights,
        *states,
        *averages,
    )


def local(
    x_clean,
    noise,
    timesteps,
    keep_mask,
    adam_step,
    inlet_weight,
    kernel_weight,
    attention_weight,
    time_weight,
    shift_weight,
    outlet_weight,
    small_params,
    state_inlet,
    state_kernel,
    state_attention,
    state_time,
    state_shift,
    state_outlet,
    state_small,
    average_inlet,
    average_kernel,
    average_attention,
    average_time,
    average_shift,
    average_outlet,
    average_small,
):
    chans = kernel_weight.shape[2]
    width_sin = time_weight.shape[0] - time_weight.shape[1]
    rows, batch = lax.axis_size("rows"), lax.axis_size("batch")
    own = timesteps.shape[0] // rows
    pair = jnp.concatenate([x_clean, noise], axis=1)
    pair = pair.reshape(rows, own, 6, -1)
    pair = jnp.pad(pair, ((0, 0), (0, 0), (0, 2), (0, 0)))
    pair = lax.all_to_all(pair, "rows", 0, 0, tiled=True)
    keep = keep_mask.reshape(rows, own, -1, chans).astype(jnp.bfloat16)
    (
        keep,
        timesteps,
        adam_step,
        inlet_low,
        kernels,
        projections,
        time_low,
        shift_low,
        outlet_low,
        small_low,
    ) = lax.optimization_barrier(
        (
            keep,
            timesteps,
            adam_step,
            inlet_weight,
            kernel_weight,
            attention_weight,
            time_weight,
            shift_weight,
            outlet_weight,
            small_params,
        )
    )
    keep = lax.all_to_all(keep, "rows", 0, 0, tiled=True)
    timesteps = lax.dynamic_slice_in_dim(timesteps, lax.axis_index("rows") * own, own, 0)
    bars = alpha_bars(timesteps)
    mix = jnp.stack([jnp.sqrt(bars), jnp.sqrt(1.0 - bars)])
    kernels = kernels.astype(jnp.bfloat16)
    projections = projections.astype(jnp.bfloat16)
    time_low = time_low.astype(jnp.bfloat16)
    shift_low = shift_low.astype(jnp.bfloat16)
    inlet = padded_taps(inlet_low).astype(jnp.bfloat16)
    outlet = padded_taps(
        jnp.transpose(outlet_low.reshape(3, 9, chans), (1, 0, 2)).reshape(27, chans)
    ).astype(jnp.bfloat16)
    qkv = jnp.concatenate([projections[0], projections[1], projections[2]], axis=1)
    embed = sinusoid(timesteps, width_sin).astype(jnp.bfloat16)
    hidden_pre = jnp.dot(
        embed, time_low[:width_sin], preferred_element_type=jnp.float32
    ) + small_low[15:17].reshape(-1)
    hidden = jax.nn.silu(hidden_pre).astype(jnp.bfloat16)
    time_emb = jnp.dot(
        hidden, time_low[width_sin:], preferred_element_type=jnp.float32
    ) + small_low[17:19].reshape(-1)
    time_act = jax.nn.silu(time_emb).astype(jnp.bfloat16)
    time_shift = jnp.dot(time_act, shift_low, preferred_element_type=jnp.float32) + small_low[14]
    ratio = bars / (1.0 - bars)
    snr_weight = jnp.minimum(ratio, GAMMA) / ratio
    denom = 3 * 256 * own * rows * batch
    coef = 2.0 * snr_weight / denom
    start, inner, stats, noisy, target = forward_part(
        FORWARD_CHUNK, mix, pair, (time_shift + small_low[9])[:, None, :], inlet, kernels[0], small_low
    )
    bias_qkv = jnp.concatenate([small_low[11], jnp.zeros_like(small_low[0]), small_low[12]])
    tall, short = state_kernel.shape[2], state_attention.shape[2]
    shard_rows = rows * padded_rows(2 * tall + 4 * short, rows)
    lanes = padded_rows(MISC_TOTAL, batch * rows)
    shards, rest = main_part(
        CHUNK,
        (batch, shard_rows, tall, short, batch * rows * lanes),
        coef,
        start,
        inner,
        stats,
        noisy,
        target,
        keep,
        (
            rows_first(kernels[0]),
            kernels[1],
            rows_first(kernels[1]),
            qkv,
            qkv.T,
            projections[3],
            projections[3].T,
            outlet,
        ),
        small_low,
        bias_qkv[None],
        (
            embed,
            hidden,
            swish_grad(hidden_pre),
            time_act,
            swish_grad(time_emb),
            time_low[width_sin:],
            shift_low,
        ),
    )
    count = adam_step[0].astype(jnp.float32)
    scalars = jnp.stack(
        [
            1.0 / (1.0 - BETA_ONE**count),
            1.0 / (1.0 - BETA_TWO**count),
            jnp.minimum(EMA_TOP, (1.0 + count) / (10.0 + count)),
        ]
    )
    fresh, rest, shard_grad, norm_tile = exchange(
        shards.reshape(batch // 2, 2, rows, shard_rows // rows, chans),
        rest.reshape(batch // 2, 2, rows, lanes, chans),
        state_kernel,
        state_attention,
        kernel_weight,
        attention_weight,
        scalars,
    )
    results = finish(
        scalars,
        norm_tile,
        fresh.reshape(batch, shard_rows, chans),
        lax.all_gather(average_kernel, "batch", axis=1, tiled=True),
        lax.all_gather(average_attention, "batch", axis=1, tiled=True),
        shard_grad.reshape(shard_rows, chans),
        state_kernel,
        state_attention,
        rest.reshape(-1, chans),
        (time_weight, shift_weight, inlet_weight, outlet_weight, small_params),
        (state_time, state_shift, state_inlet, state_outlet, state_small),
        (average_time, average_shift, average_inlet, average_outlet, average_small),
    )
    kernel_pair, attention_pair = results[:2]
    triples = [results[2 + 5 * k : 7 + 5 * k] for k in range(3)]
    first_conv, first_attention, second_conv, second_attention, loss, norm = results[17:]
    ordered = []
    for (time, shift, inlet, outlet, small), middle in zip(
        triples,
        ((kernel_pair, attention_pair), (first_conv, first_attention), (second_conv, second_attention)),
    ):
        ordered += [inlet, *middle, time, shift, outlet, small]
    return (*ordered, loss.reshape(()), norm.reshape(()))


def solution(mesh):
    return jax.shard_map(
        local,
        mesh=mesh,
        in_specs=(
            P("batch", None, "rows", None),
            P("batch", None, "rows", None),
            P("batch"),
            P("batch", "rows", None, None),
            P(),
            P(),
            P(),
            P(),
            P(),
            P(),
            P(),
            P(),
            P(),
            P(None, None, "batch", None),
            P(None, None, "batch", None),
            P(),
            P(),
            P(),
            P(),
            P(),
            P(None, "batch", None),
            P(None, "batch", None),
            P(),
            P(),
            P(),
            P(),
        ),
        out_specs=(
            P(),
            P(),
            P(),
            P(),
            P(),
            P(),
            P(),
            P(),
            P(None, "batch", None),
            P(None, "batch", None),
            P(),
            P(),
            P(),
            P(),
            P(),
            P(None, "batch", None),
            P(None, "batch", None),
            P(),
            P(),
            P(),
            P(),
            P(),
            P(),
        ),
        check_vma=False,
    )
```

```python
import functools
import math

import jax
import jax.numpy as jnp
import numpy as np
from jax import lax
from jax.experimental import pallas as pl
from jax.experimental.pallas import tpu as pltpu
from jax.sharding import PartitionSpec as P

G = 32


HIGH_PRECISION = lax.Precision.HIGHEST
CLIP = 0.05
GAMMA = 5.0
KEEP = 0.9
EPS_NORM = 1e-05
BETA_ONE = 0.9
BETA_TWO = 0.999
EPS_ADAM = 1e-08
DECAY = 0.01
EMA_TOP = 0.9999
VMEM_LIMIT = 60 << 20
CHUNK = 4
FORWARD_CHUNK = 8
GROUP = 2
COUNT = 2048.0
RATES = (0.1, 0.01, 0.03, 0.05, 0.02, 0.01, 0.2)


def bar_table():
    beta_rates = 0.0001 + (0.02 - 0.0001) * np.arange(1000, dtype=np.float64) / 999.0
    return np.exp(np.cumsum(np.log(1.0 - beta_rates))).astype(np.float32)


def alpha_bars(timesteps):
    one_hot = (timesteps[:, None] == jnp.arange(1000)[None, :]).astype(jnp.float32)
    return jnp.sum(one_hot * bar_table()[None, :], axis=1)


def sinusoid(timesteps, width):
    half = width // 2
    rates = jnp.exp(-math.log(10000.0) * jnp.arange(half).astype(jnp.float32) / (half - 1))
    angles = timesteps.astype(jnp.float32)[:, None] * rates[None, :]
    return jnp.concatenate([jnp.sin(angles), jnp.cos(angles)], axis=1)


def swish_grad(pre):
    logistic = jax.nn.sigmoid(pre)
    return logistic * (1.0 + pre * (1.0 - logistic))


def wrap(shift, size):
    return shift % size


def tap_masks():
    lane = lax.broadcasted_iota(jnp.int32, (8, 256), 1)
    row, col = lane // 16, lane % 16
    masks = []
    for i in range(3):
        for j in range(3):
            ok = (row + (i - 1) >= 0) & (row + (i - 1) < 16) & (col + (j - 1) >= 0) & (col + (j - 1) < 16)
            masks.append(ok)
    return masks


def tap_stack(tile, masks, sign):
    parts = []
    for tap in range(9):
        step = sign * (16 * (tap // 3 - 1) + tap % 3 - 1)
        moved = tile if step == 0 else pltpu.roll(tile, wrap(-step, 256), 1)
        parts.append(jnp.where(masks[tap if sign > 0 else 8 - tap], moved, 0.0))
    parts.append(jnp.zeros_like(tile))
    return jnp.concatenate(parts, axis=0).astype(jnp.bfloat16)


def group_sum(rows):
    halves = []
    for half in range(2):
        part = rows[:, 128 * half : 128 * half + 128]
        lane = lax.broadcasted_iota(jnp.int32, part.shape, 1)
        for step in (1, 2, 4):
            upper = (lane // step) % 2 == 1
            part = part + jnp.where(upper, pltpu.roll(part, step, 1), pltpu.roll(part, 128 - step, 1))
        halves.append(part)
    return jnp.concatenate(halves, axis=1)


def col_sum(x):
    return jnp.sum(x, axis=0, keepdims=True)


def stats_of(fields):
    sums = jnp.concatenate([col_sum(x) for x in fields] + [col_sum(x * x) for x in fields], axis=0)
    both = group_sum(sums) / COUNT
    n = len(fields)
    mean = both[:n]
    spread = both[n:] - mean * mean
    return mean, lax.rsqrt(spread + EPS_NORM)


def logistic(z):
    return 0.5 * jnp.tanh(0.5 * z) + 0.5


def put_shifted(buf, c, y, not_first, not_last):
    buf[c, 16:272, 256:512] = y.astype(jnp.bfloat16)
    buf[c, 16:272, 0:256] = jnp.where(not_first, pltpu.roll(y, 1, 0), 0.0).astype(jnp.bfloat16)
    buf[c, 16:272, 512:768] = jnp.where(not_last, pltpu.roll(y, 255, 0), 0.0).astype(jnp.bfloat16)


def edge_masks():
    col = lax.broadcasted_iota(jnp.int32, (256, 256), 0) % 16
    return col != 0, col != 15


def stacked(buf, i):
    chunk = buf.shape[0]
    return buf[:, 16 * i : 16 * i + 256, :].reshape(chunk * 256, 768)


def dot(a, b, dims=((1,), (0,))):
    return lax.dot_general(a, b, (dims, ((), ())), preferred_element_type=jnp.float32)


NT = ((1,), (1,))
TN = ((0,), (0,))


def conv_shifted(buf, weight):
    field = jnp.concatenate([stacked(buf, i) for i in range(3)], axis=1)
    return dot(field, weight[...])


def zero_edges(buf):
    edge = jnp.zeros((buf.shape[0], 16, 768), jnp.bfloat16)
    buf[:, 0:16, :] = edge
    buf[:, 272:288, :] = edge


def take_turns(workers):
    live, started = [], 0
    while live or started < len(workers):
        if started < len(workers):
            live.append(workers[started])
            started += 1
        live = [w for w in live if next(w, live) is not live]


def lanes_joined(blocks):
    return blocks[0] if len(blocks) == 1 else jnp.concatenate(blocks, axis=1)


def first_kernel(
    mix,
    pair,
    embed,
    time_weight,
    shift_weight,
    inlet,
    kernel_one,
    small,
    start_out,
    inner_out,
    stats_out,
    noisy_out,
    target_out,
    hidden_out,
    hidden_slope_out,
    time_act_out,
    time_slope_out,
    buf,
    tshift,
):
    chunk = start_out.shape[0]
    step = pl.program_id(0)

    @pl.when(step == 0)
    def _():
        zero_edges(buf)
        width = embed.shape[1]

        def layer(x, weight, at):
            bias = jnp.concatenate([small[at : at + 1], small[at + 1 : at + 2]], axis=1)
            z = dot(x, weight.astype(jnp.bfloat16)) + bias
            s = logistic(z)
            return (z * s).astype(jnp.bfloat16), s * (1.0 + z * (1.0 - s))

        hidden, hidden_slope = layer(embed[...], time_weight[0:width, :], 15)
        time_act, time_slope = layer(hidden, time_weight[width:, :], 17)
        hidden_out[...] = hidden
        hidden_slope_out[...] = hidden_slope
        time_act_out[...] = time_act
        time_slope_out[...] = time_slope
        both = small[14:15] + small[9:10]
        tshift[...] = dot(time_act, shift_weight[...].astype(jnp.bfloat16)) + both

    masks = tap_masks()
    not_first, not_last = edge_masks()
    part = pair.shape[3] // 2
    blank = jnp.zeros((4, 256), jnp.float32)

    def work(images):
        n = len(images)
        every = range(n)
        low, high = images[0], images[-1] + 1
        starts = []
        for c in images:
            tiles = [pair[s, c] for s in range(pair.shape[0])]
            clean = jnp.concatenate([lanes_joined([t[:, :part] for t in tiles]), blank], axis=0)
            noise = jnp.concatenate([lanes_joined([t[:, part:] for t in tiles]), blank], axis=0)
            noisy = mix[0, step * chunk + c] * clean + mix[1, step * chunk + c] * noise
            noisy = noisy.astype(jnp.bfloat16).astype(jnp.float32)
            noisy_out[c] = noisy
            target_out[c] = noise
            start = dot(tap_stack(noisy, masks, 1), inlet[...], TN) + small[8:9]
            start_out[c] = start
            starts.append(start)
        yield
        mean, rstd = stats_of(starts)
        for i, c in enumerate(images):
            scale = rstd[i : i + 1] * small[0:1]
            z = starts[i] * scale + (small[4:5] - mean[i : i + 1] * scale)
            put_shifted(buf, c, z * logistic(z), not_first, not_last)
        yield
        inner_all = conv_shifted(buf.at[low:high], kernel_one)
        yield
        inners = []
        for i, c in enumerate(images):
            inner = inner_all[256 * i : 256 * i + 256] + tshift[pl.ds(step * chunk + c, 1), :]
            inner_out[c] = inner
            inners.append(inner)
        mean_two, rstd_two = stats_of(inners)
        for i, c in enumerate(images):
            stats_out[c] = jnp.concatenate(
                [mean[i : i + 1], rstd[i : i + 1], mean_two[i : i + 1], rstd_two[i : i + 1]]
                + [jnp.zeros((4, 256), jnp.float32)],
                axis=0,
            )

    take_turns([work(list(range(g, g + GROUP))) for g in range(0, chunk, GROUP)])


def norm_grad(dys, fields, means, rstds, gain):
    n = len(dys)
    shift_sums, gain_sums = [], []
    for dy, x, mean, rstd in zip(dys, fields, means, rstds):
        shift_sums.append(col_sum(dy))
        gain_sums.append(col_sum(dy * (x * rstd - mean * rstd)))
    both = group_sum(jnp.concatenate(shift_sums + gain_sums, axis=0) * gain) / COUNT
    grads = []
    for c in range(n):
        rstd, mean = rstds[c], means[c]
        slope = -rstd * rstd * both[n + c : n + c + 1]
        base = -rstd * both[c : c + 1] - mean * slope
        grads.append(dys[c] * (rstd * gain) + (fields[c] * slope + base))
    return grads, sum(gain_sums), sum(shift_sums)


def second_kernel(
    tall,
    short,
    coef,
    start_in,
    inner_in,
    stats_in,
    noisy,
    target,
    keep,
    kernel_one_flip,
    kernel_two,
    kernel_two_flip,
    qkv,
    qkv_t,
    proj,
    proj_t,
    outlet,
    small,
    bias_qkv,
    embed,
    hidden,
    hidden_slope,
    time_act,
    time_slope,
    time_weight,
    shift_weight,
    shard_out,
    rest_out,
    grad_one_out,
    grad_two_out,
    grad_qkv_out,
    grad_proj_out,
    grad_outlet_out,
    grad_inlet_out,
    grad_small_out,
    loss_out,
    tshift_grad,
    buf,
    grad_buf,
):
    chunk = noisy.shape[0]
    step = pl.program_id(0)
    sums = (
        grad_one_out,
        grad_two_out,
        grad_qkv_out,
        grad_proj_out,
        grad_outlet_out,
        grad_inlet_out,
        grad_small_out,
        loss_out,
    )

    @pl.when(step == 0)
    def _():
        zero_edges(buf)
        zero_edges(grad_buf)
        for ref in sums:
            ref[...] = jnp.zeros(ref.shape, jnp.float32)

    masks = tap_masks()
    not_first, not_last = edge_masks()
    scale = 256 ** (-0.5)

    def gain(k):
        return small[k : k + 1]

    def shift(k):
        return small[4 + k : 5 + k]

    def normed(x, mean, rstd, k):
        slope = rstd * gain(k)
        return x * slope + (shift(k) - mean * slope)

    def row(values, c):
        return values[c : c + 1]

    def work(images):
        n = len(images)
        every = range(n)
        low, high = images[0], images[-1] + 1

        def part(x, c):
            return x[256 * c : 256 * c + 256]

        slope_two, act_two = [], []
        for c in images:
            z = normed(inner_in[c], stats_in[c, 2:3], stats_in[c, 3:4], 1)
            s = logistic(z)
            kept = jnp.concatenate([keep[s, c] for s in range(keep.shape[0])], axis=0)
            kept = kept.astype(jnp.float32) * (1.0 / KEEP)
            act = z * s * kept
            slope_two.append(s * (1.0 + z * (1.0 - s)) * kept)
            act_two.append(act.astype(jnp.bfloat16))
            put_shifted(buf, c, act, not_first, not_last)
        yield
        conv_two = conv_shifted(buf.at[low:high], kernel_two)
        yield
        middle = [start_in[c] + part(conv_two, i) + small[10:11] for i, c in enumerate(images)]
        mean, rstd = stats_of(middle)
        mean_three, rstd_three = [row(mean, i) for i in every], [row(rstd, i) for i in every]
        tokens = [
            normed(middle[i], mean_three[i], rstd_three[i], 2).astype(jnp.bfloat16) for i in every
        ]
        tokens = jnp.concatenate(tokens, axis=0)
        yield
        qkv_all = (dot(tokens, qkv[...]) + bias_qkv[0:1]).astype(jnp.bfloat16)
        triples = []
        for i in every:
            three = part(qkv_all, i)
            triples.append((three[:, 0:256], three[:, 256:512], three[:, 512:768]))
        scores = [dot(q, k, NT) for q, k, _ in triples]
        yield
        probs, probs_low = [], []
        for i in every:
            expo = jnp.exp((scores[i] - jnp.max(scores[i], axis=1, keepdims=True)) * scale)
            p = expo * (1.0 / jnp.sum(expo, axis=1, keepdims=True))
            probs.append(p)
            probs_low.append(p.astype(jnp.bfloat16))
        yield
        mixed = [dot(probs_low[i], triples[i][2]).astype(jnp.bfloat16) for i in every]
        mixed = jnp.concatenate(mixed, axis=0)
        branch = dot(mixed, proj[...])
        yield
        final = [middle[i] + part(branch, i) + small[13:14] for i in every]
        mean, rstd = stats_of(final)
        mean_four, rstd_four = [row(mean, i) for i in every], [row(rstd, i) for i in every]
        act_four, slope_four = [], []
        for i in every:
            z = normed(final[i], mean_four[i], rstd_four[i], 3)
            s = logistic(z)
            act_four.append((z * s).astype(jnp.bfloat16))
            slope_four.append(s * (1.0 + z * (1.0 - s)))
        yield
        taps_all = [dot(outlet[...], act, NT) for act in act_four]
        yield
        spreads = []
        loss_sum = 0.0
        for i, c in enumerate(images):
            predicted = 0.0
            for tap in range(9):
                move = 16 * (tap // 3 - 1) + tap % 3 - 1
                moved = taps_all[i][8 * tap : 8 * tap + 8]
                moved = moved if move == 0 else pltpu.roll(moved, wrap(-move, 256), 1)
                predicted = predicted + jnp.where(masks[tap], moved, 0.0)
            error = predicted - target[c]
            weight = coef[step * chunk + c]
            loss_sum = loss_sum + (0.5 * weight) * (error * error)
            grad_pred = (weight * error).astype(jnp.bfloat16).astype(jnp.float32)
            spreads.append(tap_stack(grad_pred, masks, -1))
        loss_out[...] += loss_sum
        yield
        grad_outlet_out[...] += sum(dot(s, act) for s, act in zip(spreads, act_four))
        grad_act = [dot(s, outlet[...], TN) for s in spreads]
        yield
        grad_four = [grad_act[i] * slope_four[i] for i in every]
        grad_final, gain_four, shift_four = norm_grad(grad_four, final, mean_four, rstd_four, gain(3))
        branch_all = jnp.concatenate([g.astype(jnp.bfloat16) for g in grad_final], axis=0)
        yield
        grad_proj_out[...] += dot(mixed, branch_all, TN)
        grad_mixed = dot(branch_all, proj_t[...]).astype(jnp.bfloat16)
        dps = [dot(part(grad_mixed, i), triples[i][2], NT) for i in every]
        dvs = [dot(probs_low[i], part(grad_mixed, i), TN) for i in every]
        yield
        dss = []
        for i in every:
            p, dp = probs[i], dps[i]
            dss.append((p * (dp - jnp.sum(p * dp, axis=1, keepdims=True))).astype(jnp.bfloat16))
        yield
        grad_qkv = []
        for i in every:
            q, k, _ = triples[i]
            dq = dot(dss[i], k) * scale
            dk = dot(dss[i], q, TN) * scale
            grad_qkv.append(jnp.concatenate([dq, dk, dvs[i]], axis=1).astype(jnp.bfloat16))
        grad_qkv_all = jnp.concatenate(grad_qkv, axis=0)
        grad_qkv_out[...] += dot(tokens, grad_qkv_all, TN)
        grad_tokens = dot(grad_qkv_all, qkv_t[...])
        yield
        bias_sums = col_sum(grad_qkv_all.astype(jnp.float32))
        grad_norm, gain_three, shift_three = norm_grad(
            [part(grad_tokens, i) for i in every], middle, mean_three, rstd_three, gain(2)
        )
        grad_middle = [grad_final[i] + grad_norm[i] for i in every]
        for i, c in enumerate(images):
            put_shifted(grad_buf, c, grad_middle[i], not_first, not_last)
        yield
        field = jnp.concatenate(act_two, axis=0)
        for i in range(3):
            grad_two_out[i] += dot(field, stacked(grad_buf.at[low:high], i), TN)
        grad_act = conv_shifted(grad_buf.at[low:high], kernel_two_flip)
        yield
        grad_two = [part(grad_act, i) * slope_two[i] for i in every]
        grad_inner, gain_two, shift_two = norm_grad(
            grad_two,
            [inner_in[c] for c in images],
            [stats_in[c, 2:3] for c in images],
            [stats_in[c, 3:4] for c in images],
            gain(1),
        )
        for i, c in enumerate(images):
            put_shifted(grad_buf, c, grad_inner[i], not_first, not_last)
        act_one, slope_one = [], []
        for c in images:
            z = normed(start_in[c], stats_in[c, 0:1], stats_in[c, 1:2], 0)
            s = logistic(z)
            act_one.append((z * s).astype(jnp.bfloat16))
            slope_one.append(s * (1.0 + z * (1.0 - s)))
        yield
        field = jnp.concatenate(act_one, axis=0)
        for i in range(3):
            grad_one_out[i] += dot(field, stacked(grad_buf.at[low:high], i), TN)
        grad_act = conv_shifted(grad_buf.at[low:high], kernel_one_flip)
        yield
        grad_one = [part(grad_act, i) * slope_one[i] for i in every]
        grad_norm, gain_one, shift_one = norm_grad(
            grad_one,
            [start_in[c] for c in images],
            [stats_in[c, 0:1] for c in images],
            [stats_in[c, 1:2] for c in images],
            gain(0),
        )
        grad_start = [grad_middle[i] + grad_norm[i] for i in every]
        patches = [tap_stack(noisy[c], masks, 1) for c in images]
        inner_sums = [col_sum(g) for g in grad_inner]
        for i, c in enumerate(images):
            tshift_grad[pl.ds(step * chunk + c, 1), :] = inner_sums[i]
        grad_small_out[...] += jnp.concatenate(
            [
                gain_one,
                gain_two,
                gain_three,
                gain_four,
                shift_one,
                shift_two,
                shift_three,
                shift_four,
                sum(col_sum(g) for g in grad_start),
                sum(inner_sums),
                sum(col_sum(g) for g in grad_middle),
                bias_sums[:, 0:256],
                bias_sums[:, 512:768],
                sum(col_sum(g) for g in grad_final),
                jnp.zeros((2, 256), jnp.float32),
            ],
            axis=0,
        )
        yield
        grad_inlet_out[...] += sum(
            dot(patch, g.astype(jnp.bfloat16)) for patch, g in zip(patches, grad_start)
        )

    take_turns([work(list(range(g, g + GROUP))) for g in range(0, chunk, GROUP)])

    @pl.when(step == pl.num_programs(0) - 1)
    def _():
        for k, grad in enumerate((grad_one_out, grad_two_out)):
            for tap in range(9):
                at = 256 * (2 - tap % 3)
                for shard, off, row, size in cuts(tap * 256, 256, tall):
                    shard_out[shard, k * tall + off : k * tall + off + size, :] = grad[
                        2 - tap // 3, row : row + size, at : at + 256
                    ]
        for k in range(4):
            grad, at = (grad_qkv_out, 256 * k) if k < 3 else (grad_proj_out, 0)
            for shard, off, row, size in cuts(0, 256, short):
                low = 2 * tall + k * short + off
                shard_out[shard, low : low + size, :] = grad[row : row + size, at : at + 256]
        used = 2 * tall + 4 * short
        if used < shard_out.shape[1]:
            shard_out[:, used:, :] = jnp.zeros(
                (shard_out.shape[0], shard_out.shape[1] - used, 256), jnp.float32
            )
        total = tshift_grad[...]
        shift_grad = full_dot(time_act[...], total, TN)
        grad_act = full_dot(total, shift_weight[...].astype(jnp.bfloat16), NT) * time_slope[...]
        two_grad = full_dot(hidden[...], grad_act, TN)
        time_two = time_weight[embed.shape[1] :, :].astype(jnp.bfloat16)
        grad_hidden = full_dot(grad_act, time_two, NT) * hidden_slope[...]
        one_grad = full_dot(embed[...], grad_hidden, TN)
        width = one_grad.shape[0]
        height = width + two_grad.shape[0]
        for half in range(2):
            span = slice(256 * half, 256 * half + 256)
            rest_out[half * height : half * height + width, :] = one_grad[:, span]
            rest_out[half * height + width : half * height + height, :] = two_grad[:, span]
        act_sum, hidden_sum = col_sum(grad_act), col_sum(grad_hidden)
        parts = [
            shift_grad,
            grad_inlet_out[...],
            grad_outlet_out[...],
            jnp.concatenate(
                [
                    grad_small_out[0:14],
                    col_sum(total),
                    hidden_sum[:, 0:256],
                    hidden_sum[:, 256:512],
                    act_sum[:, 0:256],
                    act_sum[:, 256:512],
                    jnp.zeros((5, 256), jnp.float32),
                ],
                axis=0,
            ),
            loss_out[...],
        ]
        at = 2 * height
        for part in parts:
            rest_out[at : at + part.shape[0], :] = part
            at += part.shape[0]
        if at < rest_out.shape[0]:
            rest_out[at:, :] = jnp.zeros((rest_out.shape[0] - at, 256), jnp.float32)


def cuts(first, size, height):
    parts, row = [], 0
    while row < size:
        shard, off = divmod(first + row, height)
        take = min(height - off, size - row)
        parts.append((shard, off, row, take))
        row += take
    return parts


def full_dot(a, b, dims):
    return lax.dot_general(
        a.astype(jnp.float32),
        b.astype(jnp.float32),
        (dims, ((), ())),
        precision=HIGH_PRECISION,
        preferred_element_type=jnp.float32,
    )


def resident(shape):
    return pl.BlockSpec(shape, lambda i: (0,) * len(shape), pipeline_mode=pl.Buffered(1))


def per_chunk(chunk, *tail):
    return pl.BlockSpec((chunk,) + tail, lambda i: (i,) + (0,) * len(tail))


def by_source(chunk, block):
    return pl.BlockSpec((block[0], chunk) + block[2:], lambda i: (0, i, 0, 0))


def forward_part(chunk, mix, pair, embed, time_weight, shift_weight, inlet, kernel_one, small):
    n, deep = pair.shape[1], time_weight.shape[1]
    chunk = min(chunk, n)
    shapes = [(n, 256, 256), (n, 256, 256), (n, 8, 256), (n, 8, 256), (n, 8, 256)]
    whole = [jnp.bfloat16, jnp.float32, jnp.bfloat16, jnp.float32]
    return pl.pallas_call(
        first_kernel,
        grid=(n // chunk,),
        in_specs=[
            pl.BlockSpec(memory_space=pltpu.SMEM),
            by_source(chunk, pair.shape),
            resident(embed.shape),
            resident(time_weight.shape),
            resident(shift_weight.shape),
            resident(inlet.shape),
            resident(kernel_one.shape),
            resident(small.shape),
        ],
        out_specs=[per_chunk(chunk, *s[1:]) for s in shapes] + [resident((n, deep))] * 4,
        out_shape=[jax.ShapeDtypeStruct(s, jnp.float32) for s in shapes]
        + [jax.ShapeDtypeStruct((n, deep), kind) for kind in whole],
        scratch_shapes=[
            pltpu.VMEM((chunk, 288, 768), jnp.bfloat16),
            pltpu.VMEM((n, 256), jnp.float32),
        ],
        compiler_params=pltpu.CompilerParams(vmem_limit_bytes=VMEM_LIMIT),
        cost_estimate=pl.CostEstimate(
            flops=2 * n * 256 * 256 * 2400, bytes_accessed=n * 1 << 19, transcendentals=n * 1 << 16
        ),
        name="forward_part",
    )(mix, pair, embed, time_weight, shift_weight, inlet, kernel_one, small)


def main_part(chunk, sizes, coef, start, inner, stats, noisy, target, keep, weights, small, bias_qkv, times):
    n = noisy.shape[0]
    batch, shard_rows, tall, short, rest_rows = sizes
    outs = [(batch, shard_rows, 256), (rest_rows, 256)]
    sums = [(3, 256, 768), (3, 256, 768), (256, 768), (256, 256), (80, 256), (80, 256), (16, 256), (8, 256)]
    return pl.pallas_call(
        functools.partial(second_kernel, tall, short),
        grid=(n // chunk,),
        in_specs=[
            pl.BlockSpec(memory_space=pltpu.SMEM),
            per_chunk(chunk, 256, 256),
            per_chunk(chunk, 256, 256),
            per_chunk(chunk, 8, 256),
            per_chunk(chunk, 8, 256),
            per_chunk(chunk, 8, 256),
            by_source(chunk, keep.shape),
        ]
        + [resident(w.shape) for w in weights]
        + [resident(small.shape), resident(bias_qkv.shape)]
        + [resident(t.shape) for t in times],
        out_specs=[resident(g) for g in outs],
        out_shape=[jax.ShapeDtypeStruct(g, jnp.float32) for g in outs],
        scratch_shapes=[pltpu.VMEM(g, jnp.float32) for g in sums + [(n, 256)]]
        + [pltpu.VMEM((chunk, 288, 768), jnp.bfloat16)] * 2,
        compiler_params=pltpu.CompilerParams(vmem_limit_bytes=VMEM_LIMIT),
        cost_estimate=pl.CostEstimate(
            flops=70 * n * 2 * 256**3, bytes_accessed=n * 5 << 17, transcendentals=n * 5 << 16
        ),
        name="main_part",
    )(coef, start, inner, stats, noisy, target, keep, *weights, small, bias_qkv, *times)


def rows_first(weight):
    inputs, outputs = weight.shape[0] // 9, weight.shape[1]
    flipped = jnp.transpose(weight.reshape(9, inputs, outputs)[::-1], (0, 2, 1))
    return flipped.reshape(9 * outputs, inputs)


def padded_taps(rows):
    padded = jnp.pad(rows.reshape(9, 3, 256), ((0, 1), (0, 5), (0, 0)))
    return padded.reshape(80, 256)


MESH = pl.DeviceIdType.MESH
MISC_ROWS = (640, 640, 512, 80, 80, 24, 8)
MISC_TOTAL = 2048
SPLIT_A = 11
SPLIT_B = 4
LAG = 3


def padded_rows(total, parts):
    return -(-total // (8 * parts)) * 8


def factors(rows):
    low = max(d for d in range(1, rows + 1) if rows % d == 0 and d * d <= rows)
    return low, rows // low


def exchange_kernel(
    shard_shape,
    rates,
    grads_a,
    grads_b,
    state_kernel,
    state_attention,
    weight_kernel,
    weight_attention,
    scalars,
    out_a,
    out_b,
    shard_grad,
    norm_out,
    own_a,
    own_b,
    half_a,
    half_b,
    near_a,
    near_b,
    far_a,
    far_b,
    deep_a,
    deep_b,
    piece_a,
    piece_b,
    shard_weight,
    shard_first,
    shard_second,
    square_core,
    square_rows,
    square_deep,
    local_sem,
    own_sem,
    core_send,
    core_recv,
    near_send,
    near_recv,
    far_send,
    far_recv,
    deep_send,
    deep_recv,
    shard_send,
    shard_recv,
    square_send,
    square_recv,
    deep_send_two,
    deep_recv_two,
    near_send_two,
    near_recv_two,
    far_send_two,
    far_recv_two,
    core_send_two,
    core_recv_two,
    keep_sem,
):
    depth, _, tops, wide, piece, _ = grads_a.shape
    lanes = grads_b.shape[4]
    rows = tops * wide
    pairs, tall, quads, short = shard_shape
    batch, r = lax.axis_index("batch"), lax.axis_index("rows")
    z, c = batch // 2, batch % 2
    y, x = r // wide, r % wide
    partner = z * 2 + (1 - c)
    row_peers = [(r + d) % rows for d in range(1, rows)]
    deep_peers = [(z + d) % depth for d in range(1, depth)]
    x_peers = [(x + d) % wide for d in range(1, wide)]
    y_peers = [(y + d) % tops for d in range(1, tops)]

    def remote(src, dst, send, recv, where):
        return pltpu.make_async_remote_copy(
            src_ref=src, dst_ref=dst, send_sem=send, recv_sem=recv, device_id=where, device_id_type=MESH
        )

    def begin(copies):
        for copy in copies:
            copy.start()
        return copies

    def arrived(copies):
        for copy in copies:
            copy.wait_recv()

    def blocks(kernel_ref, attention_ref, flat, base, offset):
        copies = []
        for k in range(pairs + quads):
            ref, own, size = (kernel_ref, k, tall) if k < pairs else (attention_ref, k - pairs, short)
            at = k * tall if k < pairs else pairs * tall + own * short
            far = ref.at[own] if offset is None else ref.at[own, pl.ds(offset * size, size)]
            near = flat.at[pl.ds(at, size)]
            copies.append(pltpu.make_async_copy(far, near, local_sem.at[base * (pairs + quads) + k]))
        return begin(copies)

    owns = begin(
        [
            pltpu.make_async_copy(grads_b.at[:, c], own_b, own_sem.at[0]),
            pltpu.make_async_copy(grads_a.at[:, c], own_a, own_sem.at[1]),
        ]
    )

    barrier = pltpu.get_barrier_semaphore()
    pl.semaphore_signal(barrier, inc=1, device_id=(partner, r), device_id_type=MESH)
    for peer in row_peers:
        pl.semaphore_signal(barrier, inc=1, device_id=(batch, peer), device_id_type=MESH)
    for peer in deep_peers:
        pl.semaphore_signal(barrier, inc=1, device_id=(peer * 2 + c, r), device_id_type=MESH)
    pl.semaphore_wait(barrier, rows + depth - 1)

    set_a = (grads_a, own_a, half_a, near_a, far_a, deep_a, piece_a, out_a)
    set_b = (grads_b, own_b, half_b, near_b, far_b, deep_b, piece_b, out_b)
    chunks = []
    for group, height, parts in ((set_b, lanes, SPLIT_B), (set_a, piece, SPLIT_A)):
        marks = [height // 8 * k // parts * 8 for k in range(parts + 1)]
        for low, high in zip(marks[:-1], marks[1:]):
            if high > low:
                chunks.append(group + (low, high - low, len(chunks) % 2 == 0))
    count = len(chunks)
    small = sum(1 for chunk in chunks if chunk[0] is grads_b)

    core_copies = []
    for k, (grads, _, half, _, _, _, _, _, at, size, _) in enumerate(chunks):
        span = pl.ds(at, size)
        core_copies.append(
            begin(
                [
                    remote(
                        grads.at[:, 1 - c, :, :, span],
                        half.at[:, :, :, span],
                        core_send.at[k],
                        core_recv.at[k],
                        (partner, r),
                    )
                ]
            )
        )
    fetches = (
        blocks(weight_kernel, weight_attention, shard_weight, 0, batch)
        + blocks(state_kernel.at[0], state_attention.at[0], shard_first, 1, None)
        + blocks(state_kernel.at[1], state_attention.at[1], shard_second, 2, None)
    )
    near_copies, far_copies, deep_copies = [], [], []

    def sum_near(k):
        _, own, half, near, _, _, _, _, at, size, x_first = chunks[k]
        if k == 0:
            owns[0].wait()
        if k == small:
            owns[1].wait()
        arrived(core_copies[k])
        span = pl.ds(at, size)

        def add_own(t, carry):
            i, j, l = t // rows, t // wide % tops, t % wide
            half[i, j, l, span] = half[i, j, l, span] + own[i, j, l, span]
            return carry

        lax.fori_loop(0, depth * rows, add_own, 0)
        copies = []
        for d, peer in enumerate(x_peers if x_first else y_peers):
            src = half.at[:, :, peer, span] if x_first else half.at[:, peer, :, span]
            dst = near.at[d, :, pl.ds(0, tops if x_first else wide), span]
            where = (batch, y * wide + peer) if x_first else (batch, peer * wide + x)
            copies.append(remote(src, dst, near_send.at[k, d], near_recv.at[k, d], where))
        near_copies.append(begin(copies))

    def sum_far(k):
        _, _, half, near, far, _, _, _, at, size, x_first = chunks[k]
        arrived(near_copies[k])
        span = pl.ds(at, size)
        across = tops if x_first else wide

        def add_near(t, carry):
            i, j = t // across, t % across
            place = (i, j, x) if x_first else (i, y, j)
            total = half[place + (span,)]
            for d in range((wide if x_first else tops) - 1):
                total = total + near[d, i, j, span]
            half[place + (span,)] = total
            return carry

        lax.fori_loop(0, depth * across, add_near, 0)
        copies = []
        for d, peer in enumerate(y_peers if x_first else x_peers):
            src = half.at[:, peer, x, span] if x_first else half.at[:, y, peer, span]
            where = (batch, peer * wide + x) if x_first else (batch, y * wide + peer)
            copies.append(
                remote(src, far.at[d, :, span], far_send.at[k, d], far_recv.at[k, d], where)
            )
        far_copies.append(begin(copies))

    def sum_deep(k):
        _, _, half, _, far, deep, _, _, at, size, x_first = chunks[k]
        arrived(far_copies[k])
        span = pl.ds(at, size)

        def add_far(i, carry):
            total = half[i, y, x, span]
            for d in range((tops if x_first else wide) - 1):
                total = total + far[d, i, span]
            half[i, y, x, span] = total
            return carry

        lax.fori_loop(0, depth, add_far, 0)
        copies = []
        for d, peer in enumerate(deep_peers):
            copies.append(
                remote(
                    half.at[peer, y, x, span],
                    deep.at[d, span],
                    deep_send.at[k, d],
                    deep_recv.at[k, d],
                    (peer * 2 + c, r),
                )
            )
        deep_copies.append(begin(copies))

    def finish_sum(k):
        _, _, half, _, _, deep, _, _, at, size, _ = chunks[k]
        arrived(deep_copies[k])
        span = pl.ds(at, size)
        total = half[z, y, x, span]
        for d in range(depth - 1):
            total = total + deep[d, span]
        return total

    def squares(values):
        return jnp.sum((values * values).reshape(-1, 8, 256), axis=0)

    def gather_deep(k):
        _, _, _, _, _, _, part, out, at, size, _ = chunks[k]
        span = pl.ds(at, size)
        keep = pltpu.make_async_copy(part.at[span], out.at[z, c, y, x, span], keep_sem.at[k])
        keep.start()
        copies = []
        for d, peer in enumerate(deep_peers):
            copies.append(
                remote(
                    part.at[span],
                    out.at[z, c, y, x, span],
                    deep_send_two.at[k, d],
                    deep_recv_two.at[k, d],
                    (peer * 2 + c, r),
                )
            )
        return keep, begin(copies)

    def gather_near(k):
        _, _, _, _, _, _, _, out, at, size, x_first = chunks[k]
        place = out.at[:, c, y, x, pl.ds(at, size)]
        copies = []
        for d, peer in enumerate(y_peers if x_first else x_peers):
            where = (batch, peer * wide + x) if x_first else (batch, y * wide + peer)
            copies.append(remote(place, place, near_send_two.at[k, d], near_recv_two.at[k, d], where))
        return begin(copies)

    def gather_far(k):
        _, _, _, _, _, _, _, out, at, size, x_first = chunks[k]
        span = pl.ds(at, size)
        place = out.at[:, c, :, x, span] if x_first else out.at[:, c, y, :, span]
        copies = []
        for d, peer in enumerate(x_peers if x_first else y_peers):
            where = (batch, y * wide + peer) if x_first else (batch, peer * wide + x)
            copies.append(remote(place, place, far_send_two.at[k, d], far_recv_two.at[k, d], where))
        return begin(copies)

    def gather_core(k):
        _, _, _, _, _, _, _, out, at, size, _ = chunks[k]
        place = out.at[:, c, :, :, pl.ds(at, size)]
        return begin([remote(place, place, core_send_two.at[k], core_recv_two.at[k], (partner, r))])

    keeps, firsts, seconds, thirds, lasts = [], [], [], [], []
    partial = []

    def send_deep(k):
        keep, copies = gather_deep(k)
        keeps.append(keep)
        firsts.append(copies)

    def send_near(k):
        keeps[k].wait()
        arrived(firsts[k])
        seconds.append(gather_near(k))

    def send_far(k):
        arrived(seconds[k])
        thirds.append(gather_far(k))

    def send_core(k):
        arrived(thirds[k])
        lasts.append(gather_core(k))

    def sum_last(k):
        total = finish_sum(k)
        at, size = chunks[k][8], chunks[k][9]
        counted = total
        if k < small:
            piece_b[pl.ds(at, size)] = total
            line = (batch * rows + r) * lanes + at + lax.broadcasted_iota(jnp.int32, total.shape, 0)
            counted = jnp.where(line < sum(MISC_ROWS[:-1]), total, 0.0)
            send_deep(k)
        else:
            shard_grad[r, pl.ds(at, size)] = total
        partial.append(squares(counted))

    for t in range(count + 3 * LAG):
        for stage, lag in ((sum_near, 0), (sum_far, LAG), (sum_deep, 2 * LAG), (sum_last, 3 * LAG)):
            if 0 <= t - lag < count:
                stage(t - lag)
    square = sum(partial)
    square_core[0] = square
    square_copies = begin(
        [remote(square_core.at[0], square_core.at[1], square_send.at[0], square_recv.at[0], (partner, r))]
    )
    shard_copies = begin(
        [
            remote(shard_grad.at[r], shard_grad.at[r], shard_send.at[d], shard_recv.at[d], (batch, peer))
            for d, peer in enumerate(row_peers)
        ]
    )
    arrived(square_copies)
    square_rows[r] = square_core[0] + square_core[1]
    copies = begin(
        [
            remote(
                square_rows.at[r],
                square_rows.at[r],
                square_send.at[1 + d],
                square_recv.at[1 + d],
                (batch, peer),
            )
            for d, peer in enumerate(row_peers)
        ]
    )
    for k in range(small):
        send_near(k)
    arrived(copies)
    square_copies += copies
    square_deep[z] = sum(square_rows[j] for j in range(rows))
    copies = begin(
        [
            remote(
                square_deep.at[z],
                square_deep.at[z],
                square_send.at[rows + d],
                square_recv.at[rows + d],
                (peer * 2 + c, r),
            )
            for d, peer in enumerate(deep_peers)
        ]
    )
    for fetch in fetches:
        fetch.wait()
    for k in range(small):
        send_far(k)
    arrived(copies)
    square_copies += copies
    square = sum(square_deep[j] for j in range(depth))
    norm = jnp.sqrt(jnp.sum(jnp.sum(square, axis=0, keepdims=True), axis=1, keepdims=True))
    clip = CLIP / jnp.maximum(norm, CLIP)
    norm_out[...] = jnp.broadcast_to(norm, norm_out.shape)
    for k in range(small, count):
        at, size = chunks[k][8], chunks[k][9]
        span = pl.ds(pl.multiple_of(r * piece + at, 8), size)
        g = shard_grad[r, pl.ds(at, size)] * clip
        first = BETA_ONE * shard_first[span] + (1.0 - BETA_ONE) * g
        second = BETA_TWO * shard_second[span] + (1.0 - BETA_TWO) * g * g
        line = r * piece + at + lax.broadcasted_iota(jnp.int32, g.shape, 0)
        rate = jnp.where(line < pairs * tall, rates[0], rates[1])
        weight = shard_weight[span]
        step = first * scalars[0] / (jnp.sqrt(second * scalars[1]) + EPS_ADAM)
        piece_a[pl.ds(at, size)] = weight - rate * (step + DECAY * weight)
        send_deep(k)
    for k in range(small):
        send_core(k)
    for t in range(small, count + 2 * LAG):
        for stage, lag in ((send_near, 0), (send_far, LAG), (send_core, 2 * LAG)):
            if small <= t - lag < count:
                stage(t - lag)
    arrived(shard_copies)
    for copies in lasts:
        arrived(copies)
    for copies in (
        core_copies + near_copies + far_copies + deep_copies + firsts + seconds + thirds + lasts
    ):
        for copy in copies:
            copy.wait_send()
    for copy in square_copies + shard_copies:
        copy.wait_send()


def exchange(grads_a, grads_b, state_kernel, state_attention, weight_kernel, weight_attention, scalars):
    depth, _, rows, piece, width = grads_a.shape
    tops, wide = factors(rows)
    lanes = grads_b.shape[3]
    grads_a = grads_a.reshape(depth, 2, tops, wide, piece, width)
    grads_b = grads_b.reshape(depth, 2, tops, wide, lanes, width)
    pairs, tall = state_kernel.shape[1:3]
    quads, short = state_attention.shape[1:3]
    shape = functools.partial(jax.ShapeDtypeStruct, dtype=jnp.float32)
    whole = pl.BlockSpec(memory_space=pltpu.VMEM)
    anywhere = pl.BlockSpec(memory_space=pl.ANY)
    dma = pltpu.SemaphoreType.DMA
    vmem = functools.partial(pltpu.VMEM, dtype=jnp.float32)
    most = max(tops, wide)
    return pl.pallas_call(
        functools.partial(exchange_kernel, (pairs, tall, quads, short), (RATES[1], RATES[2])),
        in_specs=[anywhere] * 6 + [pl.BlockSpec(memory_space=pltpu.SMEM)],
        out_specs=[anywhere] * 2 + [whole] * 2,
        out_shape=[
            shape(grads_a.shape),
            shape(grads_b.shape),
            shape((rows, piece, width)),
            shape((8, 128)),
        ],
        scratch_shapes=[
            vmem((depth, tops, wide, piece, width)),
            vmem((depth, tops, wide, lanes, width)),
            vmem((depth, tops, wide, piece, width)),
            vmem((depth, tops, wide, lanes, width)),
            vmem((most - 1, depth, most, piece, width)),
            vmem((most - 1, depth, most, lanes, width)),
            vmem((most - 1, depth, piece, width)),
            vmem((most - 1, depth, lanes, width)),
            vmem((depth - 1, piece, width)),
            vmem((depth - 1, lanes, width)),
            vmem((piece, width)),
            vmem((lanes, width)),
            vmem((rows * piece, width)),
            vmem((rows * piece, width)),
            vmem((rows * piece, width)),
            vmem((2, 8, width)),
            vmem((rows, 8, width)),
            vmem((depth, 8, width)),
            dma((3 * (pairs + quads),)),
            dma((2,)),
            dma((SPLIT_A + SPLIT_B,)),
            dma((SPLIT_A + SPLIT_B,)),
            dma((SPLIT_A + SPLIT_B, most - 1)),
            dma((SPLIT_A + SPLIT_B, most - 1)),
            dma((SPLIT_A + SPLIT_B, most - 1)),
            dma((SPLIT_A + SPLIT_B, most - 1)),
            dma((SPLIT_A + SPLIT_B, depth - 1)),
            dma((SPLIT_A + SPLIT_B, depth - 1)),
            dma((rows - 1,)),
            dma((rows - 1,)),
            dma((rows + depth - 1,)),
            dma((rows + depth - 1,)),
            dma((SPLIT_A + SPLIT_B, depth - 1)),
            dma((SPLIT_A + SPLIT_B, depth - 1)),
            dma((SPLIT_A + SPLIT_B, most - 1)),
            dma((SPLIT_A + SPLIT_B, most - 1)),
            dma((SPLIT_A + SPLIT_B, most - 1)),
            dma((SPLIT_A + SPLIT_B, most - 1)),
            dma((SPLIT_A + SPLIT_B,)),
            dma((SPLIT_A + SPLIT_B,)),
            dma((SPLIT_A + SPLIT_B,)),
        ],
        compiler_params=pltpu.CompilerParams(
            collective_id=0, has_side_effects=True, vmem_limit_bytes=VMEM_LIMIT
        ),
        name="exchange",
    )(grads_a, grads_b, state_kernel, state_attention, weight_kernel, weight_attention, scalars)


def finish_kernel(
    scalars,
    norm_tile,
    fresh,
    average_kernel,
    average_attention,
    shard_grad,
    state_kernel,
    state_attention,
    time_left,
    time_right,
    shift_rows,
    rest_rows,
    *refs,
):
    weights, states, averages, refs = refs[:5], refs[5:10], refs[10:15], refs[15:]
    (kernel_out, attention_out), refs = refs[:2], refs[2:]
    updated, firsts, seconds, refs = refs[:5], refs[5:10], refs[10:15], refs[15:]
    first_kernel_out, first_attention_out, second_kernel_out, second_attention_out, loss_out, norm_out = refs
    norm = norm_tile[0:1, 0:1]
    clip = CLIP / jnp.maximum(norm, CLIP)
    kept = scalars[2]

    def averaged(out, index, new, average):
        out[(0,) + index] = new
        out[(1,) + index] = kept * average + (1.0 - kept) * new

    tall, short = state_kernel.shape[2], state_attention.shape[2]
    for k in range(2):
        averaged(kernel_out, (k,), fresh[0, k * tall : k * tall + tall], average_kernel[k])
    for k in range(4):
        at = 2 * tall + k * short
        averaged(attention_out, (k,), fresh[0, at : at + short], average_attention[k])

    def moments(first, second, g):
        return BETA_ONE * first + (1.0 - BETA_ONE) * g, BETA_TWO * second + (1.0 - BETA_TWO) * g * g

    def update(k, rate, grad):
        weight = weights[k][...]
        old = (states[k][0], states[k][1]) if k < 2 else (states[k][:, 0, :], states[k][:, 1, :])
        first, second = moments(*old, grad * clip)
        firsts[k][...] = first
        seconds[k][...] = second
        step = first * scalars[0] / (jnp.sqrt(second * scalars[1]) + EPS_ADAM)
        new = weight - rate * (step + DECAY * weight)
        if k < 2:
            averaged(updated[k], (), new, averages[k][...])
        else:
            updated[k][:, 0, :] = new
            updated[k][:, 1, :] = kept * averages[k][...] + (1.0 - kept) * new

    update(0, RATES[3], jnp.concatenate([time_left[...], time_right[...]], axis=1))
    update(1, RATES[4], shift_rows[...])

    @pl.when(pl.program_id(0) == 0)
    def _():
        for refs, outs, count, height in (
            (state_kernel, (first_kernel_out, second_kernel_out), 2, tall),
            (state_attention, (first_attention_out, second_attention_out), 4, short),
        ):
            for k in range(count):
                at = k * height + (0 if count == 2 else 2 * tall)
                first, second = moments(refs[0, k], refs[1, k], shard_grad[at : at + height] * clip)
                outs[0][k] = first
                outs[1][k] = second
        inlet = jnp.concatenate([rest_rows[8 * tap : 8 * tap + 3] for tap in range(9)], axis=0)
        outlet = jnp.concatenate([rest_rows[80 + 8 * tap : 83 + 8 * tap] for tap in range(9)], axis=1)
        update(2, RATES[0], inlet)
        update(3, RATES[5], outlet)
        update(4, RATES[6], rest_rows[160:179])
        loss_out[...] = jnp.sum(col_sum(rest_rows[184:192]), axis=1, keepdims=True)
        norm_out[...] = norm


def finish(scalars, norm_tile, fresh, average_kernel, average_attention, shard_grad, state_kernel, state_attention, rest, weights, states, averages):
    batch, shard_rows, width = fresh.shape
    tall, short = state_kernel.shape[2], state_attention.shape[2]
    (time_rows, time_width), (shift_rows, _) = weights[0].shape, weights[1].shape
    time_part, shift_part = time_rows // batch, shift_rows // batch
    shape = functools.partial(jax.ShapeDtypeStruct, dtype=jnp.float32)

    def at(block, index):
        return pl.BlockSpec(block, index)

    def rows_of(k, lead):
        part, wide = ((time_part, time_width), (shift_part, width))[k]
        return pl.BlockSpec(lead + (part, wide), lambda b: (0,) * len(lead) + (b, 0))

    def five(lead):
        small = [w.shape[:1] + lead + w.shape[1:] for w in weights[2:]]
        return [rows_of(0, lead), rows_of(1, lead)] + [resident(block) for block in small]

    shift_at = 2 * time_rows // shift_part
    rest_at = (2 * time_rows + shift_rows) // 256
    return pl.pallas_call(
        finish_kernel,
        grid=(batch,),
        in_specs=[
            pl.BlockSpec(memory_space=pltpu.SMEM),
            resident(norm_tile.shape),
            at((1, shard_rows, width), lambda b: (b, 0, 0)),
            at((2, tall, width), lambda b: (0, b, 0)),
            at((4, short, width), lambda b: (0, b, 0)),
            resident(shard_grad.shape),
            resident(state_kernel.shape),
            resident(state_attention.shape),
            at((time_part, width), lambda b: (b, 0)),
            at((time_part, width), lambda b: (batch + b, 0)),
            at((shift_part, width), lambda b: (shift_at + b, 0)),
            pl.BlockSpec((256, width), lambda b: (rest_at, 0), pipeline_mode=pl.Buffered(1)),
        ]
        + five(())
        + five((2,))
        + five(()),
        out_specs=[
            at((2, 2, tall, width), lambda b: (0, 0, b, 0)),
            at((2, 4, short, width), lambda b: (0, 0, b, 0)),
        ]
        + five((2,))
        + five(())
        + five(())
        + [resident(state_kernel.shape[1:]), resident(state_attention.shape[1:])] * 2
        + [resident((1, 1))] * 2,
        out_shape=[
            shape((2, 2, batch * tall, width)),
            shape((2, 4, batch * short, width)),
        ]
        + [shape((2,) + w.shape) for w in weights[:2]]
        + [shape((w.shape[0], 2, w.shape[1])) for w in weights[2:]]
        + [shape(w.shape) for w in weights] * 2
        + [shape(state_kernel.shape[1:]), shape(state_attention.shape[1:])] * 2
        + [shape((1, 1))] * 2,
        compiler_params=pltpu.CompilerParams(vmem_limit_bytes=VMEM_LIMIT),
        cost_estimate=pl.CostEstimate(flops=40 << 20, bytes_accessed=36 << 20, transcendentals=1 << 20),
        name="finish",
    )(
        scalars,
        norm_tile,
        fresh,
        average_kernel,
        average_attention,
        shard_grad,
        state_kernel,
        state_attention,
        rest,
        rest,
        rest,
        rest,
        *weights,
        *states,
        *averages,
    )


def local(
    x_clean,
    noise,
    timesteps,
    keep_mask,
    adam_step,
    inlet_weight,
    kernel_weight,
    attention_weight,
    time_weight,
    shift_weight,
    outlet_weight,
    small_params,
    state_inlet,
    state_kernel,
    state_attention,
    state_time,
    state_shift,
    state_outlet,
    state_small,
    average_inlet,
    average_kernel,
    average_attention,
    average_time,
    average_shift,
    average_outlet,
    average_small,
):
    chans = kernel_weight.shape[2]
    width_sin = time_weight.shape[0] - time_weight.shape[1]
    rows, batch = lax.axis_size("rows"), lax.axis_size("batch")
    own = timesteps.shape[0] // rows
    keep = keep_mask.reshape(rows, own, -1, chans).astype(jnp.bfloat16)
    keep, timesteps, x_clean, noise = lax.optimization_barrier((keep, timesteps, x_clean, noise))
    keep = lax.all_to_all(keep, "rows", 0, 0, tiled=True)
    halves = [a.reshape(rows, own, 3, -1) for a in (x_clean, noise)]
    pair = jnp.pad(jnp.concatenate(halves, axis=3), ((0, 0), (0, 0), (0, 1), (0, 0)))
    pair = lax.all_to_all(pair, "rows", 0, 0, tiled=True)
    pair, inlet_low, kernels, projections, outlet_low = lax.optimization_barrier(
        (pair, inlet_weight, kernel_weight, attention_weight, outlet_weight)
    )
    timesteps = lax.dynamic_slice_in_dim(timesteps, lax.axis_index("rows") * own, own, 0)
    bars = alpha_bars(timesteps)
    mix = jnp.stack([jnp.sqrt(bars), jnp.sqrt(1.0 - bars)])
    kernels = kernels.astype(jnp.bfloat16)
    projections = projections.astype(jnp.bfloat16)
    inlet = padded_taps(inlet_low).astype(jnp.bfloat16)
    outlet = padded_taps(
        jnp.transpose(outlet_low.reshape(3, 9, chans), (1, 0, 2)).reshape(27, chans)
    ).astype(jnp.bfloat16)
    qkv = jnp.concatenate([projections[0], projections[1], projections[2]], axis=1)
    embed = sinusoid(timesteps, width_sin).astype(jnp.bfloat16)
    ratio = bars / (1.0 - bars)
    snr_weight = jnp.minimum(ratio, GAMMA) / ratio
    denom = 3 * 256 * own * rows * batch
    coef = 2.0 * snr_weight / denom
    start, inner, stats, noisy, target, hidden, hidden_slope, time_act, time_slope = forward_part(
        FORWARD_CHUNK, mix, pair, embed, time_weight, shift_weight, inlet, kernels[0], small_params
    )
    bias_qkv = jnp.concatenate(
        [small_params[11], jnp.zeros_like(small_params[0]), small_params[12]]
    )
    tall, short = state_kernel.shape[2], state_attention.shape[2]
    shard_rows = rows * padded_rows(2 * tall + 4 * short, rows)
    lanes = padded_rows(MISC_TOTAL, batch * rows)
    shards, rest = main_part(
        CHUNK,
        (batch, shard_rows, tall, short, batch * rows * lanes),
        coef,
        start,
        inner,
        stats,
        noisy,
        target,
        keep,
        (
            rows_first(kernels[0]),
            kernels[1],
            rows_first(kernels[1]),
            qkv,
            qkv.T,
            projections[3],
            projections[3].T,
            outlet,
        ),
        small_params,
        bias_qkv[None],
        (embed, hidden, hidden_slope, time_act, time_slope, time_weight, shift_weight),
    )
    count = adam_step[0].astype(jnp.float32)
    scalars = jnp.stack(
        [
            1.0 / (1.0 - BETA_ONE**count),
            1.0 / (1.0 - BETA_TWO**count),
            jnp.minimum(EMA_TOP, (1.0 + count) / (10.0 + count)),
        ]
    )
    fresh, rest, shard_grad, norm_tile = exchange(
        shards.reshape(batch // 2, 2, rows, shard_rows // rows, chans),
        rest.reshape(batch // 2, 2, rows, lanes, chans),
        state_kernel,
        state_attention,
        kernel_weight,
        attention_weight,
        scalars,
    )
    results = finish(
        scalars,
        norm_tile,
        fresh.reshape(batch, shard_rows, chans),
        lax.all_gather(average_kernel, "batch", axis=1, tiled=True),
        lax.all_gather(average_attention, "batch", axis=1, tiled=True),
        shard_grad.reshape(shard_rows, chans),
        state_kernel,
        state_attention,
        rest.reshape(-1, chans),
        (time_weight, shift_weight, inlet_weight, outlet_weight, small_params),
        (state_time, state_shift)
        + tuple(jnp.transpose(a, (1, 0, 2)) for a in (state_inlet, state_outlet, state_small)),
        (average_time, average_shift, average_inlet, average_outlet, average_small),
    )
    kernel_pair, attention_pair = results[:2]
    triples = [list(results[2 + 5 * k : 7 + 5 * k]) for k in range(3)]
    triples[0][2:] = [jnp.transpose(a, (1, 0, 2)) for a in triples[0][2:]]
    first_conv, first_attention, second_conv, second_attention, loss, norm = results[17:]
    ordered = []
    for (time, shift, inlet, outlet, small), middle in zip(
        triples,
        ((kernel_pair, attention_pair), (first_conv, first_attention), (second_conv, second_attention)),
    ):
        ordered += [inlet, *middle, time, shift, outlet, small]
    return (*ordered, loss.reshape(()), norm.reshape(()))


def solution(mesh):
    return jax.shard_map(
        local,
        mesh=mesh,
        in_specs=(
            P("batch", None, "rows", None),
            P("batch", None, "rows", None),
            P("batch"),
            P("batch", "rows", None, None),
            P(),
            P(),
            P(),
            P(),
            P(),
            P(),
            P(),
            P(),
            P(),
            P(None, None, "batch", None),
            P(None, None, "batch", None),
            P(),
            P(),
            P(),
            P(),
            P(),
            P(None, "batch", None),
            P(None, "batch", None),
            P(),
            P(),
            P(),
            P(),
        ),
        out_specs=(
            P(),
            P(),
            P(),
            P(),
            P(),
            P(),
            P(),
            P(),
            P(None, "batch", None),
            P(None, "batch", None),
            P(),
            P(),
            P(),
            P(),
            P(),
            P(None, "batch", None),
            P(None, "batch", None),
            P(),
            P(),
            P(),
            P(),
            P(),
            P(),
        ),
        check_vma=False,
    )
```

```python
import functools
import math

import jax
import jax.numpy as jnp
import numpy as np
from jax import lax
from jax.experimental import pallas as pl
from jax.experimental.pallas import tpu as pltpu
from jax.sharding import PartitionSpec as P

G = 32


HIGH_PRECISION = lax.Precision.HIGHEST
CLIP = 0.05
GAMMA = 5.0
KEEP = 0.9
EPS_NORM = 1e-05
BETA_ONE = 0.9
BETA_TWO = 0.999
EPS_ADAM = 1e-08
DECAY = 0.01
EMA_TOP = 0.9999
VMEM_LIMIT = 60 << 20
CHUNK = 4
FORWARD_CHUNK = 8
GROUP = 2
COUNT = 2048.0
RATES = (0.1, 0.01, 0.03, 0.05, 0.02, 0.01, 0.2)


def bar_table():
    beta_rates = 0.0001 + (0.02 - 0.0001) * np.arange(1000, dtype=np.float64) / 999.0
    return np.exp(np.cumsum(np.log(1.0 - beta_rates))).astype(np.float32)


def alpha_bars(timesteps):
    one_hot = (timesteps[:, None] == jnp.arange(1000)[None, :]).astype(jnp.float32)
    return jnp.sum(one_hot * bar_table()[None, :], axis=1)


def sinusoid(timesteps, width):
    half = width // 2
    rates = jnp.exp(-math.log(10000.0) * jnp.arange(half).astype(jnp.float32) / (half - 1))
    angles = timesteps.astype(jnp.float32)[:, None] * rates[None, :]
    return jnp.concatenate([jnp.sin(angles), jnp.cos(angles)], axis=1)


def swish_grad(pre):
    logistic = jax.nn.sigmoid(pre)
    return logistic * (1.0 + pre * (1.0 - logistic))


def wrap(shift, size):
    return shift % size


def tap_masks():
    lane = lax.broadcasted_iota(jnp.int32, (8, 256), 1)
    row, col = lane // 16, lane % 16
    masks = []
    for i in range(3):
        for j in range(3):
            ok = (row + (i - 1) >= 0) & (row + (i - 1) < 16) & (col + (j - 1) >= 0) & (col + (j - 1) < 16)
            masks.append(ok)
    return masks


def tap_stack(tile, masks, sign):
    parts = []
    for tap in range(9):
        step = sign * (16 * (tap // 3 - 1) + tap % 3 - 1)
        moved = tile if step == 0 else pltpu.roll(tile, wrap(-step, 256), 1)
        parts.append(jnp.where(masks[tap if sign > 0 else 8 - tap], moved, 0.0))
    parts.append(jnp.zeros_like(tile))
    return jnp.concatenate(parts, axis=0).astype(jnp.bfloat16)


def group_sum(rows):
    halves = []
    for half in range(2):
        part = rows[:, 128 * half : 128 * half + 128]
        lane = lax.broadcasted_iota(jnp.int32, part.shape, 1)
        for step in (1, 2, 4):
            upper = (lane // step) % 2 == 1
            part = part + jnp.where(upper, pltpu.roll(part, step, 1), pltpu.roll(part, 128 - step, 1))
        halves.append(part)
    return jnp.concatenate(halves, axis=1)


def col_sum(x):
    return jnp.sum(x, axis=0, keepdims=True)


def stats_of(fields):
    sums = jnp.concatenate([col_sum(x) for x in fields] + [col_sum(x * x) for x in fields], axis=0)
    both = group_sum(sums) / COUNT
    n = len(fields)
    mean = both[:n]
    spread = both[n:] - mean * mean
    return mean, lax.rsqrt(spread + EPS_NORM)


def logistic(z):
    return 0.5 * jnp.tanh(0.5 * z) + 0.5


def put_shifted(buf, c, y, not_first, not_last):
    buf[c, 16:272, 256:512] = y.astype(jnp.bfloat16)
    buf[c, 16:272, 0:256] = jnp.where(not_first, pltpu.roll(y, 1, 0), 0.0).astype(jnp.bfloat16)
    buf[c, 16:272, 512:768] = jnp.where(not_last, pltpu.roll(y, 255, 0), 0.0).astype(jnp.bfloat16)


def edge_masks():
    col = lax.broadcasted_iota(jnp.int32, (256, 256), 0) % 16
    return col != 0, col != 15


def stacked(buf, i):
    chunk = buf.shape[0]
    return buf[:, 16 * i : 16 * i + 256, :].reshape(chunk * 256, 768)


def dot(a, b, dims=((1,), (0,))):
    return lax.dot_general(a, b, (dims, ((), ())), preferred_element_type=jnp.float32)


NT = ((1,), (1,))
TN = ((0,), (0,))


def conv_shifted(buf, weight):
    field = jnp.concatenate([stacked(buf, i) for i in range(3)], axis=1)
    return dot(field, weight[...])


def zero_edges(buf):
    edge = jnp.zeros((buf.shape[0], 16, 768), jnp.bfloat16)
    buf[:, 0:16, :] = edge
    buf[:, 272:288, :] = edge


def take_turns(workers):
    live, started = [], 0
    while live or started < len(workers):
        if started < len(workers):
            live.append(workers[started])
            started += 1
        live = [w for w in live if next(w, live) is not live]


def lanes_joined(blocks):
    return blocks[0] if len(blocks) == 1 else jnp.concatenate(blocks, axis=1)


def first_kernel(
    mix,
    pair,
    embed,
    time_weight,
    shift_weight,
    inlet,
    kernel_one,
    small,
    start_out,
    inner_out,
    stats_out,
    noisy_out,
    target_out,
    hidden_out,
    hidden_slope_out,
    time_act_out,
    time_slope_out,
    buf,
    tshift,
):
    chunk = start_out.shape[0]
    step = pl.program_id(0)

    @pl.when(step == 0)
    def _():
        zero_edges(buf)
        width = embed.shape[1]

        def layer(x, weight, at):
            bias = jnp.concatenate([small[at : at + 1], small[at + 1 : at + 2]], axis=1)
            z = dot(x, weight.astype(jnp.bfloat16)) + bias
            s = logistic(z)
            return (z * s).astype(jnp.bfloat16), s * (1.0 + z * (1.0 - s))

        hidden, hidden_slope = layer(embed[...], time_weight[0:width, :], 15)
        time_act, time_slope = layer(hidden, time_weight[width:, :], 17)
        hidden_out[...] = hidden
        hidden_slope_out[...] = hidden_slope
        time_act_out[...] = time_act
        time_slope_out[...] = time_slope
        both = small[14:15] + small[9:10]
        tshift[...] = dot(time_act, shift_weight[...].astype(jnp.bfloat16)) + both

    masks = tap_masks()
    not_first, not_last = edge_masks()
    part = pair.shape[3] // 2
    blank = jnp.zeros((4, 256), jnp.float32)

    def work(images):
        n = len(images)
        every = range(n)
        low, high = images[0], images[-1] + 1
        starts = []
        for c in images:
            tiles = [pair[s, c] for s in range(pair.shape[0])]
            clean = jnp.concatenate([lanes_joined([t[:, :part] for t in tiles]), blank], axis=0)
            noise = jnp.concatenate([lanes_joined([t[:, part:] for t in tiles]), blank], axis=0)
            noisy = mix[0, step * chunk + c] * clean + mix[1, step * chunk + c] * noise
            noisy = noisy.astype(jnp.bfloat16).astype(jnp.float32)
            noisy_out[c] = noisy
            target_out[c] = noise
            start = dot(tap_stack(noisy, masks, 1), inlet[...], TN) + small[8:9]
            start_out[c] = start
            starts.append(start)
        yield
        mean, rstd = stats_of(starts)
        for i, c in enumerate(images):
            scale = rstd[i : i + 1] * small[0:1]
            z = starts[i] * scale + (small[4:5] - mean[i : i + 1] * scale)
            put_shifted(buf, c, z * logistic(z), not_first, not_last)
        yield
        inner_all = conv_shifted(buf.at[low:high], kernel_one)
        yield
        inners = []
        for i, c in enumerate(images):
            inner = inner_all[256 * i : 256 * i + 256] + tshift[pl.ds(step * chunk + c, 1), :]
            inner_out[c] = inner
            inners.append(inner)
        mean_two, rstd_two = stats_of(inners)
        for i, c in enumerate(images):
            stats_out[c] = jnp.concatenate(
                [mean[i : i + 1], rstd[i : i + 1], mean_two[i : i + 1], rstd_two[i : i + 1]]
                + [jnp.zeros((4, 256), jnp.float32)],
                axis=0,
            )

    take_turns([work(list(range(g, g + GROUP))) for g in range(0, chunk, GROUP)])


def norm_grad(dys, fields, means, rstds, gain):
    n = len(dys)
    shift_sums, gain_sums = [], []
    for dy, x, mean, rstd in zip(dys, fields, means, rstds):
        shift_sums.append(col_sum(dy))
        gain_sums.append(col_sum(dy * (x * rstd - mean * rstd)))
    both = group_sum(jnp.concatenate(shift_sums + gain_sums, axis=0) * gain) / COUNT
    grads = []
    for c in range(n):
        rstd, mean = rstds[c], means[c]
        slope = -rstd * rstd * both[n + c : n + c + 1]
        base = -rstd * both[c : c + 1] - mean * slope
        grads.append(dys[c] * (rstd * gain) + (fields[c] * slope + base))
    return grads, sum(gain_sums), sum(shift_sums)


def second_kernel(
    tall,
    short,
    coef,
    start_in,
    inner_in,
    stats_in,
    noisy,
    target,
    keep,
    kernel_one_flip,
    kernel_two,
    kernel_two_flip,
    qkv,
    qkv_t,
    proj,
    proj_t,
    outlet,
    small,
    bias_qkv,
    embed,
    hidden,
    hidden_slope,
    time_act,
    time_slope,
    time_weight,
    shift_weight,
    shard_out,
    rest_out,
    grad_one_out,
    grad_two_out,
    grad_qkv_out,
    grad_proj_out,
    grad_outlet_out,
    grad_inlet_out,
    grad_small_out,
    loss_out,
    tshift_grad,
    buf,
    grad_buf,
):
    chunk = noisy.shape[0]
    step = pl.program_id(0)
    sums = (
        grad_one_out,
        grad_two_out,
        grad_qkv_out,
        grad_proj_out,
        grad_outlet_out,
        grad_inlet_out,
        grad_small_out,
        loss_out,
    )

    @pl.when(step == 0)
    def _():
        zero_edges(buf)
        zero_edges(grad_buf)
        for ref in sums:
            ref[...] = jnp.zeros(ref.shape, jnp.float32)

    masks = tap_masks()
    not_first, not_last = edge_masks()
    scale = 256 ** (-0.5)

    def gain(k):
        return small[k : k + 1]

    def shift(k):
        return small[4 + k : 5 + k]

    def normed(x, mean, rstd, k):
        slope = rstd * gain(k)
        return x * slope + (shift(k) - mean * slope)

    def row(values, c):
        return values[c : c + 1]

    def work(images):
        n = len(images)
        every = range(n)
        low, high = images[0], images[-1] + 1

        def part(x, c):
            return x[256 * c : 256 * c + 256]

        slope_two, act_two = [], []
        for c in images:
            z = normed(inner_in[c], stats_in[c, 2:3], stats_in[c, 3:4], 1)
            s = logistic(z)
            kept = jnp.concatenate([keep[s, c] for s in range(keep.shape[0])], axis=0)
            kept = kept.astype(jnp.float32) * (1.0 / KEEP)
            act = z * s * kept
            slope_two.append(s * (1.0 + z * (1.0 - s)) * kept)
            act_two.append(act.astype(jnp.bfloat16))
            put_shifted(buf, c, act, not_first, not_last)
        yield
        conv_two = conv_shifted(buf.at[low:high], kernel_two)
        yield
        middle = [start_in[c] + part(conv_two, i) + small[10:11] for i, c in enumerate(images)]
        mean, rstd = stats_of(middle)
        mean_three, rstd_three = [row(mean, i) for i in every], [row(rstd, i) for i in every]
        tokens = [
            normed(middle[i], mean_three[i], rstd_three[i], 2).astype(jnp.bfloat16) for i in every
        ]
        tokens = jnp.concatenate(tokens, axis=0)
        yield
        qkv_all = (dot(tokens, qkv[...]) + bias_qkv[0:1]).astype(jnp.bfloat16)
        triples = []
        for i in every:
            three = part(qkv_all, i)
            triples.append((three[:, 0:256], three[:, 256:512], three[:, 512:768]))
        scores = [dot(q, k, NT) for q, k, _ in triples]
        yield
        probs, probs_low = [], []
        for i in every:
            expo = jnp.exp((scores[i] - jnp.max(scores[i], axis=1, keepdims=True)) * scale)
            p = expo * (1.0 / jnp.sum(expo, axis=1, keepdims=True))
            probs.append(p)
            probs_low.append(p.astype(jnp.bfloat16))
        yield
        mixed = [dot(probs_low[i], triples[i][2]).astype(jnp.bfloat16) for i in every]
        mixed = jnp.concatenate(mixed, axis=0)
        branch = dot(mixed, proj[...])
        yield
        final = [middle[i] + part(branch, i) + small[13:14] for i in every]
        mean, rstd = stats_of(final)
        mean_four, rstd_four = [row(mean, i) for i in every], [row(rstd, i) for i in every]
        act_four, slope_four = [], []
        for i in every:
            z = normed(final[i], mean_four[i], rstd_four[i], 3)
            s = logistic(z)
            act_four.append((z * s).astype(jnp.bfloat16))
            slope_four.append(s * (1.0 + z * (1.0 - s)))
        yield
        taps_all = [dot(outlet[...], act, NT) for act in act_four]
        yield
        spreads = []
        loss_sum = 0.0
        for i, c in enumerate(images):
            predicted = 0.0
            for tap in range(9):
                move = 16 * (tap // 3 - 1) + tap % 3 - 1
                moved = taps_all[i][8 * tap : 8 * tap + 8]
                moved = moved if move == 0 else pltpu.roll(moved, wrap(-move, 256), 1)
                predicted = predicted + jnp.where(masks[tap], moved, 0.0)
            error = predicted - target[c]
            weight = coef[step * chunk + c]
            loss_sum = loss_sum + (0.5 * weight) * (error * error)
            grad_pred = (weight * error).astype(jnp.bfloat16).astype(jnp.float32)
            spreads.append(tap_stack(grad_pred, masks, -1))
        loss_out[...] += loss_sum
        yield
        grad_outlet_out[...] += sum(dot(s, act) for s, act in zip(spreads, act_four))
        grad_act = [dot(s, outlet[...], TN) for s in spreads]
        yield
        grad_four = [grad_act[i] * slope_four[i] for i in every]
        grad_final, gain_four, shift_four = norm_grad(grad_four, final, mean_four, rstd_four, gain(3))
        branch_all = jnp.concatenate([g.astype(jnp.bfloat16) for g in grad_final], axis=0)
        yield
        grad_proj_out[...] += dot(mixed, branch_all, TN)
        grad_mixed = dot(branch_all, proj_t[...]).astype(jnp.bfloat16)
        dps = [dot(part(grad_mixed, i), triples[i][2], NT) for i in every]
        dvs = [dot(probs_low[i], part(grad_mixed, i), TN) for i in every]
        yield
        dss = []
        for i in every:
            p, dp = probs[i], dps[i]
            dss.append((p * (dp - jnp.sum(p * dp, axis=1, keepdims=True))).astype(jnp.bfloat16))
        yield
        grad_qkv = []
        for i in every:
            q, k, _ = triples[i]
            dq = dot(dss[i], k) * scale
            dk = dot(dss[i], q, TN) * scale
            grad_qkv.append(jnp.concatenate([dq, dk, dvs[i]], axis=1).astype(jnp.bfloat16))
        grad_qkv_all = jnp.concatenate(grad_qkv, axis=0)
        grad_qkv_out[...] += dot(tokens, grad_qkv_all, TN)
        grad_tokens = dot(grad_qkv_all, qkv_t[...])
        yield
        bias_sums = col_sum(grad_qkv_all.astype(jnp.float32))
        grad_norm, gain_three, shift_three = norm_grad(
            [part(grad_tokens, i) for i in every], middle, mean_three, rstd_three, gain(2)
        )
        grad_middle = [grad_final[i] + grad_norm[i] for i in every]
        for i, c in enumerate(images):
            put_shifted(grad_buf, c, grad_middle[i], not_first, not_last)
        yield
        field = jnp.concatenate(act_two, axis=0)
        for i in range(3):
            grad_two_out[i] += dot(field, stacked(grad_buf.at[low:high], i), TN)
        grad_act = conv_shifted(grad_buf.at[low:high], kernel_two_flip)
        yield
        grad_two = [part(grad_act, i) * slope_two[i] for i in every]
        grad_inner, gain_two, shift_two = norm_grad(
            grad_two,
            [inner_in[c] for c in images],
            [stats_in[c, 2:3] for c in images],
            [stats_in[c, 3:4] for c in images],
            gain(1),
        )
        for i, c in enumerate(images):
            put_shifted(grad_buf, c, grad_inner[i], not_first, not_last)
        act_one, slope_one = [], []
        for c in images:
            z = normed(start_in[c], stats_in[c, 0:1], stats_in[c, 1:2], 0)
            s = logistic(z)
            act_one.append((z * s).astype(jnp.bfloat16))
            slope_one.append(s * (1.0 + z * (1.0 - s)))
        yield
        field = jnp.concatenate(act_one, axis=0)
        for i in range(3):
            grad_one_out[i] += dot(field, stacked(grad_buf.at[low:high], i), TN)
        grad_act = conv_shifted(grad_buf.at[low:high], kernel_one_flip)
        yield
        grad_one = [part(grad_act, i) * slope_one[i] for i in every]
        grad_norm, gain_one, shift_one = norm_grad(
            grad_one,
            [start_in[c] for c in images],
            [stats_in[c, 0:1] for c in images],
            [stats_in[c, 1:2] for c in images],
            gain(0),
        )
        grad_start = [grad_middle[i] + grad_norm[i] for i in every]
        patches = [tap_stack(noisy[c], masks, 1) for c in images]
        inner_sums = [col_sum(g) for g in grad_inner]
        for i, c in enumerate(images):
            tshift_grad[pl.ds(step * chunk + c, 1), :] = inner_sums[i]
        grad_small_out[...] += jnp.concatenate(
            [
                gain_one,
                gain_two,
                gain_three,
                gain_four,
                shift_one,
                shift_two,
                shift_three,
                shift_four,
                sum(col_sum(g) for g in grad_start),
                sum(inner_sums),
                sum(col_sum(g) for g in grad_middle),
                bias_sums[:, 0:256],
                bias_sums[:, 512:768],
                sum(col_sum(g) for g in grad_final),
                jnp.zeros((2, 256), jnp.float32),
            ],
            axis=0,
        )
        yield
        grad_inlet_out[...] += sum(
            dot(patch, g.astype(jnp.bfloat16)) for patch, g in zip(patches, grad_start)
        )

    take_turns([work(list(range(g, g + GROUP))) for g in range(0, chunk, GROUP)])

    @pl.when(step == pl.num_programs(0) - 1)
    def _():
        for k, grad in enumerate((grad_one_out, grad_two_out)):
            for tap in range(9):
                at = 256 * (2 - tap % 3)
                for shard, off, row, size in cuts(tap * 256, 256, tall):
                    shard_out[shard, k * tall + off : k * tall + off + size, :] = grad[
                        2 - tap // 3, row : row + size, at : at + 256
                    ]
        for k in range(4):
            grad, at = (grad_qkv_out, 256 * k) if k < 3 else (grad_proj_out, 0)
            for shard, off, row, size in cuts(0, 256, short):
                low = 2 * tall + k * short + off
                shard_out[shard, low : low + size, :] = grad[row : row + size, at : at + 256]
        used = 2 * tall + 4 * short
        if used < shard_out.shape[1]:
            shard_out[:, used:, :] = jnp.zeros(
                (shard_out.shape[0], shard_out.shape[1] - used, 256), jnp.float32
            )
        total = tshift_grad[...]
        shift_grad = full_dot(time_act[...], total, TN)
        grad_act = full_dot(total, shift_weight[...].astype(jnp.bfloat16), NT) * time_slope[...]
        two_grad = full_dot(hidden[...], grad_act, TN)
        time_two = time_weight[embed.shape[1] :, :].astype(jnp.bfloat16)
        grad_hidden = full_dot(grad_act, time_two, NT) * hidden_slope[...]
        one_grad = full_dot(embed[...], grad_hidden, TN)
        width = one_grad.shape[0]
        height = width + two_grad.shape[0]
        for half in range(2):
            span = slice(256 * half, 256 * half + 256)
            rest_out[half * height : half * height + width, :] = one_grad[:, span]
            rest_out[half * height + width : half * height + height, :] = two_grad[:, span]
        act_sum, hidden_sum = col_sum(grad_act), col_sum(grad_hidden)
        parts = [
            shift_grad,
            grad_inlet_out[...],
            grad_outlet_out[...],
            jnp.concatenate(
                [
                    grad_small_out[0:14],
                    col_sum(total),
                    hidden_sum[:, 0:256],
                    hidden_sum[:, 256:512],
                    act_sum[:, 0:256],
                    act_sum[:, 256:512],
                    jnp.zeros((5, 256), jnp.float32),
                ],
                axis=0,
            ),
            loss_out[...],
        ]
        at = 2 * height
        for part in parts:
            rest_out[at : at + part.shape[0], :] = part
            at += part.shape[0]
        if at < rest_out.shape[0]:
            rest_out[at:, :] = jnp.zeros((rest_out.shape[0] - at, 256), jnp.float32)


def cuts(first, size, height):
    parts, row = [], 0
    while row < size:
        shard, off = divmod(first + row, height)
        take = min(height - off, size - row)
        parts.append((shard, off, row, take))
        row += take
    return parts


def full_dot(a, b, dims):
    return lax.dot_general(
        a.astype(jnp.float32),
        b.astype(jnp.float32),
        (dims, ((), ())),
        precision=HIGH_PRECISION,
        preferred_element_type=jnp.float32,
    )


def resident(shape):
    return pl.BlockSpec(shape, lambda i: (0,) * len(shape), pipeline_mode=pl.Buffered(1))


def per_chunk(chunk, *tail):
    return pl.BlockSpec((chunk,) + tail, lambda i: (i,) + (0,) * len(tail))


def by_source(chunk, block):
    return pl.BlockSpec((block[0], chunk) + block[2:], lambda i: (0, i, 0, 0))


def forward_part(chunk, mix, pair, embed, time_weight, shift_weight, inlet, kernel_one, small):
    n, deep = pair.shape[1], time_weight.shape[1]
    chunk = min(chunk, n)
    shapes = [(n, 256, 256), (n, 256, 256), (n, 8, 256), (n, 8, 256), (n, 8, 256)]
    whole = [jnp.bfloat16, jnp.float32, jnp.bfloat16, jnp.float32]
    return pl.pallas_call(
        first_kernel,
        grid=(n // chunk,),
        in_specs=[
            pl.BlockSpec(memory_space=pltpu.SMEM),
            by_source(chunk, pair.shape),
            resident(embed.shape),
            resident(time_weight.shape),
            resident(shift_weight.shape),
            resident(inlet.shape),
            resident(kernel_one.shape),
            resident(small.shape),
        ],
        out_specs=[per_chunk(chunk, *s[1:]) for s in shapes] + [resident((n, deep))] * 4,
        out_shape=[jax.ShapeDtypeStruct(s, jnp.float32) for s in shapes]
        + [jax.ShapeDtypeStruct((n, deep), kind) for kind in whole],
        scratch_shapes=[
            pltpu.VMEM((chunk, 288, 768), jnp.bfloat16),
            pltpu.VMEM((n, 256), jnp.float32),
        ],
        compiler_params=pltpu.CompilerParams(vmem_limit_bytes=VMEM_LIMIT),
        cost_estimate=pl.CostEstimate(
            flops=2 * n * 256 * 256 * 2400, bytes_accessed=n * 1 << 19, transcendentals=n * 1 << 16
        ),
        name="forward_part",
    )(mix, pair, embed, time_weight, shift_weight, inlet, kernel_one, small)


def main_part(chunk, sizes, coef, start, inner, stats, noisy, target, keep, weights, small, bias_qkv, times):
    n = noisy.shape[0]
    batch, shard_rows, tall, short, rest_rows = sizes
    outs = [(batch, shard_rows, 256), (rest_rows, 256)]
    sums = [(3, 256, 768), (3, 256, 768), (256, 768), (256, 256), (80, 256), (80, 256), (16, 256), (8, 256)]
    return pl.pallas_call(
        functools.partial(second_kernel, tall, short),
        grid=(n // chunk,),
        in_specs=[
            pl.BlockSpec(memory_space=pltpu.SMEM),
            per_chunk(chunk, 256, 256),
            per_chunk(chunk, 256, 256),
            per_chunk(chunk, 8, 256),
            per_chunk(chunk, 8, 256),
            per_chunk(chunk, 8, 256),
            by_source(chunk, keep.shape),
        ]
        + [resident(w.shape) for w in weights]
        + [resident(small.shape), resident(bias_qkv.shape)]
        + [resident(t.shape) for t in times],
        out_specs=[resident(g) for g in outs],
        out_shape=[jax.ShapeDtypeStruct(g, jnp.float32) for g in outs],
        scratch_shapes=[pltpu.VMEM(g, jnp.float32) for g in sums + [(n, 256)]]
        + [pltpu.VMEM((chunk, 288, 768), jnp.bfloat16)] * 2,
        compiler_params=pltpu.CompilerParams(vmem_limit_bytes=VMEM_LIMIT),
        cost_estimate=pl.CostEstimate(
            flops=70 * n * 2 * 256**3, bytes_accessed=n * 5 << 17, transcendentals=n * 5 << 16
        ),
        name="main_part",
    )(coef, start, inner, stats, noisy, target, keep, *weights, small, bias_qkv, *times)


def rows_first(weight):
    inputs, outputs = weight.shape[0] // 9, weight.shape[1]
    flipped = jnp.transpose(weight.reshape(9, inputs, outputs)[::-1], (0, 2, 1))
    return flipped.reshape(9 * outputs, inputs)


def padded_taps(rows):
    padded = jnp.pad(rows.reshape(9, 3, 256), ((0, 1), (0, 5), (0, 0)))
    return padded.reshape(80, 256)


MESH = pl.DeviceIdType.MESH
MISC_ROWS = (640, 640, 512, 80, 80, 24, 8)
MISC_TOTAL = 2048
SPLIT_A = 11
SPLIT_B = 4
LAG = 3


def padded_rows(total, parts):
    return -(-total // (8 * parts)) * 8


def factors(rows):
    low = max(d for d in range(1, rows + 1) if rows % d == 0 and d * d <= rows)
    return low, rows // low


def exchange_kernel(
    shard_shape,
    rates,
    grads_a,
    grads_b,
    state_kernel,
    state_attention,
    weight_kernel,
    weight_attention,
    scalars,
    out_a,
    out_b,
    shard_grad,
    norm_out,
    own_a,
    own_b,
    half_a,
    half_b,
    near_a,
    near_b,
    far_a,
    far_b,
    deep_a,
    deep_b,
    piece_a,
    piece_b,
    shard_weight,
    shard_first,
    shard_second,
    square_core,
    square_rows,
    square_deep,
    local_sem,
    own_sem,
    core_send,
    core_recv,
    near_send,
    near_recv,
    far_send,
    far_recv,
    deep_send,
    deep_recv,
    shard_send,
    shard_recv,
    square_send,
    square_recv,
    deep_send_two,
    deep_recv_two,
    near_send_two,
    near_recv_two,
    far_send_two,
    far_recv_two,
    core_send_two,
    core_recv_two,
    keep_sem,
):
    depth, _, tops, wide, piece, _ = grads_a.shape
    lanes = grads_b.shape[4]
    rows = tops * wide
    pairs, tall, quads, short = shard_shape
    batch, r = lax.axis_index("batch"), lax.axis_index("rows")
    z, c = batch // 2, batch % 2
    y, x = r // wide, r % wide
    partner = z * 2 + (1 - c)
    row_peers = [(r + d) % rows for d in range(1, rows)]
    deep_peers = [(z + d) % depth for d in range(1, depth)]
    x_peers = [(x + d) % wide for d in range(1, wide)]
    y_peers = [(y + d) % tops for d in range(1, tops)]

    def remote(src, dst, send, recv, where):
        return pltpu.make_async_remote_copy(
            src_ref=src, dst_ref=dst, send_sem=send, recv_sem=recv, device_id=where, device_id_type=MESH
        )

    def begin(copies):
        for copy in copies:
            copy.start()
        return copies

    def arrived(copies):
        for copy in copies:
            copy.wait_recv()

    def blocks(kernel_ref, attention_ref, flat, base, offset):
        copies = []
        for k in range(pairs + quads):
            ref, own, size = (kernel_ref, k, tall) if k < pairs else (attention_ref, k - pairs, short)
            at = k * tall if k < pairs else pairs * tall + own * short
            far = ref.at[own] if offset is None else ref.at[own, pl.ds(offset * size, size)]
            near = flat.at[pl.ds(at, size)]
            copies.append(pltpu.make_async_copy(far, near, local_sem.at[base * (pairs + quads) + k]))
        return begin(copies)

    owns = begin(
        [
            pltpu.make_async_copy(grads_b.at[:, c], own_b, own_sem.at[0]),
            pltpu.make_async_copy(grads_a.at[:, c], own_a, own_sem.at[1]),
        ]
    )

    barrier = pltpu.get_barrier_semaphore()
    pl.semaphore_signal(barrier, inc=1, device_id=(partner, r), device_id_type=MESH)
    for peer in row_peers:
        pl.semaphore_signal(barrier, inc=1, device_id=(batch, peer), device_id_type=MESH)
    for peer in deep_peers:
        pl.semaphore_signal(barrier, inc=1, device_id=(peer * 2 + c, r), device_id_type=MESH)
    pl.semaphore_wait(barrier, rows + depth - 1)

    set_a = (grads_a, own_a, half_a, near_a, far_a, deep_a, piece_a, out_a)
    set_b = (grads_b, own_b, half_b, near_b, far_b, deep_b, piece_b, out_b)
    chunks = []
    for group, height, parts in ((set_b, lanes, SPLIT_B), (set_a, piece, SPLIT_A)):
        marks = [height // 8 * k // parts * 8 for k in range(parts + 1)]
        for low, high in zip(marks[:-1], marks[1:]):
            if high > low:
                chunks.append(group + (low, high - low, len(chunks) % 2 == 0))
    count = len(chunks)
    small = sum(1 for chunk in chunks if chunk[0] is grads_b)

    core_copies = []
    for k, (grads, _, half, _, _, _, _, _, at, size, _) in enumerate(chunks):
        span = pl.ds(at, size)
        core_copies.append(
            begin(
                [
                    remote(
                        grads.at[:, 1 - c, :, :, span],
                        half.at[:, :, :, span],
                        core_send.at[k],
                        core_recv.at[k],
                        (partner, r),
                    )
                ]
            )
        )
    fetches = (
        blocks(weight_kernel, weight_attention, shard_weight, 0, batch)
        + blocks(state_kernel.at[0], state_attention.at[0], shard_first, 1, None)
        + blocks(state_kernel.at[1], state_attention.at[1], shard_second, 2, None)
    )
    near_copies, far_copies, deep_copies = [], [], []

    def sum_near(k):
        _, own, half, near, _, _, _, _, at, size, x_first = chunks[k]
        if k == 0:
            owns[0].wait()
        if k == small:
            owns[1].wait()
        arrived(core_copies[k])
        span = pl.ds(at, size)

        def add_own(t, carry):
            i, j, l = t // rows, t // wide % tops, t % wide
            half[i, j, l, span] = half[i, j, l, span] + own[i, j, l, span]
            return carry

        lax.fori_loop(0, depth * rows, add_own, 0)
        copies = []
        for d, peer in enumerate(x_peers if x_first else y_peers):
            src = half.at[:, :, peer, span] if x_first else half.at[:, peer, :, span]
            dst = near.at[d, :, pl.ds(0, tops if x_first else wide), span]
            where = (batch, y * wide + peer) if x_first else (batch, peer * wide + x)
            copies.append(remote(src, dst, near_send.at[k, d], near_recv.at[k, d], where))
        near_copies.append(begin(copies))

    def sum_far(k):
        _, _, half, near, far, _, _, _, at, size, x_first = chunks[k]
        arrived(near_copies[k])
        span = pl.ds(at, size)
        across = tops if x_first else wide

        def add_near(t, carry):
            i, j = t // across, t % across
            place = (i, j, x) if x_first else (i, y, j)
            total = half[place + (span,)]
            for d in range((wide if x_first else tops) - 1):
                total = total + near[d, i, j, span]
            half[place + (span,)] = total
            return carry

        lax.fori_loop(0, depth * across, add_near, 0)
        copies = []
        for d, peer in enumerate(y_peers if x_first else x_peers):
            src = half.at[:, peer, x, span] if x_first else half.at[:, y, peer, span]
            where = (batch, peer * wide + x) if x_first else (batch, y * wide + peer)
            copies.append(
                remote(src, far.at[d, :, span], far_send.at[k, d], far_recv.at[k, d], where)
            )
        far_copies.append(begin(copies))

    def sum_deep(k):
        _, _, half, _, far, deep, _, _, at, size, x_first = chunks[k]
        arrived(far_copies[k])
        span = pl.ds(at, size)

        def add_far(i, carry):
            total = half[i, y, x, span]
            for d in range((tops if x_first else wide) - 1):
                total = total + far[d, i, span]
            half[i, y, x, span] = total
            return carry

        lax.fori_loop(0, depth, add_far, 0)
        copies = []
        for d, peer in enumerate(deep_peers):
            copies.append(
                remote(
                    half.at[peer, y, x, span],
                    deep.at[d, span],
                    deep_send.at[k, d],
                    deep_recv.at[k, d],
                    (peer * 2 + c, r),
                )
            )
        deep_copies.append(begin(copies))

    def finish_sum(k):
        _, _, half, _, _, deep, _, _, at, size, _ = chunks[k]
        arrived(deep_copies[k])
        span = pl.ds(at, size)
        total = half[z, y, x, span]
        for d in range(depth - 1):
            total = total + deep[d, span]
        return total

    def squares(values):
        return jnp.sum((values * values).reshape(-1, 8, 256), axis=0)

    def gather_deep(k):
        _, _, _, _, _, _, part, out, at, size, _ = chunks[k]
        span = pl.ds(at, size)
        keep = pltpu.make_async_copy(part.at[span], out.at[z, c, y, x, span], keep_sem.at[k])
        keep.start()
        copies = []
        for d, peer in enumerate(deep_peers):
            copies.append(
                remote(
                    part.at[span],
                    out.at[z, c, y, x, span],
                    deep_send_two.at[k, d],
                    deep_recv_two.at[k, d],
                    (peer * 2 + c, r),
                )
            )
        return keep, begin(copies)

    def gather_near(k):
        _, _, _, _, _, _, _, out, at, size, x_first = chunks[k]
        place = out.at[:, c, y, x, pl.ds(at, size)]
        copies = []
        for d, peer in enumerate(y_peers if x_first else x_peers):
            where = (batch, peer * wide + x) if x_first else (batch, y * wide + peer)
            copies.append(remote(place, place, near_send_two.at[k, d], near_recv_two.at[k, d], where))
        return begin(copies)

    def gather_far(k):
        _, _, _, _, _, _, _, out, at, size, x_first = chunks[k]
        span = pl.ds(at, size)
        place = out.at[:, c, :, x, span] if x_first else out.at[:, c, y, :, span]
        copies = []
        for d, peer in enumerate(x_peers if x_first else y_peers):
            where = (batch, y * wide + peer) if x_first else (batch, peer * wide + x)
            copies.append(remote(place, place, far_send_two.at[k, d], far_recv_two.at[k, d], where))
        return begin(copies)

    def gather_core(k):
        _, _, _, _, _, _, _, out, at, size, _ = chunks[k]
        place = out.at[:, c, :, :, pl.ds(at, size)]
        return begin([remote(place, place, core_send_two.at[k], core_recv_two.at[k], (partner, r))])

    keeps, firsts, seconds, thirds, lasts = [], [], [], [], []
    partial = []

    def send_deep(k):
        keep, copies = gather_deep(k)
        keeps.append(keep)
        firsts.append(copies)

    def send_near(k):
        keeps[k].wait()
        arrived(firsts[k])
        seconds.append(gather_near(k))

    def send_far(k):
        arrived(seconds[k])
        thirds.append(gather_far(k))

    def send_core(k):
        arrived(thirds[k])
        lasts.append(gather_core(k))

    def sum_last(k):
        total = finish_sum(k)
        at, size = chunks[k][8], chunks[k][9]
        counted = total
        if k < small:
            piece_b[pl.ds(at, size)] = total
            line = (batch * rows + r) * lanes + at + lax.broadcasted_iota(jnp.int32, total.shape, 0)
            counted = jnp.where(line < sum(MISC_ROWS[:-1]), total, 0.0)
            send_deep(k)
        else:
            shard_grad[r, pl.ds(at, size)] = total
        partial.append(squares(counted))

    for t in range(count + 3 * LAG):
        for stage, lag in ((sum_near, 0), (sum_far, LAG), (sum_deep, 2 * LAG), (sum_last, 3 * LAG)):
            if 0 <= t - lag < count:
                stage(t - lag)
    square = sum(partial)
    square_core[0] = square
    square_copies = begin(
        [remote(square_core.at[0], square_core.at[1], square_send.at[0], square_recv.at[0], (partner, r))]
    )
    shard_copies = begin(
        [
            remote(shard_grad.at[r], shard_grad.at[r], shard_send.at[d], shard_recv.at[d], (batch, peer))
            for d, peer in enumerate(row_peers)
        ]
    )
    arrived(square_copies)
    square_rows[r] = square_core[0] + square_core[1]
    copies = begin(
        [
            remote(
                square_rows.at[r],
                square_rows.at[r],
                square_send.at[1 + d],
                square_recv.at[1 + d],
                (batch, peer),
            )
            for d, peer in enumerate(row_peers)
        ]
    )
    for k in range(small):
        send_near(k)
    arrived(copies)
    square_copies += copies
    square_deep[z] = sum(square_rows[j] for j in range(rows))
    copies = begin(
        [
            remote(
                square_deep.at[z],
                square_deep.at[z],
                square_send.at[rows + d],
                square_recv.at[rows + d],
                (peer * 2 + c, r),
            )
            for d, peer in enumerate(deep_peers)
        ]
    )
    for fetch in fetches:
        fetch.wait()
    for k in range(small):
        send_far(k)
    arrived(copies)
    square_copies += copies
    square = sum(square_deep[j] for j in range(depth))
    norm = jnp.sqrt(jnp.sum(jnp.sum(square, axis=0, keepdims=True), axis=1, keepdims=True))
    clip = CLIP / jnp.maximum(norm, CLIP)
    norm_out[...] = jnp.broadcast_to(norm, norm_out.shape)
    for k in range(small, count):
        at, size = chunks[k][8], chunks[k][9]
        span = pl.ds(pl.multiple_of(r * piece + at, 8), size)
        g = shard_grad[r, pl.ds(at, size)] * clip
        first = BETA_ONE * shard_first[span] + (1.0 - BETA_ONE) * g
        second = BETA_TWO * shard_second[span] + (1.0 - BETA_TWO) * g * g
        line = r * piece + at + lax.broadcasted_iota(jnp.int32, g.shape, 0)
        rate = jnp.where(line < pairs * tall, rates[0], rates[1])
        weight = shard_weight[span]
        step = first * scalars[0] / (jnp.sqrt(second * scalars[1]) + EPS_ADAM)
        piece_a[pl.ds(at, size)] = weight - rate * (step + DECAY * weight)
        send_deep(k)
    for k in range(small):
        send_core(k)
    for t in range(small, count + 2 * LAG):
        for stage, lag in ((send_near, 0), (send_far, LAG), (send_core, 2 * LAG)):
            if small <= t - lag < count:
                stage(t - lag)
    arrived(shard_copies)
    for copies in lasts:
        arrived(copies)
    for copies in (
        core_copies + near_copies + far_copies + deep_copies + firsts + seconds + thirds + lasts
    ):
        for copy in copies:
            copy.wait_send()
    for copy in square_copies + shard_copies:
        copy.wait_send()


def exchange(grads_a, grads_b, state_kernel, state_attention, weight_kernel, weight_attention, scalars):
    depth, _, rows, piece, width = grads_a.shape
    tops, wide = factors(rows)
    lanes = grads_b.shape[3]
    grads_a = grads_a.reshape(depth, 2, tops, wide, piece, width)
    grads_b = grads_b.reshape(depth, 2, tops, wide, lanes, width)
    pairs, tall = state_kernel.shape[1:3]
    quads, short = state_attention.shape[1:3]
    shape = functools.partial(jax.ShapeDtypeStruct, dtype=jnp.float32)
    whole = pl.BlockSpec(memory_space=pltpu.VMEM)
    anywhere = pl.BlockSpec(memory_space=pl.ANY)
    dma = pltpu.SemaphoreType.DMA
    vmem = functools.partial(pltpu.VMEM, dtype=jnp.float32)
    most = max(tops, wide)
    return pl.pallas_call(
        functools.partial(exchange_kernel, (pairs, tall, quads, short), (RATES[1], RATES[2])),
        in_specs=[anywhere] * 6 + [pl.BlockSpec(memory_space=pltpu.SMEM)],
        out_specs=[anywhere] * 2 + [whole] * 2,
        out_shape=[
            shape(grads_a.shape),
            shape(grads_b.shape),
            shape((rows, piece, width)),
            shape((8, 128)),
        ],
        scratch_shapes=[
            vmem((depth, tops, wide, piece, width)),
            vmem((depth, tops, wide, lanes, width)),
            vmem((depth, tops, wide, piece, width)),
            vmem((depth, tops, wide, lanes, width)),
            vmem((most - 1, depth, most, piece, width)),
            vmem((most - 1, depth, most, lanes, width)),
            vmem((most - 1, depth, piece, width)),
            vmem((most - 1, depth, lanes, width)),
            vmem((depth - 1, piece, width)),
            vmem((depth - 1, lanes, width)),
            vmem((piece, width)),
            vmem((lanes, width)),
            vmem((rows * piece, width)),
            vmem((rows * piece, width)),
            vmem((rows * piece, width)),
            vmem((2, 8, width)),
            vmem((rows, 8, width)),
            vmem((depth, 8, width)),
            dma((3 * (pairs + quads),)),
            dma((2,)),
            dma((SPLIT_A + SPLIT_B,)),
            dma((SPLIT_A + SPLIT_B,)),
            dma((SPLIT_A + SPLIT_B, most - 1)),
            dma((SPLIT_A + SPLIT_B, most - 1)),
            dma((SPLIT_A + SPLIT_B, most - 1)),
            dma((SPLIT_A + SPLIT_B, most - 1)),
            dma((SPLIT_A + SPLIT_B, depth - 1)),
            dma((SPLIT_A + SPLIT_B, depth - 1)),
            dma((rows - 1,)),
            dma((rows - 1,)),
            dma((rows + depth - 1,)),
            dma((rows + depth - 1,)),
            dma((SPLIT_A + SPLIT_B, depth - 1)),
            dma((SPLIT_A + SPLIT_B, depth - 1)),
            dma((SPLIT_A + SPLIT_B, most - 1)),
            dma((SPLIT_A + SPLIT_B, most - 1)),
            dma((SPLIT_A + SPLIT_B, most - 1)),
            dma((SPLIT_A + SPLIT_B, most - 1)),
            dma((SPLIT_A + SPLIT_B,)),
            dma((SPLIT_A + SPLIT_B,)),
            dma((SPLIT_A + SPLIT_B,)),
        ],
        compiler_params=pltpu.CompilerParams(
            collective_id=0, has_side_effects=True, vmem_limit_bytes=VMEM_LIMIT
        ),
        name="exchange",
    )(grads_a, grads_b, state_kernel, state_attention, weight_kernel, weight_attention, scalars)


def finish_kernel(
    scalars,
    norm_tile,
    fresh,
    average_kernel,
    average_attention,
    shard_grad,
    state_kernel,
    state_attention,
    time_left,
    time_right,
    shift_rows,
    rest_rows,
    *refs,
):
    weights, states, averages, refs = refs[:5], refs[5:10], refs[10:15], refs[15:]
    (kernel_out, attention_out), refs = refs[:2], refs[2:]
    updated, firsts, seconds, refs = refs[:5], refs[5:10], refs[10:15], refs[15:]
    first_kernel_out, first_attention_out, second_kernel_out, second_attention_out, loss_out, norm_out = refs
    norm = norm_tile[0:1, 0:1]
    clip = CLIP / jnp.maximum(norm, CLIP)
    kept = scalars[2]

    def averaged(out, index, new, average):
        out[(0,) + index] = new
        out[(1,) + index] = kept * average + (1.0 - kept) * new

    tall, short = state_kernel.shape[2], state_attention.shape[2]
    for k in range(2):
        averaged(kernel_out, (k,), fresh[0, k * tall : k * tall + tall], average_kernel[k])
    for k in range(4):
        at = 2 * tall + k * short
        averaged(attention_out, (k,), fresh[0, at : at + short], average_attention[k])

    def moments(first, second, g):
        return BETA_ONE * first + (1.0 - BETA_ONE) * g, BETA_TWO * second + (1.0 - BETA_TWO) * g * g

    def update(k, rate, grad):
        weight = weights[k][...]
        old = (states[k][0], states[k][1]) if k < 2 else (states[k][:, 0, :], states[k][:, 1, :])
        first, second = moments(*old, grad * clip)
        firsts[k][...] = first
        seconds[k][...] = second
        step = first * scalars[0] / (jnp.sqrt(second * scalars[1]) + EPS_ADAM)
        new = weight - rate * (step + DECAY * weight)
        if k < 2:
            averaged(updated[k], (), new, averages[k][...])
        else:
            updated[k][:, 0, :] = new
            updated[k][:, 1, :] = kept * averages[k][...] + (1.0 - kept) * new

    update(0, RATES[3], jnp.concatenate([time_left[...], time_right[...]], axis=1))
    update(1, RATES[4], shift_rows[...])

    @pl.when(pl.program_id(0) == 0)
    def _():
        for refs, outs, count, height in (
            (state_kernel, (first_kernel_out, second_kernel_out), 2, tall),
            (state_attention, (first_attention_out, second_attention_out), 4, short),
        ):
            for k in range(count):
                at = k * height + (0 if count == 2 else 2 * tall)
                first, second = moments(refs[0, k], refs[1, k], shard_grad[at : at + height] * clip)
                outs[0][k] = first
                outs[1][k] = second
        inlet = jnp.concatenate([rest_rows[8 * tap : 8 * tap + 3] for tap in range(9)], axis=0)
        outlet = jnp.concatenate([rest_rows[80 + 8 * tap : 83 + 8 * tap] for tap in range(9)], axis=1)
        update(2, RATES[0], inlet)
        update(3, RATES[5], outlet)
        update(4, RATES[6], rest_rows[160:179])
        loss_out[...] = jnp.sum(col_sum(rest_rows[184:192]), axis=1, keepdims=True)
        norm_out[...] = norm


def finish(scalars, norm_tile, fresh, average_kernel, average_attention, shard_grad, state_kernel, state_attention, rest, weights, states, averages):
    batch, shard_rows, width = fresh.shape
    tall, short = state_kernel.shape[2], state_attention.shape[2]
    (time_rows, time_width), (shift_rows, _) = weights[0].shape, weights[1].shape
    time_part, shift_part = time_rows // batch, shift_rows // batch
    shape = functools.partial(jax.ShapeDtypeStruct, dtype=jnp.float32)

    def at(block, index):
        return pl.BlockSpec(block, index)

    def rows_of(k, lead):
        part, wide = ((time_part, time_width), (shift_part, width))[k]
        return pl.BlockSpec(lead + (part, wide), lambda b: (0,) * len(lead) + (b, 0))

    def five(lead):
        small = [w.shape[:1] + lead + w.shape[1:] for w in weights[2:]]
        return [rows_of(0, lead), rows_of(1, lead)] + [resident(block) for block in small]

    shift_at = 2 * time_rows // shift_part
    rest_at = (2 * time_rows + shift_rows) // 256
    return pl.pallas_call(
        finish_kernel,
        grid=(batch,),
        in_specs=[
            pl.BlockSpec(memory_space=pltpu.SMEM),
            resident(norm_tile.shape),
            at((1, shard_rows, width), lambda b: (b, 0, 0)),
            at((2, tall, width), lambda b: (0, b, 0)),
            at((4, short, width), lambda b: (0, b, 0)),
            resident(shard_grad.shape),
            resident(state_kernel.shape),
            resident(state_attention.shape),
            at((time_part, width), lambda b: (b, 0)),
            at((time_part, width), lambda b: (batch + b, 0)),
            at((shift_part, width), lambda b: (shift_at + b, 0)),
            pl.BlockSpec((256, width), lambda b: (rest_at, 0), pipeline_mode=pl.Buffered(1)),
        ]
        + five(())
        + five((2,))
        + five(()),
        out_specs=[
            at((2, 2, tall, width), lambda b: (0, 0, b, 0)),
            at((2, 4, short, width), lambda b: (0, 0, b, 0)),
        ]
        + five((2,))
        + five(())
        + five(())
        + [resident(state_kernel.shape[1:]), resident(state_attention.shape[1:])] * 2
        + [resident((1, 1))] * 2,
        out_shape=[
            shape((2, 2, batch * tall, width)),
            shape((2, 4, batch * short, width)),
        ]
        + [shape((2,) + w.shape) for w in weights[:2]]
        + [shape((w.shape[0], 2, w.shape[1])) for w in weights[2:]]
        + [shape(w.shape) for w in weights] * 2
        + [shape(state_kernel.shape[1:]), shape(state_attention.shape[1:])] * 2
        + [shape((1, 1))] * 2,
        compiler_params=pltpu.CompilerParams(vmem_limit_bytes=VMEM_LIMIT),
        cost_estimate=pl.CostEstimate(flops=40 << 20, bytes_accessed=36 << 20, transcendentals=1 << 20),
        name="finish",
    )(
        scalars,
        norm_tile,
        fresh,
        average_kernel,
        average_attention,
        shard_grad,
        state_kernel,
        state_attention,
        rest,
        rest,
        rest,
        rest,
        *weights,
        *states,
        *averages,
    )


def local(
    x_clean,
    noise,
    timesteps,
    keep_mask,
    adam_step,
    inlet_weight,
    kernel_weight,
    attention_weight,
    time_weight,
    shift_weight,
    outlet_weight,
    small_params,
    state_inlet,
    state_kernel,
    state_attention,
    state_time,
    state_shift,
    state_outlet,
    state_small,
    average_inlet,
    average_kernel,
    average_attention,
    average_time,
    average_shift,
    average_outlet,
    average_small,
):
    chans = kernel_weight.shape[2]
    width_sin = time_weight.shape[0] - time_weight.shape[1]
    rows, batch = lax.axis_size("rows"), lax.axis_size("batch")
    own = timesteps.shape[0] // rows
    keep = keep_mask.reshape(rows, own, -1, chans).astype(jnp.bfloat16)
    keep, timesteps, x_clean, noise = lax.optimization_barrier((keep, timesteps, x_clean, noise))
    keep = lax.all_to_all(keep, "rows", 0, 0, tiled=True)
    halves = [a.reshape(rows, own, 3, -1) for a in (x_clean, noise)]
    pair = jnp.pad(jnp.concatenate(halves, axis=3), ((0, 0), (0, 0), (0, 1), (0, 0)))
    here = lax.axis_index("rows")
    parts = [lax.dynamic_index_in_dim(pair, here, 0, keepdims=False)]
    for d in range(1, rows):
        block = lax.dynamic_index_in_dim(pair, (here + d) % rows, 0, keepdims=False)
        parts.append(lax.ppermute(block, "rows", [(i, (i + d) % rows) for i in range(rows)]))
    steps = ((here - jnp.arange(rows)) % rows)[:, None, None, None]
    pair = jnp.broadcast_to(parts[0], (rows,) + parts[0].shape)
    for d in range(1, rows):
        pair = jnp.where(steps == d, parts[d], pair)
    pair, inlet_low, kernels, projections, outlet_low = lax.optimization_barrier(
        (pair, inlet_weight, kernel_weight, attention_weight, outlet_weight)
    )
    timesteps = lax.dynamic_slice_in_dim(timesteps, lax.axis_index("rows") * own, own, 0)
    bars = alpha_bars(timesteps)
    mix = jnp.stack([jnp.sqrt(bars), jnp.sqrt(1.0 - bars)])
    kernels = kernels.astype(jnp.bfloat16)
    projections = projections.astype(jnp.bfloat16)
    inlet = padded_taps(inlet_low).astype(jnp.bfloat16)
    outlet = padded_taps(
        jnp.transpose(outlet_low.reshape(3, 9, chans), (1, 0, 2)).reshape(27, chans)
    ).astype(jnp.bfloat16)
    qkv = jnp.concatenate([projections[0], projections[1], projections[2]], axis=1)
    embed = sinusoid(timesteps, width_sin).astype(jnp.bfloat16)
    ratio = bars / (1.0 - bars)
    snr_weight = jnp.minimum(ratio, GAMMA) / ratio
    denom = 3 * 256 * own * rows * batch
    coef = 2.0 * snr_weight / denom
    start, inner, stats, noisy, target, hidden, hidden_slope, time_act, time_slope = forward_part(
        FORWARD_CHUNK, mix, pair, embed, time_weight, shift_weight, inlet, kernels[0], small_params
    )
    bias_qkv = jnp.concatenate(
        [small_params[11], jnp.zeros_like(small_params[0]), small_params[12]]
    )
    tall, short = state_kernel.shape[2], state_attention.shape[2]
    shard_rows = rows * padded_rows(2 * tall + 4 * short, rows)
    lanes = padded_rows(MISC_TOTAL, batch * rows)
    shards, rest = main_part(
        CHUNK,
        (batch, shard_rows, tall, short, batch * rows * lanes),
        coef,
        start,
        inner,
        stats,
        noisy,
        target,
        keep,
        (
            rows_first(kernels[0]),
            kernels[1],
            rows_first(kernels[1]),
            qkv,
            qkv.T,
            projections[3],
            projections[3].T,
            outlet,
        ),
        small_params,
        bias_qkv[None],
        (embed, hidden, hidden_slope, time_act, time_slope, time_weight, shift_weight),
    )
    count = adam_step[0].astype(jnp.float32)
    scalars = jnp.stack(
        [
            1.0 / (1.0 - BETA_ONE**count),
            1.0 / (1.0 - BETA_TWO**count),
            jnp.minimum(EMA_TOP, (1.0 + count) / (10.0 + count)),
        ]
    )
    fresh, rest, shard_grad, norm_tile = exchange(
        shards.reshape(batch // 2, 2, rows, shard_rows // rows, chans),
        rest.reshape(batch // 2, 2, rows, lanes, chans),
        state_kernel,
        state_attention,
        kernel_weight,
        attention_weight,
        scalars,
    )
    results = finish(
        scalars,
        norm_tile,
        fresh.reshape(batch, shard_rows, chans),
        lax.all_gather(average_kernel, "batch", axis=1, tiled=True),
        lax.all_gather(average_attention, "batch", axis=1, tiled=True),
        shard_grad.reshape(shard_rows, chans),
        state_kernel,
        state_attention,
        rest.reshape(-1, chans),
        (time_weight, shift_weight, inlet_weight, outlet_weight, small_params),
        (state_time, state_shift)
        + tuple(jnp.transpose(a, (1, 0, 2)) for a in (state_inlet, state_outlet, state_small)),
        (average_time, average_shift, average_inlet, average_outlet, average_small),
    )
    kernel_pair, attention_pair = results[:2]
    triples = [list(results[2 + 5 * k : 7 + 5 * k]) for k in range(3)]
    triples[0][2:] = [jnp.transpose(a, (1, 0, 2)) for a in triples[0][2:]]
    first_conv, first_attention, second_conv, second_attention, loss, norm = results[17:]
    ordered = []
    for (time, shift, inlet, outlet, small), middle in zip(
        triples,
        ((kernel_pair, attention_pair), (first_conv, first_attention), (second_conv, second_attention)),
    ):
        ordered += [inlet, *middle, time, shift, outlet, small]
    return (*ordered, loss.reshape(()), norm.reshape(()))


def solution(mesh):
    return jax.shard_map(
        local,
        mesh=mesh,
        in_specs=(
            P("batch", None, "rows", None),
            P("batch", None, "rows", None),
            P("batch"),
            P("batch", "rows", None, None),
            P(),
            P(),
            P(),
            P(),
            P(),
            P(),
            P(),
            P(),
            P(),
            P(None, None, "batch", None),
            P(None, None, "batch", None),
            P(),
            P(),
            P(),
            P(),
            P(),
            P(None, "batch", None),
            P(None, "batch", None),
            P(),
            P(),
            P(),
            P(),
        ),
        out_specs=(
            P(),
            P(),
            P(),
            P(),
            P(),
            P(),
            P(),
            P(),
            P(None, "batch", None),
            P(None, "batch", None),
            P(),
            P(),
            P(),
            P(),
            P(),
            P(None, "batch", None),
            P(None, "batch", None),
            P(),
            P(),
            P(),
            P(),
            P(),
            P(),
        ),
        check_vma=False,
    )
```

```python
import functools
import math

import jax
import jax.numpy as jnp
import numpy as np
from jax import lax
from jax.experimental import pallas as pl
from jax.experimental.pallas import tpu as pltpu
from jax.sharding import PartitionSpec as P

G = 32


CLIP = 0.05
GAMMA = 5.0
KEEP = 0.9
EPS_NORM = 1e-05
BETA_ONE = 0.9
BETA_TWO = 0.999
EPS_ADAM = 1e-08
DECAY = 0.01
EMA_TOP = 0.9999
VMEM_LIMIT = 60 << 20
CHUNK = 4
FORWARD_CHUNK = 8
GROUP = 2
COUNT = 2048.0
RATES = (0.1, 0.01, 0.03, 0.05, 0.02, 0.01, 0.2)


def bar_table():
    beta_rates = 0.0001 + (0.02 - 0.0001) * np.arange(1000, dtype=np.float64) / 999.0
    return np.exp(np.cumsum(np.log(1.0 - beta_rates))).astype(np.float32)


def alpha_bars(timesteps):
    one_hot = (timesteps[:, None] == jnp.arange(1000)[None, :]).astype(jnp.float32)
    return jnp.sum(one_hot * bar_table()[None, :], axis=1)


def sinusoid(timesteps, width):
    half = width // 2
    rates = jnp.exp(-math.log(10000.0) * jnp.arange(half).astype(jnp.float32) / (half - 1))
    angles = timesteps.astype(jnp.float32)[:, None] * rates[None, :]
    return jnp.concatenate([jnp.sin(angles), jnp.cos(angles)], axis=1)


def wrap(shift, size):
    return shift % size


def tap_masks():
    lane = lax.broadcasted_iota(jnp.int32, (8, 256), 1)
    row, col = lane // 16, lane % 16
    masks = []
    for i in range(3):
        for j in range(3):
            ok = (row + (i - 1) >= 0) & (row + (i - 1) < 16) & (col + (j - 1) >= 0) & (col + (j - 1) < 16)
            masks.append(ok)
    return masks


def tap_stack(tile, masks, sign):
    parts = []
    for tap in range(9):
        step = sign * (16 * (tap // 3 - 1) + tap % 3 - 1)
        moved = tile if step == 0 else pltpu.roll(tile, wrap(-step, 256), 1)
        parts.append(jnp.where(masks[tap if sign > 0 else 8 - tap], moved, 0.0))
    parts.append(jnp.zeros_like(tile))
    return jnp.concatenate(parts, axis=0).astype(jnp.bfloat16)


def group_sum(rows):
    halves = []
    for half in range(2):
        part = rows[:, 128 * half : 128 * half + 128]
        lane = lax.broadcasted_iota(jnp.int32, part.shape, 1)
        for step in (1, 2, 4):
            upper = (lane // step) % 2 == 1
            part = part + jnp.where(upper, pltpu.roll(part, step, 1), pltpu.roll(part, 128 - step, 1))
        halves.append(part)
    return jnp.concatenate(halves, axis=1)


def col_sum(x):
    return jnp.sum(x, axis=0, keepdims=True)


def stats_of(fields):
    sums = jnp.concatenate([col_sum(x) for x in fields] + [col_sum(x * x) for x in fields], axis=0)
    both = group_sum(sums) / COUNT
    n = len(fields)
    mean = both[:n]
    spread = both[n:] - mean * mean
    return mean, lax.rsqrt(spread + EPS_NORM)


def logistic(z):
    return 0.5 * jnp.tanh(0.5 * z) + 0.5


def put_shifted(buf, c, y, not_first, not_last):
    buf[c, 16:272, 256:512] = y.astype(jnp.bfloat16)
    buf[c, 16:272, 0:256] = jnp.where(not_first, pltpu.roll(y, 1, 0), 0.0).astype(jnp.bfloat16)
    buf[c, 16:272, 512:768] = jnp.where(not_last, pltpu.roll(y, 255, 0), 0.0).astype(jnp.bfloat16)


def edge_masks():
    col = lax.broadcasted_iota(jnp.int32, (256, 256), 0) % 16
    return col != 0, col != 15


def stacked(buf, i):
    chunk = buf.shape[0]
    return buf[:, 16 * i : 16 * i + 256, :].reshape(chunk * 256, 768)


def dot(a, b, dims=((1,), (0,))):
    return lax.dot_general(a, b, (dims, ((), ())), preferred_element_type=jnp.float32)


NT = ((1,), (1,))
TN = ((0,), (0,))


def conv_shifted(buf, weight):
    field = jnp.concatenate([stacked(buf, i) for i in range(3)], axis=1)
    return dot(field, weight[...])


def zero_edges(buf):
    edge = jnp.zeros((buf.shape[0], 16, 768), jnp.bfloat16)
    buf[:, 0:16, :] = edge
    buf[:, 272:288, :] = edge


def take_turns(workers):
    live, started = [], 0
    while live or started < len(workers):
        if started < len(workers):
            live.append(workers[started])
            started += 1
        live = [w for w in live if next(w, live) is not live]


def lanes_joined(blocks):
    return blocks[0] if len(blocks) == 1 else jnp.concatenate(blocks, axis=1)


def first_kernel(
    mix,
    pair,
    embed,
    time_weight,
    shift_weight,
    inlet,
    kernel_one,
    small,
    start_out,
    inner_out,
    stats_out,
    noisy_out,
    target_out,
    hidden_out,
    hidden_slope_out,
    time_act_out,
    time_slope_out,
    buf,
    tshift,
):
    chunk = start_out.shape[0]
    step = pl.program_id(0)

    @pl.when(step == 0)
    def _():
        zero_edges(buf)
        width = embed.shape[1]

        def layer(x, weight, at):
            bias = jnp.concatenate([small[at : at + 1], small[at + 1 : at + 2]], axis=1)
            z = dot(x, weight.astype(jnp.bfloat16)) + bias
            s = logistic(z)
            return (z * s).astype(jnp.bfloat16), s * (1.0 + z * (1.0 - s))

        hidden, hidden_slope = layer(embed[...], time_weight[0:width, :], 15)
        time_act, time_slope = layer(hidden, time_weight[width:, :], 17)
        hidden_out[...] = hidden
        hidden_slope_out[...] = hidden_slope
        time_act_out[...] = time_act
        time_slope_out[...] = time_slope
        both = small[14:15] + small[9:10]
        tshift[...] = dot(time_act, shift_weight[...].astype(jnp.bfloat16)) + both

    masks = tap_masks()
    not_first, not_last = edge_masks()
    part = pair.shape[3] // 2
    blank = jnp.zeros((4, 256), jnp.float32)

    def work(images):
        n = len(images)
        every = range(n)
        low, high = images[0], images[-1] + 1
        starts = []
        for c in images:
            tiles = [pair[s, c] for s in range(pair.shape[0])]
            clean = jnp.concatenate([lanes_joined([t[:, :part] for t in tiles]), blank], axis=0)
            noise = jnp.concatenate([lanes_joined([t[:, part:] for t in tiles]), blank], axis=0)
            noisy = mix[0, step * chunk + c] * clean + mix[1, step * chunk + c] * noise
            noisy = noisy.astype(jnp.bfloat16).astype(jnp.float32)
            noisy_out[c] = noisy
            target_out[c] = noise
            start = dot(tap_stack(noisy, masks, 1), inlet[...], TN) + small[8:9]
            start_out[c] = start
            starts.append(start)
        yield
        mean, rstd = stats_of(starts)
        for i, c in enumerate(images):
            scale = rstd[i : i + 1] * small[0:1]
            z = starts[i] * scale + (small[4:5] - mean[i : i + 1] * scale)
            put_shifted(buf, c, z * logistic(z), not_first, not_last)
        yield
        inner_all = conv_shifted(buf.at[low:high], kernel_one)
        yield
        inners = []
        for i, c in enumerate(images):
            inner = inner_all[256 * i : 256 * i + 256] + tshift[pl.ds(step * chunk + c, 1), :]
            inner_out[c] = inner
            inners.append(inner)
        mean_two, rstd_two = stats_of(inners)
        for i, c in enumerate(images):
            stats_out[c] = jnp.concatenate(
                [mean[i : i + 1], rstd[i : i + 1], mean_two[i : i + 1], rstd_two[i : i + 1]]
                + [jnp.zeros((4, 256), jnp.float32)],
                axis=0,
            )

    take_turns([work(list(range(g, g + GROUP))) for g in range(0, chunk, GROUP)])


def norm_grad(dys, fields, means, rstds, gain):
    n = len(dys)
    shift_sums, gain_sums = [], []
    for dy, x, mean, rstd in zip(dys, fields, means, rstds):
        shift_sums.append(col_sum(dy))
        gain_sums.append(col_sum(dy * (x * rstd - mean * rstd)))
    both = group_sum(jnp.concatenate(shift_sums + gain_sums, axis=0) * gain) / COUNT
    grads = []
    for c in range(n):
        rstd, mean = rstds[c], means[c]
        slope = -rstd * rstd * both[n + c : n + c + 1]
        base = -rstd * both[c : c + 1] - mean * slope
        grads.append(dys[c] * (rstd * gain) + (fields[c] * slope + base))
    return grads, sum(gain_sums), sum(shift_sums)


def second_kernel(
    tall,
    short,
    coef,
    start_in,
    inner_in,
    stats_in,
    noisy,
    target,
    keep,
    kernel_one_flip,
    kernel_two,
    kernel_two_flip,
    qkv,
    qkv_t,
    proj,
    proj_t,
    outlet,
    small,
    bias_qkv,
    embed,
    hidden,
    hidden_slope,
    time_act,
    time_slope,
    time_weight,
    shift_weight,
    shard_out,
    rest_out,
    grad_one_out,
    grad_two_out,
    grad_qkv_out,
    grad_proj_out,
    grad_outlet_out,
    grad_inlet_out,
    grad_small_out,
    loss_out,
    tshift_grad,
    buf,
    grad_buf,
):
    chunk = noisy.shape[0]
    step = pl.program_id(0)
    sums = (
        grad_one_out,
        grad_two_out,
        grad_qkv_out,
        grad_proj_out,
        grad_outlet_out,
        grad_inlet_out,
        grad_small_out,
        loss_out,
    )

    @pl.when(step == 0)
    def _():
        zero_edges(buf)
        zero_edges(grad_buf)
        for ref in sums:
            ref[...] = jnp.zeros(ref.shape, jnp.float32)

    masks = tap_masks()
    not_first, not_last = edge_masks()
    scale = 256 ** (-0.5)

    def gain(k):
        return small[k : k + 1]

    def shift(k):
        return small[4 + k : 5 + k]

    def normed(x, mean, rstd, k):
        slope = rstd * gain(k)
        return x * slope + (shift(k) - mean * slope)

    def row(values, c):
        return values[c : c + 1]

    def work(images):
        n = len(images)
        every = range(n)
        low, high = images[0], images[-1] + 1

        def part(x, c):
            return x[256 * c : 256 * c + 256]

        slope_two, act_two = [], []
        for c in images:
            z = normed(inner_in[c], stats_in[c, 2:3], stats_in[c, 3:4], 1)
            s = logistic(z)
            kept = jnp.concatenate([keep[s, c] for s in range(keep.shape[0])], axis=0)
            kept = kept.astype(jnp.float32) * (1.0 / KEEP)
            act = z * s * kept
            slope_two.append(s * (1.0 + z * (1.0 - s)) * kept)
            act_two.append(act.astype(jnp.bfloat16))
            put_shifted(buf, c, act, not_first, not_last)
        yield
        conv_two = conv_shifted(buf.at[low:high], kernel_two)
        yield
        middle = [start_in[c] + part(conv_two, i) + small[10:11] for i, c in enumerate(images)]
        mean, rstd = stats_of(middle)
        mean_three, rstd_three = [row(mean, i) for i in every], [row(rstd, i) for i in every]
        tokens = [
            normed(middle[i], mean_three[i], rstd_three[i], 2).astype(jnp.bfloat16) for i in every
        ]
        tokens = jnp.concatenate(tokens, axis=0)
        yield
        qkv_all = (dot(tokens, qkv[...]) + bias_qkv[0:1]).astype(jnp.bfloat16)
        triples = []
        for i in every:
            three = part(qkv_all, i)
            triples.append((three[:, 0:256], three[:, 256:512], three[:, 512:768]))
        scores = [dot(q, k, NT) for q, k, _ in triples]
        yield
        probs, probs_low = [], []
        for i in every:
            expo = jnp.exp((scores[i] - jnp.max(scores[i], axis=1, keepdims=True)) * scale)
            p = expo * (1.0 / jnp.sum(expo, axis=1, keepdims=True))
            probs.append(p)
            probs_low.append(p.astype(jnp.bfloat16))
        yield
        mixed = [dot(probs_low[i], triples[i][2]).astype(jnp.bfloat16) for i in every]
        mixed = jnp.concatenate(mixed, axis=0)
        branch = dot(mixed, proj[...])
        yield
        final = [middle[i] + part(branch, i) + small[13:14] for i in every]
        mean, rstd = stats_of(final)
        mean_four, rstd_four = [row(mean, i) for i in every], [row(rstd, i) for i in every]
        act_four, slope_four = [], []
        for i in every:
            z = normed(final[i], mean_four[i], rstd_four[i], 3)
            s = logistic(z)
            act_four.append((z * s).astype(jnp.bfloat16))
            slope_four.append(s * (1.0 + z * (1.0 - s)))
        yield
        taps_all = [dot(outlet[...], act, NT) for act in act_four]
        yield
        spreads = []
        loss_sum = 0.0
        for i, c in enumerate(images):
            predicted = 0.0
            for tap in range(9):
                move = 16 * (tap // 3 - 1) + tap % 3 - 1
                moved = taps_all[i][8 * tap : 8 * tap + 8]
                moved = moved if move == 0 else pltpu.roll(moved, wrap(-move, 256), 1)
                predicted = predicted + jnp.where(masks[tap], moved, 0.0)
            error = predicted - target[c]
            weight = coef[step * chunk + c]
            loss_sum = loss_sum + (0.5 * weight) * (error * error)
            grad_pred = (weight * error).astype(jnp.bfloat16).astype(jnp.float32)
            spreads.append(tap_stack(grad_pred, masks, -1))
        loss_out[...] += loss_sum
        yield
        grad_outlet_out[...] += sum(dot(s, act) for s, act in zip(spreads, act_four))
        grad_act = [dot(s, outlet[...], TN) for s in spreads]
        yield
        grad_four = [grad_act[i] * slope_four[i] for i in every]
        grad_final, gain_four, shift_four = norm_grad(grad_four, final, mean_four, rstd_four, gain(3))
        branch_all = jnp.concatenate([g.astype(jnp.bfloat16) for g in grad_final], axis=0)
        yield
        grad_proj_out[...] += dot(mixed, branch_all, TN)
        grad_mixed = dot(branch_all, proj_t[...]).astype(jnp.bfloat16)
        dps = [dot(part(grad_mixed, i), triples[i][2], NT) for i in every]
        dvs = [dot(probs_low[i], part(grad_mixed, i), TN) for i in every]
        yield
        dss = []
        for i in every:
            p, dp = probs[i], dps[i]
            dss.append((p * (dp - jnp.sum(p * dp, axis=1, keepdims=True))).astype(jnp.bfloat16))
        yield
        grad_qkv = []
        for i in every:
            q, k, _ = triples[i]
            dq = dot(dss[i], k) * scale
            dk = dot(dss[i], q, TN) * scale
            grad_qkv.append(jnp.concatenate([dq, dk, dvs[i]], axis=1).astype(jnp.bfloat16))
        grad_qkv_all = jnp.concatenate(grad_qkv, axis=0)
        grad_qkv_out[...] += dot(tokens, grad_qkv_all, TN)
        grad_tokens = dot(grad_qkv_all, qkv_t[...])
        yield
        bias_sums = col_sum(grad_qkv_all.astype(jnp.float32))
        grad_norm, gain_three, shift_three = norm_grad(
            [part(grad_tokens, i) for i in every], middle, mean_three, rstd_three, gain(2)
        )
        grad_middle = [grad_final[i] + grad_norm[i] for i in every]
        for i, c in enumerate(images):
            put_shifted(grad_buf, c, grad_middle[i], not_first, not_last)
        yield
        field = jnp.concatenate(act_two, axis=0)
        for i in range(3):
            grad_two_out[i] += dot(field, stacked(grad_buf.at[low:high], i), TN)
        grad_act = conv_shifted(grad_buf.at[low:high], kernel_two_flip)
        yield
        grad_two = [part(grad_act, i) * slope_two[i] for i in every]
        grad_inner, gain_two, shift_two = norm_grad(
            grad_two,
            [inner_in[c] for c in images],
            [stats_in[c, 2:3] for c in images],
            [stats_in[c, 3:4] for c in images],
            gain(1),
        )
        for i, c in enumerate(images):
            put_shifted(grad_buf, c, grad_inner[i], not_first, not_last)
        act_one, slope_one = [], []
        for c in images:
            z = normed(start_in[c], stats_in[c, 0:1], stats_in[c, 1:2], 0)
            s = logistic(z)
            act_one.append((z * s).astype(jnp.bfloat16))
            slope_one.append(s * (1.0 + z * (1.0 - s)))
        yield
        field = jnp.concatenate(act_one, axis=0)
        for i in range(3):
            grad_one_out[i] += dot(field, stacked(grad_buf.at[low:high], i), TN)
        grad_act = conv_shifted(grad_buf.at[low:high], kernel_one_flip)
        yield
        grad_one = [part(grad_act, i) * slope_one[i] for i in every]
        grad_norm, gain_one, shift_one = norm_grad(
            grad_one,
            [start_in[c] for c in images],
            [stats_in[c, 0:1] for c in images],
            [stats_in[c, 1:2] for c in images],
            gain(0),
        )
        grad_start = [grad_middle[i] + grad_norm[i] for i in every]
        patches = [tap_stack(noisy[c], masks, 1) for c in images]
        inner_sums = [col_sum(g) for g in grad_inner]
        for i, c in enumerate(images):
            tshift_grad[pl.ds(step * chunk + c, 1), :] = inner_sums[i]
        grad_small_out[...] += jnp.concatenate(
            [
                gain_one,
                gain_two,
                gain_three,
                gain_four,
                shift_one,
                shift_two,
                shift_three,
                shift_four,
                sum(col_sum(g) for g in grad_start),
                sum(inner_sums),
                sum(col_sum(g) for g in grad_middle),
                bias_sums[:, 0:256],
                bias_sums[:, 512:768],
                sum(col_sum(g) for g in grad_final),
                jnp.zeros((2, 256), jnp.float32),
            ],
            axis=0,
        )
        yield
        grad_inlet_out[...] += sum(
            dot(patch, g.astype(jnp.bfloat16)) for patch, g in zip(patches, grad_start)
        )

    take_turns([work(list(range(g, g + GROUP))) for g in range(0, chunk, GROUP)])

    @pl.when(step == pl.num_programs(0) - 1)
    def _():
        for k, grad in enumerate((grad_one_out, grad_two_out)):
            for tap in range(9):
                at = 256 * (2 - tap % 3)
                for shard, off, row, size in cuts(tap * 256, 256, tall):
                    shard_out[shard, k * tall + off : k * tall + off + size, :] = grad[
                        2 - tap // 3, row : row + size, at : at + 256
                    ]
        for k in range(4):
            grad, at = (grad_qkv_out, 256 * k) if k < 3 else (grad_proj_out, 0)
            for shard, off, row, size in cuts(0, 256, short):
                low = 2 * tall + k * short + off
                shard_out[shard, low : low + size, :] = grad[row : row + size, at : at + 256]
        used = 2 * tall + 4 * short
        if used < shard_out.shape[1]:
            shard_out[:, used:, :] = jnp.zeros(
                (shard_out.shape[0], shard_out.shape[1] - used, 256), jnp.float32
            )
        total = tshift_grad[...]
        shift_grad = rows_dot(time_act[...], total)
        grad_act = back_dot(total, shift_weight[...].astype(jnp.bfloat16)) * time_slope[...]
        two_grad = rows_dot(hidden[...], grad_act)
        time_two = time_weight[embed.shape[1] :, :].astype(jnp.bfloat16)
        grad_hidden = back_dot(grad_act, time_two) * hidden_slope[...]
        one_grad = rows_dot(embed[...], grad_hidden)
        width = one_grad.shape[0]
        height = width + two_grad.shape[0]
        for half in range(2):
            span = slice(256 * half, 256 * half + 256)
            rest_out[half * height : half * height + width, :] = one_grad[:, span]
            rest_out[half * height + width : half * height + height, :] = two_grad[:, span]
        act_sum, hidden_sum = col_sum(grad_act), col_sum(grad_hidden)
        parts = [
            shift_grad,
            grad_inlet_out[...],
            grad_outlet_out[...],
            jnp.concatenate(
                [
                    grad_small_out[0:14],
                    col_sum(total),
                    hidden_sum[:, 0:256],
                    hidden_sum[:, 256:512],
                    act_sum[:, 0:256],
                    act_sum[:, 256:512],
                    jnp.zeros((5, 256), jnp.float32),
                ],
                axis=0,
            ),
            loss_out[...],
        ]
        at = 2 * height
        for part in parts:
            rest_out[at : at + part.shape[0], :] = part
            at += part.shape[0]
        if at < rest_out.shape[0]:
            rest_out[at:, :] = jnp.zeros((rest_out.shape[0] - at, 256), jnp.float32)


def cuts(first, size, height):
    parts, row = [], 0
    while row < size:
        shard, off = divmod(first + row, height)
        take = min(height - off, size - row)
        parts.append((shard, off, row, take))
        row += take
    return parts


def thirds(x):
    high = x.astype(jnp.bfloat16).astype(jnp.float32)
    middle = (x - high).astype(jnp.bfloat16).astype(jnp.float32)
    return jnp.concatenate([high, middle, x - high - middle], axis=0).astype(jnp.bfloat16)


def rows_dot(low, x):
    wide = low.astype(jnp.float32)
    return dot(jnp.concatenate([wide] * 3, axis=0).astype(jnp.bfloat16), thirds(x), TN)


def back_dot(x, weight):
    n = x.shape[0]
    parts = dot(thirds(x), weight, NT)
    return parts[0:n] + (parts[n : 2 * n] + parts[2 * n :])


def resident(shape):
    return pl.BlockSpec(shape, lambda i: (0,) * len(shape), pipeline_mode=pl.Buffered(1))


def per_chunk(chunk, *tail):
    return pl.BlockSpec((chunk,) + tail, lambda i: (i,) + (0,) * len(tail))


def by_source(chunk, block):
    return pl.BlockSpec((block[0], chunk) + block[2:], lambda i: (0, i, 0, 0))


def forward_part(chunk, mix, pair, embed, time_weight, shift_weight, inlet, kernel_one, small):
    n, deep = pair.shape[1], time_weight.shape[1]
    chunk = min(chunk, n)
    shapes = [(n, 256, 256), (n, 256, 256), (n, 8, 256), (n, 8, 256), (n, 8, 256)]
    whole = [jnp.bfloat16, jnp.float32, jnp.bfloat16, jnp.float32]
    return pl.pallas_call(
        first_kernel,
        grid=(n // chunk,),
        in_specs=[
            pl.BlockSpec(memory_space=pltpu.SMEM),
            by_source(chunk, pair.shape),
            resident(embed.shape),
            resident(time_weight.shape),
            resident(shift_weight.shape),
            resident(inlet.shape),
            resident(kernel_one.shape),
            resident(small.shape),
        ],
        out_specs=[per_chunk(chunk, *s[1:]) for s in shapes] + [resident((n, deep))] * 4,
        out_shape=[jax.ShapeDtypeStruct(s, jnp.float32) for s in shapes]
        + [jax.ShapeDtypeStruct((n, deep), kind) for kind in whole],
        scratch_shapes=[
            pltpu.VMEM((chunk, 288, 768), jnp.bfloat16),
            pltpu.VMEM((n, 256), jnp.float32),
        ],
        compiler_params=pltpu.CompilerParams(vmem_limit_bytes=VMEM_LIMIT),
        cost_estimate=pl.CostEstimate(
            flops=2 * n * 256 * 256 * 2400, bytes_accessed=n * 1 << 19, transcendentals=n * 1 << 16
        ),
        name="forward_part",
    )(mix, pair, embed, time_weight, shift_weight, inlet, kernel_one, small)


def main_part(chunk, sizes, coef, start, inner, stats, noisy, target, keep, weights, small, bias_qkv, times):
    n = noisy.shape[0]
    batch, shard_rows, tall, short, rest_rows = sizes
    outs = [(batch, shard_rows, 256), (rest_rows, 256)]
    sums = [(3, 256, 768), (3, 256, 768), (256, 768), (256, 256), (80, 256), (80, 256), (16, 256), (8, 256)]
    return pl.pallas_call(
        functools.partial(second_kernel, tall, short),
        grid=(n // chunk,),
        in_specs=[
            pl.BlockSpec(memory_space=pltpu.SMEM),
            per_chunk(chunk, 256, 256),
            per_chunk(chunk, 256, 256),
            per_chunk(chunk, 8, 256),
            per_chunk(chunk, 8, 256),
            per_chunk(chunk, 8, 256),
            by_source(chunk, keep.shape),
        ]
        + [resident(w.shape) for w in weights]
        + [resident(small.shape), resident(bias_qkv.shape)]
        + [resident(t.shape) for t in times],
        out_specs=[resident(g) for g in outs],
        out_shape=[jax.ShapeDtypeStruct(g, jnp.float32) for g in outs],
        scratch_shapes=[pltpu.VMEM(g, jnp.float32) for g in sums + [(n, 256)]]
        + [pltpu.VMEM((chunk, 288, 768), jnp.bfloat16)] * 2,
        compiler_params=pltpu.CompilerParams(vmem_limit_bytes=VMEM_LIMIT),
        cost_estimate=pl.CostEstimate(
            flops=70 * n * 2 * 256**3, bytes_accessed=n * 5 << 17, transcendentals=n * 5 << 16
        ),
        name="main_part",
    )(coef, start, inner, stats, noisy, target, keep, *weights, small, bias_qkv, *times)


def rows_first(weight):
    inputs, outputs = weight.shape[0] // 9, weight.shape[1]
    flipped = jnp.transpose(weight.reshape(9, inputs, outputs)[::-1], (0, 2, 1))
    return flipped.reshape(9 * outputs, inputs)


def padded_taps(rows):
    padded = jnp.pad(rows.reshape(9, 3, 256), ((0, 1), (0, 5), (0, 0)))
    return padded.reshape(80, 256)


MESH = pl.DeviceIdType.MESH
MISC_ROWS = (640, 640, 512, 80, 80, 24, 8)
MISC_TOTAL = 2048
SPLIT_A = 11
SPLIT_B = 4
LAG = 3


def padded_rows(total, parts):
    return -(-total // (8 * parts)) * 8


def factors(rows):
    low = max(d for d in range(1, rows + 1) if rows % d == 0 and d * d <= rows)
    return low, rows // low


def exchange_kernel(
    shard_shape,
    rates,
    grads_a,
    grads_b,
    state_kernel,
    state_attention,
    weight_kernel,
    weight_attention,
    scalars,
    out_a,
    out_b,
    shard_grad,
    norm_out,
    own_a,
    own_b,
    half_a,
    half_b,
    near_a,
    near_b,
    far_a,
    far_b,
    deep_a,
    deep_b,
    piece_a,
    piece_b,
    shard_weight,
    shard_first,
    shard_second,
    square_core,
    square_rows,
    square_deep,
    local_sem,
    own_sem,
    core_send,
    core_recv,
    near_send,
    near_recv,
    far_send,
    far_recv,
    deep_send,
    deep_recv,
    shard_send,
    shard_recv,
    square_send,
    square_recv,
    deep_send_two,
    deep_recv_two,
    near_send_two,
    near_recv_two,
    far_send_two,
    far_recv_two,
    core_send_two,
    core_recv_two,
    keep_sem,
):
    depth, _, tops, wide, piece, _ = grads_a.shape
    lanes = grads_b.shape[4]
    rows = tops * wide
    pairs, tall, quads, short = shard_shape
    batch, r = lax.axis_index("batch"), lax.axis_index("rows")
    z, c = batch // 2, batch % 2
    y, x = r // wide, r % wide
    partner = z * 2 + (1 - c)
    row_peers = [(r + d) % rows for d in range(1, rows)]
    deep_peers = [(z + d) % depth for d in range(1, depth)]
    x_peers = [(x + d) % wide for d in range(1, wide)]
    y_peers = [(y + d) % tops for d in range(1, tops)]

    def remote(src, dst, send, recv, where):
        return pltpu.make_async_remote_copy(
            src_ref=src, dst_ref=dst, send_sem=send, recv_sem=recv, device_id=where, device_id_type=MESH
        )

    def begin(copies):
        for copy in copies:
            copy.start()
        return copies

    def arrived(copies):
        for copy in copies:
            copy.wait_recv()

    def blocks(kernel_ref, attention_ref, flat, base, offset):
        copies = []
        for k in range(pairs + quads):
            ref, own, size = (kernel_ref, k, tall) if k < pairs else (attention_ref, k - pairs, short)
            at = k * tall if k < pairs else pairs * tall + own * short
            far = ref.at[own] if offset is None else ref.at[own, pl.ds(offset * size, size)]
            near = flat.at[pl.ds(at, size)]
            copies.append(pltpu.make_async_copy(far, near, local_sem.at[base * (pairs + quads) + k]))
        return begin(copies)

    owns = begin(
        [
            pltpu.make_async_copy(grads_b.at[:, c], own_b, own_sem.at[0]),
            pltpu.make_async_copy(grads_a.at[:, c], own_a, own_sem.at[1]),
        ]
    )

    barrier = pltpu.get_barrier_semaphore()
    pl.semaphore_signal(barrier, inc=1, device_id=(partner, r), device_id_type=MESH)
    for peer in row_peers:
        pl.semaphore_signal(barrier, inc=1, device_id=(batch, peer), device_id_type=MESH)
    for peer in deep_peers:
        pl.semaphore_signal(barrier, inc=1, device_id=(peer * 2 + c, r), device_id_type=MESH)
    pl.semaphore_wait(barrier, rows + depth - 1)

    set_a = (grads_a, own_a, half_a, near_a, far_a, deep_a, piece_a, out_a)
    set_b = (grads_b, own_b, half_b, near_b, far_b, deep_b, piece_b, out_b)
    chunks = []
    for group, height, parts in ((set_b, lanes, SPLIT_B), (set_a, piece, SPLIT_A)):
        marks = [height // 8 * k // parts * 8 for k in range(parts + 1)]
        for low, high in zip(marks[:-1], marks[1:]):
            if high > low:
                chunks.append(group + (low, high - low, len(chunks) % 2 == 0))
    count = len(chunks)
    small = sum(1 for chunk in chunks if chunk[0] is grads_b)

    core_copies = []
    for k, (grads, _, half, _, _, _, _, _, at, size, _) in enumerate(chunks):
        span = pl.ds(at, size)
        core_copies.append(
            begin(
                [
                    remote(
                        grads.at[:, 1 - c, :, :, span],
                        half.at[:, :, :, span],
                        core_send.at[k],
                        core_recv.at[k],
                        (partner, r),
                    )
                ]
            )
        )
    fetches = (
        blocks(weight_kernel, weight_attention, shard_weight, 0, batch)
        + blocks(state_kernel.at[0], state_attention.at[0], shard_first, 1, None)
        + blocks(state_kernel.at[1], state_attention.at[1], shard_second, 2, None)
    )
    near_copies, far_copies, deep_copies = [], [], []

    def sum_near(k):
        _, own, half, near, _, _, _, _, at, size, x_first = chunks[k]
        if k == 0:
            owns[0].wait()
        if k == small:
            owns[1].wait()
        arrived(core_copies[k])
        span = pl.ds(at, size)

        def add_own(t, carry):
            i, j, l = t // rows, t // wide % tops, t % wide
            half[i, j, l, span] = half[i, j, l, span] + own[i, j, l, span]
            return carry

        lax.fori_loop(0, depth * rows, add_own, 0)
        copies = []
        for d, peer in enumerate(x_peers if x_first else y_peers):
            src = half.at[:, :, peer, span] if x_first else half.at[:, peer, :, span]
            dst = near.at[d, :, pl.ds(0, tops if x_first else wide), span]
            where = (batch, y * wide + peer) if x_first else (batch, peer * wide + x)
            copies.append(remote(src, dst, near_send.at[k, d], near_recv.at[k, d], where))
        near_copies.append(begin(copies))

    def sum_far(k):
        _, _, half, near, far, _, _, _, at, size, x_first = chunks[k]
        arrived(near_copies[k])
        span = pl.ds(at, size)
        across = tops if x_first else wide

        def add_near(t, carry):
            i, j = t // across, t % across
            place = (i, j, x) if x_first else (i, y, j)
            total = half[place + (span,)]
            for d in range((wide if x_first else tops) - 1):
                total = total + near[d, i, j, span]
            half[place + (span,)] = total
            return carry

        lax.fori_loop(0, depth * across, add_near, 0)
        copies = []
        for d, peer in enumerate(y_peers if x_first else x_peers):
            src = half.at[:, peer, x, span] if x_first else half.at[:, y, peer, span]
            where = (batch, peer * wide + x) if x_first else (batch, y * wide + peer)
            copies.append(
                remote(src, far.at[d, :, span], far_send.at[k, d], far_recv.at[k, d], where)
            )
        far_copies.append(begin(copies))

    def sum_deep(k):
        _, _, half, _, far, deep, _, _, at, size, x_first = chunks[k]
        arrived(far_copies[k])
        span = pl.ds(at, size)

        def add_far(i, carry):
            total = half[i, y, x, span]
            for d in range((tops if x_first else wide) - 1):
                total = total + far[d, i, span]
            half[i, y, x, span] = total
            return carry

        lax.fori_loop(0, depth, add_far, 0)
        copies = []
        for d, peer in enumerate(deep_peers):
            copies.append(
                remote(
                    half.at[peer, y, x, span],
                    deep.at[d, span],
                    deep_send.at[k, d],
                    deep_recv.at[k, d],
                    (peer * 2 + c, r),
                )
            )
        deep_copies.append(begin(copies))

    def finish_sum(k):
        _, _, half, _, _, deep, _, _, at, size, _ = chunks[k]
        arrived(deep_copies[k])
        span = pl.ds(at, size)
        total = half[z, y, x, span]
        for d in range(depth - 1):
            total = total + deep[d, span]
        return total

    def squares(values):
        return jnp.sum((values * values).reshape(-1, 8, 256), axis=0)

    def gather_deep(k):
        _, _, _, _, _, _, part, out, at, size, _ = chunks[k]
        span = pl.ds(at, size)
        keep = pltpu.make_async_copy(part.at[span], out.at[z, c, y, x, span], keep_sem.at[k])
        keep.start()
        copies = []
        for d, peer in enumerate(deep_peers):
            copies.append(
                remote(
                    part.at[span],
                    out.at[z, c, y, x, span],
                    deep_send_two.at[k, d],
                    deep_recv_two.at[k, d],
                    (peer * 2 + c, r),
                )
            )
        return keep, begin(copies)

    def gather_near(k):
        _, _, _, _, _, _, _, out, at, size, x_first = chunks[k]
        place = out.at[:, c, y, x, pl.ds(at, size)]
        copies = []
        for d, peer in enumerate(y_peers if x_first else x_peers):
            where = (batch, peer * wide + x) if x_first else (batch, y * wide + peer)
            copies.append(remote(place, place, near_send_two.at[k, d], near_recv_two.at[k, d], where))
        return begin(copies)

    def gather_far(k):
        _, _, _, _, _, _, _, out, at, size, x_first = chunks[k]
        span = pl.ds(at, size)
        place = out.at[:, c, :, x, span] if x_first else out.at[:, c, y, :, span]
        copies = []
        for d, peer in enumerate(x_peers if x_first else y_peers):
            where = (batch, y * wide + peer) if x_first else (batch, peer * wide + x)
            copies.append(remote(place, place, far_send_two.at[k, d], far_recv_two.at[k, d], where))
        return begin(copies)

    def gather_core(k):
        _, _, _, _, _, _, _, out, at, size, _ = chunks[k]
        place = out.at[:, c, :, :, pl.ds(at, size)]
        return begin([remote(place, place, core_send_two.at[k], core_recv_two.at[k], (partner, r))])

    keeps, firsts, seconds, thirds, lasts = [], [], [], [], []
    partial = []

    def send_deep(k):
        keep, copies = gather_deep(k)
        keeps.append(keep)
        firsts.append(copies)

    def send_near(k):
        keeps[k].wait()
        arrived(firsts[k])
        seconds.append(gather_near(k))

    def send_far(k):
        arrived(seconds[k])
        thirds.append(gather_far(k))

    def send_core(k):
        arrived(thirds[k])
        lasts.append(gather_core(k))

    def sum_last(k):
        total = finish_sum(k)
        at, size = chunks[k][8], chunks[k][9]
        counted = total
        if k < small:
            piece_b[pl.ds(at, size)] = total
            line = (batch * rows + r) * lanes + at + lax.broadcasted_iota(jnp.int32, total.shape, 0)
            counted = jnp.where(line < sum(MISC_ROWS[:-1]), total, 0.0)
            send_deep(k)
        else:
            shard_grad[r, pl.ds(at, size)] = total
        partial.append(squares(counted))

    for t in range(count + 3 * LAG):
        for stage, lag in ((sum_near, 0), (sum_far, LAG), (sum_deep, 2 * LAG), (sum_last, 3 * LAG)):
            if 0 <= t - lag < count:
                stage(t - lag)
    square = sum(partial)
    square_core[0] = square
    square_copies = begin(
        [remote(square_core.at[0], square_core.at[1], square_send.at[0], square_recv.at[0], (partner, r))]
    )
    arrived(square_copies)
    square_rows[r] = square_core[0] + square_core[1]
    copies = begin(
        [
            remote(
                square_rows.at[r],
                square_rows.at[r],
                square_send.at[1 + d],
                square_recv.at[1 + d],
                (batch, peer),
            )
            for d, peer in enumerate(row_peers)
        ]
    )
    shard_copies = begin(
        [
            remote(shard_grad.at[r], shard_grad.at[r], shard_send.at[d], shard_recv.at[d], (batch, peer))
            for d, peer in enumerate(row_peers)
        ]
    )
    for k in range(small):
        send_near(k)
    arrived(copies)
    square_copies += copies
    square_deep[z] = sum(square_rows[j] for j in range(rows))
    copies = begin(
        [
            remote(
                square_deep.at[z],
                square_deep.at[z],
                square_send.at[rows + d],
                square_recv.at[rows + d],
                (peer * 2 + c, r),
            )
            for d, peer in enumerate(deep_peers)
        ]
    )
    for fetch in fetches:
        fetch.wait()
    for k in range(small):
        send_far(k)
    arrived(copies)
    square_copies += copies
    square = sum(square_deep[j] for j in range(depth))
    norm = jnp.sqrt(jnp.sum(jnp.sum(square, axis=0, keepdims=True), axis=1, keepdims=True))
    clip = CLIP / jnp.maximum(norm, CLIP)
    norm_out[...] = jnp.broadcast_to(norm, norm_out.shape)
    for k in range(small, count):
        at, size = chunks[k][8], chunks[k][9]
        span = pl.ds(pl.multiple_of(r * piece + at, 8), size)
        g = shard_grad[r, pl.ds(at, size)] * clip
        first = BETA_ONE * shard_first[span] + (1.0 - BETA_ONE) * g
        second = BETA_TWO * shard_second[span] + (1.0 - BETA_TWO) * g * g
        line = r * piece + at + lax.broadcasted_iota(jnp.int32, g.shape, 0)
        rate = jnp.where(line < pairs * tall, rates[0], rates[1])
        weight = shard_weight[span]
        step = first * scalars[0] / (jnp.sqrt(second * scalars[1]) + EPS_ADAM)
        piece_a[pl.ds(at, size)] = weight - rate * (step + DECAY * weight)
        send_deep(k)
    for k in range(small):
        send_core(k)
    for t in range(small, count + 2 * LAG):
        for stage, lag in ((send_near, 0), (send_far, LAG), (send_core, 2 * LAG)):
            if small <= t - lag < count:
                stage(t - lag)
    arrived(shard_copies)
    for copies in lasts:
        arrived(copies)
    for copies in (
        core_copies + near_copies + far_copies + deep_copies + firsts + seconds + thirds + lasts
    ):
        for copy in copies:
            copy.wait_send()
    for copy in square_copies + shard_copies:
        copy.wait_send()


def exchange(grads_a, grads_b, state_kernel, state_attention, weight_kernel, weight_attention, scalars):
    depth, _, rows, piece, width = grads_a.shape
    tops, wide = factors(rows)
    lanes = grads_b.shape[3]
    grads_a = grads_a.reshape(depth, 2, tops, wide, piece, width)
    grads_b = grads_b.reshape(depth, 2, tops, wide, lanes, width)
    pairs, tall = state_kernel.shape[1:3]
    quads, short = state_attention.shape[1:3]
    shape = functools.partial(jax.ShapeDtypeStruct, dtype=jnp.float32)
    whole = pl.BlockSpec(memory_space=pltpu.VMEM)
    anywhere = pl.BlockSpec(memory_space=pl.ANY)
    dma = pltpu.SemaphoreType.DMA
    vmem = functools.partial(pltpu.VMEM, dtype=jnp.float32)
    most = max(tops, wide)
    return pl.pallas_call(
        functools.partial(exchange_kernel, (pairs, tall, quads, short), (RATES[1], RATES[2])),
        in_specs=[anywhere] * 6 + [pl.BlockSpec(memory_space=pltpu.SMEM)],
        out_specs=[anywhere] * 2 + [whole] * 2,
        out_shape=[
            shape(grads_a.shape),
            shape(grads_b.shape),
            shape((rows, piece, width)),
            shape((8, 128)),
        ],
        scratch_shapes=[
            vmem((depth, tops, wide, piece, width)),
            vmem((depth, tops, wide, lanes, width)),
            vmem((depth, tops, wide, piece, width)),
            vmem((depth, tops, wide, lanes, width)),
            vmem((most - 1, depth, most, piece, width)),
            vmem((most - 1, depth, most, lanes, width)),
            vmem((most - 1, depth, piece, width)),
            vmem((most - 1, depth, lanes, width)),
            vmem((depth - 1, piece, width)),
            vmem((depth - 1, lanes, width)),
            vmem((piece, width)),
            vmem((lanes, width)),
            vmem((rows * piece, width)),
            vmem((rows * piece, width)),
            vmem((rows * piece, width)),
            vmem((2, 8, width)),
            vmem((rows, 8, width)),
            vmem((depth, 8, width)),
            dma((3 * (pairs + quads),)),
            dma((2,)),
            dma((SPLIT_A + SPLIT_B,)),
            dma((SPLIT_A + SPLIT_B,)),
            dma((SPLIT_A + SPLIT_B, most - 1)),
            dma((SPLIT_A + SPLIT_B, most - 1)),
            dma((SPLIT_A + SPLIT_B, most - 1)),
            dma((SPLIT_A + SPLIT_B, most - 1)),
            dma((SPLIT_A + SPLIT_B, depth - 1)),
            dma((SPLIT_A + SPLIT_B, depth - 1)),
            dma((rows - 1,)),
            dma((rows - 1,)),
            dma((rows + depth - 1,)),
            dma((rows + depth - 1,)),
            dma((SPLIT_A + SPLIT_B, depth - 1)),
            dma((SPLIT_A + SPLIT_B, depth - 1)),
            dma((SPLIT_A + SPLIT_B, most - 1)),
            dma((SPLIT_A + SPLIT_B, most - 1)),
            dma((SPLIT_A + SPLIT_B, most - 1)),
            dma((SPLIT_A + SPLIT_B, most - 1)),
            dma((SPLIT_A + SPLIT_B,)),
            dma((SPLIT_A + SPLIT_B,)),
            dma((SPLIT_A + SPLIT_B,)),
        ],
        compiler_params=pltpu.CompilerParams(
            collective_id=0, has_side_effects=True, vmem_limit_bytes=VMEM_LIMIT
        ),
        name="exchange",
    )(grads_a, grads_b, state_kernel, state_attention, weight_kernel, weight_attention, scalars)


def finish_kernel(
    scalars,
    norm_tile,
    fresh,
    average_kernel,
    average_attention,
    shard_grad,
    state_kernel,
    state_attention,
    time_left,
    time_right,
    shift_rows,
    rest_rows,
    *refs,
):
    weights, states, averages, refs = refs[:5], refs[5:10], refs[10:15], refs[15:]
    (kernel_out, attention_out), refs = refs[:2], refs[2:]
    updated, firsts, seconds, refs = refs[:5], refs[5:10], refs[10:15], refs[15:]
    first_kernel_out, first_attention_out, second_kernel_out, second_attention_out, loss_out, norm_out = refs
    norm = norm_tile[0:1, 0:1]
    clip = CLIP / jnp.maximum(norm, CLIP)
    kept = scalars[2]

    def averaged(out, index, new, average):
        out[(0,) + index] = new
        out[(1,) + index] = kept * average + (1.0 - kept) * new

    tall, short = state_kernel.shape[2], state_attention.shape[2]
    for k in range(2):
        averaged(kernel_out, (k,), fresh[0, k * tall : k * tall + tall], average_kernel[k])
    for k in range(4):
        at = 2 * tall + k * short
        averaged(attention_out, (k,), fresh[0, at : at + short], average_attention[k])

    def moments(first, second, g):
        return BETA_ONE * first + (1.0 - BETA_ONE) * g, BETA_TWO * second + (1.0 - BETA_TWO) * g * g

    def update(k, rate, grad):
        weight = weights[k][...]
        old = (states[k][0], states[k][1]) if k < 2 else (states[k][:, 0, :], states[k][:, 1, :])
        first, second = moments(*old, grad * clip)
        firsts[k][...] = first
        seconds[k][...] = second
        step = first * scalars[0] / (jnp.sqrt(second * scalars[1]) + EPS_ADAM)
        new = weight - rate * (step + DECAY * weight)
        if k < 2:
            averaged(updated[k], (), new, averages[k][...])
        else:
            updated[k][:, 0, :] = new
            updated[k][:, 1, :] = kept * averages[k][...] + (1.0 - kept) * new

    update(0, RATES[3], jnp.concatenate([time_left[...], time_right[...]], axis=1))
    update(1, RATES[4], shift_rows[...])

    @pl.when(pl.program_id(0) == 0)
    def _():
        for refs, outs, count, height in (
            (state_kernel, (first_kernel_out, second_kernel_out), 2, tall),
            (state_attention, (first_attention_out, second_attention_out), 4, short),
        ):
            for k in range(count):
                at = k * height + (0 if count == 2 else 2 * tall)
                first, second = moments(refs[0, k], refs[1, k], shard_grad[at : at + height] * clip)
                outs[0][k] = first
                outs[1][k] = second
        inlet = jnp.concatenate([rest_rows[8 * tap : 8 * tap + 3] for tap in range(9)], axis=0)
        outlet = jnp.concatenate([rest_rows[80 + 8 * tap : 83 + 8 * tap] for tap in range(9)], axis=1)
        update(2, RATES[0], inlet)
        update(3, RATES[5], outlet)
        update(4, RATES[6], rest_rows[160:179])
        loss_out[...] = jnp.sum(col_sum(rest_rows[184:192]), axis=1, keepdims=True)
        norm_out[...] = norm


def finish(scalars, norm_tile, fresh, average_kernel, average_attention, shard_grad, state_kernel, state_attention, rest, weights, states, averages):
    batch, shard_rows, width = fresh.shape
    tall, short = state_kernel.shape[2], state_attention.shape[2]
    (time_rows, time_width), (shift_rows, _) = weights[0].shape, weights[1].shape
    time_part, shift_part = time_rows // batch, shift_rows // batch
    shape = functools.partial(jax.ShapeDtypeStruct, dtype=jnp.float32)

    def at(block, index):
        return pl.BlockSpec(block, index)

    def rows_of(k, lead):
        part, wide = ((time_part, time_width), (shift_part, width))[k]
        return pl.BlockSpec(lead + (part, wide), lambda b: (0,) * len(lead) + (b, 0))

    def five(lead):
        small = [w.shape[:1] + lead + w.shape[1:] for w in weights[2:]]
        return [rows_of(0, lead), rows_of(1, lead)] + [resident(block) for block in small]

    shift_at = 2 * time_rows // shift_part
    rest_at = (2 * time_rows + shift_rows) // 256
    return pl.pallas_call(
        finish_kernel,
        grid=(batch,),
        in_specs=[
            pl.BlockSpec(memory_space=pltpu.SMEM),
            resident(norm_tile.shape),
            at((1, shard_rows, width), lambda b: (b, 0, 0)),
            at((2, tall, width), lambda b: (0, b, 0)),
            at((4, short, width), lambda b: (0, b, 0)),
            resident(shard_grad.shape),
            resident(state_kernel.shape),
            resident(state_attention.shape),
            at((time_part, width), lambda b: (b, 0)),
            at((time_part, width), lambda b: (batch + b, 0)),
            at((shift_part, width), lambda b: (shift_at + b, 0)),
            pl.BlockSpec((256, width), lambda b: (rest_at, 0), pipeline_mode=pl.Buffered(1)),
        ]
        + five(())
        + five((2,))
        + five(()),
        out_specs=[
            at((2, 2, tall, width), lambda b: (0, 0, b, 0)),
            at((2, 4, short, width), lambda b: (0, 0, b, 0)),
        ]
        + five((2,))
        + five(())
        + five(())
        + [resident(state_kernel.shape[1:]), resident(state_attention.shape[1:])] * 2
        + [resident((1, 1))] * 2,
        out_shape=[
            shape((2, 2, batch * tall, width)),
            shape((2, 4, batch * short, width)),
        ]
        + [shape((2,) + w.shape) for w in weights[:2]]
        + [shape((w.shape[0], 2, w.shape[1])) for w in weights[2:]]
        + [shape(w.shape) for w in weights] * 2
        + [shape(state_kernel.shape[1:]), shape(state_attention.shape[1:])] * 2
        + [shape((1, 1))] * 2,
        compiler_params=pltpu.CompilerParams(vmem_limit_bytes=VMEM_LIMIT),
        cost_estimate=pl.CostEstimate(flops=40 << 20, bytes_accessed=36 << 20, transcendentals=1 << 20),
        name="finish",
    )(
        scalars,
        norm_tile,
        fresh,
        average_kernel,
        average_attention,
        shard_grad,
        state_kernel,
        state_attention,
        rest,
        rest,
        rest,
        rest,
        *weights,
        *states,
        *averages,
    )


def local(
    x_clean,
    noise,
    timesteps,
    keep_mask,
    adam_step,
    inlet_weight,
    kernel_weight,
    attention_weight,
    time_weight,
    shift_weight,
    outlet_weight,
    small_params,
    state_inlet,
    state_kernel,
    state_attention,
    state_time,
    state_shift,
    state_outlet,
    state_small,
    average_inlet,
    average_kernel,
    average_attention,
    average_time,
    average_shift,
    average_outlet,
    average_small,
):
    chans = kernel_weight.shape[2]
    width_sin = time_weight.shape[0] - time_weight.shape[1]
    rows, batch = lax.axis_size("rows"), lax.axis_size("batch")
    own = timesteps.shape[0] // rows
    keep = keep_mask.reshape(rows, own, -1, chans).astype(jnp.bfloat16)
    keep, timesteps, x_clean, noise = lax.optimization_barrier((keep, timesteps, x_clean, noise))
    keep = lax.all_to_all(keep, "rows", 0, 0, tiled=True)
    halves = [a.reshape(rows, own, 3, -1) for a in (x_clean, noise)]
    pair = jnp.pad(jnp.concatenate(halves, axis=3), ((0, 0), (0, 0), (0, 1), (0, 0)))
    here = lax.axis_index("rows")
    parts = [lax.dynamic_index_in_dim(pair, here, 0, keepdims=False)]
    for d in range(1, rows):
        block = lax.dynamic_index_in_dim(pair, (here + d) % rows, 0, keepdims=False)
        parts.append(lax.ppermute(block, "rows", [(i, (i + d) % rows) for i in range(rows)]))
    steps = ((here - jnp.arange(rows)) % rows)[:, None, None, None]
    pair = jnp.broadcast_to(parts[0], (rows,) + parts[0].shape)
    for d in range(1, rows):
        pair = jnp.where(steps == d, parts[d], pair)
    pair, inlet_low, kernels, projections, outlet_low = lax.optimization_barrier(
        (pair, inlet_weight, kernel_weight, attention_weight, outlet_weight)
    )
    timesteps = lax.dynamic_slice_in_dim(timesteps, lax.axis_index("rows") * own, own, 0)
    bars = alpha_bars(timesteps)
    mix = jnp.stack([jnp.sqrt(bars), jnp.sqrt(1.0 - bars)])
    kernels = kernels.astype(jnp.bfloat16)
    projections = projections.astype(jnp.bfloat16)
    inlet = padded_taps(inlet_low).astype(jnp.bfloat16)
    outlet = padded_taps(
        jnp.transpose(outlet_low.reshape(3, 9, chans), (1, 0, 2)).reshape(27, chans)
    ).astype(jnp.bfloat16)
    qkv = jnp.concatenate([projections[0], projections[1], projections[2]], axis=1)
    embed = sinusoid(timesteps, width_sin).astype(jnp.bfloat16)
    ratio = bars / (1.0 - bars)
    snr_weight = jnp.minimum(ratio, GAMMA) / ratio
    denom = 3 * 256 * own * rows * batch
    coef = 2.0 * snr_weight / denom
    start, inner, stats, noisy, target, hidden, hidden_slope, time_act, time_slope = forward_part(
        FORWARD_CHUNK, mix, pair, embed, time_weight, shift_weight, inlet, kernels[0], small_params
    )
    bias_qkv = jnp.concatenate(
        [small_params[11], jnp.zeros_like(small_params[0]), small_params[12]]
    )
    tall, short = state_kernel.shape[2], state_attention.shape[2]
    shard_rows = rows * padded_rows(2 * tall + 4 * short, rows)
    lanes = padded_rows(MISC_TOTAL, batch * rows)
    shards, rest = main_part(
        CHUNK,
        (batch, shard_rows, tall, short, batch * rows * lanes),
        coef,
        start,
        inner,
        stats,
        noisy,
        target,
        keep,
        (
            rows_first(kernels[0]),
            kernels[1],
            rows_first(kernels[1]),
            qkv,
            qkv.T,
            projections[3],
            projections[3].T,
            outlet,
        ),
        small_params,
        bias_qkv[None],
        (embed, hidden, hidden_slope, time_act, time_slope, time_weight, shift_weight),
    )
    count = adam_step[0].astype(jnp.float32)
    scalars = jnp.stack(
        [
            1.0 / (1.0 - BETA_ONE**count),
            1.0 / (1.0 - BETA_TWO**count),
            jnp.minimum(EMA_TOP, (1.0 + count) / (10.0 + count)),
        ]
    )
    fresh, rest, shard_grad, norm_tile = exchange(
        shards.reshape(batch // 2, 2, rows, shard_rows // rows, chans),
        rest.reshape(batch // 2, 2, rows, lanes, chans),
        state_kernel,
        state_attention,
        kernel_weight,
        attention_weight,
        scalars,
    )
    results = finish(
        scalars,
        norm_tile,
        fresh.reshape(batch, shard_rows, chans),
        lax.all_gather(average_kernel, "batch", axis=1, tiled=True),
        lax.all_gather(average_attention, "batch", axis=1, tiled=True),
        shard_grad.reshape(shard_rows, chans),
        state_kernel,
        state_attention,
        rest.reshape(-1, chans),
        (time_weight, shift_weight, inlet_weight, outlet_weight, small_params),
        (state_time, state_shift)
        + tuple(jnp.transpose(a, (1, 0, 2)) for a in (state_inlet, state_outlet, state_small)),
        (average_time, average_shift, average_inlet, average_outlet, average_small),
    )
    kernel_pair, attention_pair = results[:2]
    triples = [list(results[2 + 5 * k : 7 + 5 * k]) for k in range(3)]
    triples[0][2:] = [jnp.transpose(a, (1, 0, 2)) for a in triples[0][2:]]
    first_conv, first_attention, second_conv, second_attention, loss, norm = results[17:]
    ordered = []
    for (time, shift, inlet, outlet, small), middle in zip(
        triples,
        ((kernel_pair, attention_pair), (first_conv, first_attention), (second_conv, second_attention)),
    ):
        ordered += [inlet, *middle, time, shift, outlet, small]
    return (*ordered, loss.reshape(()), norm.reshape(()))


def solution(mesh):
    return jax.shard_map(
        local,
        mesh=mesh,
        in_specs=(
            P("batch", None, "rows", None),
            P("batch", None, "rows", None),
            P("batch"),
            P("batch", "rows", None, None),
            P(),
            P(),
            P(),
            P(),
            P(),
            P(),
            P(),
            P(),
            P(),
            P(None, None, "batch", None),
            P(None, None, "batch", None),
            P(),
            P(),
            P(),
            P(),
            P(),
            P(None, "batch", None),
            P(None, "batch", None),
            P(),
            P(),
            P(),
            P(),
        ),
        out_specs=(
            P(),
            P(),
            P(),
            P(),
            P(),
            P(),
            P(),
            P(),
            P(None, "batch", None),
            P(None, "batch", None),
            P(),
            P(),
            P(),
            P(),
            P(),
            P(None, "batch", None),
            P(None, "batch", None),
            P(),
            P(),
            P(),
            P(),
            P(),
            P(),
        ),
        check_vma=False,
    )
```

```python
import functools
import math

import jax
import jax.numpy as jnp
import numpy as np
from jax import lax
from jax.experimental import pallas as pl
from jax.experimental.pallas import tpu as pltpu
from jax.sharding import PartitionSpec as P

G = 32


CLIP = 0.05
GAMMA = 5.0
KEEP = 0.9
EPS_NORM = 1e-05
BETA_ONE = 0.9
BETA_TWO = 0.999
EPS_ADAM = 1e-08
DECAY = 0.01
EMA_TOP = 0.9999
VMEM_LIMIT = 60 << 20
CHUNK = 4
FORWARD_CHUNK = 8
SHARDS = 4
GROUP = 2
COUNT = 2048.0
RATES = (0.1, 0.01, 0.03, 0.05, 0.02, 0.01, 0.2)


def bar_table():
    beta_rates = 0.0001 + (0.02 - 0.0001) * np.arange(1000, dtype=np.float64) / 999.0
    return np.exp(np.cumsum(np.log(1.0 - beta_rates))).astype(np.float32)


def alpha_bars(timesteps):
    one_hot = (timesteps[:, None] == jnp.arange(1000)[None, :]).astype(jnp.float32)
    return jnp.sum(one_hot * bar_table()[None, :], axis=1)


def sinusoid(timesteps, width):
    half = width // 2
    rates = jnp.exp(-math.log(10000.0) * jnp.arange(half).astype(jnp.float32) / (half - 1))
    angles = timesteps.astype(jnp.float32)[:, None] * rates[None, :]
    return jnp.concatenate([jnp.sin(angles), jnp.cos(angles)], axis=1)


def wrap(shift, size):
    return shift % size


def tap_masks():
    lane = lax.broadcasted_iota(jnp.int32, (8, 256), 1)
    row, col = lane // 16, lane % 16
    masks = []
    for i in range(3):
        for j in range(3):
            ok = (row + (i - 1) >= 0) & (row + (i - 1) < 16) & (col + (j - 1) >= 0) & (col + (j - 1) < 16)
            masks.append(ok)
    return masks


def tap_stack(tile, masks, sign):
    parts = []
    for tap in range(9):
        step = sign * (16 * (tap // 3 - 1) + tap % 3 - 1)
        moved = tile if step == 0 else pltpu.roll(tile, wrap(-step, 256), 1)
        parts.append(jnp.where(masks[tap if sign > 0 else 8 - tap], moved, 0.0))
    parts.append(jnp.zeros_like(tile))
    return jnp.concatenate(parts, axis=0).astype(jnp.bfloat16)


def group_sum(rows):
    halves = []
    for half in range(2):
        part = rows[:, 128 * half : 128 * half + 128]
        lane = lax.broadcasted_iota(jnp.int32, part.shape, 1)
        for step in (1, 2, 4):
            upper = (lane // step) % 2 == 1
            part = part + jnp.where(upper, pltpu.roll(part, step, 1), pltpu.roll(part, 128 - step, 1))
        halves.append(part)
    return jnp.concatenate(halves, axis=1)


def col_sum(x):
    return jnp.sum(x, axis=0, keepdims=True)


def stats_of(fields):
    sums = jnp.concatenate([col_sum(x) for x in fields] + [col_sum(x * x) for x in fields], axis=0)
    both = group_sum(sums) / COUNT
    n = len(fields)
    mean = both[:n]
    spread = both[n:] - mean * mean
    return mean, lax.rsqrt(spread + EPS_NORM)


def logistic(z):
    return 0.5 * jnp.tanh(0.5 * z) + 0.5


def put_shifted(buf, c, y, not_first, not_last):
    buf[c, 16:272, 256:512] = y.astype(jnp.bfloat16)
    buf[c, 16:272, 0:256] = jnp.where(not_first, pltpu.roll(y, 1, 0), 0.0).astype(jnp.bfloat16)
    buf[c, 16:272, 512:768] = jnp.where(not_last, pltpu.roll(y, 255, 0), 0.0).astype(jnp.bfloat16)


def edge_masks():
    col = lax.broadcasted_iota(jnp.int32, (256, 256), 0) % 16
    return col != 0, col != 15


def stacked(buf, i):
    chunk = buf.shape[0]
    return buf[:, 16 * i : 16 * i + 256, :].reshape(chunk * 256, 768)


def dot(a, b, dims=((1,), (0,))):
    return lax.dot_general(a, b, (dims, ((), ())), preferred_element_type=jnp.float32)


NT = ((1,), (1,))
TN = ((0,), (0,))


def conv_shifted(buf, weight):
    field = jnp.concatenate([stacked(buf, i) for i in range(3)], axis=1)
    return dot(field, weight[...])


def zero_edges(buf):
    edge = jnp.zeros((buf.shape[0], 16, 768), jnp.bfloat16)
    buf[:, 0:16, :] = edge
    buf[:, 272:288, :] = edge


def take_turns(workers):
    live, started = [], 0
    while live or started < len(workers):
        if started < len(workers):
            live.append(workers[started])
            started += 1
        live = [w for w in live if next(w, live) is not live]


def lanes_joined(blocks):
    return blocks[0] if len(blocks) == 1 else jnp.concatenate(blocks, axis=1)


def first_kernel(
    mix,
    pair,
    embed,
    time_weight,
    shift_weight,
    inlet,
    kernel_one,
    small,
    start_out,
    inner_out,
    stats_out,
    noisy_out,
    target_out,
    hidden_out,
    hidden_slope_out,
    time_act_out,
    time_slope_out,
    buf,
    tshift,
):
    chunk = start_out.shape[0]
    step = pl.program_id(0)

    @pl.when(step == 0)
    def _():
        zero_edges(buf)
        width = embed.shape[1]

        def layer(x, weight, at):
            bias = jnp.concatenate([small[at : at + 1], small[at + 1 : at + 2]], axis=1)
            z = dot(x, weight.astype(jnp.bfloat16)) + bias
            s = logistic(z)
            return (z * s).astype(jnp.bfloat16), s * (1.0 + z * (1.0 - s))

        hidden, hidden_slope = layer(embed[...], time_weight[0:width, :], 15)
        time_act, time_slope = layer(hidden, time_weight[width:, :], 17)
        hidden_out[...] = hidden
        hidden_slope_out[...] = hidden_slope
        time_act_out[...] = time_act
        time_slope_out[...] = time_slope
        both = small[14:15] + small[9:10]
        tshift[...] = dot(time_act, shift_weight[...].astype(jnp.bfloat16)) + both

    masks = tap_masks()
    not_first, not_last = edge_masks()
    part = pair.shape[3] // 2
    blank = jnp.zeros((4, 256), jnp.float32)

    def work(images):
        n = len(images)
        every = range(n)
        low, high = images[0], images[-1] + 1
        starts = []
        for c in images:
            tiles = [pair[s, c] for s in range(pair.shape[0])]
            clean = jnp.concatenate([lanes_joined([t[:, :part] for t in tiles]), blank], axis=0)
            noise = jnp.concatenate([lanes_joined([t[:, part:] for t in tiles]), blank], axis=0)
            noisy = mix[0, step * chunk + c] * clean + mix[1, step * chunk + c] * noise
            noisy = noisy.astype(jnp.bfloat16).astype(jnp.float32)
            noisy_out[c] = noisy
            target_out[c] = noise
            start = dot(tap_stack(noisy, masks, 1), inlet[...], TN) + small[8:9]
            start_out[c] = start
            starts.append(start)
        yield
        mean, rstd = stats_of(starts)
        for i, c in enumerate(images):
            scale = rstd[i : i + 1] * small[0:1]
            z = starts[i] * scale + (small[4:5] - mean[i : i + 1] * scale)
            put_shifted(buf, c, z * logistic(z), not_first, not_last)
        yield
        inner_all = conv_shifted(buf.at[low:high], kernel_one)
        yield
        inners = []
        for i, c in enumerate(images):
            inner = inner_all[256 * i : 256 * i + 256] + tshift[pl.ds(step * chunk + c, 1), :]
            inner_out[c] = inner
            inners.append(inner)
        mean_two, rstd_two = stats_of(inners)
        for i, c in enumerate(images):
            stats_out[c] = jnp.concatenate(
                [mean[i : i + 1], rstd[i : i + 1], mean_two[i : i + 1], rstd_two[i : i + 1]]
                + [jnp.zeros((4, 256), jnp.float32)],
                axis=0,
            )

    take_turns([work(list(range(g, g + GROUP))) for g in range(0, chunk, GROUP)])


def norm_grad(dys, fields, means, rstds, gain):
    n = len(dys)
    shift_sums, gain_sums = [], []
    for dy, x, mean, rstd in zip(dys, fields, means, rstds):
        shift_sums.append(col_sum(dy))
        gain_sums.append(col_sum(dy * (x * rstd - mean * rstd)))
    both = group_sum(jnp.concatenate(shift_sums + gain_sums, axis=0) * gain) / COUNT
    grads = []
    for c in range(n):
        rstd, mean = rstds[c], means[c]
        slope = -rstd * rstd * both[n + c : n + c + 1]
        base = -rstd * both[c : c + 1] - mean * slope
        grads.append(dys[c] * (rstd * gain) + (fields[c] * slope + base))
    return grads, sum(gain_sums), sum(shift_sums)


def second_kernel(
    tall,
    short,
    coef,
    start_in,
    inner_in,
    stats_in,
    noisy,
    target,
    keep,
    kernel_one_flip,
    kernel_two,
    kernel_two_flip,
    qkv,
    qkv_t,
    proj,
    proj_t,
    outlet,
    small,
    bias_qkv,
    embed,
    hidden,
    hidden_slope,
    time_act,
    time_slope,
    time_weight,
    shift_weight,
    shard_out,
    rest_out,
    grad_one_out,
    grad_two_out,
    grad_qkv_out,
    grad_proj_out,
    grad_outlet_out,
    grad_inlet_out,
    grad_small_out,
    loss_out,
    tshift_grad,
    buf,
    grad_buf,
):
    chunk = noisy.shape[0]
    step = pl.program_id(0)
    sums = (
        grad_one_out,
        grad_two_out,
        grad_qkv_out,
        grad_proj_out,
        grad_outlet_out,
        grad_inlet_out,
        grad_small_out,
        loss_out,
    )

    @pl.when(step == 0)
    def _():
        zero_edges(buf)
        zero_edges(grad_buf)
        for ref in sums:
            ref[...] = jnp.zeros(ref.shape, jnp.float32)

    masks = tap_masks()
    not_first, not_last = edge_masks()
    scale = 256 ** (-0.5)

    def gain(k):
        return small[k : k + 1]

    def shift(k):
        return small[4 + k : 5 + k]

    def normed(x, mean, rstd, k):
        slope = rstd * gain(k)
        return x * slope + (shift(k) - mean * slope)

    def row(values, c):
        return values[c : c + 1]

    def work(images):
        n = len(images)
        every = range(n)
        low, high = images[0], images[-1] + 1

        def part(x, c):
            return x[256 * c : 256 * c + 256]

        slope_two, act_two = [], []
        for c in images:
            z = normed(inner_in[c], stats_in[c, 2:3], stats_in[c, 3:4], 1)
            s = logistic(z)
            kept = jnp.concatenate([keep[s, c] for s in range(keep.shape[0])], axis=0)
            kept = kept.astype(jnp.float32) * (1.0 / KEEP)
            act = z * s * kept
            slope_two.append(s * (1.0 + z * (1.0 - s)) * kept)
            act_two.append(act.astype(jnp.bfloat16))
            put_shifted(buf, c, act, not_first, not_last)
        yield
        conv_two = conv_shifted(buf.at[low:high], kernel_two)
        yield
        middle = [start_in[c] + part(conv_two, i) + small[10:11] for i, c in enumerate(images)]
        mean, rstd = stats_of(middle)
        mean_three, rstd_three = [row(mean, i) for i in every], [row(rstd, i) for i in every]
        tokens = [
            normed(middle[i], mean_three[i], rstd_three[i], 2).astype(jnp.bfloat16) for i in every
        ]
        tokens = jnp.concatenate(tokens, axis=0)
        yield
        qkv_all = (dot(tokens, qkv[...]) + bias_qkv[0:1]).astype(jnp.bfloat16)
        triples = []
        for i in every:
            three = part(qkv_all, i)
            triples.append((three[:, 0:256], three[:, 256:512], three[:, 512:768]))
        scores = [dot(q, k, NT) for q, k, _ in triples]
        yield
        probs, probs_low = [], []
        for i in every:
            expo = jnp.exp((scores[i] - jnp.max(scores[i], axis=1, keepdims=True)) * scale)
            p = expo * (1.0 / jnp.sum(expo, axis=1, keepdims=True))
            probs.append(p)
            probs_low.append(p.astype(jnp.bfloat16))
        yield
        mixed = [dot(probs_low[i], triples[i][2]).astype(jnp.bfloat16) for i in every]
        mixed = jnp.concatenate(mixed, axis=0)
        branch = dot(mixed, proj[...])
        yield
        final = [middle[i] + part(branch, i) + small[13:14] for i in every]
        mean, rstd = stats_of(final)
        mean_four, rstd_four = [row(mean, i) for i in every], [row(rstd, i) for i in every]
        act_four, slope_four = [], []
        for i in every:
            z = normed(final[i], mean_four[i], rstd_four[i], 3)
            s = logistic(z)
            act_four.append((z * s).astype(jnp.bfloat16))
            slope_four.append(s * (1.0 + z * (1.0 - s)))
        yield
        taps_all = [dot(outlet[...], act, NT) for act in act_four]
        yield
        spreads = []
        loss_sum = 0.0
        for i, c in enumerate(images):
            predicted = 0.0
            for tap in range(9):
                move = 16 * (tap // 3 - 1) + tap % 3 - 1
                moved = taps_all[i][8 * tap : 8 * tap + 8]
                moved = moved if move == 0 else pltpu.roll(moved, wrap(-move, 256), 1)
                predicted = predicted + jnp.where(masks[tap], moved, 0.0)
            error = predicted - target[c]
            weight = coef[step * chunk + c]
            loss_sum = loss_sum + (0.5 * weight) * (error * error)
            grad_pred = (weight * error).astype(jnp.bfloat16).astype(jnp.float32)
            spreads.append(tap_stack(grad_pred, masks, -1))
        loss_out[...] += loss_sum
        yield
        grad_outlet_out[...] += sum(dot(s, act) for s, act in zip(spreads, act_four))
        grad_act = [dot(s, outlet[...], TN) for s in spreads]
        yield
        grad_four = [grad_act[i] * slope_four[i] for i in every]
        grad_final, gain_four, shift_four = norm_grad(grad_four, final, mean_four, rstd_four, gain(3))
        branch_all = jnp.concatenate([g.astype(jnp.bfloat16) for g in grad_final], axis=0)
        yield
        grad_proj_out[...] += dot(mixed, branch_all, TN)
        grad_mixed = dot(branch_all, proj_t[...]).astype(jnp.bfloat16)
        dps = [dot(part(grad_mixed, i), triples[i][2], NT) for i in every]
        dvs = [dot(probs_low[i], part(grad_mixed, i), TN) for i in every]
        yield
        dss = []
        for i in every:
            p, dp = probs[i], dps[i]
            dss.append((p * (dp - jnp.sum(p * dp, axis=1, keepdims=True))).astype(jnp.bfloat16))
        yield
        grad_qkv = []
        for i in every:
            q, k, _ = triples[i]
            dq = dot(dss[i], k) * scale
            dk = dot(dss[i], q, TN) * scale
            grad_qkv.append(jnp.concatenate([dq, dk, dvs[i]], axis=1).astype(jnp.bfloat16))
        grad_qkv_all = jnp.concatenate(grad_qkv, axis=0)
        grad_qkv_out[...] += dot(tokens, grad_qkv_all, TN)
        grad_tokens = dot(grad_qkv_all, qkv_t[...])
        yield
        bias_sums = col_sum(grad_qkv_all.astype(jnp.float32))
        grad_norm, gain_three, shift_three = norm_grad(
            [part(grad_tokens, i) for i in every], middle, mean_three, rstd_three, gain(2)
        )
        grad_middle = [grad_final[i] + grad_norm[i] for i in every]
        for i, c in enumerate(images):
            put_shifted(grad_buf, c, grad_middle[i], not_first, not_last)
        yield
        field = jnp.concatenate(act_two, axis=0)
        for i in range(3):
            grad_two_out[i] += dot(field, stacked(grad_buf.at[low:high], i), TN)
        grad_act = conv_shifted(grad_buf.at[low:high], kernel_two_flip)
        yield
        grad_two = [part(grad_act, i) * slope_two[i] for i in every]
        grad_inner, gain_two, shift_two = norm_grad(
            grad_two,
            [inner_in[c] for c in images],
            [stats_in[c, 2:3] for c in images],
            [stats_in[c, 3:4] for c in images],
            gain(1),
        )
        for i, c in enumerate(images):
            put_shifted(grad_buf, c, grad_inner[i], not_first, not_last)
        act_one, slope_one = [], []
        for c in images:
            z = normed(start_in[c], stats_in[c, 0:1], stats_in[c, 1:2], 0)
            s = logistic(z)
            act_one.append((z * s).astype(jnp.bfloat16))
            slope_one.append(s * (1.0 + z * (1.0 - s)))
        yield
        field = jnp.concatenate(act_one, axis=0)
        for i in range(3):
            grad_one_out[i] += dot(field, stacked(grad_buf.at[low:high], i), TN)
        grad_act = conv_shifted(grad_buf.at[low:high], kernel_one_flip)
        yield
        grad_one = [part(grad_act, i) * slope_one[i] for i in every]
        grad_norm, gain_one, shift_one = norm_grad(
            grad_one,
            [start_in[c] for c in images],
            [stats_in[c, 0:1] for c in images],
            [stats_in[c, 1:2] for c in images],
            gain(0),
        )
        grad_start = [grad_middle[i] + grad_norm[i] for i in every]
        patches = [tap_stack(noisy[c], masks, 1) for c in images]
        inner_sums = [col_sum(g) for g in grad_inner]
        for i, c in enumerate(images):
            tshift_grad[pl.ds(step * chunk + c, 1), :] = inner_sums[i]
        grad_small_out[...] += jnp.concatenate(
            [
                gain_one,
                gain_two,
                gain_three,
                gain_four,
                shift_one,
                shift_two,
                shift_three,
                shift_four,
                sum(col_sum(g) for g in grad_start),
                sum(inner_sums),
                sum(col_sum(g) for g in grad_middle),
                bias_sums[:, 0:256],
                bias_sums[:, 512:768],
                sum(col_sum(g) for g in grad_final),
                jnp.zeros((2, 256), jnp.float32),
            ],
            axis=0,
        )
        yield
        grad_inlet_out[...] += sum(
            dot(patch, g.astype(jnp.bfloat16)) for patch, g in zip(patches, grad_start)
        )

    take_turns([work(list(range(g, g + GROUP))) for g in range(0, chunk, GROUP)])

    @pl.when(step == pl.num_programs(0) - 1)
    def _():
        for k, grad in enumerate((grad_one_out, grad_two_out)):
            for tap in range(9):
                at = 256 * (2 - tap % 3)
                for shard, off, row, size in cuts(tap * 256, 256, tall):
                    shard_out[shard, k * tall + off : k * tall + off + size, :] = grad[
                        2 - tap // 3, row : row + size, at : at + 256
                    ]
        for k in range(4):
            grad, at = (grad_qkv_out, 256 * k) if k < 3 else (grad_proj_out, 0)
            for shard, off, row, size in cuts(0, 256, short):
                low = 2 * tall + k * short + off
                shard_out[shard, low : low + size, :] = grad[row : row + size, at : at + 256]
        used = 2 * tall + 4 * short
        if used < shard_out.shape[1]:
            shard_out[:, used:, :] = jnp.zeros(
                (shard_out.shape[0], shard_out.shape[1] - used, 256), jnp.float32
            )
        total = tshift_grad[...]
        shift_grad = rows_dot(time_act[...], total)
        grad_act = back_dot(total, shift_weight[...].astype(jnp.bfloat16)) * time_slope[...]
        two_grad = rows_dot(hidden[...], grad_act)
        time_two = time_weight[embed.shape[1] :, :].astype(jnp.bfloat16)
        grad_hidden = back_dot(grad_act, time_two) * hidden_slope[...]
        one_grad = rows_dot(embed[...], grad_hidden)
        width = one_grad.shape[0]
        height = width + two_grad.shape[0]
        for half in range(2):
            span = slice(256 * half, 256 * half + 256)
            rest_out[half * height : half * height + width, :] = one_grad[:, span]
            rest_out[half * height + width : half * height + height, :] = two_grad[:, span]
        act_sum, hidden_sum = col_sum(grad_act), col_sum(grad_hidden)
        parts = [
            shift_grad,
            grad_inlet_out[...],
            grad_outlet_out[...],
            jnp.concatenate(
                [
                    grad_small_out[0:14],
                    col_sum(total),
                    hidden_sum[:, 0:256],
                    hidden_sum[:, 256:512],
                    act_sum[:, 0:256],
                    act_sum[:, 256:512],
                    jnp.zeros((5, 256), jnp.float32),
                ],
                axis=0,
            ),
            loss_out[...],
        ]
        at = 2 * height
        for part in parts:
            rest_out[at : at + part.shape[0], :] = part
            at += part.shape[0]
        if at < rest_out.shape[0]:
            rest_out[at:, :] = jnp.zeros((rest_out.shape[0] - at, 256), jnp.float32)


def cuts(first, size, height):
    parts, row = [], 0
    while row < size:
        shard, off = divmod(first + row, height)
        take = min(height - off, size - row)
        parts.append((shard, off, row, take))
        row += take
    return parts


def thirds(x):
    high = x.astype(jnp.bfloat16).astype(jnp.float32)
    middle = (x - high).astype(jnp.bfloat16).astype(jnp.float32)
    return jnp.concatenate([high, middle, x - high - middle], axis=0).astype(jnp.bfloat16)


def rows_dot(low, x):
    wide = low.astype(jnp.float32)
    return dot(jnp.concatenate([wide] * 3, axis=0).astype(jnp.bfloat16), thirds(x), TN)


def back_dot(x, weight):
    n = x.shape[0]
    parts = dot(thirds(x), weight, NT)
    return parts[0:n] + (parts[n : 2 * n] + parts[2 * n :])


def resident(shape):
    return pl.BlockSpec(shape, lambda i: (0,) * len(shape), pipeline_mode=pl.Buffered(1))


def per_chunk(chunk, *tail):
    return pl.BlockSpec((chunk,) + tail, lambda i: (i,) + (0,) * len(tail))


def by_source(chunk, block):
    return pl.BlockSpec((block[0], chunk) + block[2:], lambda i: (0, i, 0, 0))


def forward_part(chunk, mix, pair, embed, time_weight, shift_weight, inlet, kernel_one, small):
    n, deep = pair.shape[1], time_weight.shape[1]
    chunk = min(chunk, n)
    shapes = [(n, 256, 256), (n, 256, 256), (n, 8, 256), (n, 8, 256), (n, 8, 256)]
    whole = [jnp.bfloat16, jnp.float32, jnp.bfloat16, jnp.float32]
    return pl.pallas_call(
        first_kernel,
        grid=(n // chunk,),
        in_specs=[
            pl.BlockSpec(memory_space=pltpu.SMEM),
            by_source(chunk, pair.shape),
            resident(embed.shape),
            resident(time_weight.shape),
            resident(shift_weight.shape),
            resident(inlet.shape),
            resident(kernel_one.shape),
            resident(small.shape),
        ],
        out_specs=[per_chunk(chunk, *s[1:]) for s in shapes] + [resident((n, deep))] * 4,
        out_shape=[jax.ShapeDtypeStruct(s, jnp.float32) for s in shapes]
        + [jax.ShapeDtypeStruct((n, deep), kind) for kind in whole],
        scratch_shapes=[
            pltpu.VMEM((chunk, 288, 768), jnp.bfloat16),
            pltpu.VMEM((n, 256), jnp.float32),
        ],
        compiler_params=pltpu.CompilerParams(vmem_limit_bytes=VMEM_LIMIT),
        cost_estimate=pl.CostEstimate(
            flops=2 * n * 256 * 256 * 2400, bytes_accessed=n * 1 << 19, transcendentals=n * 1 << 16
        ),
        name="forward_part",
    )(mix, pair, embed, time_weight, shift_weight, inlet, kernel_one, small)


def main_part(chunk, sizes, coef, start, inner, stats, noisy, target, keep, weights, small, bias_qkv, times):
    n = noisy.shape[0]
    batch, shard_rows, tall, short, rest_rows = sizes
    outs = [(batch, shard_rows, 256), (rest_rows, 256)]
    sums = [(3, 256, 768), (3, 256, 768), (256, 768), (256, 256), (80, 256), (80, 256), (16, 256), (8, 256)]
    return pl.pallas_call(
        functools.partial(second_kernel, tall, short),
        grid=(n // chunk,),
        in_specs=[
            pl.BlockSpec(memory_space=pltpu.SMEM),
            per_chunk(chunk, 256, 256),
            per_chunk(chunk, 256, 256),
            per_chunk(chunk, 8, 256),
            per_chunk(chunk, 8, 256),
            per_chunk(chunk, 8, 256),
            by_source(chunk, keep.shape),
        ]
        + [resident(w.shape) for w in weights]
        + [resident(small.shape), resident(bias_qkv.shape)]
        + [resident(t.shape) for t in times],
        out_specs=[resident(g) for g in outs],
        out_shape=[jax.ShapeDtypeStruct(g, jnp.float32) for g in outs],
        scratch_shapes=[pltpu.VMEM(g, jnp.float32) for g in sums + [(n, 256)]]
        + [pltpu.VMEM((chunk, 288, 768), jnp.bfloat16)] * 2,
        compiler_params=pltpu.CompilerParams(vmem_limit_bytes=VMEM_LIMIT),
        cost_estimate=pl.CostEstimate(
            flops=70 * n * 2 * 256**3, bytes_accessed=n * 5 << 17, transcendentals=n * 5 << 16
        ),
        name="main_part",
    )(coef, start, inner, stats, noisy, target, keep, *weights, small, bias_qkv, *times)


def rows_first(weight):
    inputs, outputs = weight.shape[0] // 9, weight.shape[1]
    flipped = jnp.transpose(weight.reshape(9, inputs, outputs)[::-1], (0, 2, 1))
    return flipped.reshape(9 * outputs, inputs)


def padded_taps(rows):
    padded = jnp.pad(rows.reshape(9, 3, 256), ((0, 1), (0, 5), (0, 0)))
    return padded.reshape(80, 256)


MESH = pl.DeviceIdType.MESH
MISC_ROWS = (640, 640, 512, 80, 80, 24, 8)
MISC_TOTAL = 2048
SPLIT_A = 11
SPLIT_B = 4
LAG = 3


def padded_rows(total, parts):
    return -(-total // (8 * parts)) * 8


def factors(rows):
    low = max(d for d in range(1, rows + 1) if rows % d == 0 and d * d <= rows)
    return low, rows // low


def exchange_kernel(
    shard_shape,
    rates,
    grads_a,
    grads_b,
    state_kernel,
    state_attention,
    weight_kernel,
    weight_attention,
    scalars,
    out_a,
    out_b,
    shard_grad,
    norm_out,
    own_a,
    own_b,
    half_a,
    half_b,
    near_a,
    near_b,
    far_a,
    far_b,
    deep_a,
    deep_b,
    piece_a,
    piece_b,
    shard_weight,
    shard_first,
    shard_second,
    square_core,
    square_rows,
    square_deep,
    local_sem,
    own_sem,
    core_send,
    core_recv,
    near_send,
    near_recv,
    far_send,
    far_recv,
    deep_send,
    deep_recv,
    shard_send,
    shard_recv,
    square_send,
    square_recv,
    deep_send_two,
    deep_recv_two,
    near_send_two,
    near_recv_two,
    far_send_two,
    far_recv_two,
    core_send_two,
    core_recv_two,
    keep_sem,
):
    depth, _, tops, wide, piece, _ = grads_a.shape
    lanes = grads_b.shape[4]
    rows = tops * wide
    pairs, tall, quads, short = shard_shape
    batch, r = lax.axis_index("batch"), lax.axis_index("rows")
    z, c = batch // 2, batch % 2
    y, x = r // wide, r % wide
    partner = z * 2 + (1 - c)
    row_peers = [(r + d) % rows for d in range(1, rows)]
    deep_peers = [(z + d) % depth for d in range(1, depth)]
    x_peers = [(x + d) % wide for d in range(1, wide)]
    y_peers = [(y + d) % tops for d in range(1, tops)]

    def remote(src, dst, send, recv, where):
        return pltpu.make_async_remote_copy(
            src_ref=src, dst_ref=dst, send_sem=send, recv_sem=recv, device_id=where, device_id_type=MESH
        )

    def begin(copies):
        for copy in copies:
            copy.start()
        return copies

    def arrived(copies):
        for copy in copies:
            copy.wait_recv()

    def blocks(kernel_ref, attention_ref, flat, base, offset):
        copies = []
        for k in range(pairs + quads):
            ref, own, size = (kernel_ref, k, tall) if k < pairs else (attention_ref, k - pairs, short)
            at = k * tall if k < pairs else pairs * tall + own * short
            far = ref.at[own] if offset is None else ref.at[own, pl.ds(offset * size, size)]
            near = flat.at[pl.ds(at, size)]
            copies.append(pltpu.make_async_copy(far, near, local_sem.at[base * (pairs + quads) + k]))
        return begin(copies)

    owns = begin(
        [
            pltpu.make_async_copy(grads_b.at[:, c], own_b, own_sem.at[0]),
            pltpu.make_async_copy(grads_a.at[:, c], own_a, own_sem.at[1]),
        ]
    )

    barrier = pltpu.get_barrier_semaphore()
    pl.semaphore_signal(barrier, inc=1, device_id=(partner, r), device_id_type=MESH)
    for peer in row_peers:
        pl.semaphore_signal(barrier, inc=1, device_id=(batch, peer), device_id_type=MESH)
    for peer in deep_peers:
        pl.semaphore_signal(barrier, inc=1, device_id=(peer * 2 + c, r), device_id_type=MESH)
    pl.semaphore_wait(barrier, rows + depth - 1)

    set_a = (grads_a, own_a, half_a, near_a, far_a, deep_a, piece_a, out_a)
    set_b = (grads_b, own_b, half_b, near_b, far_b, deep_b, piece_b, out_b)
    chunks = []
    for group, height, parts in ((set_b, lanes, SPLIT_B), (set_a, piece, SPLIT_A)):
        marks = [height // 8 * k // parts * 8 for k in range(parts + 1)]
        for low, high in zip(marks[:-1], marks[1:]):
            if high > low:
                chunks.append(group + (low, high - low, len(chunks) % 2 == 0))
    count = len(chunks)
    small = sum(1 for chunk in chunks if chunk[0] is grads_b)

    core_copies = []
    for k, (grads, _, half, _, _, _, _, _, at, size, _) in enumerate(chunks):
        span = pl.ds(at, size)
        core_copies.append(
            begin(
                [
                    remote(
                        grads.at[:, 1 - c, :, :, span],
                        half.at[:, :, :, span],
                        core_send.at[k],
                        core_recv.at[k],
                        (partner, r),
                    )
                ]
            )
        )
    fetches = (
        blocks(weight_kernel, weight_attention, shard_weight, 0, batch)
        + blocks(state_kernel.at[0], state_attention.at[0], shard_first, 1, None)
        + blocks(state_kernel.at[1], state_attention.at[1], shard_second, 2, None)
    )
    near_copies, far_copies, deep_copies = [], [], []

    def sum_near(k):
        _, own, half, near, _, _, _, _, at, size, x_first = chunks[k]
        if k == 0:
            owns[0].wait()
        if k == small:
            owns[1].wait()
        arrived(core_copies[k])
        span = pl.ds(at, size)

        def add_own(t, carry):
            i, j, l = t // rows, t // wide % tops, t % wide
            half[i, j, l, span] = half[i, j, l, span] + own[i, j, l, span]
            return carry

        lax.fori_loop(0, depth * rows, add_own, 0)
        copies = []
        for d, peer in enumerate(x_peers if x_first else y_peers):
            src = half.at[:, :, peer, span] if x_first else half.at[:, peer, :, span]
            dst = near.at[d, :, pl.ds(0, tops if x_first else wide), span]
            where = (batch, y * wide + peer) if x_first else (batch, peer * wide + x)
            copies.append(remote(src, dst, near_send.at[k, d], near_recv.at[k, d], where))
        near_copies.append(begin(copies))

    def sum_far(k):
        _, _, half, near, far, _, _, _, at, size, x_first = chunks[k]
        arrived(near_copies[k])
        span = pl.ds(at, size)
        across = tops if x_first else wide

        def add_near(t, carry):
            i, j = t // across, t % across
            place = (i, j, x) if x_first else (i, y, j)
            total = half[place + (span,)]
            for d in range((wide if x_first else tops) - 1):
                total = total + near[d, i, j, span]
            half[place + (span,)] = total
            return carry

        lax.fori_loop(0, depth * across, add_near, 0)
        copies = []
        for d, peer in enumerate(y_peers if x_first else x_peers):
            src = half.at[:, peer, x, span] if x_first else half.at[:, y, peer, span]
            where = (batch, peer * wide + x) if x_first else (batch, y * wide + peer)
            copies.append(
                remote(src, far.at[d, :, span], far_send.at[k, d], far_recv.at[k, d], where)
            )
        far_copies.append(begin(copies))

    def sum_deep(k):
        _, _, half, _, far, deep, _, _, at, size, x_first = chunks[k]
        arrived(far_copies[k])
        span = pl.ds(at, size)

        def add_far(i, carry):
            total = half[i, y, x, span]
            for d in range((tops if x_first else wide) - 1):
                total = total + far[d, i, span]
            half[i, y, x, span] = total
            return carry

        lax.fori_loop(0, depth, add_far, 0)
        copies = []
        for d, peer in enumerate(deep_peers):
            copies.append(
                remote(
                    half.at[peer, y, x, span],
                    deep.at[d, span],
                    deep_send.at[k, d],
                    deep_recv.at[k, d],
                    (peer * 2 + c, r),
                )
            )
        deep_copies.append(begin(copies))

    def finish_sum(k):
        _, _, half, _, _, deep, _, _, at, size, _ = chunks[k]
        arrived(deep_copies[k])
        span = pl.ds(at, size)
        total = half[z, y, x, span]
        for d in range(depth - 1):
            total = total + deep[d, span]
        return total

    def squares(values):
        return jnp.sum((values * values).reshape(-1, 8, 256), axis=0)

    def gather_deep(k):
        _, _, _, _, _, _, part, out, at, size, _ = chunks[k]
        span = pl.ds(at, size)
        keep = pltpu.make_async_copy(part.at[span], out.at[z, c, y, x, span], keep_sem.at[k])
        keep.start()
        copies = []
        for d, peer in enumerate(deep_peers):
            copies.append(
                remote(
                    part.at[span],
                    out.at[z, c, y, x, span],
                    deep_send_two.at[k, d],
                    deep_recv_two.at[k, d],
                    (peer * 2 + c, r),
                )
            )
        return keep, begin(copies)

    def gather_near(k):
        _, _, _, _, _, _, _, out, at, size, x_first = chunks[k]
        place = out.at[:, c, y, x, pl.ds(at, size)]
        copies = []
        for d, peer in enumerate(y_peers if x_first else x_peers):
            where = (batch, peer * wide + x) if x_first else (batch, y * wide + peer)
            copies.append(remote(place, place, near_send_two.at[k, d], near_recv_two.at[k, d], where))
        return begin(copies)

    def gather_far(k):
        _, _, _, _, _, _, _, out, at, size, x_first = chunks[k]
        span = pl.ds(at, size)
        place = out.at[:, c, :, x, span] if x_first else out.at[:, c, y, :, span]
        copies = []
        for d, peer in enumerate(x_peers if x_first else y_peers):
            where = (batch, y * wide + peer) if x_first else (batch, peer * wide + x)
            copies.append(remote(place, place, far_send_two.at[k, d], far_recv_two.at[k, d], where))
        return begin(copies)

    def gather_core(k):
        _, _, _, _, _, _, _, out, at, size, _ = chunks[k]
        place = out.at[:, c, :, :, pl.ds(at, size)]
        return begin([remote(place, place, core_send_two.at[k], core_recv_two.at[k], (partner, r))])

    keeps, firsts, seconds, thirds, lasts = [], [], [], [], []
    partial = []

    def send_deep(k):
        keep, copies = gather_deep(k)
        keeps.append(keep)
        firsts.append(copies)

    def send_near(k):
        keeps[k].wait()
        arrived(firsts[k])
        seconds.append(gather_near(k))

    def send_far(k):
        arrived(seconds[k])
        thirds.append(gather_far(k))

    def send_core(k):
        arrived(thirds[k])
        lasts.append(gather_core(k))

    def sum_last(k):
        total = finish_sum(k)
        at, size = chunks[k][8], chunks[k][9]
        counted = total
        if k < small:
            piece_b[pl.ds(at, size)] = total
            line = (batch * rows + r) * lanes + at + lax.broadcasted_iota(jnp.int32, total.shape, 0)
            counted = jnp.where(line < sum(MISC_ROWS[:-1]), total, 0.0)
            send_deep(k)
        else:
            shard_grad[r, pl.ds(at, size)] = total
        partial.append(squares(counted))

    for t in range(count + 3 * LAG):
        for stage, lag in ((sum_near, 0), (sum_far, LAG), (sum_deep, 2 * LAG), (sum_last, 3 * LAG)):
            if 0 <= t - lag < count:
                stage(t - lag)
    square = sum(partial)
    square_core[0] = square
    square_copies = begin(
        [remote(square_core.at[0], square_core.at[1], square_send.at[0], square_recv.at[0], (partner, r))]
    )
    arrived(square_copies)
    square_rows[r] = square_core[0] + square_core[1]
    copies = begin(
        [
            remote(
                square_rows.at[r],
                square_rows.at[r],
                square_send.at[1 + d],
                square_recv.at[1 + d],
                (batch, peer),
            )
            for d, peer in enumerate(row_peers)
        ]
    )
    shard_copies = begin(
        [
            remote(shard_grad.at[r], shard_grad.at[r], shard_send.at[d], shard_recv.at[d], (batch, peer))
            for d, peer in enumerate(row_peers)
        ]
    )
    for k in range(small):
        send_near(k)
    arrived(copies)
    square_copies += copies
    square_deep[z] = sum(square_rows[j] for j in range(rows))
    copies = begin(
        [
            remote(
                square_deep.at[z],
                square_deep.at[z],
                square_send.at[rows + d],
                square_recv.at[rows + d],
                (peer * 2 + c, r),
            )
            for d, peer in enumerate(deep_peers)
        ]
    )
    for fetch in fetches:
        fetch.wait()
    for k in range(small):
        send_far(k)
    arrived(copies)
    square_copies += copies
    square = sum(square_deep[j] for j in range(depth))
    norm = jnp.sqrt(jnp.sum(jnp.sum(square, axis=0, keepdims=True), axis=1, keepdims=True))
    clip = CLIP / jnp.maximum(norm, CLIP)
    norm_out[...] = jnp.broadcast_to(norm, norm_out.shape)
    for k in range(small, count):
        at, size = chunks[k][8], chunks[k][9]
        span = pl.ds(pl.multiple_of(r * piece + at, 8), size)
        g = shard_grad[r, pl.ds(at, size)] * clip
        first = BETA_ONE * shard_first[span] + (1.0 - BETA_ONE) * g
        second = BETA_TWO * shard_second[span] + (1.0 - BETA_TWO) * g * g
        line = r * piece + at + lax.broadcasted_iota(jnp.int32, g.shape, 0)
        rate = jnp.where(line < pairs * tall, rates[0], rates[1])
        weight = shard_weight[span]
        step = first * scalars[0] / (jnp.sqrt(second * scalars[1]) + EPS_ADAM)
        piece_a[pl.ds(at, size)] = weight - rate * (step + DECAY * weight)
        send_deep(k)
    for k in range(small):
        send_core(k)
    for t in range(small, count + 2 * LAG):
        for stage, lag in ((send_near, 0), (send_far, LAG), (send_core, 2 * LAG)):
            if small <= t - lag < count:
                stage(t - lag)
    arrived(shard_copies)
    for copies in lasts:
        arrived(copies)
    for copies in (
        core_copies + near_copies + far_copies + deep_copies + firsts + seconds + thirds + lasts
    ):
        for copy in copies:
            copy.wait_send()
    for copy in square_copies + shard_copies:
        copy.wait_send()


def exchange(grads_a, grads_b, state_kernel, state_attention, weight_kernel, weight_attention, scalars):
    depth, _, rows, piece, width = grads_a.shape
    tops, wide = factors(rows)
    lanes = grads_b.shape[3]
    grads_a = grads_a.reshape(depth, 2, tops, wide, piece, width)
    grads_b = grads_b.reshape(depth, 2, tops, wide, lanes, width)
    pairs, tall = state_kernel.shape[1:3]
    quads, short = state_attention.shape[1:3]
    shape = functools.partial(jax.ShapeDtypeStruct, dtype=jnp.float32)
    whole = pl.BlockSpec(memory_space=pltpu.VMEM)
    anywhere = pl.BlockSpec(memory_space=pl.ANY)
    dma = pltpu.SemaphoreType.DMA
    vmem = functools.partial(pltpu.VMEM, dtype=jnp.float32)
    most = max(tops, wide)
    return pl.pallas_call(
        functools.partial(exchange_kernel, (pairs, tall, quads, short), (RATES[1], RATES[2])),
        in_specs=[anywhere] * 6 + [pl.BlockSpec(memory_space=pltpu.SMEM)],
        out_specs=[anywhere] * 2 + [whole] * 2,
        out_shape=[
            shape(grads_a.shape),
            shape(grads_b.shape),
            shape((rows, piece, width)),
            shape((8, 128)),
        ],
        scratch_shapes=[
            vmem((depth, tops, wide, piece, width)),
            vmem((depth, tops, wide, lanes, width)),
            vmem((depth, tops, wide, piece, width)),
            vmem((depth, tops, wide, lanes, width)),
            vmem((most - 1, depth, most, piece, width)),
            vmem((most - 1, depth, most, lanes, width)),
            vmem((most - 1, depth, piece, width)),
            vmem((most - 1, depth, lanes, width)),
            vmem((depth - 1, piece, width)),
            vmem((depth - 1, lanes, width)),
            vmem((piece, width)),
            vmem((lanes, width)),
            vmem((rows * piece, width)),
            vmem((rows * piece, width)),
            vmem((rows * piece, width)),
            vmem((2, 8, width)),
            vmem((rows, 8, width)),
            vmem((depth, 8, width)),
            dma((3 * (pairs + quads),)),
            dma((2,)),
            dma((SPLIT_A + SPLIT_B,)),
            dma((SPLIT_A + SPLIT_B,)),
            dma((SPLIT_A + SPLIT_B, most - 1)),
            dma((SPLIT_A + SPLIT_B, most - 1)),
            dma((SPLIT_A + SPLIT_B, most - 1)),
            dma((SPLIT_A + SPLIT_B, most - 1)),
            dma((SPLIT_A + SPLIT_B, depth - 1)),
            dma((SPLIT_A + SPLIT_B, depth - 1)),
            dma((rows - 1,)),
            dma((rows - 1,)),
            dma((rows + depth - 1,)),
            dma((rows + depth - 1,)),
            dma((SPLIT_A + SPLIT_B, depth - 1)),
            dma((SPLIT_A + SPLIT_B, depth - 1)),
            dma((SPLIT_A + SPLIT_B, most - 1)),
            dma((SPLIT_A + SPLIT_B, most - 1)),
            dma((SPLIT_A + SPLIT_B, most - 1)),
            dma((SPLIT_A + SPLIT_B, most - 1)),
            dma((SPLIT_A + SPLIT_B,)),
            dma((SPLIT_A + SPLIT_B,)),
            dma((SPLIT_A + SPLIT_B,)),
        ],
        compiler_params=pltpu.CompilerParams(
            collective_id=0, has_side_effects=True, vmem_limit_bytes=VMEM_LIMIT
        ),
        name="exchange",
    )(grads_a, grads_b, state_kernel, state_attention, weight_kernel, weight_attention, scalars)


def finish_kernel(
    scalars,
    norm_tile,
    fresh,
    average_kernel,
    average_attention,
    shard_grad,
    state_kernel,
    state_attention,
    time_left,
    time_right,
    shift_rows,
    rest_rows,
    *refs,
):
    weights, states, averages, refs = refs[:5], refs[5:10], refs[10:15], refs[15:]
    (kernel_out, attention_out), refs = refs[:2], refs[2:]
    updated, firsts, seconds, refs = refs[:5], refs[5:10], refs[10:15], refs[15:]
    first_kernel_out, first_attention_out, second_kernel_out, second_attention_out, loss_out, norm_out = refs
    norm = norm_tile[0:1, 0:1]
    clip = CLIP / jnp.maximum(norm, CLIP)
    kept = scalars[2]

    def averaged(out, index, new, average):
        out[(0,) + index] = new
        out[(1,) + index] = kept * average + (1.0 - kept) * new

    tall, short = state_kernel.shape[2], state_attention.shape[2]
    for i in range(fresh.shape[0]):
        for k in range(2):
            place = (k, slice(i * tall, i * tall + tall))
            averaged(kernel_out, place, fresh[i, k * tall : k * tall + tall], average_kernel[place])
        for k in range(4):
            place = (k, slice(i * short, i * short + short))
            at = 2 * tall + k * short
            averaged(attention_out, place, fresh[i, at : at + short], average_attention[place])

    def moments(first, second, g):
        return BETA_ONE * first + (1.0 - BETA_ONE) * g, BETA_TWO * second + (1.0 - BETA_TWO) * g * g

    def update(k, rate, grad):
        weight = weights[k][...]
        old = (states[k][0], states[k][1]) if k < 2 else (states[k][:, 0, :], states[k][:, 1, :])
        first, second = moments(*old, grad * clip)
        firsts[k][...] = first
        seconds[k][...] = second
        step = first * scalars[0] / (jnp.sqrt(second * scalars[1]) + EPS_ADAM)
        new = weight - rate * (step + DECAY * weight)
        if k < 2:
            averaged(updated[k], (), new, averages[k][...])
        else:
            updated[k][:, 0, :] = new
            updated[k][:, 1, :] = kept * averages[k][...] + (1.0 - kept) * new

    update(0, RATES[3], jnp.concatenate([time_left[...], time_right[...]], axis=1))
    update(1, RATES[4], shift_rows[...])

    @pl.when(pl.program_id(0) == 0)
    def _():
        for refs, outs, count, height in (
            (state_kernel, (first_kernel_out, second_kernel_out), 2, tall),
            (state_attention, (first_attention_out, second_attention_out), 4, short),
        ):
            for k in range(count):
                at = k * height + (0 if count == 2 else 2 * tall)
                first, second = moments(refs[0, k], refs[1, k], shard_grad[at : at + height] * clip)
                outs[0][k] = first
                outs[1][k] = second
        inlet = jnp.concatenate([rest_rows[8 * tap : 8 * tap + 3] for tap in range(9)], axis=0)
        outlet = jnp.concatenate([rest_rows[80 + 8 * tap : 83 + 8 * tap] for tap in range(9)], axis=1)
        update(2, RATES[0], inlet)
        update(3, RATES[5], outlet)
        update(4, RATES[6], rest_rows[160:179])
        loss_out[...] = jnp.sum(col_sum(rest_rows[184:192]), axis=1, keepdims=True)
        norm_out[...] = norm


def finish(scalars, norm_tile, fresh, average_kernel, average_attention, shard_grad, state_kernel, state_attention, rest, weights, states, averages):
    batch, shard_rows, width = fresh.shape
    tall, short = state_kernel.shape[2], state_attention.shape[2]
    (time_rows, time_width), (shift_rows, _) = weights[0].shape, weights[1].shape
    steps = batch // SHARDS
    time_part, shift_part = time_rows // steps, shift_rows // steps
    shape = functools.partial(jax.ShapeDtypeStruct, dtype=jnp.float32)

    def at(block, index):
        return pl.BlockSpec(block, index)

    def rows_of(k, lead):
        part, wide = ((time_part, time_width), (shift_part, width))[k]
        return pl.BlockSpec(lead + (part, wide), lambda b: (0,) * len(lead) + (b, 0))

    def five(lead):
        small = [w.shape[:1] + lead + w.shape[1:] for w in weights[2:]]
        return [rows_of(0, lead), rows_of(1, lead)] + [resident(block) for block in small]

    shift_at = 2 * time_rows // shift_part
    rest_at = (2 * time_rows + shift_rows) // 256
    return pl.pallas_call(
        finish_kernel,
        grid=(steps,),
        in_specs=[
            pl.BlockSpec(memory_space=pltpu.SMEM),
            resident(norm_tile.shape),
            at((SHARDS, shard_rows, width), lambda b: (b, 0, 0)),
            at((2, SHARDS * tall, width), lambda b: (0, b, 0)),
            at((4, SHARDS * short, width), lambda b: (0, b, 0)),
            resident(shard_grad.shape),
            resident(state_kernel.shape),
            resident(state_attention.shape),
            at((time_part, width), lambda b: (b, 0)),
            at((time_part, width), lambda b: (steps + b, 0)),
            at((shift_part, width), lambda b: (shift_at + b, 0)),
            pl.BlockSpec((256, width), lambda b: (rest_at, 0), pipeline_mode=pl.Buffered(1)),
        ]
        + five(())
        + five((2,))
        + five(()),
        out_specs=[
            at((2, 2, SHARDS * tall, width), lambda b: (0, 0, b, 0)),
            at((2, 4, SHARDS * short, width), lambda b: (0, 0, b, 0)),
        ]
        + five((2,))
        + five(())
        + five(())
        + [resident(state_kernel.shape[1:]), resident(state_attention.shape[1:])] * 2
        + [resident((1, 1))] * 2,
        out_shape=[
            shape((2, 2, batch * tall, width)),
            shape((2, 4, batch * short, width)),
        ]
        + [shape((2,) + w.shape) for w in weights[:2]]
        + [shape((w.shape[0], 2, w.shape[1])) for w in weights[2:]]
        + [shape(w.shape) for w in weights] * 2
        + [shape(state_kernel.shape[1:]), shape(state_attention.shape[1:])] * 2
        + [shape((1, 1))] * 2,
        compiler_params=pltpu.CompilerParams(vmem_limit_bytes=VMEM_LIMIT),
        cost_estimate=pl.CostEstimate(flops=40 << 20, bytes_accessed=36 << 20, transcendentals=1 << 20),
        name="finish",
    )(
        scalars,
        norm_tile,
        fresh,
        average_kernel,
        average_attention,
        shard_grad,
        state_kernel,
        state_attention,
        rest,
        rest,
        rest,
        rest,
        *weights,
        *states,
        *averages,
    )


def local(
    x_clean,
    noise,
    timesteps,
    keep_mask,
    adam_step,
    inlet_weight,
    kernel_weight,
    attention_weight,
    time_weight,
    shift_weight,
    outlet_weight,
    small_params,
    state_inlet,
    state_kernel,
    state_attention,
    state_time,
    state_shift,
    state_outlet,
    state_small,
    average_inlet,
    average_kernel,
    average_attention,
    average_time,
    average_shift,
    average_outlet,
    average_small,
):
    chans = kernel_weight.shape[2]
    width_sin = time_weight.shape[0] - time_weight.shape[1]
    rows, batch = lax.axis_size("rows"), lax.axis_size("batch")
    own = timesteps.shape[0] // rows
    keep = keep_mask.reshape(rows, own, -1, chans).astype(jnp.bfloat16)
    keep, timesteps, x_clean, noise = lax.optimization_barrier((keep, timesteps, x_clean, noise))
    keep = lax.all_to_all(keep, "rows", 0, 0, tiled=True)
    halves = [a.reshape(rows, own, 3, -1) for a in (x_clean, noise)]
    pair = jnp.pad(jnp.concatenate(halves, axis=3), ((0, 0), (0, 0), (0, 1), (0, 0)))
    here = lax.axis_index("rows")
    parts = [lax.dynamic_index_in_dim(pair, here, 0, keepdims=False)]
    for d in range(1, rows):
        block = lax.dynamic_index_in_dim(pair, (here + d) % rows, 0, keepdims=False)
        parts.append(lax.ppermute(block, "rows", [(i, (i + d) % rows) for i in range(rows)]))
    steps = ((here - jnp.arange(rows)) % rows)[:, None, None, None]
    pair = jnp.broadcast_to(parts[0], (rows,) + parts[0].shape)
    for d in range(1, rows):
        pair = jnp.where(steps == d, parts[d], pair)
    pair, inlet_low, kernels, projections, outlet_low = lax.optimization_barrier(
        (pair, inlet_weight, kernel_weight, attention_weight, outlet_weight)
    )
    timesteps = lax.dynamic_slice_in_dim(timesteps, lax.axis_index("rows") * own, own, 0)
    bars = alpha_bars(timesteps)
    mix = jnp.stack([jnp.sqrt(bars), jnp.sqrt(1.0 - bars)])
    kernels = kernels.astype(jnp.bfloat16)
    projections = projections.astype(jnp.bfloat16)
    inlet = padded_taps(inlet_low).astype(jnp.bfloat16)
    outlet = padded_taps(
        jnp.transpose(outlet_low.reshape(3, 9, chans), (1, 0, 2)).reshape(27, chans)
    ).astype(jnp.bfloat16)
    qkv = jnp.concatenate([projections[0], projections[1], projections[2]], axis=1)
    embed = sinusoid(timesteps, width_sin).astype(jnp.bfloat16)
    ratio = bars / (1.0 - bars)
    snr_weight = jnp.minimum(ratio, GAMMA) / ratio
    denom = 3 * 256 * own * rows * batch
    coef = 2.0 * snr_weight / denom
    start, inner, stats, noisy, target, hidden, hidden_slope, time_act, time_slope = forward_part(
        FORWARD_CHUNK, mix, pair, embed, time_weight, shift_weight, inlet, kernels[0], small_params
    )
    bias_qkv = jnp.concatenate(
        [small_params[11], jnp.zeros_like(small_params[0]), small_params[12]]
    )
    tall, short = state_kernel.shape[2], state_attention.shape[2]
    shard_rows = rows * padded_rows(2 * tall + 4 * short, rows)
    lanes = padded_rows(MISC_TOTAL, batch * rows)
    shards, rest = main_part(
        CHUNK,
        (batch, shard_rows, tall, short, batch * rows * lanes),
        coef,
        start,
        inner,
        stats,
        noisy,
        target,
        keep,
        (
            rows_first(kernels[0]),
            kernels[1],
            rows_first(kernels[1]),
            qkv,
            qkv.T,
            projections[3],
            projections[3].T,
            outlet,
        ),
        small_params,
        bias_qkv[None],
        (embed, hidden, hidden_slope, time_act, time_slope, time_weight, shift_weight),
    )
    count = adam_step[0].astype(jnp.float32)
    scalars = jnp.stack(
        [
            1.0 / (1.0 - BETA_ONE**count),
            1.0 / (1.0 - BETA_TWO**count),
            jnp.minimum(EMA_TOP, (1.0 + count) / (10.0 + count)),
        ]
    )
    fresh, rest, shard_grad, norm_tile = exchange(
        shards.reshape(batch // 2, 2, rows, shard_rows // rows, chans),
        rest.reshape(batch // 2, 2, rows, lanes, chans),
        state_kernel,
        state_attention,
        kernel_weight,
        attention_weight,
        scalars,
    )
    results = finish(
        scalars,
        norm_tile,
        fresh.reshape(batch, shard_rows, chans),
        lax.all_gather(average_kernel, "batch", axis=1, tiled=True),
        lax.all_gather(average_attention, "batch", axis=1, tiled=True),
        shard_grad.reshape(shard_rows, chans),
        state_kernel,
        state_attention,
        rest.reshape(-1, chans),
        (time_weight, shift_weight, inlet_weight, outlet_weight, small_params),
        (state_time, state_shift)
        + tuple(jnp.transpose(a, (1, 0, 2)) for a in (state_inlet, state_outlet, state_small)),
        (average_time, average_shift, average_inlet, average_outlet, average_small),
    )
    kernel_pair, attention_pair = results[:2]
    triples = [list(results[2 + 5 * k : 7 + 5 * k]) for k in range(3)]
    triples[0][2:] = [jnp.transpose(a, (1, 0, 2)) for a in triples[0][2:]]
    first_conv, first_attention, second_conv, second_attention, loss, norm = results[17:]
    ordered = []
    for (time, shift, inlet, outlet, small), middle in zip(
        triples,
        ((kernel_pair, attention_pair), (first_conv, first_attention), (second_conv, second_attention)),
    ):
        ordered += [inlet, *middle, time, shift, outlet, small]
    return (*ordered, loss.reshape(()), norm.reshape(()))


def solution(mesh):
    return jax.shard_map(
        local,
        mesh=mesh,
        in_specs=(
            P("batch", None, "rows", None),
            P("batch", None, "rows", None),
            P("batch"),
            P("batch", "rows", None, None),
            P(),
            P(),
            P(),
            P(),
            P(),
            P(),
            P(),
            P(),
            P(),
            P(None, None, "batch", None),
            P(None, None, "batch", None),
            P(),
            P(),
            P(),
            P(),
            P(),
            P(None, "batch", None),
            P(None, "batch", None),
            P(),
            P(),
            P(),
            P(),
        ),
        out_specs=(
            P(),
            P(),
            P(),
            P(),
            P(),
            P(),
            P(),
            P(),
            P(None, "batch", None),
            P(None, "batch", None),
            P(),
            P(),
            P(),
            P(),
            P(),
            P(None, "batch", None),
            P(None, "batch", None),
            P(),
            P(),
            P(),
            P(),
            P(),
            P(),
        ),
        check_vma=False,
    )
```
